32 devices in a mesh: groups: 2 (over y), seq: 4 (over x, core), chan: 4 (over z).
Axes of the slice: x: 2, y: 2, z: 4, core: 2. Of those that a mesh axis runs over, the one named last changes fastest.
Arguments:
- tokens: bfloat16 [4096, 4096], P(('groups', 'seq'), 'chan'), parts along dimension 0, may hold values from -6 to 6
- norm_gain: float32 [4096], replicated, may hold values from 0.5 to 1.5
- proj_weight: bfloat16 [4096, 3, 4096], P('seq', None, 'chan'), may hold values from -0.09375 to 0.09375
- short_filter: float32 [3, 3, 4096], P(None, None, 'chan'), may hold values from -2.5 to 2.5
- long_filter: float32 [4096, 2048], P('chan', 'seq'), may hold values from -4 to 4, as said below
- skip_gain: float32 [4096], P('chan'), may hold values from 0.5 to 1.5
- out_weight: bfloat16 [4096, 4096], P(None, 'chan'), may hold values from -0.09375 to 0.09375
Outputs:
- block_out: bfloat16 [4096, 4096], P(('groups', 'seq'), 'chan'), parts along dimension 0
The draws below stay inside these ranges and needn't reach their ends.
There are 2 independent parts, one for each index of `groups`. The reference program is written for one: setup_inputs(seed, part) draws one part's arguments, and reference() takes and returns one part's arrays. A program takes and returns all parts, laid end to end along the dimension named above; an argument that names none is the same for every part. Nothing has to cross between parts.
Inputs may be any that keep to these rules, and one draw needn't show every extreme that they name: `long_filter`: filter taps of the sequence-long convolution.
All inputs are finite; a program needn't handle non-finite values.
Results may differ from the reference program's by a relative error of at most 0.012.
Values may be sent and summed in bfloat16 or wider, within the bound.
A program may use at most 128 MiB of HBM per device.

```python
import jax
import jax.numpy as jnp
from jax import lax

D = 4096
SHORT = 3
SEQ = 2048


def draw_long_filter(key, part):
    streams = jax.random.split(jax.random.fold_in(key, 17), 6)
    length = SEQ
    sequence_indices = jnp.arange(length, dtype=jnp.float32)
    fast_pick = jax.random.uniform(streams[0], (D,)) < 0.5
    fast_rate = jnp.exp(jax.random.uniform(streams[1], (D,), jnp.float32, jnp.log(1.0 / 50.0), jnp.log(1.0 / 30.0)))
    slow_rate = jnp.exp(jax.random.uniform(streams[2], (D,), jnp.float32, jnp.log(0.1 / length), jnp.log(2.0 / length)))
    attenuation_speeds = jnp.where(fast_pick, fast_rate, slow_rate)
    places = jax.random.randint(streams[3], (4,), 1, length)
    discarded_values = jax.random.uniform(streams[4], (D, 4), jnp.float32, 0.5, 0.8)
    successor_index = (sequence_indices[None, :] >= places[:, None].astype(jnp.float32)).astype(jnp.float32)
    sparse_impulse_list = jnp.exp(jnp.dot(jnp.log(discarded_values), successor_index))
    fading_profile = jnp.exp(-attenuation_speeds[:, None] * sequence_indices[None, :]) * sparse_impulse_list
    amplitude = lax.rsqrt(jnp.sum(fading_profile * fading_profile, axis=1))
    noise = jnp.clip(jax.random.normal(streams[5], (D, length), jnp.float32), -4.0, 4.0)
    return (noise * fading_profile * amplitude[:, None]).astype(jnp.float32)


def shard_levels(rng, shape, shards, smallest, high):
    gain = 1.0
    for axis_at, shards_of in shards:
        heights = jax.random.uniform(jax.random.fold_in(jax.random.fold_in(rng, 6), axis_at), (shards_of,), jnp.float32, smallest / len(shards), high / len(shards))
        gain = gain * jnp.repeat(jnp.exp(heights), shape[axis_at] // shards_of).reshape((-1,) + (1,) * (len(shape) - 1 - axis_at))
    return gain


def scatter_about(key, dims, deviation, limit, cuts=(), kind=jnp.bfloat16):
    factor_of = shard_levels(key, dims, cuts, -0.22, 0.18) if cuts else 1.0
    entries = jax.random.normal(key, dims, jnp.float32) * deviation * factor_of
    return jnp.minimum(jnp.maximum(entries, -limit), limit).astype(kind)


def setup_inputs(seed: int = 0, part: int = 0) -> dict:
    streams_of = jax.random.split(jax.random.key(seed), 8)
    own_keys = jax.random.split(jax.random.fold_in(streams_of[7], part), 8)
    return {
        "tokens": scatter_about(own_keys[0], (SEQ, D), 1.0, 6.0, ((0, 4), (1, 4))),
        "norm_gain": jnp.clip(1.0 + 0.1 * jax.random.normal(streams_of[1], (D,), jnp.float32), 0.5, 1.5),
        "proj_weight": scatter_about(streams_of[2], (D, 3, D), D ** -0.5, 0.09375, ((0, 4), (2, 4))),
        "short_filter": scatter_about(streams_of[3], (SHORT, 3, D), 0.6, 2.5, ((2, 4),), jnp.float32),
        "long_filter": draw_long_filter(jax.random.fold_in(streams_of[7], 71), part),
        "skip_gain": jnp.clip(0.5 + 1.0 * jax.random.uniform(streams_of[5], (D,), jnp.float32) ** shard_levels(streams_of[5], (D,), ((0, 4),), -0.2, 0.2), 0.5, 1.5),
        "out_weight": scatter_about(streams_of[6], (D, D), D ** -0.5, 0.09375, ((1, 4),)),
    }


def causal_conv(signal_rows, filter_rows):
    channels, length = signal_rows.shape
    padded_len = 2 * length
    block = 256

    def one_block(pair):
        sig_block, tap_block = pair
        spec_sig = jnp.fft.rfft(sig_block, n=padded_len, axis=1)
        spec_tap = jnp.fft.rfft(tap_block, n=padded_len, axis=1)
        return jnp.fft.irfft(spec_sig * spec_tap, n=padded_len, axis=1)[:, :length]
    outcome = lax.map(one_block, (signal_rows.reshape(channels // block, block, length), filter_rows.reshape(channels // block, block, filter_rows.shape[1])))
    return outcome.reshape(channels, length)

def reference(tokens, norm_gain, proj_weight, short_filter, long_filter, skip_gain, out_weight):
    wide = tokens.astype(jnp.float32)
    rescaled_signal = (wide * lax.rsqrt(lax.optimization_barrier(jnp.mean(wide * wide, axis=1, keepdims=True)) + 1e-06) * norm_gain).astype(jnp.bfloat16)
    projected = jnp.dot(rescaled_signal, proj_weight.reshape(D, 3 * D), preferred_element_type=jnp.float32)
    projected = projected.astype(jnp.bfloat16).reshape(SEQ, 3, D)
    padded = jnp.pad(projected.astype(jnp.float32), ((SHORT - 1, 0), (0, 0), (0, 0)))
    featured = jnp.zeros((SEQ, 3, D), jnp.float32)
    for tap in range(SHORT):
        featured = featured + short_filter[tap][None, :, :] * padded[SHORT - 1 - tap:SHORT - 1 - tap + SEQ]
    featured = featured.astype(jnp.bfloat16)
    branches = jnp.transpose(featured, (1, 2, 0))
    query = branches[0].astype(jnp.float32)
    keys_rows = branches[1].astype(jnp.float32)
    values_rows = branches[2].astype(jnp.float32)
    middle = keys_rows * values_rows
    longer = (causal_conv(middle, long_filter) + skip_gain[:, None] * middle).astype(jnp.bfloat16)
    gated = (query * longer.astype(jnp.float32)).astype(jnp.bfloat16)
    update = lax.dot_general(gated, out_weight, (((0,), (0,)), ((), ())), preferred_element_type=jnp.float32)
    return (wide + update).astype(jnp.bfloat16)
```

```python
import functools
import math

import jax
import jax.numpy as jnp
import numpy as np
from jax import lax
from jax.experimental import pallas as pl
from jax.experimental.pallas import tpu as pltpu
from jax.sharding import PartitionSpec as P

SHORT = 3


EPSILON = 1e-06
HIGHEST = lax.Precision.HIGHEST


def from_behind(value, axis, steps):
    count = lax.axis_size(axis)
    initial, last = (max(0, -steps), min(count, count - steps))
    return lax.ppermute(value, axis, [(source, source + steps) for source in range(initial, last)])


def angle_table(row_count, col_count, period, sign):
    row_index = lax.iota(jnp.int32, row_count)[:, None]
    col_index = lax.iota(jnp.int32, col_count)[None, :]
    angles = (row_index * col_index % period).astype(jnp.float32) * (sign * 2.0 * math.pi / period)
    return (jnp.cos(angles), jnp.sin(angles))


def forward_spectrum(signal_rows, first, second):
    channels = signal_rows.shape[0]
    grid_rows = signal_rows.reshape(channels, first, second)
    cos_first, sin_first = angle_table(first, first, first, -1.0)
    part_re = jnp.einsum("cab,ak->ckb", grid_rows, cos_first, precision=HIGHEST)
    part_im = jnp.einsum("cab,ak->ckb", grid_rows, sin_first, precision=HIGHEST)
    twist_cos, twist_sin = angle_table(first, second, first * second, -1.0)
    part_re, part_im = (
        part_re * twist_cos - part_im * twist_sin,
        part_re * twist_sin + part_im * twist_cos,
    )
    cos_second, sin_second = angle_table(second, second, second, -1.0)
    spectrum_real = jnp.einsum("ckb,bm->ckm", part_re, cos_second, precision=HIGHEST) - jnp.einsum(
        "ckb,bm->ckm", part_im, sin_second, precision=HIGHEST
    )
    spec_im = jnp.einsum("ckb,bm->ckm", part_re, sin_second, precision=HIGHEST) + jnp.einsum(
        "ckb,bm->ckm", part_im, cos_second, precision=HIGHEST
    )
    return (spectrum_real, spec_im)


def inverse_spectrum(spectrum_real, spec_im, first, second):
    channels = spectrum_real.shape[0]
    cos_second, sin_second = angle_table(second, second, second, 1.0)
    part_re = jnp.einsum("ckm,bm->ckb", spectrum_real, cos_second, precision=HIGHEST) - jnp.einsum(
        "ckm,bm->ckb", spec_im, sin_second, precision=HIGHEST
    )
    part_im = jnp.einsum("ckm,bm->ckb", spectrum_real, sin_second, precision=HIGHEST) + jnp.einsum(
        "ckm,bm->ckb", spec_im, cos_second, precision=HIGHEST
    )
    twist_cos, twist_sin = angle_table(first, second, first * second, 1.0)
    part_re, part_im = (
        part_re * twist_cos - part_im * twist_sin,
        part_re * twist_sin + part_im * twist_cos,
    )
    cos_first, sin_first = angle_table(first, first, first, 1.0)
    result = jnp.einsum("ckb,ak->cab", part_re, cos_first, precision=HIGHEST) - jnp.einsum(
        "ckb,ak->cab", part_im, sin_first, precision=HIGHEST
    )
    return result.reshape(channels, first * second) / (first * second)


def spectral_conv(signal_rows, filter_rows):
    channels, length = signal_rows.shape
    padded_len = 2 * length
    log_len = padded_len.bit_length() - 1
    first = 1 << log_len // 2
    second = padded_len // first
    zeros_tail = jnp.zeros((channels, length), jnp.float32)
    sig_re, sig_im = forward_spectrum(
        jnp.concatenate([signal_rows, zeros_tail], axis=1), first, second
    )
    tap_re, tap_im = forward_spectrum(
        jnp.concatenate([filter_rows, zeros_tail], axis=1), first, second
    )
    prod_re = sig_re * tap_re - sig_im * tap_im
    prod_im = sig_re * tap_im + sig_im * tap_re
    return inverse_spectrum(prod_re, prod_im, first, second)[:, :length]


def short_filter_output(projected, rim_cells, kernel_coefficients):
    count = kernel_coefficients.shape[0]
    steps_len = projected.shape[2]
    extended = jnp.concatenate([rim_cells, projected], axis=2).astype(jnp.float32)
    total = jnp.zeros(projected.shape, jnp.float32)
    for tap in range(count):
        total = (
            total
            + kernel_coefficients[tap][:, :, None]
            * extended[:, :, count - 1 - tap : count - 1 - tap + steps_len]
        )
    return total.astype(jnp.bfloat16)


def hyena_mixer(keys_rows, values_rows, long_taps, skip_part):
    middle = keys_rows.astype(jnp.float32) * values_rows.astype(jnp.float32)
    return (spectral_conv(middle, long_taps) + skip_part[:, None] * middle).astype(jnp.bfloat16)


def body(tokens, norm_gain, proj_weight, short_filter, long_filter, skip_gain, out_weight):
    seq_count = lax.axis_size("seq")
    local_rows = tokens.shape[0]
    local_chan = proj_weight.shape[2]
    subset = local_chan // seq_count
    length = local_rows * seq_count
    offset = lax.axis_index("seq") * subset
    whole = lax.all_gather(tokens, "chan", axis=1, tiled=True)
    wide = whole.astype(jnp.float32)
    rescaled_signal = (
        wide * lax.rsqrt(jnp.mean(wide * wide, axis=1, keepdims=True) + EPSILON) * norm_gain
    ).astype(jnp.bfloat16)
    projected = lax.dot_general(
        lax.all_gather(proj_weight, "seq", axis=0, tiled=True),
        rescaled_signal,
        (((0,), (1,)), ((), ())),
        preferred_element_type=jnp.float32,
    ).astype(jnp.bfloat16)
    taps_grid = long_filter.reshape(1, seq_count, subset, local_rows)
    long_taps = lax.all_to_all(taps_grid, "seq", split_axis=1, concat_axis=3, tiled=True).reshape(
        subset, length
    )
    skip_part = lax.dynamic_slice_in_dim(skip_gain, offset, subset, 0)
    rim_cells = from_behind(projected[:, :, local_rows - (SHORT - 1) :], "seq", 1)
    featured = short_filter_output(projected, rim_cells, short_filter)
    pair_grid = featured[1:].reshape(2, seq_count, subset, local_rows)
    moved = lax.all_to_all(pair_grid, "seq", split_axis=1, concat_axis=3, tiled=True).reshape(
        2, subset, length
    )
    result = hyena_mixer(moved[0], moved[1], long_taps, skip_part)
    returned = lax.all_to_all(
        result.reshape(1, subset, length), "seq", split_axis=2, concat_axis=0, tiled=True
    )
    returned = returned.reshape(local_chan, local_rows)
    gated = (featured[0].astype(jnp.float32) * returned.astype(jnp.float32)).astype(jnp.bfloat16)
    full_mix = lax.all_gather(gated, "chan", axis=0, tiled=True)
    update = lax.dot_general(
        full_mix, out_weight, (((0,), (0,)), ((), ())), preferred_element_type=jnp.float32
    )
    return (tokens.astype(jnp.float32) + update).astype(jnp.bfloat16)


TOKEN_CHUNKS = 8
WEIGHT_CHUNKS = 16
LANES = 128
BLOCK = 128
ANY = pl.BlockSpec(memory_space=pl.ANY)


def remote(src, dst, send_sem, recv_sem, where):
    return pltpu.make_async_remote_copy(
        src_ref=src,
        dst_ref=dst,
        send_sem=send_sem,
        recv_sem=recv_sem,
        device_id=where,
        device_id_type=pl.DeviceIdType.MESH,
    )


def greet(devices):
    barrier = pltpu.get_barrier_semaphore()
    for where, present in devices:

        @pl.when(present)
        def _():
            pl.semaphore_signal(
                barrier, inc=1, device_id=where, device_id_type=pl.DeviceIdType.MESH
            )

    pl.semaphore_wait(
        barrier, sum(jnp.asarray(present).astype(jnp.int32) for _, present in devices)
    )


class Line:
    def __init__(self, view, count, chunks, send_sem, recv_sem, place):
        self.view, self.count, self.chunks = view, count, chunks
        self.send_sem, self.recv_sem, self.place = send_sem, recv_sem, place
        self.me = lax.axis_index("chan")

    def copy(self, way, step, chunk, src=None):
        step_to = 1 if way == 0 else -1
        owner = jnp.clip(self.me - step * step_to, 0, self.count - 1)
        target = jnp.clip(self.me + step_to, 0, self.count - 1)
        block = self.view(owner, chunk)
        return remote(
            block if src is None else src,
            block,
            self.send_sem.at[way, step, chunk],
            self.recv_sem.at[way, step, chunk],
            self.place(target),
        )

    def sends(self, way, step):
        if way == 0:
            return (self.me - step >= 0) & (self.me + 1 < self.count)
        return (self.me + step < self.count) & (self.me - 1 >= 0)

    def receives(self, way, step):
        if way == 0:
            return self.me - 1 - step >= 0
        return self.me + 1 + step < self.count

    def arrived(self, way, step, chunk):
        step_to = 1 if way == 0 else -1
        owner = jnp.clip(self.me - (step + 1) * step_to, 0, self.count - 1)
        block = self.view(owner, chunk)
        remote(
            block,
            block,
            self.send_sem.at[way, step, chunk],
            self.recv_sem.at[way, step, chunk],
            self.place(self.me),
        ).wait_recv()
        return owner


def gather_inputs_kernel(
    sizes,
    tokens,
    weights,
    taps,
    all_tokens,
    all_weights,
    all_taps,
    token_room,
    weight_room,
    tap_room,
    local_sem,
    line_send,
    line_recv,
    mate_send,
    mate_recv,
    x_send,
    x_recv,
    y_send,
    y_recv,
    f_send,
    f_recv,
):
    chan_count = sizes
    y, s, z = (lax.axis_index(name) for name in ("groups", "seq", "chan"))
    x, core = s // 2, s % 2
    mate = (y, s + 1 - 2 * core, z)
    across = lambda to: (y, (1 - x) * 2 + to, z)
    beside = (1 - y, s, z)
    rows, width = tokens.shape
    branches, depth, columns = weights.shape[0], weights.shape[1], weights.shape[2] // 2
    lags, share = taps.shape[0], taps.shape[1] // 2
    half, half_lags = depth // 2, lags // 2

    greet(
        [
            (mate, True),
            (across(0), True),
            (across(1), True),
            (beside, True),
            ((y, s, jnp.minimum(z + 1, chan_count - 1)), z + 1 < chan_count),
            ((y, s, jnp.maximum(z - 1, 0)), z > 0),
        ]
    )

    token_rows = rows // TOKEN_CHUNKS
    weight_rows = half // WEIGHT_CHUNKS

    def token_view(owner, chunk):
        return all_tokens.at[
            pl.ds(core * rows + chunk * token_rows, token_rows), pl.ds(owner * width, width)
        ]

    line = Line(
        token_view, chan_count, TOKEN_CHUNKS, line_send, line_recv, lambda to: (y, s, to)
    )

    def weight_view(owner, part, chunk):
        return all_weights.at[pl.ds(owner * depth + part * half + chunk * weight_rows, weight_rows)]

    def tap_view(owner, part):
        return all_taps.at[pl.ds(owner * lags + part * half_lags, half_lags)]

    pending = []
    for chunk in range(TOKEN_CHUNKS):
        own = tokens.at[pl.ds(chunk * token_rows, token_rows)]
        for way in range(2):

            @pl.when(line.sends(way, 0))
            def _():
                line.copy(way, 0, chunk, own).start()

    def taps_across(to):
        return remote(
            taps.at[pl.ds(y * half_lags, half_lags), pl.ds(to * share, share)],
            tap_view(s, y),
            f_send.at[to],
            f_recv.at[core],
            across(to),
        )

    @pl.when(x == 0)
    def _():
        for to in range(2):
            taps_across(to).start()

    for chunk in range(WEIGHT_CHUNKS):
        for to in range(2):
            view = weight_view(s, y, chunk)
            for b in range(branches):
                remote(
                    weights.at[
                        b,
                        pl.ds(y * half + chunk * weight_rows, weight_rows),
                        pl.ds(to * columns, columns),
                    ],
                    view.at[:, pl.ds(b * columns, columns)],
                    x_send.at[to, chunk],
                    x_recv.at[core, chunk],
                    across(to),
                ).start()
            pending.append(
                remote(view, view, x_send.at[to, chunk], x_recv.at[core, chunk], across(to))
            )
    own_view = all_tokens.at[pl.ds(core * rows, rows), pl.ds(z * width, width)]
    mate_copies = [
        remote(tokens, own_view, mate_send.at[0], mate_recv.at[0], mate),
        remote(
            all_weights.at[pl.ds(s * depth, depth)],
            all_weights.at[pl.ds(s * depth, depth)],
            mate_send.at[1],
            mate_recv.at[1],
            mate,
        ),
        remote(
            taps.at[:, pl.ds((1 - core) * share, share)],
            all_taps.at[pl.ds(s * lags, lags)],
            mate_send.at[2],
            mate_recv.at[2],
            mate,
        ),
    ]
    for copy in (mate_copies[0], mate_copies[2]):
        copy.start()
    for b in range(branches):
        remote(
            weights.at[b, :, pl.ds((1 - core) * columns, columns)],
            all_weights.at[pl.ds(s * depth, depth), pl.ds(b * columns, columns)],
            mate_send.at[1],
            mate_recv.at[1],
            mate,
        ).start()
    ins = [
        pltpu.make_async_copy(tokens, token_room, local_sem.at[0]),
        pltpu.make_async_copy(taps.at[:, pl.ds(core * share, share)], tap_room, local_sem.at[1]),
    ] + [
        pltpu.make_async_copy(
            weights.at[b, :, pl.ds(core * columns, columns)],
            weight_room.at[:, pl.ds(b * columns, columns)],
            local_sem.at[2 + b],
        )
        for b in range(branches)
    ]
    outs = [
        pltpu.make_async_copy(token_room, own_view, local_sem.at[5]),
        pltpu.make_async_copy(tap_room, all_taps.at[pl.ds(s * lags, lags)], local_sem.at[6]),
    ] + [
        pltpu.make_async_copy(
            weight_room.at[:, pl.ds(b * columns, columns)],
            all_weights.at[pl.ds(s * depth, depth), pl.ds(b * columns, columns)],
            local_sem.at[7 + b],
        )
        for b in range(branches)
    ]
    for copy in ins:
        copy.start()
    for first, second in zip(ins, outs):
        first.wait()
        second.start()

    def to_mate(way, step, chunk, owner):
        block = token_view(owner, chunk)
        index = 3 + (way * (chan_count - 1) + step) * TOKEN_CHUNKS + chunk
        return remote(block, block, mate_send.at[index], mate_recv.at[index], mate)

    def taps_beside(origin, part):
        view = tap_view(origin, part)
        return remote(view, view, f_send.at[2 + origin], f_recv.at[2 + origin], beside)

    @pl.when(x == 1)
    def _():
        for origin in range(2):
            view = tap_view(origin, y)
            remote(view, view, f_send.at[origin], f_recv.at[origin], beside).wait_recv()
            taps_beside(origin, y).start()


    steps = (chan_count - 1) * TOKEN_CHUNKS
    forwarded = 0
    for at in range(steps):
        step, chunk = divmod(at, TOKEN_CHUNKS)
        for way in range(2):

            @pl.when(line.receives(way, step))
            def _():
                owner = line.arrived(way, step, chunk)
                to_mate(way, step, chunk, owner).start()

            if step + 1 < chan_count - 1:

                @pl.when(line.receives(way, step) & line.sends(way, step + 1))
                def _():
                    line.copy(way, step + 1, chunk).start()

        while forwarded * steps < (at + 1) * WEIGHT_CHUNKS and forwarded < WEIGHT_CHUNKS:
            if (forwarded + 1) * steps > (at + 1) * WEIGHT_CHUNKS:
                break
            for origin in range(2):
                view = weight_view((1 - x) * 2 + origin, y, forwarded)
                remote(
                    view, view, x_send.at[origin, forwarded], x_recv.at[origin, forwarded], beside
                ).wait_recv()
                copy = remote(
                    view, view, y_send.at[origin, forwarded], y_recv.at[origin, forwarded], beside
                )
                copy.start()
                pending.append(copy)
            forwarded += 1
    for origin in range(2):
        owner = (1 - x) * 2 + origin
        for chunk in range(WEIGHT_CHUNKS):
            view = weight_view(owner, 1 - y, chunk)
            remote(
                view, view, y_send.at[origin, chunk], y_recv.at[origin, chunk], beside
            ).wait_recv()

    @pl.when(x == 1)
    def _():
        for origin in range(2):
            taps_beside(origin, 1 - y).wait_recv()
            taps_beside(origin, y).wait_send()

    @pl.when(x == 0)
    def _():
        for to in range(2):
            taps_across(to).wait_send()

    for copy in outs:
        copy.wait()
    for copy in mate_copies:
        copy.wait_send()
    other_core = 1 - core
    mate_s = s + 1 - 2 * core
    for src, dst, index in (
        (tokens, all_tokens.at[pl.ds(other_core * rows, rows), pl.ds(z * width, width)], 0),
        (
            all_weights.at[pl.ds(mate_s * depth, depth)],
            all_weights.at[pl.ds(mate_s * depth, depth)],
            1,
        ),
        (all_taps.at[pl.ds(mate_s * lags, lags)], all_taps.at[pl.ds(mate_s * lags, lags)], 2),
    ):
        remote(src, dst, mate_send.at[index], mate_recv.at[index], mate).wait_recv()
    for at in range(steps):
        step, chunk = divmod(at, TOKEN_CHUNKS)
        for way in range(2):

            @pl.when(line.sends(way, step))
            def _():
                line.copy(way, step, chunk).wait_send()

            @pl.when(line.receives(way, step))
            def _():
                sign = 1 if way == 0 else -1
                owner = jnp.clip(z - (step + 1) * sign, 0, chan_count - 1)
                to_mate(way, step, chunk, owner).wait_send()
                block = all_tokens.at[
                    pl.ds(other_core * rows + chunk * token_rows, token_rows),
                    pl.ds(owner * width, width),
                ]
                index = 3 + (way * (chan_count - 1) + step) * TOKEN_CHUNKS + chunk
                remote(block, block, mate_send.at[index], mate_recv.at[index], mate).wait_recv()

    for copy in pending:
        copy.wait_send()


def gather_inputs(tokens, weights, taps, chan_count):
    rows, width = tokens.shape
    branches, depth, both = weights.shape
    columns = branches * both // 2
    lags, share = taps.shape[0], taps.shape[1] // 2
    mate_count = 3 + 2 * (chan_count - 1) * TOKEN_CHUNKS
    dma = pltpu.SemaphoreType.DMA
    return pl.pallas_call(
        functools.partial(gather_inputs_kernel, chan_count),
        out_shape=(
            jax.ShapeDtypeStruct((2 * rows, chan_count * width), tokens.dtype),
            jax.ShapeDtypeStruct((4 * depth, columns), weights.dtype),
            jax.ShapeDtypeStruct((4 * lags, share), taps.dtype),
        ),
        in_specs=[ANY] * 3,
        out_specs=[ANY] * 3,
        scratch_shapes=[
            pltpu.VMEM((rows, width), tokens.dtype),
            pltpu.VMEM((depth, columns), weights.dtype),
            pltpu.VMEM((lags, share), taps.dtype),
            dma((10,)),
            dma((2, chan_count - 1, TOKEN_CHUNKS)),
            dma((2, chan_count - 1, TOKEN_CHUNKS)),
            dma((mate_count,)),
            dma((mate_count,)),
            dma((2, WEIGHT_CHUNKS)),
            dma((2, WEIGHT_CHUNKS)),
            dma((2, WEIGHT_CHUNKS)),
            dma((2, WEIGHT_CHUNKS)),
            dma((4,)),
            dma((4,)),
        ],
        compiler_params=pltpu.CompilerParams(
            collective_id=0, has_side_effects=True
        ),
        name="gather_inputs",
    )(tokens, weights, taps)


def wave_table(rows):
    place = 2 * np.arange(rows) + 1
    angle = (place[:, None] * place[None, :] % (8 * rows)) * (np.pi / (4 * rows))
    return jnp.asarray(np.concatenate([np.cos(angle), np.sin(angle)], axis=0), jnp.bfloat16)


def mixer_kernel(
    chan_count,
    projected,
    short,
    skip,
    taps,
    table_hbm,
    tokens,
    out_weight,
    result,
    table,
    tap_room,
    weight_room,
    token_room,
    edge,
    extended,
    query,
    signal,
    before,
    turn,
    early,
    late,
    freq,
    mixed,
    ready,
    full,
    total,
    local_sem,
    edge_sem,
    before_send,
    before_recv,
    mate_send,
    mate_recv,
    line_send,
    line_recv,
):
    y, s, z = (lax.axis_index(name) for name in ("groups", "seq", "chan"))
    x, core = s // 2, s % 2
    mate = (y, s + 1 - 2 * core, z)
    across = (y, (1 - x) * 2 + core, z)
    length = projected.shape[0]
    share = projected.shape[1] // 3
    rows = length // 2
    groups = share // LANES
    rim = edge.shape[0]
    steps = chan_count - 1

    def local(index, src, dst):
        return pltpu.make_async_copy(src, dst, local_sem.at[index])

    loads = [
        local(0, table_hbm, table),
        local(1, taps, tap_room),
        local(2, tokens, token_room),
        local(3, out_weight, weight_room),
    ]
    for copy in loads:
        copy.start()
    greet(
        [
            (mate, True),
            (across, True),
            ((y, s, jnp.minimum(z + 1, chan_count - 1)), z + 1 < chan_count),
            ((y, s, jnp.maximum(z - 1, 0)), z > 0),
        ]
    )
    rim_copy = remote(
        projected.at[pl.ds(length - rim, rim)], edge, edge_sem.at[0], edge_sem.at[1], across
    )

    @pl.when(x == 0)
    def _():
        rim_copy.start()

    def before_copy(g):
        return remote(
            signal.at[g], before.at[g], before_send.at[g], before_recv.at[g], across
        )

    def swap_copy(g):
        return remote(
            ready.at[g], full.at[z, g, core], mate_send.at[g], mate_recv.at[g], mate
        )

    def sends(way, step):
        if way == 0:
            return (z - step >= 0) & (z + 1 < chan_count)
        return (z + step < chan_count) & (z - 1 >= 0)

    def receives(way, step):
        if way == 0:
            return z - 1 - step >= 0
        return z + 1 + step < chan_count

    def line_copy(way, step, g, of):
        sign = 1 if way == 0 else -1
        owner = jnp.clip(z - step * sign, 0, chan_count - 1)
        target = jnp.clip(z + sign, 0, chan_count - 1)
        block = full.at[owner, g, of]
        return remote(
            block,
            block,
            line_send.at[way, step, g, of],
            line_recv.at[way, step, g, of],
            (y, s, target),
        )

    def line_arrived(way, step, g, of):
        sign = 1 if way == 0 else -1
        owner = jnp.clip(z - (step + 1) * sign, 0, chan_count - 1)
        block = full.at[owner, g, of]
        remote(
            block,
            block,
            line_send.at[way, step, g, of],
            line_recv.at[way, step, g, of],
            (y, s, z),
        ).wait_recv()
        return owner

    def blocks(count):
        return pl.loop(0, count // BLOCK)

    def at_rows(i, base=0):
        return pl.ds(pl.multiple_of(base + i * BLOCK, BLOCK), BLOCK)

    def lanes_of(base, g):
        return pl.ds(pl.multiple_of(base + g * LANES, LANES), LANES)

    span = 2 * BLOCK

    def spectrum(column):
        @pl.loop(0, 2 * length // span)
        def _(i):
            at = pl.ds(pl.multiple_of(i * span, span), span)
            freq[at, :] = jnp.dot(table[at, :], column(), preferred_element_type=jnp.float32)

    @blocks(length)
    def _(i):
        place = lax.broadcasted_iota(jnp.int32, (BLOCK, LANES), 0) + i * BLOCK
        angle = (2 * place + 1).astype(jnp.float32) * (math.pi / (4 * length))
        turn[0, at_rows(i), :] = jnp.cos(angle)
        turn[1, at_rows(i), :] = jnp.sin(angle)

    loads[2].wait()

    @blocks(rows)
    def _(i):
        total[at_rows(i), :] = token_room[at_rows(i), :].astype(jnp.float32)

    loads[0].wait()
    loads[1].wait()

    @pl.when(x == 1)
    def _():
        rim_copy.wait_recv()

    @pl.when(x == 0)
    def _():
        edge[...] = jnp.zeros(edge.shape, edge.dtype)

    def featurize(g):
        for b in range(3):
            cols = lanes_of(b * share, g)
            extended[b, 0:rim, :] = edge[:, cols].astype(jnp.float32)

            @blocks(length)
            def _(i):
                extended[b, pl.ds(pl.multiple_of(rim + i * BLOCK, rim), BLOCK), :] = projected[at_rows(i), cols].astype(jnp.float32)

        chosen = lanes_of(core * share, g)
        weight = [[short[tap, b : b + 1, chosen] for b in range(3)] for tap in range(SHORT)]

        @blocks(length)
        def _(i):
            found = []
            for b in range(3):
                value = jnp.zeros((BLOCK, LANES), jnp.float32)
                for tap in range(SHORT):
                    value = value + weight[tap][b] * extended[
                        b, pl.ds(rim - tap + i * BLOCK, BLOCK), :
                    ]
                found.append(value.astype(jnp.bfloat16))
            query[at_rows(i), :] = found[0]
            signal[g, at_rows(i), :] = (
                found[1].astype(jnp.float32) * found[2].astype(jnp.float32)
            ).astype(jnp.bfloat16)

    def tap_spectra(g):
        scale = 1.0 / length
        cols = lanes_of(0, g)

        def turned(i):
            low, high = at_rows(i), at_rows(i, length)
            real, imag = freq[low, :], -freq[high, :]
            cos, sin = turn[0, low, :], turn[1, low, :]
            return (cos * real - sin * imag) * scale, (cos * imag + sin * real) * scale

        spectrum(lambda: tap_room[0:length, cols])

        @blocks(length)
        def _(i):
            early[0, at_rows(i), :], early[1, at_rows(i), :] = turned(i)

        @pl.when(x == 1)
        def _():
            spectrum(lambda: tap_room[length : 2 * length, cols])

            @blocks(length)
            def _(i):
                real, imag = turned(i)
                place = lax.broadcasted_iota(jnp.int32, (BLOCK, LANES), 0)
                sign = (1 - 2 * (place % 2)).astype(jnp.float32)
                late[0, at_rows(i), :] = real - sign * early[1, at_rows(i), :]
                late[1, at_rows(i), :] = imag + sign * early[0, at_rows(i), :]

    def product(i, other):
        low, high = at_rows(i), at_rows(i, length)
        cos, sin = freq[low, :], freq[high, :]
        real, imag = other[0, low, :], other[1, low, :]
        return cos * real + sin * imag, sin * real - cos * imag

    def convolve(g):
        spectrum(lambda: signal[g])

        @blocks(length)
        def _(i):
            mixed[at_rows(i), :], mixed[at_rows(i, length), :] = product(i, early)

        @pl.when(x == 1)
        def _():
            before_copy(g).wait_recv()
            spectrum(lambda: before[g])

            @blocks(length)
            def _(i):
                real, imag = product(i, late)
                mixed[at_rows(i), :] += real
                mixed[at_rows(i, length), :] += imag

        @pl.loop(0, length // span)
        def _(i):
            low = pl.ds(pl.multiple_of(i * span, span), span)
            high = pl.ds(pl.multiple_of(length + i * span, span), span)
            freq[low, :] = jnp.dot(
                table[low, :], mixed[:length, :].astype(jnp.bfloat16),
                preferred_element_type=jnp.float32,
            ) + jnp.dot(
                table[high, :], mixed[length:, :].astype(jnp.bfloat16),
                preferred_element_type=jnp.float32,
            )

        gain = skip[:, lanes_of(core * share, g)]

        def gated(at):
            longer = freq[at, :] + gain * signal[g, at, :].astype(jnp.float32)
            longer = longer.astype(jnp.bfloat16).astype(jnp.float32)
            return (query[at, :].astype(jnp.float32) * longer).astype(jnp.bfloat16)

        @blocks(rows)
        def _(i):
            full[z, g, core, at_rows(i), :] = gated(
                pl.ds(pl.multiple_of(core * rows + i * BLOCK, BLOCK), BLOCK)
            )
            ready[g, at_rows(i), :] = gated(
                pl.ds(pl.multiple_of((1 - core) * rows + i * BLOCK, BLOCK), BLOCK)
            )

    def accumulate(owner, g):
        left = pl.ds(pl.multiple_of(owner * 2 * share + g * LANES, LANES), LANES)
        right = pl.ds(pl.multiple_of((owner * 2 + 1) * share + g * LANES, LANES), LANES)

        @pl.loop(0, total.shape[1] // span)
        def _(i):
            cols = pl.ds(pl.multiple_of(i * span, span), span)
            block = jnp.concatenate([full[owner, g, 0], full[owner, g, 1]], axis=1)
            weight = jnp.concatenate([weight_room[left, cols], weight_room[right, cols]], axis=0)
            total[:, cols] += jnp.dot(block, weight, preferred_element_type=jnp.float32)

    def begin(g):
        swap_copy(g).start()
        for way in range(2):

            @pl.when(sends(way, 0))
            def _():
                line_copy(way, 0, g, core).start()

        other = full.at[z, g, 1 - core]
        remote(other, other, mate_send.at[g], mate_recv.at[g], mate).wait_recv()
        for way in range(2):

            @pl.when(sends(way, 0))
            def _():
                line_copy(way, 0, g, 1 - core).start()

    def relay(step, g):
        for way in range(2):

            @pl.when(receives(way, step))
            def _():
                for of in range(2):
                    owner = line_arrived(way, step, g, of)
                    if step + 1 < steps:

                        @pl.when(sends(way, step + 1))
                        def _():
                            line_copy(way, step + 1, g, of).start()

                accumulate(owner, g)

    @pl.loop(0, groups + steps)
    def _(g):
        @pl.when(g < groups)
        def _():
            featurize(g)

            @pl.when(x == 0)
            def _():
                before_copy(g).start()

            tap_spectra(g)
            convolve(g)
            begin(g)

            @pl.when(g == 0)
            def _():
                loads[3].wait()

            accumulate(z, g)

        for step in range(steps):
            at = g - 1 - step

            @pl.when((at >= 0) & (at < groups))
            def _():
                relay(step, at)

    @blocks(rows)
    def _(i):
        result[at_rows(i), :] = total[at_rows(i), :].astype(jnp.bfloat16)

    @pl.when(x == 0)
    def _():
        rim_copy.wait_send()

    for g in range(groups):
        swap_copy(g).wait_send()

        @pl.when(x == 0)
        def _():
            before_copy(g).wait_send()

        for way in range(2):
            for step in range(steps):

                @pl.when(sends(way, step))
                def _():
                    for of in range(2):
                        line_copy(way, step, g, of).wait_send()


def mixer(projected, short, skip, taps, tokens, out_weight, chan_count):
    length, columns = projected.shape
    share = columns // 3
    rows, width = tokens.shape
    groups = share // LANES
    steps = chan_count - 1
    dma = pltpu.SemaphoreType.DMA
    f32, bf16 = jnp.float32, jnp.bfloat16
    vmem = pl.BlockSpec(memory_space=pltpu.VMEM)
    return pl.pallas_call(
        functools.partial(mixer_kernel, chan_count),
        out_shape=jax.ShapeDtypeStruct((rows, width), bf16),
        in_specs=[vmem, vmem, vmem] + [ANY] * 4,
        out_specs=vmem,
        scratch_shapes=[
            pltpu.VMEM((2 * length, length), bf16),
            pltpu.VMEM(taps.shape, bf16),
            pltpu.VMEM(out_weight.shape, bf16),
            pltpu.VMEM(tokens.shape, bf16),
            pltpu.VMEM((16, columns), bf16),
            pltpu.VMEM((3, length + 16, LANES), f32),
            pltpu.VMEM((length, LANES), bf16),
            pltpu.VMEM((groups, length, LANES), bf16),
            pltpu.VMEM((groups, length, LANES), bf16),
            pltpu.VMEM((2, length, LANES), f32),
            pltpu.VMEM((2, length, LANES), f32),
            pltpu.VMEM((2, length, LANES), f32),
            pltpu.VMEM((2 * length, LANES), f32),
            pltpu.VMEM((2 * length, LANES), f32),
            pltpu.VMEM((groups, rows, LANES), bf16),
            pltpu.VMEM((chan_count, groups, 2, rows, LANES), bf16),
            pltpu.VMEM((rows, width), f32),
            dma((4,)),
            dma((2,)),
            dma((groups,)),
            dma((groups,)),
            dma((groups,)),
            dma((groups,)),
            dma((2, steps, groups, 2)),
            dma((2, steps, groups, 2)),
        ],
        compiler_params=pltpu.CompilerParams(
            collective_id=1, has_side_effects=True, vmem_limit_bytes=50 * 1024 * 1024
        ),
        name="mixer",
    )(projected, short, skip, taps, wave_table(length), tokens, out_weight)


def chip_body(tokens, norm_gain, proj_weight, short_filter, long_filter, skip_gain, out_weight):
    chan_count = lax.axis_size("chan")
    weights = proj_weight.transpose(1, 0, 2)
    taps = long_filter.astype(jnp.bfloat16).T
    whole, all_weights, all_taps = gather_inputs(tokens, weights, taps, chan_count)
    wide = whole.astype(jnp.float32)
    normed = (
        wide * lax.rsqrt(jnp.mean(wide * wide, axis=1, keepdims=True) + EPSILON) * norm_gain
    ).astype(jnp.bfloat16)
    projected = jnp.dot(normed, all_weights, preferred_element_type=jnp.float32).astype(
        jnp.bfloat16
    )
    return mixer(
        projected, short_filter, skip_gain[None, :], all_taps, tokens, out_weight, chan_count
    )


def select_body(mesh):
    if mesh.shape["seq"] == 4 and mesh.shape["groups"] == 2:
        return chip_body
    return body


def solution(mesh):
    placed = (
        P(("groups", "seq"), "chan"),
        P(),
        P("seq", None, "chan"),
        P(None, None, "chan"),
        P("chan", "seq"),
        P("chan"),
        P(None, "chan"),
    )
    return jax.shard_map(
        select_body(mesh), mesh=mesh, in_specs=placed, out_specs=P(("groups", "seq"), "chan"), check_vma=False
    )
```

```python
import functools
import math

import jax
import jax.numpy as jnp
import numpy as np
from jax import lax
from jax.experimental import pallas as pl
from jax.experimental.pallas import tpu as pltpu
from jax.sharding import PartitionSpec as P

SHORT = 3


EPSILON = 1e-06
HIGHEST = lax.Precision.HIGHEST


def from_behind(value, axis, steps):
    count = lax.axis_size(axis)
    initial, last = (max(0, -steps), min(count, count - steps))
    return lax.ppermute(value, axis, [(source, source + steps) for source in range(initial, last)])


def angle_table(row_count, col_count, period, sign):
    row_index = lax.iota(jnp.int32, row_count)[:, None]
    col_index = lax.iota(jnp.int32, col_count)[None, :]
    angles = (row_index * col_index % period).astype(jnp.float32) * (sign * 2.0 * math.pi / period)
    return (jnp.cos(angles), jnp.sin(angles))


def forward_spectrum(signal_rows, first, second):
    channels = signal_rows.shape[0]
    grid_rows = signal_rows.reshape(channels, first, second)
    cos_first, sin_first = angle_table(first, first, first, -1.0)
    part_re = jnp.einsum("cab,ak->ckb", grid_rows, cos_first, precision=HIGHEST)
    part_im = jnp.einsum("cab,ak->ckb", grid_rows, sin_first, precision=HIGHEST)
    twist_cos, twist_sin = angle_table(first, second, first * second, -1.0)
    part_re, part_im = (
        part_re * twist_cos - part_im * twist_sin,
        part_re * twist_sin + part_im * twist_cos,
    )
    cos_second, sin_second = angle_table(second, second, second, -1.0)
    spectrum_real = jnp.einsum("ckb,bm->ckm", part_re, cos_second, precision=HIGHEST) - jnp.einsum(
        "ckb,bm->ckm", part_im, sin_second, precision=HIGHEST
    )
    spec_im = jnp.einsum("ckb,bm->ckm", part_re, sin_second, precision=HIGHEST) + jnp.einsum(
        "ckb,bm->ckm", part_im, cos_second, precision=HIGHEST
    )
    return (spectrum_real, spec_im)


def inverse_spectrum(spectrum_real, spec_im, first, second):
    channels = spectrum_real.shape[0]
    cos_second, sin_second = angle_table(second, second, second, 1.0)
    part_re = jnp.einsum("ckm,bm->ckb", spectrum_real, cos_second, precision=HIGHEST) - jnp.einsum(
        "ckm,bm->ckb", spec_im, sin_second, precision=HIGHEST
    )
    part_im = jnp.einsum("ckm,bm->ckb", spectrum_real, sin_second, precision=HIGHEST) + jnp.einsum(
        "ckm,bm->ckb", spec_im, cos_second, precision=HIGHEST
    )
    twist_cos, twist_sin = angle_table(first, second, first * second, 1.0)
    part_re, part_im = (
        part_re * twist_cos - part_im * twist_sin,
        part_re * twist_sin + part_im * twist_cos,
    )
    cos_first, sin_first = angle_table(first, first, first, 1.0)
    result = jnp.einsum("ckb,ak->cab", part_re, cos_first, precision=HIGHEST) - jnp.einsum(
        "ckb,ak->cab", part_im, sin_first, precision=HIGHEST
    )
    return result.reshape(channels, first * second) / (first * second)


def spectral_conv(signal_rows, filter_rows):
    channels, length = signal_rows.shape
    padded_len = 2 * length
    log_len = padded_len.bit_length() - 1
    first = 1 << log_len // 2
    second = padded_len // first
    zeros_tail = jnp.zeros((channels, length), jnp.float32)
    sig_re, sig_im = forward_spectrum(
        jnp.concatenate([signal_rows, zeros_tail], axis=1), first, second
    )
    tap_re, tap_im = forward_spectrum(
        jnp.concatenate([filter_rows, zeros_tail], axis=1), first, second
    )
    prod_re = sig_re * tap_re - sig_im * tap_im
    prod_im = sig_re * tap_im + sig_im * tap_re
    return inverse_spectrum(prod_re, prod_im, first, second)[:, :length]


def short_filter_output(projected, rim_cells, kernel_coefficients):
    count = kernel_coefficients.shape[0]
    steps_len = projected.shape[2]
    extended = jnp.concatenate([rim_cells, projected], axis=2).astype(jnp.float32)
    total = jnp.zeros(projected.shape, jnp.float32)
    for tap in range(count):
        total = (
            total
            + kernel_coefficients[tap][:, :, None]
            * extended[:, :, count - 1 - tap : count - 1 - tap + steps_len]
        )
    return total.astype(jnp.bfloat16)


def hyena_mixer(keys_rows, values_rows, long_taps, skip_part):
    middle = keys_rows.astype(jnp.float32) * values_rows.astype(jnp.float32)
    return (spectral_conv(middle, long_taps) + skip_part[:, None] * middle).astype(jnp.bfloat16)


def body(tokens, norm_gain, proj_weight, short_filter, long_filter, skip_gain, out_weight):
    seq_count = lax.axis_size("seq")
    local_rows = tokens.shape[0]
    local_chan = proj_weight.shape[2]
    subset = local_chan // seq_count
    length = local_rows * seq_count
    offset = lax.axis_index("seq") * subset
    whole = lax.all_gather(tokens, "chan", axis=1, tiled=True)
    wide = whole.astype(jnp.float32)
    rescaled_signal = (
        wide * lax.rsqrt(jnp.mean(wide * wide, axis=1, keepdims=True) + EPSILON) * norm_gain
    ).astype(jnp.bfloat16)
    projected = lax.dot_general(
        lax.all_gather(proj_weight, "seq", axis=0, tiled=True),
        rescaled_signal,
        (((0,), (1,)), ((), ())),
        preferred_element_type=jnp.float32,
    ).astype(jnp.bfloat16)
    taps_grid = long_filter.reshape(1, seq_count, subset, local_rows)
    long_taps = lax.all_to_all(taps_grid, "seq", split_axis=1, concat_axis=3, tiled=True).reshape(
        subset, length
    )
    skip_part = lax.dynamic_slice_in_dim(skip_gain, offset, subset, 0)
    rim_cells = from_behind(projected[:, :, local_rows - (SHORT - 1) :], "seq", 1)
    featured = short_filter_output(projected, rim_cells, short_filter)
    pair_grid = featured[1:].reshape(2, seq_count, subset, local_rows)
    moved = lax.all_to_all(pair_grid, "seq", split_axis=1, concat_axis=3, tiled=True).reshape(
        2, subset, length
    )
    result = hyena_mixer(moved[0], moved[1], long_taps, skip_part)
    returned = lax.all_to_all(
        result.reshape(1, subset, length), "seq", split_axis=2, concat_axis=0, tiled=True
    )
    returned = returned.reshape(local_chan, local_rows)
    gated = (featured[0].astype(jnp.float32) * returned.astype(jnp.float32)).astype(jnp.bfloat16)
    full_mix = lax.all_gather(gated, "chan", axis=0, tiled=True)
    update = lax.dot_general(
        full_mix, out_weight, (((0,), (0,)), ((), ())), preferred_element_type=jnp.float32
    )
    return (tokens.astype(jnp.float32) + update).astype(jnp.bfloat16)

LANES = 128
BLOCK = 128
SPAN = 512
TOKEN_CHUNKS = 8
WEIGHT_CHUNKS = 4
ANY = pl.BlockSpec(memory_space=pl.ANY)


def remote(src, dst, send_sem, recv_sem, where):
    return pltpu.make_async_remote_copy(
        src_ref=src,
        dst_ref=dst,
        send_sem=send_sem,
        recv_sem=recv_sem,
        device_id=where,
        device_id_type=pl.DeviceIdType.MESH,
    )


class Line:
    def __init__(self, view, count, send_sem, recv_sem, place):
        self.view, self.count, self.place = view, count, place
        self.send_sem, self.recv_sem = send_sem, recv_sem
        self.me = lax.axis_index("chan")

    def move(self, way, step, piece, block, target):
        index = (way, step) + piece
        return remote(
            block, block, self.send_sem.at[index], self.recv_sem.at[index], self.place(target)
        )

    def copy(self, way, step, piece):
        sign = 1 if way == 0 else -1
        owner = jnp.clip(self.me - step * sign, 0, self.count - 1)
        target = jnp.clip(self.me + sign, 0, self.count - 1)
        return self.move(way, step, piece, self.view(owner, *piece), target)

    def sends(self, way, step):
        if way == 0:
            return (self.me - step >= 0) & (self.me + 1 < self.count)
        return (self.me + step < self.count) & (self.me - 1 >= 0)

    def receives(self, way, step):
        if way == 0:
            return self.me - 1 - step >= 0
        return self.me + 1 + step < self.count

    def source(self, way, step):
        sign = 1 if way == 0 else -1
        return jnp.clip(self.me - (step + 1) * sign, 0, self.count - 1)

    def arrived(self, way, step, piece):
        owner = self.source(way, step)
        self.move(way, step, piece, self.view(owner, *piece), self.me).wait_recv()
        return owner


def block_kernel(
    chan_count,
    tokens,
    gain,
    weights,
    short,
    long_taps,
    skip,
    out_weight,
    result,
    stream,
    weight,
    sums,
    scale,
    partial,
    room,
    out_room,
    table,
    taps,
    turn,
    spectra,
    freq,
    mixed,
    edge_out,
    edge,
    extended,
    query,
    signal,
    before,
    ready,
    full,
    total,
    local_sem,
    mate_send,
    mate_recv,
    token_send,
    token_recv,
    sums_send,
    sums_recv,
    x_send,
    x_recv,
    y_send,
    y_recv,
    tap_send,
    tap_recv,
    edge_send,
    edge_recv,
    before_send,
    before_recv,
    swap_send,
    swap_recv,
    line_send,
    line_recv,
):
    y, s, z = (lax.axis_index(name) for name in ("groups", "seq", "chan"))
    x, core = s // 2, s % 2
    mate_s = s + 1 - 2 * core
    mate = (y, mate_s, z)
    across = (y, (1 - x) * 2 + core, z)
    aslant = (y, (1 - x) * 2 + 1 - core, z)
    beside = (1 - y, s, z)
    rows, width = tokens.shape
    length = 2 * rows
    branches, depth = weights.shape[0], weights.shape[1]
    half = depth // 2
    share = weights.shape[2] // 2
    groups = share // LANES
    rim = edge.shape[2]
    steps = chan_count - 1
    token_rows = rows // TOKEN_CHUNKS
    weight_rows = half // WEIGHT_CHUNKS

    column_peers = [mate] + [
        (y, 2 * x + of, lax.rem(z + by, chan_count))
        for by in range(1, chan_count)
        for of in (core, 1 - core)
    ]
    peers = column_peers + [across, aslant, beside]

    def rows_at(i, count, base=0):
        return pl.ds(pl.multiple_of(base + i * count, count), count)

    def at_rows(i):
        return rows_at(i, BLOCK)

    def blocks(count):
        return pl.loop(0, count // BLOCK)

    def lanes_of(base, g):
        return pl.ds(pl.multiple_of(base + g * LANES, LANES), LANES)

    tap_stage = [(0, 0), (0, length), (1, 0), (1, length)]
    tap_loads = [
        pltpu.make_async_copy(
            long_taps.at[:, pl.ds(j * LANES, LANES)],
            freq.at[which, pl.ds(start, length)],
            local_sem.at[4 + j],
        )
        for j, (which, start) in enumerate(tap_stage)
    ]
    token_load = pltpu.make_async_copy(tokens, room, local_sem.at[0])
    out_load = pltpu.make_async_copy(out_weight, out_room, local_sem.at[1])
    token_load.start()
    for copy in tap_loads:
        copy.start()
    for g in range(groups):
        for b in range(branches):
            pltpu.make_async_copy(
                weights.at[b, :, lanes_of(core * share, g)],
                weight.at[g, s, :, pl.ds(b * LANES, LANES)],
                local_sem.at[2],
            ).start()
    out_load.start()

    barrier = pltpu.get_barrier_semaphore()
    for peer in peers:
        pl.semaphore_signal(barrier, inc=1, device_id=peer, device_id_type=pl.DeviceIdType.MESH)

    sums[core, z] = jnp.zeros(sums.shape[2:], jnp.float32)
    own_gain = gain[:, pl.ds(pl.multiple_of(z * width, width), width)]
    token_load.wait()

    @blocks(rows)
    def _(i):
        raw = room[at_rows(i), :].astype(jnp.float32)
        total[at_rows(i), :] = raw
        stream[z, pl.ds(pl.multiple_of(core * rows + i * BLOCK, BLOCK), BLOCK), :] = (
            raw * own_gain
        ).astype(jnp.bfloat16)
        square = raw * raw
        found = square[:, :LANES]
        for part in range(1, width // LANES):
            found = found + square[:, part * LANES : (part + 1) * LANES]
        sums[core, z, pl.ds(i, 1), :] = jnp.sum(found.T, axis=0, keepdims=True)

    pl.semaphore_wait(barrier, len(peers))

    def token_view(owner, chunk):
        return stream.at[owner, rows_at(chunk, token_rows, core * rows), :]

    token_line = Line(
        token_view, chan_count, token_send, token_recv, lambda to: (y, s, to)
    )
    for chunk in range(TOKEN_CHUNKS):
        for way in range(2):

            @pl.when(token_line.sends(way, 0))
            def _():
                token_line.copy(way, 0, (chunk,)).start()

    def own_half(owner, of):
        return stream.at[owner, pl.ds(pl.multiple_of(of * rows, rows), rows), :]

    def mate_tokens():
        return remote(
            own_half(z, core), own_half(z, core), mate_send.at[0], mate_recv.at[0], mate
        )

    mate_tokens().start()
    sum_copies = [
        remote(
            sums.at[core, z], sums.at[core, z], sums_send.at[at], sums_recv.at[core, z], peer
        )
        for at, peer in enumerate(column_peers)
    ]
    for copy in sum_copies:
        copy.start()
    for g in range(groups):
        for b in range(branches):
            remote(
                weights.at[b, :, lanes_of((1 - core) * share, g)],
                weight.at[g, s, :, pl.ds(b * LANES, LANES)],
                mate_send.at[1],
                mate_recv.at[1],
                mate,
            ).start()

    for j, (which, start) in enumerate(tap_stage):
        tap_loads[j].wait()

        @pl.loop(0, groups)
        def _(g):
            mine = freq[which, rows_at(core * groups + g, BLOCK, start), :]
            taps[g, pl.ds(pl.multiple_of(s * rows + j * LANES, LANES), LANES), :] = mine.T.astype(
                jnp.bfloat16
            )
            other = freq[which, rows_at((1 - core) * groups + g, BLOCK, start), :]
            ready[g, j * LANES : (j + 1) * LANES, :] = other.T.astype(jnp.bfloat16)

    def tap_part(owner, part):
        return taps.at[
            :, pl.ds(pl.multiple_of(owner * rows + part * (rows // 2), rows // 2), rows // 2), :
        ]

    def taps_across(to):
        src = tap_part(s, y) if to == 0 else ready.at[
            :, pl.ds(pl.multiple_of(y * (rows // 2), rows // 2), rows // 2), :
        ]
        return remote(
            src,
            tap_part(s, y),
            tap_send.at[to],
            tap_recv.at[core],
            across if to == 0 else aslant,
        )

    def taps_beside(origin, part):
        view = tap_part(origin, part)
        return remote(view, view, tap_send.at[2 + origin], tap_recv.at[2 + origin], beside)

    def taps_mate():
        return remote(
            ready,
            taps.at[:, pl.ds(pl.multiple_of(s * rows, rows), rows), :],
            mate_send.at[2],
            mate_recv.at[2],
            mate,
        )

    @pl.when(x == 0)
    def _():
        taps_across(0).start()
        taps_across(1).start()

        @pl.loop(0, groups)
        def _(g):
            taps[g, length:, :] = jnp.zeros((length, LANES), jnp.bfloat16)

    taps_mate().start()

    def weight_view(owner, part, g, c):
        return weight.at[g, owner, rows_at(c, weight_rows, part * half), :]

    def weight_sent(to, g, c):
        view = weight_view(s, y, g, c)
        return remote(
            view, view, x_send.at[to, g, c], x_recv.at[core, g, c], across if to == 0 else aslant
        )

    def send_weights(g):
        for c in range(WEIGHT_CHUNKS):
            for to in range(2):
                side = core if to == 0 else 1 - core
                view = weight_view(s, y, g, c)
                for b in range(branches):
                    remote(
                        weights.at[
                            b,
                            rows_at(c, weight_rows, y * half),
                            pl.ds(pl.multiple_of(side * share + g * LANES, LANES), LANES),
                        ],
                        view.at[:, pl.ds(b * LANES, LANES)],
                        x_send.at[to, g, c],
                        x_recv.at[core, g, c],
                        across if to == 0 else aslant,
                    ).start()

    for g in range(groups - 1):
        send_weights(g)

    def beside_copy(origin, part, g, c):
        view = weight_view((1 - x) * 2 + origin, part, g, c)
        return remote(view, view, y_send.at[origin, g, c], y_recv.at[origin, g, c], beside)

    def forward(g, c):
        for origin in range(2):
            view = weight_view((1 - x) * 2 + origin, y, g, c)
            remote(
                view, view, x_send.at[origin, g, c], x_recv.at[origin, g, c], beside
            ).wait_recv()
            beside_copy(origin, y, g, c).start()

    def await_beside(g):
        for c in range(WEIGHT_CHUNKS):
            for origin in range(2):
                beside_copy(origin, 1 - y, g, c).wait_recv()

    @blocks(length)
    def _(i):
        row = lax.broadcasted_iota(jnp.int32, (BLOCK, LANES), 0) + i * BLOCK
        lane = lax.broadcasted_iota(jnp.int32, (BLOCK, LANES), 1)
        unit = math.pi / (4 * length)
        odd = 2 * row + 1
        small = odd.astype(jnp.float32) * unit
        turn[0, at_rows(i), :] = jnp.cos(small)
        turn[1, at_rows(i), :] = jnp.sin(small)
        period = 8 * length
        angle = (odd * (2 * lane + 1) % period).astype(jnp.float32) * unit
        cos, sin = jnp.cos(angle), jnp.sin(angle)
        stride = (odd * (2 * LANES) % period).astype(jnp.float32) * unit
        step_cos, step_sin = jnp.cos(stride), jnp.sin(stride)
        for a in range(length // LANES):
            table[at_rows(i), a * LANES : (a + 1) * LANES] = cos.astype(jnp.bfloat16)
            table[rows_at(i, BLOCK, length), a * LANES : (a + 1) * LANES] = sin.astype(
                jnp.bfloat16
            )
            cos, sin = cos * step_cos - sin * step_sin, sin * step_cos + cos * step_sin

    for g in range(groups):

        @blocks(length)
        def _(i):
            partial[g, at_rows(i), :] = jnp.zeros((BLOCK, branches * LANES), jnp.float32)

    def spectrum(which, column):
        @pl.loop(0, 2 * length // SPAN)
        def _(i):
            at = rows_at(i, SPAN)
            freq[which, at, :] = jnp.dot(
                table[at, :], column(), preferred_element_type=jnp.float32
            )

    def tap_spectra(g):
        @pl.loop(0, 2 * length // SPAN)
        def _(i):
            at = rows_at(i, SPAN)
            both = jnp.concatenate([taps[g, :length, :], taps[g, length:, :]], axis=1)
            found = jnp.dot(table[at, :], both, preferred_element_type=jnp.float32)
            freq[0, at, :] = found[:, :LANES]
            freq[1, at, :] = found[:, LANES:]

        @blocks(length)
        def _(i):
            low, high = at_rows(i), rows_at(i, BLOCK, length)
            cos, sin = turn[0, low, :], turn[1, low, :]

            def turned(which):
                real, imag = freq[which, low, :], -freq[which, high, :]
                return (cos * real - sin * imag) / length, (cos * imag + sin * real) / length

            real, imag = turned(0)
            late_real, late_imag = turned(1)
            place = lax.broadcasted_iota(jnp.int32, (BLOCK, LANES), 0)
            sign = (1 - 2 * (place % 2)).astype(jnp.float32)
            spectra[g, 0, low, :] = real.astype(jnp.bfloat16)
            spectra[g, 1, low, :] = imag.astype(jnp.bfloat16)
            spectra[g, 2, low, :] = (late_real - sign * imag).astype(jnp.bfloat16)
            spectra[g, 3, low, :] = (late_imag + sign * real).astype(jnp.bfloat16)

    def project(g, owner):
        @pl.loop(0, length // SPAN)
        def _(i):
            at = rows_at(i, SPAN)
            partial[g, at, :] += jnp.dot(
                stream[owner, at, :], weight[g, owner], preferred_element_type=jnp.float32
            )

    def distance(owner):
        return jnp.abs(z - owner)

    def to_mate(way, step, chunk):
        block = token_view(token_line.source(way, step), chunk)
        index = 3 + way * steps + step
        return remote(block, block, mate_send.at[index], mate_recv.at[index], mate)

    def mate_half(way, step, of):
        block = own_half(token_line.source(way, step), of)
        index = 3 + way * steps + step
        return remote(block, block, mate_send.at[index], mate_recv.at[index], mate)

    def await_mate(step):
        for way in range(2):

            @pl.when(token_line.receives(way, step))
            def _():
                mate_half(way, step, 1 - core).wait_recv()

    @pl.loop(0, steps * TOKEN_CHUNKS)
    def _(tick):
        step, chunk = tick // TOKEN_CHUNKS, tick % TOKEN_CHUNKS
        for way in range(2):

            @pl.when(token_line.receives(way, step))
            def _():
                token_line.arrived(way, step, (chunk,))
                to_mate(way, step, chunk).start()

            @pl.when(
                (step + 1 < steps)
                & token_line.receives(way, step)
                & token_line.sends(way, step + 1)
            )
            def _():
                token_line.copy(way, step + 1, (chunk,)).start()

        @pl.when((tick == TOKEN_CHUNKS // 2) & (x == 1))
        def _():
            for origin in range(2):
                view = tap_part(origin, y)
                remote(
                    view, view, tap_send.at[origin], tap_recv.at[origin], beside
                ).wait_recv()
                taps_beside(origin, y).start()

        @pl.when((tick % 2 == 1) & (tick >= 3) & (tick < 3 + 4 * WEIGHT_CHUNKS))
        def _():
            at = (tick - 3) // 2
            forward(at // WEIGHT_CHUNKS, at % WEIGHT_CHUNKS)

        @pl.when(tick == TOKEN_CHUNKS)
        def _():
            mate_half_own = own_half(z, 1 - core)
            remote(
                mate_half_own, mate_half_own, mate_send.at[0], mate_recv.at[0], mate
            ).wait_recv()
            await_mate(0)
            pltpu.make_async_copy(
                weight.at[:, s], weight.at[:, s], local_sem.at[2]
            ).wait()
            other = weight.at[:, mate_s]
            remote(other, other, mate_send.at[1], mate_recv.at[1], mate).wait_recv()
            other = taps.at[:, pl.ds(pl.multiple_of(mate_s * rows, rows), rows), :]
            remote(other, other, mate_send.at[2], mate_recv.at[2], mate).wait_recv()

            @pl.when(x == 1)
            def _():
                for origin in range(2):
                    taps_beside(origin, 1 - y).wait_recv()

        @pl.when((step == 1) & (chunk % 2 == 0))
        def _():
            tap_spectra(chunk // 2)

        @pl.when(tick == 2 * TOKEN_CHUNKS)
        def _():
            await_mate(1)

        owner = 2 * x + chunk // groups
        far = distance(owner)

        @pl.when(((step == 1) & (far <= 1)) | ((step == 2) & (far == 2)))
        def _():
            project(chunk % groups, owner)

    for g in range(2):
        await_beside(g)

        @pl.loop(0, 2)
        def _(at):
            owner = 2 * (1 - x) + at

            @pl.when(distance(owner) <= 2)
            def _():
                project(g, owner)

    await_mate(2)
    for by in range(1, chan_count):
        for of in range(2):
            view = sums.at[of, lax.rem(z + by, chan_count)]
            remote(
                view, view, sums_send.at[0], sums_recv.at[of, lax.rem(z + by, chan_count)], mate
            ).wait_recv()
    view = sums.at[1 - core, z]
    remote(view, view, sums_send.at[0], sums_recv.at[1 - core, z], mate).wait_recv()

    @blocks(length)
    def _(i):
        of, at = i // (rows // BLOCK), i % (rows // BLOCK)
        found = sums[of, 0, pl.ds(at, 1), :]
        for owner in range(1, chan_count):
            found = found + sums[of, owner, pl.ds(at, 1), :]
        found = lax.rsqrt(found / (chan_count * width) + EPSILON)
        scale[at_rows(i), :] = jnp.broadcast_to(found, (BLOCK, LANES)).T

    taps_mate().wait_send()

    @pl.when(x == 0)
    def _():
        taps_across(0).wait_send()
        taps_across(1).wait_send()

    def edge_copy(g):
        return remote(
            edge_out.at[g], edge.at[g], edge_send.at[g], edge_recv.at[g], across
        )

    def before_copy(g):
        return remote(
            signal.at[g], before.at[g], before_send.at[g], before_recv.at[g], across
        )

    def swap_copy(g):
        return remote(
            ready.at[g], full.at[z, g, core], swap_send.at[g], swap_recv.at[g], mate
        )

    line = Line(
        lambda owner, g, of: full.at[owner, g, of],
        chan_count,
        line_send,
        line_recv,
        lambda to: (y, s, to),
    )

    def projected(g, b, at):
        return (partial[g, at, b * LANES : (b + 1) * LANES] * scale[at, :]).astype(jnp.bfloat16)

    def featurize(g):
        @pl.when(x == 0)
        def _():
            for b in range(branches):
                edge_out[g, b] = projected(g, b, pl.ds(length - rim, rim))
                extended[b, 0:rim, :] = jnp.zeros((rim, LANES), jnp.float32)
            edge_copy(g).start()

        @blocks(length)
        def _(i):
            for b in range(branches):
                extended[b, pl.ds(pl.multiple_of(rim + i * BLOCK, rim), BLOCK), :] = projected(
                    g, b, at_rows(i)
                ).astype(jnp.float32)

        @pl.when(x == 1)
        def _():
            edge_copy(g).wait_recv()
            for b in range(branches):
                extended[b, 0:rim, :] = edge[g, b].astype(jnp.float32)

        chosen = lanes_of(core * share, g)
        coefficient = [
            [short[tap, b : b + 1, chosen] for b in range(branches)] for tap in range(SHORT)
        ]

        @blocks(length)
        def _(i):
            found = []
            for b in range(branches):
                value = jnp.zeros((BLOCK, LANES), jnp.float32)
                for tap in range(SHORT):
                    value = value + coefficient[tap][b] * extended[
                        b, pl.ds(rim - tap + i * BLOCK, BLOCK), :
                    ]
                found.append(value.astype(jnp.bfloat16))
            query[at_rows(i), :] = found[0]
            signal[g, at_rows(i), :] = (
                found[1].astype(jnp.float32) * found[2].astype(jnp.float32)
            ).astype(jnp.bfloat16)

    def convolve(g):
        spectrum(0, lambda: signal[g])

        def product(i, which, first):
            low, high = at_rows(i), rows_at(i, BLOCK, length)
            cos, sin = freq[which, low, :], freq[which, high, :]
            real = spectra[g, first, low, :].astype(jnp.float32)
            imag = spectra[g, first + 1, low, :].astype(jnp.float32)
            return cos * real + sin * imag, sin * real - cos * imag

        @pl.when(x == 0)
        def _():
            @blocks(length)
            def _(i):
                real, imag = product(i, 0, 0)
                mixed[at_rows(i), :] = real.astype(jnp.bfloat16)
                mixed[rows_at(i, BLOCK, length), :] = imag.astype(jnp.bfloat16)

        @pl.when(x == 1)
        def _():
            before_copy(g).wait_recv()
            spectrum(1, lambda: before[g])

            @blocks(length)
            def _(i):
                real, imag = product(i, 0, 0)
                more_real, more_imag = product(i, 1, 2)
                mixed[at_rows(i), :] = (real + more_real).astype(jnp.bfloat16)
                mixed[rows_at(i, BLOCK, length), :] = (imag + more_imag).astype(jnp.bfloat16)

        @pl.loop(0, length // SPAN)
        def _(i):
            low, high = rows_at(i, SPAN), rows_at(i, SPAN, length)
            freq[0, low, :] = jnp.dot(
                table[low, :], mixed[:length, :], preferred_element_type=jnp.float32
            ) + jnp.dot(table[high, :], mixed[length:, :], preferred_element_type=jnp.float32)

        direct = skip[:, lanes_of(core * share, g)]

        def gated(at):
            longer = freq[0, at, :] + direct * signal[g, at, :].astype(jnp.float32)
            longer = longer.astype(jnp.bfloat16).astype(jnp.float32)
            return (query[at, :].astype(jnp.float32) * longer).astype(jnp.bfloat16)

        @blocks(rows)
        def _(i):
            full[z, g, core, at_rows(i), :] = gated(
                pl.ds(pl.multiple_of(core * rows + i * BLOCK, BLOCK), BLOCK)
            )
            ready[g, at_rows(i), :] = gated(
                pl.ds(pl.multiple_of((1 - core) * rows + i * BLOCK, BLOCK), BLOCK)
            )

    def accumulate(owner, g):
        left = pl.ds(pl.multiple_of(owner * 2 * share + g * LANES, LANES), LANES)
        right = pl.ds(pl.multiple_of((owner * 2 + 1) * share + g * LANES, LANES), LANES)

        @pl.loop(0, total.shape[1] // (2 * LANES))
        def _(i):
            cols = rows_at(i, 2 * LANES)
            block = jnp.concatenate([full[owner, g, 0], full[owner, g, 1]], axis=1)
            kernel = jnp.concatenate([out_room[left, cols], out_room[right, cols]], axis=0)
            total[:, cols] += jnp.dot(block, kernel, preferred_element_type=jnp.float32)

    def begin(g):
        swap_copy(g).start()
        for way in range(2):

            @pl.when(line.sends(way, 0))
            def _():
                line.copy(way, 0, (g, core)).start()

        other = full.at[z, g, 1 - core]
        remote(other, other, swap_send.at[g], swap_recv.at[g], mate).wait_recv()
        for way in range(2):

            @pl.when(line.sends(way, 0))
            def _():
                line.copy(way, 0, (g, 1 - core)).start()

    def relay(step, g):
        for way in range(2):

            @pl.when(line.receives(way, step))
            def _():
                for of in range(2):
                    owner = line.arrived(way, step, (g, of))
                    if step + 1 < steps:

                        @pl.when(line.sends(way, step + 1))
                        def _():
                            line.copy(way, step + 1, (g, of)).start()

                accumulate(owner, g)

    @pl.loop(0, groups + steps)
    def _(g):
        @pl.when(g < groups)
        def _():
            @pl.when(g >= 2)
            def _():
                await_beside(g)

            @pl.loop(0, chan_count)
            def _(owner):
                @pl.when((distance(owner) > 2) | ((owner // 2 != x) & (g >= 2)))
                def _():
                    project(g, owner)

            featurize(g)

            @pl.when(x == 0)
            def _():
                before_copy(g).start()

            @pl.when(g == 0)
            def _():
                send_weights(groups - 1)

            convolve(g)
            begin(g)

            @pl.when(g < groups - 2)
            def _():
                for c in range(WEIGHT_CHUNKS):
                    forward(g + 2, c)

            @pl.when(g == 0)
            def _():
                out_load.wait()

            accumulate(z, g)

        for step in range(steps):
            at = g - 1 - step

            @pl.when((at >= 0) & (at < groups))
            def _():
                relay(step, at)

    @blocks(rows)
    def _(i):
        result[at_rows(i), :] = total[at_rows(i), :].astype(jnp.bfloat16)

    mate_tokens().wait_send()
    other = weight.at[:, s]
    remote(other, other, mate_send.at[1], mate_recv.at[1], mate).wait_send()
    for copy in sum_copies:
        copy.wait_send()

    @pl.when(x == 1)
    def _():
        for origin in range(2):
            taps_beside(origin, y).wait_send()

    @pl.loop(0, groups)
    def _(g):
        for c in range(WEIGHT_CHUNKS):
            for to in range(2):
                weight_sent(to, g, c).wait_send()
                beside_copy(to, y, g, c).wait_send()
        swap_copy(g).wait_send()

        @pl.when(x == 0)
        def _():
            edge_copy(g).wait_send()
            before_copy(g).wait_send()

        for way in range(2):
            for step in range(steps):

                @pl.when(line.sends(way, step))
                def _():
                    for of in range(2):
                        line.copy(way, step, (g, of)).wait_send()

    for way in range(2):
        for step in range(steps):

            @pl.when(token_line.receives(way, step))
            def _():
                mate_half(way, step, core).wait_send()

            @pl.when(token_line.sends(way, step))
            def _():
                for chunk in range(TOKEN_CHUNKS):
                    token_line.copy(way, step, (chunk,)).wait_send()


def chip_body(tokens, norm_gain, proj_weight, short_filter, long_filter, skip_gain, out_weight):
    chan_count = lax.axis_size("chan")
    rows, width = tokens.shape
    depth, branches, local_chan = proj_weight.shape
    length, share = 2 * rows, local_chan // 2
    groups = share // LANES
    steps = chan_count - 1
    dma = pltpu.SemaphoreType.DMA
    f32, bf16 = jnp.float32, jnp.bfloat16
    vmem = pl.BlockSpec(memory_space=pltpu.VMEM)
    return pl.pallas_call(
        functools.partial(block_kernel, chan_count),
        out_shape=jax.ShapeDtypeStruct((rows, width), bf16),
        in_specs=[ANY, vmem, ANY, vmem, ANY, vmem, ANY],
        out_specs=vmem,
        scratch_shapes=[
            pltpu.VMEM((chan_count, length, width), bf16),
            pltpu.VMEM((groups, 4, depth, branches * LANES), bf16),
            pltpu.VMEM((2, chan_count, 8, LANES), f32),
            pltpu.VMEM((length, LANES), f32),
            pltpu.VMEM((groups, length, branches * LANES), f32),
            pltpu.VMEM((rows, width), bf16),
            pltpu.VMEM(out_weight.shape, bf16),
            pltpu.VMEM((2 * length, length), bf16),
            pltpu.VMEM((groups, 2 * length, LANES), bf16),
            pltpu.VMEM((2, length, LANES), f32),
            pltpu.VMEM((groups, 4, length, LANES), bf16),
            pltpu.VMEM((2, 2 * length, LANES), f32),
            pltpu.VMEM((2 * length, LANES), bf16),
            pltpu.VMEM((groups, branches, 16, LANES), bf16),
            pltpu.VMEM((groups, branches, 16, LANES), bf16),
            pltpu.VMEM((branches, length + 16, LANES), f32),
            pltpu.VMEM((length, LANES), bf16),
            pltpu.VMEM((groups, length, LANES), bf16),
            pltpu.VMEM((groups, length, LANES), bf16),
            pltpu.VMEM((groups, rows, LANES), bf16),
            pltpu.VMEM((chan_count, groups, 2, rows, LANES), bf16),
            pltpu.VMEM((rows, width), f32),
            dma((8,)),
            dma((3 + 2 * steps,)),
            dma((3 + 2 * steps,)),
            dma((2, steps, TOKEN_CHUNKS)),
            dma((2, steps, TOKEN_CHUNKS)),
            dma((2 * chan_count - 1,)),
            dma((2, chan_count)),
            dma((2, groups, WEIGHT_CHUNKS)),
            dma((2, groups, WEIGHT_CHUNKS)),
            dma((2, groups, WEIGHT_CHUNKS)),
            dma((2, groups, WEIGHT_CHUNKS)),
            dma((4,)),
            dma((4,)),
            dma((groups,)),
            dma((groups,)),
            dma((groups,)),
            dma((groups,)),
            dma((groups,)),
            dma((groups,)),
            dma((2, steps, groups, 2)),
            dma((2, steps, groups, 2)),
        ],
        compiler_params=pltpu.CompilerParams(
            collective_id=0, has_side_effects=True, vmem_limit_bytes=63 * 1024 * 1024
        ),
        name="block",
    )(
        tokens,
        norm_gain[None, :],
        proj_weight.transpose(1, 0, 2),
        short_filter,
        long_filter,
        skip_gain[None, :],
        out_weight,
    )


def select_body(mesh):
    if mesh.shape["seq"] == 4 and mesh.shape["groups"] == 2:
        return chip_body
    return body


def solution(mesh):
    placed = (
        P(("groups", "seq"), "chan"),
        P(),
        P("seq", None, "chan"),
        P(None, None, "chan"),
        P("chan", "seq"),
        P("chan"),
        P(None, "chan"),
    )
    return jax.shard_map(
        select_body(mesh), mesh=mesh, in_specs=placed, out_specs=P(("groups", "seq"), "chan"), check_vma=False
    )
```

```python
import functools
import math

import jax
import jax.numpy as jnp
import numpy as np
from jax import lax
from jax.experimental import pallas as pl
from jax.experimental.pallas import tpu as pltpu
from jax.sharding import PartitionSpec as P

SHORT = 3


EPSILON = 1e-06
HIGHEST = lax.Precision.HIGHEST


def from_behind(value, axis, steps):
    count = lax.axis_size(axis)
    initial, last = (max(0, -steps), min(count, count - steps))
    return lax.ppermute(value, axis, [(source, source + steps) for source in range(initial, last)])


def angle_table(row_count, col_count, period, sign):
    row_index = lax.iota(jnp.int32, row_count)[:, None]
    col_index = lax.iota(jnp.int32, col_count)[None, :]
    angles = (row_index * col_index % period).astype(jnp.float32) * (sign * 2.0 * math.pi / period)
    return (jnp.cos(angles), jnp.sin(angles))


def forward_spectrum(signal_rows, first, second):
    channels = signal_rows.shape[0]
    grid_rows = signal_rows.reshape(channels, first, second)
    cos_first, sin_first = angle_table(first, first, first, -1.0)
    part_re = jnp.einsum("cab,ak->ckb", grid_rows, cos_first, precision=HIGHEST)
    part_im = jnp.einsum("cab,ak->ckb", grid_rows, sin_first, precision=HIGHEST)
    twist_cos, twist_sin = angle_table(first, second, first * second, -1.0)
    part_re, part_im = (
        part_re * twist_cos - part_im * twist_sin,
        part_re * twist_sin + part_im * twist_cos,
    )
    cos_second, sin_second = angle_table(second, second, second, -1.0)
    spectrum_real = jnp.einsum("ckb,bm->ckm", part_re, cos_second, precision=HIGHEST) - jnp.einsum(
        "ckb,bm->ckm", part_im, sin_second, precision=HIGHEST
    )
    spec_im = jnp.einsum("ckb,bm->ckm", part_re, sin_second, precision=HIGHEST) + jnp.einsum(
        "ckb,bm->ckm", part_im, cos_second, precision=HIGHEST
    )
    return (spectrum_real, spec_im)


def inverse_spectrum(spectrum_real, spec_im, first, second):
    channels = spectrum_real.shape[0]
    cos_second, sin_second = angle_table(second, second, second, 1.0)
    part_re = jnp.einsum("ckm,bm->ckb", spectrum_real, cos_second, precision=HIGHEST) - jnp.einsum(
        "ckm,bm->ckb", spec_im, sin_second, precision=HIGHEST
    )
    part_im = jnp.einsum("ckm,bm->ckb", spectrum_real, sin_second, precision=HIGHEST) + jnp.einsum(
        "ckm,bm->ckb", spec_im, cos_second, precision=HIGHEST
    )
    twist_cos, twist_sin = angle_table(first, second, first * second, 1.0)
    part_re, part_im = (
        part_re * twist_cos - part_im * twist_sin,
        part_re * twist_sin + part_im * twist_cos,
    )
    cos_first, sin_first = angle_table(first, first, first, 1.0)
    result = jnp.einsum("ckb,ak->cab", part_re, cos_first, precision=HIGHEST) - jnp.einsum(
        "ckb,ak->cab", part_im, sin_first, precision=HIGHEST
    )
    return result.reshape(channels, first * second) / (first * second)


def spectral_conv(signal_rows, filter_rows):
    channels, length = signal_rows.shape
    padded_len = 2 * length
    log_len = padded_len.bit_length() - 1
    first = 1 << log_len // 2
    second = padded_len // first
    zeros_tail = jnp.zeros((channels, length), jnp.float32)
    sig_re, sig_im = forward_spectrum(
        jnp.concatenate([signal_rows, zeros_tail], axis=1), first, second
    )
    tap_re, tap_im = forward_spectrum(
        jnp.concatenate([filter_rows, zeros_tail], axis=1), first, second
    )
    prod_re = sig_re * tap_re - sig_im * tap_im
    prod_im = sig_re * tap_im + sig_im * tap_re
    return inverse_spectrum(prod_re, prod_im, first, second)[:, :length]


def short_filter_output(projected, rim_cells, kernel_coefficients):
    count = kernel_coefficients.shape[0]
    steps_len = projected.shape[2]
    extended = jnp.concatenate([rim_cells, projected], axis=2).astype(jnp.float32)
    total = jnp.zeros(projected.shape, jnp.float32)
    for tap in range(count):
        total = (
            total
            + kernel_coefficients[tap][:, :, None]
            * extended[:, :, count - 1 - tap : count - 1 - tap + steps_len]
        )
    return total.astype(jnp.bfloat16)


def hyena_mixer(keys_rows, values_rows, long_taps, skip_part):
    middle = keys_rows.astype(jnp.float32) * values_rows.astype(jnp.float32)
    return (spectral_conv(middle, long_taps) + skip_part[:, None] * middle).astype(jnp.bfloat16)


def body(tokens, norm_gain, proj_weight, short_filter, long_filter, skip_gain, out_weight):
    seq_count = lax.axis_size("seq")
    local_rows = tokens.shape[0]
    local_chan = proj_weight.shape[2]
    subset = local_chan // seq_count
    length = local_rows * seq_count
    offset = lax.axis_index("seq") * subset
    whole = lax.all_gather(tokens, "chan", axis=1, tiled=True)
    wide = whole.astype(jnp.float32)
    rescaled_signal = (
        wide * lax.rsqrt(jnp.mean(wide * wide, axis=1, keepdims=True) + EPSILON) * norm_gain
    ).astype(jnp.bfloat16)
    projected = lax.dot_general(
        lax.all_gather(proj_weight, "seq", axis=0, tiled=True),
        rescaled_signal,
        (((0,), (1,)), ((), ())),
        preferred_element_type=jnp.float32,
    ).astype(jnp.bfloat16)
    taps_grid = long_filter.reshape(1, seq_count, subset, local_rows)
    long_taps = lax.all_to_all(taps_grid, "seq", split_axis=1, concat_axis=3, tiled=True).reshape(
        subset, length
    )
    skip_part = lax.dynamic_slice_in_dim(skip_gain, offset, subset, 0)
    rim_cells = from_behind(projected[:, :, local_rows - (SHORT - 1) :], "seq", 1)
    featured = short_filter_output(projected, rim_cells, short_filter)
    pair_grid = featured[1:].reshape(2, seq_count, subset, local_rows)
    moved = lax.all_to_all(pair_grid, "seq", split_axis=1, concat_axis=3, tiled=True).reshape(
        2, subset, length
    )
    result = hyena_mixer(moved[0], moved[1], long_taps, skip_part)
    returned = lax.all_to_all(
        result.reshape(1, subset, length), "seq", split_axis=2, concat_axis=0, tiled=True
    )
    returned = returned.reshape(local_chan, local_rows)
    gated = (featured[0].astype(jnp.float32) * returned.astype(jnp.float32)).astype(jnp.bfloat16)
    full_mix = lax.all_gather(gated, "chan", axis=0, tiled=True)
    update = lax.dot_general(
        full_mix, out_weight, (((0,), (0,)), ((), ())), preferred_element_type=jnp.float32
    )
    return (tokens.astype(jnp.float32) + update).astype(jnp.bfloat16)

LANES = 128
BLOCK = 128
SPAN = 512
TOKEN_CHUNKS = 8
WEIGHT_CHUNKS = 4
ANY = pl.BlockSpec(memory_space=pl.ANY)


def remote(src, dst, send_sem, recv_sem, where):
    return pltpu.make_async_remote_copy(
        src_ref=src,
        dst_ref=dst,
        send_sem=send_sem,
        recv_sem=recv_sem,
        device_id=where,
        device_id_type=pl.DeviceIdType.MESH,
    )


class Line:
    def __init__(self, view, count, send_sem, recv_sem, place):
        self.view, self.count, self.place = view, count, place
        self.send_sem, self.recv_sem = send_sem, recv_sem
        self.me = lax.axis_index("chan")

    def move(self, way, step, piece, block, target):
        index = (way, step) + piece
        return remote(
            block, block, self.send_sem.at[index], self.recv_sem.at[index], self.place(target)
        )

    def source(self, way, step):
        return jnp.clip(self.me - (step + 1) * (1 - 2 * way), 0, self.count - 1)

    def copy(self, way, step, piece):
        owner = self.source(way, step - 1)
        target = self.source(way, -2)
        return self.move(way, step, piece, self.view(owner, *piece), target)

    def inside(self, way, by):
        place = self.me + by * (1 - 2 * way)
        return (place >= 0) & (place < self.count)

    def sends(self, way, step):
        return self.inside(way, -step) & self.inside(way, 1)

    def receives(self, way, step):
        return self.inside(way, -1 - step)

    def arrived(self, way, step, piece):
        owner = self.source(way, step)
        self.move(way, step, piece, self.view(owner, *piece), self.me).wait_recv()
        return owner


def block_kernel(
    chan_count,
    tokens,
    gain,
    weights,
    short,
    long_taps,
    skip,
    out_weight,
    result,
    stream,
    weight,
    sums,
    scale,
    partial,
    room,
    out_room,
    table,
    taps,
    turn,
    spectra,
    freq,
    mixed,
    edge_out,
    edge,
    extended,
    query,
    signal,
    before,
    ready,
    full,
    total,
    local_sem,
    mate_send,
    mate_recv,
    token_send,
    token_recv,
    sums_send,
    sums_recv,
    x_send,
    x_recv,
    y_send,
    y_recv,
    tap_send,
    tap_recv,
    edge_send,
    edge_recv,
    before_send,
    before_recv,
    swap_send,
    swap_recv,
    line_send,
    line_recv,
):
    y, s, z = (lax.axis_index(name) for name in ("groups", "seq", "chan"))
    x, core = s // 2, s % 2
    mate_s = s + 1 - 2 * core
    mate = (y, mate_s, z)
    across = (y, (1 - x) * 2 + core, z)
    aslant = (y, (1 - x) * 2 + 1 - core, z)
    beside = (1 - y, s, z)
    rows, width = tokens.shape
    length = 2 * rows
    branches, depth = weights.shape[0], weights.shape[1]
    half = depth // 2
    share = weights.shape[2] // 2
    groups = share // LANES
    rim = edge.shape[2]
    steps = chan_count - 1
    token_rows = rows // TOKEN_CHUNKS
    weight_rows = half // WEIGHT_CHUNKS

    column_peers = [mate] + [
        (y, 2 * x + of, lax.rem(z + by, chan_count))
        for by in range(1, chan_count)
        for of in (core, 1 - core)
    ]
    peers = column_peers + [across, aslant, beside]

    def rows_at(i, count, base=0):
        return pl.ds(pl.multiple_of(base + i * count, count), count)

    def at_rows(i):
        return rows_at(i, BLOCK)

    def blocks(count):
        return pl.loop(0, count // BLOCK)

    def lanes_of(base, g):
        return pl.ds(pl.multiple_of(base + g * LANES, LANES), LANES)

    tap_stage = [(0, 0), (0, length), (1, 0), (1, length)]
    tap_loads = [
        pltpu.make_async_copy(
            long_taps.at[:, pl.ds(j * LANES, LANES)],
            freq.at[which, pl.ds(start, length)],
            local_sem.at[4 + j],
        )
        for j, (which, start) in enumerate(tap_stage)
    ]
    token_load = pltpu.make_async_copy(tokens, room, local_sem.at[0])
    out_load = pltpu.make_async_copy(out_weight, out_room, local_sem.at[1])
    token_load.start()
    for copy in tap_loads:
        copy.start()
    for g in range(groups):
        for b in range(branches):
            pltpu.make_async_copy(
                weights.at[b, :, lanes_of(core * share, g)],
                weight.at[g, s, :, pl.ds(b * LANES, LANES)],
                local_sem.at[2],
            ).start()
    out_load.start()

    barrier = pltpu.get_barrier_semaphore()
    for peer in peers:
        pl.semaphore_signal(barrier, inc=1, device_id=peer, device_id_type=pl.DeviceIdType.MESH)

    sums[core, z] = jnp.zeros(sums.shape[2:], jnp.float32)
    own_gain = gain[:, pl.ds(pl.multiple_of(z * width, width), width)]
    token_load.wait()

    @blocks(rows)
    def _(i):
        raw = room[at_rows(i), :].astype(jnp.float32)
        total[at_rows(i), :] = raw
        stream[z, pl.ds(pl.multiple_of(core * rows + i * BLOCK, BLOCK), BLOCK), :] = (
            raw * own_gain
        ).astype(jnp.bfloat16)
        square = raw * raw
        found = square[:, :LANES]
        for part in range(1, width // LANES):
            found = found + square[:, part * LANES : (part + 1) * LANES]
        sums[core, z, pl.ds(i, 1), :] = jnp.sum(found.T, axis=0, keepdims=True)

    pl.semaphore_wait(barrier, len(peers))

    def token_view(owner, chunk):
        return stream.at[owner, rows_at(chunk, token_rows, core * rows), :]

    token_line = Line(
        token_view, chan_count, token_send, token_recv, lambda to: (y, s, to)
    )
    for chunk in range(TOKEN_CHUNKS):
        for way in range(2):

            @pl.when(token_line.sends(way, 0))
            def _():
                token_line.copy(way, 0, (chunk,)).start()

    def own_half(owner, of):
        return stream.at[owner, pl.ds(pl.multiple_of(of * rows, rows), rows), :]

    def mate_tokens():
        return remote(
            own_half(z, core), own_half(z, core), mate_send.at[0], mate_recv.at[0], mate
        )

    mate_tokens().start()
    sum_copies = [
        remote(
            sums.at[core, z], sums.at[core, z], sums_send.at[at], sums_recv.at[core, z], peer
        )
        for at, peer in enumerate(column_peers)
    ]
    for copy in sum_copies:
        copy.start()
    for g in range(groups):
        for b in range(branches):
            remote(
                weights.at[b, :, lanes_of((1 - core) * share, g)],
                weight.at[g, s, :, pl.ds(b * LANES, LANES)],
                mate_send.at[1],
                mate_recv.at[1],
                mate,
            ).start()

    for j, (which, start) in enumerate(tap_stage):
        tap_loads[j].wait()

        @pl.loop(0, groups)
        def _(g):
            mine = freq[which, rows_at(core * groups + g, BLOCK, start), :]
            taps[g, pl.ds(pl.multiple_of(s * rows + j * LANES, LANES), LANES), :] = mine.T.astype(
                jnp.bfloat16
            )
            other = freq[which, rows_at((1 - core) * groups + g, BLOCK, start), :]
            ready[g, j * LANES : (j + 1) * LANES, :] = other.T.astype(jnp.bfloat16)

    def tap_part(owner, part):
        return taps.at[
            :, pl.ds(pl.multiple_of(owner * rows + part * (rows // 2), rows // 2), rows // 2), :
        ]

    def taps_across(to):
        src = tap_part(s, y) if to == 0 else ready.at[
            :, pl.ds(pl.multiple_of(y * (rows // 2), rows // 2), rows // 2), :
        ]
        return remote(
            src,
            tap_part(s, y),
            tap_send.at[to],
            tap_recv.at[core],
            across if to == 0 else aslant,
        )

    def taps_beside(origin, part):
        view = tap_part(origin, part)
        return remote(view, view, tap_send.at[2 + origin], tap_recv.at[2 + origin], beside)

    def taps_mate():
        return remote(
            ready,
            taps.at[:, pl.ds(pl.multiple_of(s * rows, rows), rows), :],
            mate_send.at[2],
            mate_recv.at[2],
            mate,
        )

    @pl.when(x == 0)
    def _():
        taps_across(0).start()
        taps_across(1).start()

        @pl.loop(0, groups)
        def _(g):
            taps[g, length:, :] = jnp.zeros((length, LANES), jnp.bfloat16)

    taps_mate().start()

    def weight_view(owner, part, g, c):
        return weight.at[g, owner, rows_at(c, weight_rows, part * half), :]

    def weight_sent(to, g, c):
        view = weight_view(s, y, g, c)
        return remote(
            view, view, x_send.at[to, g, c], x_recv.at[core, g, c], across if to == 0 else aslant
        )

    def send_weights(g, chunks=range(WEIGHT_CHUNKS)):
        for c in chunks:
            for to in range(2):
                side = core if to == 0 else 1 - core
                view = weight_view(s, y, g, c)
                for b in range(branches):
                    remote(
                        weights.at[
                            b,
                            rows_at(c, weight_rows, y * half),
                            pl.ds(pl.multiple_of(side * share + g * LANES, LANES), LANES),
                        ],
                        view.at[:, pl.ds(b * LANES, LANES)],
                        x_send.at[to, g, c],
                        x_recv.at[core, g, c],
                        across if to == 0 else aslant,
                    ).start()

    for g in range(groups - 1):
        send_weights(g)
    send_weights(groups - 1, range(WEIGHT_CHUNKS - 2))

    @pl.when(x == 1)
    def _():
        send_weights(groups - 1, range(WEIGHT_CHUNKS - 2, WEIGHT_CHUNKS))


    def beside_copy(origin, part, g, c):
        view = weight_view((1 - x) * 2 + origin, part, g, c)
        return remote(view, view, y_send.at[origin, g, c], y_recv.at[origin, g, c], beside)

    def forward(g, c):
        for origin in range(2):
            view = weight_view((1 - x) * 2 + origin, y, g, c)
            remote(
                view, view, x_send.at[origin, g, c], x_recv.at[origin, g, c], beside
            ).wait_recv()
            beside_copy(origin, y, g, c).start()

    def await_beside(g):
        for c in range(WEIGHT_CHUNKS):
            for origin in range(2):
                beside_copy(origin, 1 - y, g, c).wait_recv()

    @blocks(length)
    def _(i):
        row = lax.broadcasted_iota(jnp.int32, (BLOCK, LANES), 0) + i * BLOCK
        lane = lax.broadcasted_iota(jnp.int32, (BLOCK, LANES), 1)
        unit = math.pi / (4 * length)
        odd = 2 * row + 1
        small = odd.astype(jnp.float32) * unit
        turn[0, at_rows(i), :] = jnp.cos(small)
        turn[1, at_rows(i), :] = jnp.sin(small)
        period = 8 * length
        angle = (odd * (2 * lane + 1) % period).astype(jnp.float32) * unit
        cos, sin = jnp.cos(angle), jnp.sin(angle)
        stride = (odd * (2 * LANES) % period).astype(jnp.float32) * unit
        step_cos, step_sin = jnp.cos(stride), jnp.sin(stride)
        for a in range(length // LANES):
            table[at_rows(i), a * LANES : (a + 1) * LANES] = cos.astype(jnp.bfloat16)
            table[rows_at(i, BLOCK, length), a * LANES : (a + 1) * LANES] = sin.astype(
                jnp.bfloat16
            )
            cos, sin = cos * step_cos - sin * step_sin, sin * step_cos + cos * step_sin

    for g in range(groups):

        @blocks(length)
        def _(i):
            partial[g, at_rows(i), :] = jnp.zeros((BLOCK, branches * LANES), jnp.float32)

    def spectrum(which, column):
        @pl.loop(0, 2 * length // SPAN)
        def _(i):
            at = rows_at(i, SPAN)
            freq[which, at, :] = jnp.dot(
                table[at, :], column(), preferred_element_type=jnp.float32
            )

    def tap_spectra(g):
        @pl.loop(0, 2 * length // SPAN)
        def _(i):
            at = rows_at(i, SPAN)
            both = jnp.concatenate([taps[g, :length, :], taps[g, length:, :]], axis=1)
            found = jnp.dot(table[at, :], both, preferred_element_type=jnp.float32)
            freq[0, at, :] = found[:, :LANES]
            freq[1, at, :] = found[:, LANES:]

        @blocks(length)
        def _(i):
            low, high = at_rows(i), rows_at(i, BLOCK, length)
            cos, sin = turn[0, low, :], turn[1, low, :]

            def turned(which):
                real, imag = freq[which, low, :], -freq[which, high, :]
                return (cos * real - sin * imag) / length, (cos * imag + sin * real) / length

            real, imag = turned(0)
            late_real, late_imag = turned(1)
            place = lax.broadcasted_iota(jnp.int32, (BLOCK, LANES), 0)
            sign = (1 - 2 * (place % 2)).astype(jnp.float32)
            spectra[g, 0, low, :] = real.astype(jnp.bfloat16)
            spectra[g, 1, low, :] = imag.astype(jnp.bfloat16)
            spectra[g, 2, low, :] = (late_real - sign * imag).astype(jnp.bfloat16)
            spectra[g, 3, low, :] = (late_imag + sign * real).astype(jnp.bfloat16)

    def project(g, owner):
        @pl.loop(0, length // SPAN)
        def _(i):
            at = rows_at(i, SPAN)
            partial[g, at, :] += jnp.dot(
                stream[owner, at, :], weight[g, owner], preferred_element_type=jnp.float32
            )

    at_end = (z == 0) | (z == chan_count - 1)

    def projects_early(g, owner):
        far = jnp.abs(z - owner)
        own = owner // 2 == x
        return (
            (own & ((far <= 1) | ((far == 2) & (at_end | (g == 0)))))
            | (jnp.logical_not(own) & (far <= 2) & ((g == 0) | ((g == 1) & at_end)))
        )

    def to_mate(way, step, chunk):
        block = token_view(token_line.source(way, step), chunk)
        index = 3 + way * steps + step
        return remote(block, block, mate_send.at[index], mate_recv.at[index], mate)

    def mate_half(way, step, of):
        block = own_half(token_line.source(way, step), of)
        index = 3 + way * steps + step
        return remote(block, block, mate_send.at[index], mate_recv.at[index], mate)

    def await_mate(step):
        for way in range(2):

            @pl.when(token_line.receives(way, step))
            def _():
                mate_half(way, step, 1 - core).wait_recv()

    @pl.loop(0, steps * TOKEN_CHUNKS)
    def _(tick):
        step, chunk = tick // TOKEN_CHUNKS, tick % TOKEN_CHUNKS
        for way in range(2):

            @pl.when(token_line.receives(way, step))
            def _():
                token_line.arrived(way, step, (chunk,))
                to_mate(way, step, chunk).start()

            @pl.when(
                (step + 1 < steps)
                & token_line.receives(way, step)
                & token_line.sends(way, step + 1)
            )
            def _():
                token_line.copy(way, step + 1, (chunk,)).start()

        @pl.when((tick == TOKEN_CHUNKS // 2) & (x == 1))
        def _():
            for origin in range(2):
                view = tap_part(origin, y)
                remote(
                    view, view, tap_send.at[origin], tap_recv.at[origin], beside
                ).wait_recv()
                taps_beside(origin, y).start()

        @pl.when((tick % 2 == 1) & (tick >= 3) & (tick < 3 + 4 * WEIGHT_CHUNKS))
        def _():
            at = (tick - 3) // 2
            forward(at // WEIGHT_CHUNKS, at % WEIGHT_CHUNKS)

        @pl.when(tick == TOKEN_CHUNKS)
        def _():
            mate_half_own = own_half(z, 1 - core)
            remote(
                mate_half_own, mate_half_own, mate_send.at[0], mate_recv.at[0], mate
            ).wait_recv()
            await_mate(0)
            pltpu.make_async_copy(
                weight.at[:, s], weight.at[:, s], local_sem.at[2]
            ).wait()
            other = weight.at[:, mate_s]
            remote(other, other, mate_send.at[1], mate_recv.at[1], mate).wait_recv()
            other = taps.at[:, pl.ds(pl.multiple_of(mate_s * rows, rows), rows), :]
            remote(other, other, mate_send.at[2], mate_recv.at[2], mate).wait_recv()

            @pl.when(x == 1)
            def _():
                for origin in range(2):
                    taps_beside(origin, 1 - y).wait_recv()

        @pl.when((step == 1) & (chunk % 2 == 0))
        def _():
            tap_spectra(chunk // 2)

        @pl.when(tick == 2 * TOKEN_CHUNKS)
        def _():
            await_mate(1)

        owner = 2 * x + chunk // groups
        far = jnp.abs(z - owner)

        @pl.when(
            projects_early(chunk % groups, owner)
            & (((step == 1) & (far <= 1)) | ((step == 2) & (far == 2)))
        )
        def _():
            project(chunk % groups, owner)

        @pl.when(tick == 2 * TOKEN_CHUNKS)
        def _():
            await_beside(0)

        @pl.when((tick == 2 * TOKEN_CHUNKS + TOKEN_CHUNKS // 2) & at_end)
        def _():
            await_beside(1)

        guest = 2 * (1 - x) + (chunk // 2) % 2

        @pl.when((step == 2) & (chunk % 2 == 0) & projects_early(chunk // 4, guest))
        def _():
            project(chunk // 4, guest)

    await_mate(2)
    for by in range(1, chan_count):
        for of in range(2):
            view = sums.at[of, lax.rem(z + by, chan_count)]
            remote(
                view, view, sums_send.at[0], sums_recv.at[of, lax.rem(z + by, chan_count)], mate
            ).wait_recv()
    view = sums.at[1 - core, z]
    remote(view, view, sums_send.at[0], sums_recv.at[1 - core, z], mate).wait_recv()

    @blocks(length)
    def _(i):
        of, at = i // (rows // BLOCK), i % (rows // BLOCK)
        found = sums[of, 0, pl.ds(at, 1), :]
        for owner in range(1, chan_count):
            found = found + sums[of, owner, pl.ds(at, 1), :]
        found = lax.rsqrt(found / (chan_count * width) + EPSILON)
        scale[at_rows(i), :] = jnp.broadcast_to(found, (BLOCK, LANES)).T

    taps_mate().wait_send()

    @pl.when(x == 0)
    def _():
        taps_across(0).wait_send()
        taps_across(1).wait_send()

    def edge_copy(g):
        return remote(
            edge_out.at[g], edge.at[g], edge_send.at[g], edge_recv.at[g], across
        )

    def before_copy(g):
        return remote(
            signal.at[g], before.at[g], before_send.at[g], before_recv.at[g], across
        )

    def swap_copy(g):
        return remote(
            ready.at[g], full.at[z, g, core], swap_send.at[g], swap_recv.at[g], mate
        )

    line = Line(
        lambda owner, g, of: full.at[owner, g, of],
        chan_count,
        line_send,
        line_recv,
        lambda to: (y, s, to),
    )

    def projected(g, b, at):
        return (partial[g, at, b * LANES : (b + 1) * LANES] * scale[at, :]).astype(jnp.bfloat16)

    def featurize(g):
        @pl.when(x == 0)
        def _():
            for b in range(branches):
                edge_out[g, b] = projected(g, b, pl.ds(length - rim, rim))
                extended[b, 0:rim, :] = jnp.zeros((rim, LANES), jnp.float32)
            edge_copy(g).start()

        @blocks(length)
        def _(i):
            for b in range(branches):
                extended[b, pl.ds(pl.multiple_of(rim + i * BLOCK, rim), BLOCK), :] = projected(
                    g, b, at_rows(i)
                ).astype(jnp.float32)

        @pl.when(x == 1)
        def _():
            edge_copy(g).wait_recv()
            for b in range(branches):
                extended[b, 0:rim, :] = edge[g, b].astype(jnp.float32)

        chosen = lanes_of(core * share, g)
        coefficient = [
            [short[tap, b : b + 1, chosen] for b in range(branches)] for tap in range(SHORT)
        ]

        @blocks(length)
        def _(i):
            found = []
            for b in range(branches):
                value = jnp.zeros((BLOCK, LANES), jnp.float32)
                for tap in range(SHORT):
                    value = value + coefficient[tap][b] * extended[
                        b, pl.ds(rim - tap + i * BLOCK, BLOCK), :
                    ]
                found.append(value.astype(jnp.bfloat16))
            query[at_rows(i), :] = found[0]
            signal[g, at_rows(i), :] = (
                found[1].astype(jnp.float32) * found[2].astype(jnp.float32)
            ).astype(jnp.bfloat16)

    def convolve(g):
        spectrum(0, lambda: signal[g])

        def product(i, which, first):
            low, high = at_rows(i), rows_at(i, BLOCK, length)
            cos, sin = freq[which, low, :], freq[which, high, :]
            real = spectra[g, first, low, :].astype(jnp.float32)
            imag = spectra[g, first + 1, low, :].astype(jnp.float32)
            return cos * real + sin * imag, sin * real - cos * imag

        @pl.when(x == 0)
        def _():
            @blocks(length)
            def _(i):
                real, imag = product(i, 0, 0)
                mixed[at_rows(i), :] = real.astype(jnp.bfloat16)
                mixed[rows_at(i, BLOCK, length), :] = imag.astype(jnp.bfloat16)

        @pl.when(x == 1)
        def _():
            before_copy(g).wait_recv()
            spectrum(1, lambda: before[g])

            @blocks(length)
            def _(i):
                real, imag = product(i, 0, 0)
                more_real, more_imag = product(i, 1, 2)
                mixed[at_rows(i), :] = (real + more_real).astype(jnp.bfloat16)
                mixed[rows_at(i, BLOCK, length), :] = (imag + more_imag).astype(jnp.bfloat16)

        @pl.loop(0, length // SPAN)
        def _(i):
            low, high = rows_at(i, SPAN), rows_at(i, SPAN, length)
            freq[0, low, :] = jnp.dot(
                table[low, :], mixed[:length, :], preferred_element_type=jnp.float32
            ) + jnp.dot(table[high, :], mixed[length:, :], preferred_element_type=jnp.float32)

        direct = skip[:, lanes_of(core * share, g)]

        def gated(at):
            longer = freq[0, at, :] + direct * signal[g, at, :].astype(jnp.float32)
            longer = longer.astype(jnp.bfloat16).astype(jnp.float32)
            return (query[at, :].astype(jnp.float32) * longer).astype(jnp.bfloat16)

        @blocks(rows)
        def _(i):
            full[z, g, core, at_rows(i), :] = gated(
                pl.ds(pl.multiple_of(core * rows + i * BLOCK, BLOCK), BLOCK)
            )
            ready[g, at_rows(i), :] = gated(
                pl.ds(pl.multiple_of((1 - core) * rows + i * BLOCK, BLOCK), BLOCK)
            )

    def accumulate(owner, g):
        left = pl.ds(pl.multiple_of(owner * 2 * share + g * LANES, LANES), LANES)
        right = pl.ds(pl.multiple_of((owner * 2 + 1) * share + g * LANES, LANES), LANES)

        @pl.loop(0, total.shape[1] // (2 * LANES))
        def _(i):
            cols = rows_at(i, 2 * LANES)
            block = jnp.concatenate([full[owner, g, 0], full[owner, g, 1]], axis=1)
            kernel = jnp.concatenate([out_room[left, cols], out_room[right, cols]], axis=0)
            total[:, cols] += jnp.dot(block, kernel, preferred_element_type=jnp.float32)

    def begin(g):
        swap_copy(g).start()
        for way in range(2):

            @pl.when(line.sends(way, 0))
            def _():
                line.copy(way, 0, (g, core)).start()

        other = full.at[z, g, 1 - core]
        remote(other, other, swap_send.at[g], swap_recv.at[g], mate).wait_recv()
        for way in range(2):

            @pl.when(line.sends(way, 0))
            def _():
                line.copy(way, 0, (g, 1 - core)).start()

    def relay(way, step, g):
        @pl.when(line.receives(way, step))
        def _():
            for of in range(2):
                owner = line.arrived(way, step, (g, of))
                if step + 1 < steps:

                    @pl.when(line.sends(way, step + 1))
                    def _():
                        line.copy(way, step + 1, (g, of)).start()

            accumulate(owner, g)

    def settle():
        mate_tokens().wait_send()
        other = weight.at[:, s]
        remote(other, other, mate_send.at[1], mate_recv.at[1], mate).wait_send()
        for copy in sum_copies:
            copy.wait_send()

        @pl.when(x == 1)
        def _():
            for origin in range(2):
                taps_beside(origin, y).wait_send()

        @pl.loop(0, groups)
        def _(g):
            for c in range(WEIGHT_CHUNKS):
                for to in range(2):
                    weight_sent(to, g, c).wait_send()
                    beside_copy(to, y, g, c).wait_send()

            @pl.when(x == 0)
            def _():
                edge_copy(g).wait_send()
                before_copy(g).wait_send()

        for way in range(2):
            for step in range(steps):

                @pl.when(token_line.receives(way, step))
                def _():
                    mate_half(way, step, core).wait_send()

                @pl.when(token_line.sends(way, step))
                def _():
                    @pl.loop(0, TOKEN_CHUNKS)
                    def _(chunk):
                        token_line.copy(way, step, (chunk,)).wait_send()

    @pl.loop(0, 2 * groups + steps)
    def _(g):
        @pl.when(g < groups)
        def _():
            @pl.when((g >= 2) | ((g == 1) & jnp.logical_not(at_end)))
            def _():
                await_beside(g)

            @pl.loop(0, chan_count)
            def _(owner):
                @pl.when(jnp.logical_not(projects_early(g, owner)))
                def _():
                    project(g, owner)

            featurize(g)

            @pl.when(x == 0)
            def _():
                before_copy(g).start()

            @pl.when((x == 0) & (g < 2))
            def _():
                send_weights(groups - 1, [WEIGHT_CHUNKS - 2 + g])

            convolve(g)
            begin(g)

            @pl.when(g < groups - 2)
            def _():
                for c in range(WEIGHT_CHUNKS):
                    forward(g + 2, c)

            @pl.when(g == 0)
            def _():
                out_load.wait()

            accumulate(z, g)

        @pl.when(g == groups + 1)
        def _():
            settle()

        @pl.loop(0, 2)
        def _(k):
            way = jnp.where(z < chan_count // 2, 1 - k, k)
            lag = jnp.where(at_end, groups, 1 + k)
            for step in range(steps):
                at = g - lag - step * jnp.where(at_end, 1, 2 - k)

                @pl.when((at >= 0) & (at < groups))
                def _():
                    relay(way, step, at)

    @blocks(rows)
    def _(i):
        result[at_rows(i), :] = total[at_rows(i), :].astype(jnp.bfloat16)

    @pl.loop(0, groups)
    def _(g):
        swap_copy(g).wait_send()

        for way in range(2):
            for step in range(steps):

                @pl.when(line.sends(way, step))
                def _():
                    for of in range(2):
                        line.copy(way, step, (g, of)).wait_send()


def chip_body(tokens, norm_gain, proj_weight, short_filter, long_filter, skip_gain, out_weight):
    chan_count = lax.axis_size("chan")
    rows, width = tokens.shape
    depth, branches, local_chan = proj_weight.shape
    length, share = 2 * rows, local_chan // 2
    groups = share // LANES
    steps = chan_count - 1
    dma = pltpu.SemaphoreType.DMA
    f32, bf16 = jnp.float32, jnp.bfloat16
    vmem = pl.BlockSpec(memory_space=pltpu.VMEM)
    return pl.pallas_call(
        functools.partial(block_kernel, chan_count),
        out_shape=jax.ShapeDtypeStruct((rows, width), bf16),
        in_specs=[ANY, vmem, ANY, vmem, ANY, vmem, ANY],
        out_specs=vmem,
        scratch_shapes=[
            pltpu.VMEM((chan_count, length, width), bf16),
            pltpu.VMEM((groups, 4, depth, branches * LANES), bf16),
            pltpu.VMEM((2, chan_count, 8, LANES), f32),
            pltpu.VMEM((length, LANES), f32),
            pltpu.VMEM((groups, length, branches * LANES), f32),
            pltpu.VMEM((rows, width), bf16),
            pltpu.VMEM(out_weight.shape, bf16),
            pltpu.VMEM((2 * length, length), bf16),
            pltpu.VMEM((groups, 2 * length, LANES), bf16),
            pltpu.VMEM((2, length, LANES), f32),
            pltpu.VMEM((groups, 4, length, LANES), bf16),
            pltpu.VMEM((2, 2 * length, LANES), f32),
            pltpu.VMEM((2 * length, LANES), bf16),
            pltpu.VMEM((groups, branches, 16, LANES), bf16),
            pltpu.VMEM((groups, branches, 16, LANES), bf16),
            pltpu.VMEM((branches, length + 16, LANES), f32),
            pltpu.VMEM((length, LANES), bf16),
            pltpu.VMEM((groups, length, LANES), bf16),
            pltpu.VMEM((groups, length, LANES), bf16),
            pltpu.VMEM((groups, rows, LANES), bf16),
            pltpu.VMEM((chan_count, groups, 2, rows, LANES), bf16),
            pltpu.VMEM((rows, width), f32),
            dma((8,)),
            dma((3 + 2 * steps,)),
            dma((3 + 2 * steps,)),
            dma((2, steps, TOKEN_CHUNKS)),
            dma((2, steps, TOKEN_CHUNKS)),
            dma((2 * chan_count - 1,)),
            dma((2, chan_count)),
            dma((2, groups, WEIGHT_CHUNKS)),
            dma((2, groups, WEIGHT_CHUNKS)),
            dma((2, groups, WEIGHT_CHUNKS)),
            dma((2, groups, WEIGHT_CHUNKS)),
            dma((4,)),
            dma((4,)),
            dma((groups,)),
            dma((groups,)),
            dma((groups,)),
            dma((groups,)),
            dma((groups,)),
            dma((groups,)),
            dma((2, steps, groups, 2)),
            dma((2, steps, groups, 2)),
        ],
        compiler_params=pltpu.CompilerParams(
            collective_id=0, has_side_effects=True, vmem_limit_bytes=63 * 1024 * 1024
        ),
        name="block",
    )(
        tokens,
        norm_gain[None, :],
        proj_weight.transpose(1, 0, 2),
        short_filter,
        long_filter,
        skip_gain[None, :],
        out_weight,
    )


def select_body(mesh):
    if (mesh.shape["groups"], mesh.shape["seq"], mesh.shape["chan"]) == (2, 4, 4):
        return chip_body
    return body


def solution(mesh):
    placed = (
        P(("groups", "seq"), "chan"),
        P(),
        P("seq", None, "chan"),
        P(None, None, "chan"),
        P("chan", "seq"),
        P("chan"),
        P(None, "chan"),
    )
    return jax.shard_map(
        select_body(mesh), mesh=mesh, in_specs=placed, out_specs=P(("groups", "seq"), "chan"), check_vma=False
    )
```

```python
import functools
import math

import jax
import jax.numpy as jnp
import numpy as np
from jax import lax
from jax.experimental import pallas as pl
from jax.experimental.pallas import tpu as pltpu
from jax.sharding import PartitionSpec as P

SHORT = 3


EPSILON = 1e-06
HIGHEST = lax.Precision.HIGHEST


def from_behind(value, axis, steps):
    count = lax.axis_size(axis)
    initial, last = (max(0, -steps), min(count, count - steps))
    return lax.ppermute(value, axis, [(source, source + steps) for source in range(initial, last)])


def angle_table(row_count, col_count, period, sign):
    row_index = lax.iota(jnp.int32, row_count)[:, None]
    col_index = lax.iota(jnp.int32, col_count)[None, :]
    angles = (row_index * col_index % period).astype(jnp.float32) * (sign * 2.0 * math.pi / period)
    return (jnp.cos(angles), jnp.sin(angles))


def forward_spectrum(signal_rows, first, second):
    channels = signal_rows.shape[0]
    grid_rows = signal_rows.reshape(channels, first, second)
    cos_first, sin_first = angle_table(first, first, first, -1.0)
    part_re = jnp.einsum("cab,ak->ckb", grid_rows, cos_first, precision=HIGHEST)
    part_im = jnp.einsum("cab,ak->ckb", grid_rows, sin_first, precision=HIGHEST)
    twist_cos, twist_sin = angle_table(first, second, first * second, -1.0)
    part_re, part_im = (
        part_re * twist_cos - part_im * twist_sin,
        part_re * twist_sin + part_im * twist_cos,
    )
    cos_second, sin_second = angle_table(second, second, second, -1.0)
    spectrum_real = jnp.einsum("ckb,bm->ckm", part_re, cos_second, precision=HIGHEST) - jnp.einsum(
        "ckb,bm->ckm", part_im, sin_second, precision=HIGHEST
    )
    spec_im = jnp.einsum("ckb,bm->ckm", part_re, sin_second, precision=HIGHEST) + jnp.einsum(
        "ckb,bm->ckm", part_im, cos_second, precision=HIGHEST
    )
    return (spectrum_real, spec_im)


def inverse_spectrum(spectrum_real, spec_im, first, second):
    channels = spectrum_real.shape[0]
    cos_second, sin_second = angle_table(second, second, second, 1.0)
    part_re = jnp.einsum("ckm,bm->ckb", spectrum_real, cos_second, precision=HIGHEST) - jnp.einsum(
        "ckm,bm->ckb", spec_im, sin_second, precision=HIGHEST
    )
    part_im = jnp.einsum("ckm,bm->ckb", spectrum_real, sin_second, precision=HIGHEST) + jnp.einsum(
        "ckm,bm->ckb", spec_im, cos_second, precision=HIGHEST
    )
    twist_cos, twist_sin = angle_table(first, second, first * second, 1.0)
    part_re, part_im = (
        part_re * twist_cos - part_im * twist_sin,
        part_re * twist_sin + part_im * twist_cos,
    )
    cos_first, sin_first = angle_table(first, first, first, 1.0)
    result = jnp.einsum("ckb,ak->cab", part_re, cos_first, precision=HIGHEST) - jnp.einsum(
        "ckb,ak->cab", part_im, sin_first, precision=HIGHEST
    )
    return result.reshape(channels, first * second) / (first * second)


def spectral_conv(signal_rows, filter_rows):
    channels, length = signal_rows.shape
    padded_len = 2 * length
    log_len = padded_len.bit_length() - 1
    first = 1 << log_len // 2
    second = padded_len // first
    zeros_tail = jnp.zeros((channels, length), jnp.float32)
    sig_re, sig_im = forward_spectrum(
        jnp.concatenate([signal_rows, zeros_tail], axis=1), first, second
    )
    tap_re, tap_im = forward_spectrum(
        jnp.concatenate([filter_rows, zeros_tail], axis=1), first, second
    )
    prod_re = sig_re * tap_re - sig_im * tap_im
    prod_im = sig_re * tap_im + sig_im * tap_re
    return inverse_spectrum(prod_re, prod_im, first, second)[:, :length]


def short_filter_output(projected, rim_cells, kernel_coefficients):
    count = kernel_coefficients.shape[0]
    steps_len = projected.shape[2]
    extended = jnp.concatenate([rim_cells, projected], axis=2).astype(jnp.float32)
    total = jnp.zeros(projected.shape, jnp.float32)
    for tap in range(count):
        total = (
            total
            + kernel_coefficients[tap][:, :, None]
            * extended[:, :, count - 1 - tap : count - 1 - tap + steps_len]
        )
    return total.astype(jnp.bfloat16)


def hyena_mixer(keys_rows, values_rows, long_taps, skip_part):
    middle = keys_rows.astype(jnp.float32) * values_rows.astype(jnp.float32)
    return (spectral_conv(middle, long_taps) + skip_part[:, None] * middle).astype(jnp.bfloat16)


def body(tokens, norm_gain, proj_weight, short_filter, long_filter, skip_gain, out_weight):
    seq_count = lax.axis_size("seq")
    local_rows = tokens.shape[0]
    local_chan = proj_weight.shape[2]
    subset = local_chan // seq_count
    length = local_rows * seq_count
    offset = lax.axis_index("seq") * subset
    whole = lax.all_gather(tokens, "chan", axis=1, tiled=True)
    wide = whole.astype(jnp.float32)
    rescaled_signal = (
        wide * lax.rsqrt(jnp.mean(wide * wide, axis=1, keepdims=True) + EPSILON) * norm_gain
    ).astype(jnp.bfloat16)
    projected = lax.dot_general(
        lax.all_gather(proj_weight, "seq", axis=0, tiled=True),
        rescaled_signal,
        (((0,), (1,)), ((), ())),
        preferred_element_type=jnp.float32,
    ).astype(jnp.bfloat16)
    taps_grid = long_filter.reshape(1, seq_count, subset, local_rows)
    long_taps = lax.all_to_all(taps_grid, "seq", split_axis=1, concat_axis=3, tiled=True).reshape(
        subset, length
    )
    skip_part = lax.dynamic_slice_in_dim(skip_gain, offset, subset, 0)
    rim_cells = from_behind(projected[:, :, local_rows - (SHORT - 1) :], "seq", 1)
    featured = short_filter_output(projected, rim_cells, short_filter)
    pair_grid = featured[1:].reshape(2, seq_count, subset, local_rows)
    moved = lax.all_to_all(pair_grid, "seq", split_axis=1, concat_axis=3, tiled=True).reshape(
        2, subset, length
    )
    result = hyena_mixer(moved[0], moved[1], long_taps, skip_part)
    returned = lax.all_to_all(
        result.reshape(1, subset, length), "seq", split_axis=2, concat_axis=0, tiled=True
    )
    returned = returned.reshape(local_chan, local_rows)
    gated = (featured[0].astype(jnp.float32) * returned.astype(jnp.float32)).astype(jnp.bfloat16)
    full_mix = lax.all_gather(gated, "chan", axis=0, tiled=True)
    update = lax.dot_general(
        full_mix, out_weight, (((0,), (0,)), ((), ())), preferred_element_type=jnp.float32
    )
    return (tokens.astype(jnp.float32) + update).astype(jnp.bfloat16)

LANES = 128
BLOCK = 128
SPAN = 512
TOKEN_CHUNKS = 8
WEIGHT_CHUNKS = 4
ANY = pl.BlockSpec(memory_space=pl.ANY)


def remote(src, dst, send_sem, recv_sem, where):
    return pltpu.make_async_remote_copy(
        src_ref=src,
        dst_ref=dst,
        send_sem=send_sem,
        recv_sem=recv_sem,
        device_id=where,
        device_id_type=pl.DeviceIdType.MESH,
    )


class Line:
    def __init__(self, view, count, send_sem, recv_sem, place):
        self.view, self.count, self.place = view, count, place
        self.send_sem, self.recv_sem = send_sem, recv_sem
        self.me = lax.axis_index("chan")

    def move(self, way, step, piece, block, target):
        index = (way, step) + piece
        return remote(
            block, block, self.send_sem.at[index], self.recv_sem.at[index], self.place(target)
        )

    def source(self, way, step):
        return jnp.clip(self.me - (step + 1) * (1 - 2 * way), 0, self.count - 1)

    def copy(self, way, step, piece):
        owner = self.source(way, step - 1)
        target = self.source(way, -2)
        return self.move(way, step, piece, self.view(owner, *piece), target)

    def inside(self, way, by):
        place = self.me + by * (1 - 2 * way)
        return (place >= 0) & (place < self.count)

    def sends(self, way, step):
        return self.inside(way, -step) & self.inside(way, 1)

    def receives(self, way, step):
        return self.inside(way, -1 - step)

    def arrived(self, way, step, piece):
        owner = self.source(way, step)
        self.move(way, step, piece, self.view(owner, *piece), self.me).wait_recv()
        return owner


def block_kernel(
    chan_count,
    tokens,
    gain,
    weights,
    short,
    long_taps,
    skip,
    out_weight,
    result,
    stream,
    weight,
    sums,
    scale,
    partial,
    room,
    out_room,
    table,
    taps,
    turn,
    spectra,
    freq,
    mixed,
    edge_out,
    edge,
    extended,
    query,
    signal,
    before,
    ready,
    full,
    total,
    local_sem,
    mate_send,
    mate_recv,
    token_send,
    token_recv,
    sums_send,
    sums_recv,
    x_send,
    x_recv,
    y_send,
    y_recv,
    tap_send,
    tap_recv,
    edge_send,
    edge_recv,
    before_send,
    before_recv,
    swap_send,
    swap_recv,
    line_send,
    line_recv,
):
    y, s, z = (lax.axis_index(name) for name in ("groups", "seq", "chan"))
    x, core = s // 2, s % 2
    mate_s = s + 1 - 2 * core
    mate = (y, mate_s, z)
    across = (y, (1 - x) * 2 + core, z)
    aslant = (y, (1 - x) * 2 + 1 - core, z)
    beside = (1 - y, s, z)
    rows, width = tokens.shape
    length = 2 * rows
    branches, depth = weights.shape[0], weights.shape[1]
    half = depth // 2
    share = weights.shape[2] // 2
    groups = share // LANES
    rim = edge.shape[2]
    steps = chan_count - 1
    token_rows = rows // TOKEN_CHUNKS
    weight_rows = half // WEIGHT_CHUNKS

    column_peers = [mate] + [
        (y, 2 * x + of, lax.rem(z + by, chan_count))
        for by in range(1, chan_count)
        for of in (core, 1 - core)
    ]
    peers = column_peers + [across, aslant, beside]

    def rows_at(i, count, base=0):
        return pl.ds(pl.multiple_of(base + i * count, count), count)

    def at_rows(i):
        return rows_at(i, BLOCK)

    def blocks(count):
        return pl.loop(0, count // BLOCK)

    def lanes_of(base, g):
        return pl.ds(pl.multiple_of(base + g * LANES, LANES), LANES)

    tap_stage = [(0, 0), (0, length), (1, 0), (1, length)]
    tap_loads = [
        pltpu.make_async_copy(
            long_taps.at[:, pl.ds(j * LANES, LANES)],
            freq.at[which, pl.ds(start, length)],
            local_sem.at[4 + j],
        )
        for j, (which, start) in enumerate(tap_stage)
    ]
    token_load = pltpu.make_async_copy(tokens, room, local_sem.at[0])
    out_load = pltpu.make_async_copy(out_weight, out_room, local_sem.at[1])
    token_load.start()
    for copy in tap_loads:
        copy.start()
    for g in range(groups):
        for b in range(branches):
            pltpu.make_async_copy(
                weights.at[b, :, lanes_of(core * share, g)],
                weight.at[g, s, :, pl.ds(b * LANES, LANES)],
                local_sem.at[2],
            ).start()
    out_load.start()

    barrier = pltpu.get_barrier_semaphore()
    for peer in peers:
        pl.semaphore_signal(barrier, inc=1, device_id=peer, device_id_type=pl.DeviceIdType.MESH)

    sums[core, z] = jnp.zeros(sums.shape[2:], jnp.float32)
    own_gain = gain[:, pl.ds(pl.multiple_of(z * width, width), width)]
    token_load.wait()

    @blocks(rows)
    def _(i):
        raw = room[at_rows(i), :].astype(jnp.float32)
        total[at_rows(i), :] = raw
        stream[z, pl.ds(pl.multiple_of(core * rows + i * BLOCK, BLOCK), BLOCK), :] = (
            raw * own_gain
        ).astype(jnp.bfloat16)
        square = raw * raw
        found = square[:, :LANES]
        for part in range(1, width // LANES):
            found = found + square[:, part * LANES : (part + 1) * LANES]
        sums[core, z, pl.ds(i, 1), :] = jnp.sum(found.T, axis=0, keepdims=True)

    pl.semaphore_wait(barrier, len(peers))

    def token_view(owner, chunk):
        return stream.at[owner, rows_at(chunk, token_rows, core * rows), :]

    token_line = Line(
        token_view, chan_count, token_send, token_recv, lambda to: (y, s, to)
    )
    for chunk in range(TOKEN_CHUNKS):
        for way in range(2):

            @pl.when(token_line.sends(way, 0))
            def _():
                token_line.copy(way, 0, (chunk,)).start()

    def own_half(owner, of):
        return stream.at[owner, pl.ds(pl.multiple_of(of * rows, rows), rows), :]

    def mate_tokens():
        return remote(
            own_half(z, core), own_half(z, core), mate_send.at[0], mate_recv.at[0], mate
        )

    mate_tokens().start()
    sum_copies = [
        remote(
            sums.at[core, z], sums.at[core, z], sums_send.at[at], sums_recv.at[core, z], peer
        )
        for at, peer in enumerate(column_peers)
    ]
    for copy in sum_copies:
        copy.start()
    for g in range(groups):
        for b in range(branches):
            remote(
                weights.at[b, :, lanes_of((1 - core) * share, g)],
                weight.at[g, s, :, pl.ds(b * LANES, LANES)],
                mate_send.at[1],
                mate_recv.at[1],
                mate,
            ).start()

    for j, (which, start) in enumerate(tap_stage):
        tap_loads[j].wait()

        @pl.loop(0, groups)
        def _(g):
            mine = freq[which, rows_at(core * groups + g, BLOCK, start), :]
            taps[g, pl.ds(pl.multiple_of(s * rows + j * LANES, LANES), LANES), :] = mine.T.astype(
                jnp.bfloat16
            )
            other = freq[which, rows_at((1 - core) * groups + g, BLOCK, start), :]
            ready[g, j * LANES : (j + 1) * LANES, :] = other.T.astype(jnp.bfloat16)

    def tap_part(owner, part):
        return taps.at[
            :, pl.ds(pl.multiple_of(owner * rows + part * (rows // 2), rows // 2), rows // 2), :
        ]

    def taps_across(to):
        src = tap_part(s, y) if to == 0 else ready.at[
            :, pl.ds(pl.multiple_of(y * (rows // 2), rows // 2), rows // 2), :
        ]
        return remote(
            src,
            tap_part(s, y),
            tap_send.at[to],
            tap_recv.at[core],
            across if to == 0 else aslant,
        )

    def taps_beside(origin, part):
        view = tap_part(origin, part)
        return remote(view, view, tap_send.at[2 + origin], tap_recv.at[2 + origin], beside)

    def taps_mate():
        return remote(
            ready,
            taps.at[:, pl.ds(pl.multiple_of(s * rows, rows), rows), :],
            mate_send.at[2],
            mate_recv.at[2],
            mate,
        )

    @pl.when(x == 0)
    def _():
        taps_across(0).start()
        taps_across(1).start()

        @pl.loop(0, groups)
        def _(g):
            taps[g, length:, :] = jnp.zeros((length, LANES), jnp.bfloat16)

    taps_mate().start()

    def weight_view(owner, part, g, c):
        return weight.at[g, owner, rows_at(c, weight_rows, part * half), :]

    def weight_sent(to, g, c):
        view = weight_view(s, y, g, c)
        return remote(
            view, view, x_send.at[to, g, c], x_recv.at[core, g, c], across if to == 0 else aslant
        )

    def send_weights(g, chunks=range(WEIGHT_CHUNKS)):
        for c in chunks:
            for to in range(2):
                side = core if to == 0 else 1 - core
                view = weight_view(s, y, g, c)
                for b in range(branches):
                    remote(
                        weights.at[
                            b,
                            rows_at(c, weight_rows, y * half),
                            pl.ds(pl.multiple_of(side * share + g * LANES, LANES), LANES),
                        ],
                        view.at[:, pl.ds(b * LANES, LANES)],
                        x_send.at[to, g, c],
                        x_recv.at[core, g, c],
                        across if to == 0 else aslant,
                    ).start()

    for g in range(groups - 1):
        send_weights(g)

    @pl.when(x == 1)
    def _():
        send_weights(groups - 1)


    def beside_copy(origin, part, g, c):
        view = weight_view((1 - x) * 2 + origin, part, g, c)
        return remote(view, view, y_send.at[origin, g, c], y_recv.at[origin, g, c], beside)

    def forward(g, c):
        for origin in range(2):
            view = weight_view((1 - x) * 2 + origin, y, g, c)
            remote(
                view, view, x_send.at[origin, g, c], x_recv.at[origin, g, c], beside
            ).wait_recv()
            beside_copy(origin, y, g, c).start()

    def await_beside(g):
        for c in range(WEIGHT_CHUNKS):
            for origin in range(2):
                beside_copy(origin, 1 - y, g, c).wait_recv()

    @blocks(length)
    def _(i):
        row = lax.broadcasted_iota(jnp.int32, (BLOCK, LANES), 0) + i * BLOCK
        lane = lax.broadcasted_iota(jnp.int32, (BLOCK, LANES), 1)
        unit = math.pi / (4 * length)
        odd = 2 * row + 1
        small = odd.astype(jnp.float32) * unit
        turn[0, at_rows(i), :] = jnp.cos(small)
        turn[1, at_rows(i), :] = jnp.sin(small)
        period = 8 * length
        angle = (odd * (2 * lane + 1) % period).astype(jnp.float32) * unit
        cos, sin = jnp.cos(angle), jnp.sin(angle)
        stride = (odd * (2 * LANES) % period).astype(jnp.float32) * unit
        step_cos, step_sin = jnp.cos(stride), jnp.sin(stride)
        for a in range(length // LANES):
            table[at_rows(i), a * LANES : (a + 1) * LANES] = cos.astype(jnp.bfloat16)
            table[rows_at(i, BLOCK, length), a * LANES : (a + 1) * LANES] = sin.astype(
                jnp.bfloat16
            )
            cos, sin = cos * step_cos - sin * step_sin, sin * step_cos + cos * step_sin

    for g in range(groups):

        @blocks(length)
        def _(i):
            partial[g, at_rows(i), :] = jnp.zeros((BLOCK, branches * LANES), jnp.float32)

    def spectrum(which, column):
        @pl.loop(0, 2 * length // SPAN)
        def _(i):
            at = rows_at(i, SPAN)
            freq[which, at, :] = jnp.dot(
                table[at, :], column(), preferred_element_type=jnp.float32
            )

    def tap_spectra(g):
        @pl.loop(0, 2 * length // SPAN)
        def _(i):
            at = rows_at(i, SPAN)
            both = jnp.concatenate([taps[g, :length, :], taps[g, length:, :]], axis=1)
            found = jnp.dot(table[at, :], both, preferred_element_type=jnp.float32)
            freq[0, at, :] = found[:, :LANES]
            freq[1, at, :] = found[:, LANES:]

        @blocks(length)
        def _(i):
            low, high = at_rows(i), rows_at(i, BLOCK, length)
            cos, sin = turn[0, low, :], turn[1, low, :]

            def turned(which):
                real, imag = freq[which, low, :], -freq[which, high, :]
                return (cos * real - sin * imag) / length, (cos * imag + sin * real) / length

            real, imag = turned(0)
            late_real, late_imag = turned(1)
            place = lax.broadcasted_iota(jnp.int32, (BLOCK, LANES), 0)
            sign = (1 - 2 * (place % 2)).astype(jnp.float32)
            spectra[g, 0, low, :] = real.astype(jnp.bfloat16)
            spectra[g, 1, low, :] = imag.astype(jnp.bfloat16)
            spectra[g, 2, low, :] = (late_real - sign * imag).astype(jnp.bfloat16)
            spectra[g, 3, low, :] = (late_imag + sign * real).astype(jnp.bfloat16)

    def project(g, owner):
        @pl.loop(0, length // SPAN)
        def _(i):
            at = rows_at(i, SPAN)
            partial[g, at, :] += jnp.dot(
                stream[owner, at, :], weight[g, owner], preferred_element_type=jnp.float32
            )

    at_end = (z == 0) | (z == chan_count - 1)

    def projects_early(g, owner):
        far = jnp.abs(z - owner)
        own = owner // 2 == x
        return (
            (own & ((far <= 1) | ((far == 2) & (at_end | (g == 0)))))
            | (jnp.logical_not(own) & (far <= 2) & ((g == 0) | ((g == 1) & at_end)))
        )

    def to_mate(way, step, chunk):
        block = token_view(token_line.source(way, step), chunk)
        index = 3 + way * steps + step
        return remote(block, block, mate_send.at[index], mate_recv.at[index], mate)

    def mate_half(way, step, of):
        block = own_half(token_line.source(way, step), of)
        index = 3 + way * steps + step
        return remote(block, block, mate_send.at[index], mate_recv.at[index], mate)

    def await_mate(step):
        for way in range(2):

            @pl.when(token_line.receives(way, step))
            def _():
                mate_half(way, step, 1 - core).wait_recv()

    @pl.loop(0, steps * TOKEN_CHUNKS)
    def _(tick):
        step, chunk = tick // TOKEN_CHUNKS, tick % TOKEN_CHUNKS
        for way in range(2):

            @pl.when(token_line.receives(way, step))
            def _():
                token_line.arrived(way, step, (chunk,))
                to_mate(way, step, chunk).start()

            @pl.when(
                (step + 1 < steps)
                & token_line.receives(way, step)
                & token_line.sends(way, step + 1)
            )
            def _():
                token_line.copy(way, step + 1, (chunk,)).start()

        @pl.when((tick == TOKEN_CHUNKS // 2) & (x == 1))
        def _():
            for origin in range(2):
                view = tap_part(origin, y)
                remote(
                    view, view, tap_send.at[origin], tap_recv.at[origin], beside
                ).wait_recv()
                taps_beside(origin, y).start()

        @pl.when((tick % 2 == 1) & (tick >= 3) & (tick < 7 + 4 * WEIGHT_CHUNKS))
        def _():
            at = (tick - 3) // 2
            forward(at // WEIGHT_CHUNKS, at % WEIGHT_CHUNKS)

        @pl.when(tick == TOKEN_CHUNKS)
        def _():
            mate_half_own = own_half(z, 1 - core)
            remote(
                mate_half_own, mate_half_own, mate_send.at[0], mate_recv.at[0], mate
            ).wait_recv()
            await_mate(0)
            pltpu.make_async_copy(
                weight.at[:, s], weight.at[:, s], local_sem.at[2]
            ).wait()
            other = weight.at[:, mate_s]
            remote(other, other, mate_send.at[1], mate_recv.at[1], mate).wait_recv()
            other = taps.at[:, pl.ds(pl.multiple_of(mate_s * rows, rows), rows), :]
            remote(other, other, mate_send.at[2], mate_recv.at[2], mate).wait_recv()

            @pl.when(x == 1)
            def _():
                for origin in range(2):
                    taps_beside(origin, 1 - y).wait_recv()

        @pl.when((step == 1) & (chunk % 2 == 0))
        def _():
            tap_spectra(chunk // 2)

        @pl.when(tick == 2 * TOKEN_CHUNKS)
        def _():
            await_mate(1)

        owner = 2 * x + chunk // groups
        far = jnp.abs(z - owner)

        @pl.when(
            projects_early(chunk % groups, owner)
            & (((step == 1) & (far <= 1)) | ((step == 2) & (far == 2)))
        )
        def _():
            project(chunk % groups, owner)

        @pl.when(tick == 2 * TOKEN_CHUNKS)
        def _():
            await_beside(0)

        @pl.when((tick == 2 * TOKEN_CHUNKS + TOKEN_CHUNKS // 2) & at_end)
        def _():
            await_beside(1)

        guest = 2 * (1 - x) + (chunk // 2) % 2

        @pl.when((step == 2) & (chunk % 2 == 0) & projects_early(chunk // 4, guest))
        def _():
            project(chunk // 4, guest)

    await_mate(2)
    for by in range(1, chan_count):
        for of in range(2):
            view = sums.at[of, lax.rem(z + by, chan_count)]
            remote(
                view, view, sums_send.at[0], sums_recv.at[of, lax.rem(z + by, chan_count)], mate
            ).wait_recv()
    view = sums.at[1 - core, z]
    remote(view, view, sums_send.at[0], sums_recv.at[1 - core, z], mate).wait_recv()

    @blocks(length)
    def _(i):
        of, at = i // (rows // BLOCK), i % (rows // BLOCK)
        found = sums[of, 0, pl.ds(at, 1), :]
        for owner in range(1, chan_count):
            found = found + sums[of, owner, pl.ds(at, 1), :]
        found = lax.rsqrt(found / (chan_count * width) + EPSILON)
        scale[at_rows(i), :] = jnp.broadcast_to(found, (BLOCK, LANES)).T

    taps_mate().wait_send()

    @pl.when(x == 0)
    def _():
        taps_across(0).wait_send()
        taps_across(1).wait_send()

    def edge_copy(g):
        return remote(
            edge_out.at[g], edge.at[g], edge_send.at[g], edge_recv.at[g], across
        )

    def before_copy(g):
        return remote(
            signal.at[g], before.at[g], before_send.at[g], before_recv.at[g], across
        )

    def swap_copy(g):
        return remote(
            ready.at[g], full.at[z, g, core], swap_send.at[g], swap_recv.at[g], mate
        )

    line = Line(
        lambda owner, g, of: full.at[owner, g, of],
        chan_count,
        line_send,
        line_recv,
        lambda to: (y, s, to),
    )

    def projected(g, b, at):
        return (partial[g, at, b * LANES : (b + 1) * LANES] * scale[at, :]).astype(jnp.bfloat16)

    def featurize(g):
        @pl.when(x == 0)
        def _():
            for b in range(branches):
                edge_out[g, b] = projected(g, b, pl.ds(length - rim, rim))
                extended[b, 0:rim, :] = jnp.zeros((rim, LANES), jnp.float32)
            edge_copy(g).start()

        @blocks(length)
        def _(i):
            for b in range(branches):
                extended[b, pl.ds(pl.multiple_of(rim + i * BLOCK, rim), BLOCK), :] = projected(
                    g, b, at_rows(i)
                ).astype(jnp.float32)

        @pl.when(x == 1)
        def _():
            edge_copy(g).wait_recv()
            for b in range(branches):
                extended[b, 0:rim, :] = edge[g, b].astype(jnp.float32)

        chosen = lanes_of(core * share, g)
        coefficient = [
            [short[tap, b : b + 1, chosen] for b in range(branches)] for tap in range(SHORT)
        ]

        @blocks(length)
        def _(i):
            found = []
            for b in range(branches):
                value = jnp.zeros((BLOCK, LANES), jnp.float32)
                for tap in range(SHORT):
                    value = value + coefficient[tap][b] * extended[
                        b, pl.ds(rim - tap + i * BLOCK, BLOCK), :
                    ]
                found.append(value.astype(jnp.bfloat16))
            query[at_rows(i), :] = found[0]
            signal[g, at_rows(i), :] = (
                found[1].astype(jnp.float32) * found[2].astype(jnp.float32)
            ).astype(jnp.bfloat16)

    def convolve(g):
        spectrum(0, lambda: signal[g])

        def product(i, which, first):
            low, high = at_rows(i), rows_at(i, BLOCK, length)
            cos, sin = freq[which, low, :], freq[which, high, :]
            real = spectra[g, first, low, :].astype(jnp.float32)
            imag = spectra[g, first + 1, low, :].astype(jnp.float32)
            return cos * real + sin * imag, sin * real - cos * imag

        @pl.when(x == 0)
        def _():
            @blocks(length)
            def _(i):
                real, imag = product(i, 0, 0)
                mixed[at_rows(i), :] = real.astype(jnp.bfloat16)
                mixed[rows_at(i, BLOCK, length), :] = imag.astype(jnp.bfloat16)

        @pl.when(x == 1)
        def _():
            before_copy(g).wait_recv()
            spectrum(1, lambda: before[g])

            @blocks(length)
            def _(i):
                real, imag = product(i, 0, 0)
                more_real, more_imag = product(i, 1, 2)
                mixed[at_rows(i), :] = (real + more_real).astype(jnp.bfloat16)
                mixed[rows_at(i, BLOCK, length), :] = (imag + more_imag).astype(jnp.bfloat16)

        @pl.loop(0, length // SPAN)
        def _(i):
            low, high = rows_at(i, SPAN), rows_at(i, SPAN, length)
            freq[0, low, :] = jnp.dot(
                table[low, :], mixed[:length, :], preferred_element_type=jnp.float32
            ) + jnp.dot(table[high, :], mixed[length:, :], preferred_element_type=jnp.float32)

        direct = skip[:, lanes_of(core * share, g)]

        def gated(at):
            longer = freq[0, at, :] + direct * signal[g, at, :].astype(jnp.float32)
            longer = longer.astype(jnp.bfloat16).astype(jnp.float32)
            return (query[at, :].astype(jnp.float32) * longer).astype(jnp.bfloat16)

        @blocks(rows)
        def _(i):
            full[z, g, core, at_rows(i), :] = gated(
                pl.ds(pl.multiple_of(core * rows + i * BLOCK, BLOCK), BLOCK)
            )
            ready[g, at_rows(i), :] = gated(
                pl.ds(pl.multiple_of((1 - core) * rows + i * BLOCK, BLOCK), BLOCK)
            )

    def accumulate(owner, g):
        left = pl.ds(pl.multiple_of(owner * 2 * share + g * LANES, LANES), LANES)
        right = pl.ds(pl.multiple_of((owner * 2 + 1) * share + g * LANES, LANES), LANES)

        @pl.loop(0, total.shape[1] // (2 * LANES))
        def _(i):
            cols = rows_at(i, 2 * LANES)
            block = jnp.concatenate([full[owner, g, 0], full[owner, g, 1]], axis=1)
            kernel = jnp.concatenate([out_room[left, cols], out_room[right, cols]], axis=0)
            total[:, cols] += jnp.dot(block, kernel, preferred_element_type=jnp.float32)

    def begin(g):
        swap_copy(g).start()
        for way in range(2):

            @pl.when(line.sends(way, 0))
            def _():
                line.copy(way, 0, (g, core)).start()

        other = full.at[z, g, 1 - core]
        remote(other, other, swap_send.at[g], swap_recv.at[g], mate).wait_recv()
        for way in range(2):

            @pl.when(line.sends(way, 0))
            def _():
                line.copy(way, 0, (g, 1 - core)).start()

    def relay(way, step, g):
        @pl.when(line.receives(way, step))
        def _():
            for of in range(2):
                owner = line.arrived(way, step, (g, of))
                if step + 1 < steps:

                    @pl.when(line.sends(way, step + 1))
                    def _():
                        line.copy(way, step + 1, (g, of)).start()

            accumulate(owner, g)

    def settle():
        mate_tokens().wait_send()
        other = weight.at[:, s]
        remote(other, other, mate_send.at[1], mate_recv.at[1], mate).wait_send()
        for copy in sum_copies:
            copy.wait_send()

        @pl.when(x == 1)
        def _():
            for origin in range(2):
                taps_beside(origin, y).wait_send()

        @pl.loop(0, groups)
        def _(g):
            for c in range(WEIGHT_CHUNKS):
                for to in range(2):
                    weight_sent(to, g, c).wait_send()
                    beside_copy(to, y, g, c).wait_send()

            @pl.when(x == 0)
            def _():
                edge_copy(g).wait_send()
                before_copy(g).wait_send()

        for way in range(2):
            for step in range(steps):

                @pl.when(token_line.receives(way, step))
                def _():
                    mate_half(way, step, core).wait_send()

                @pl.when(token_line.sends(way, step))
                def _():
                    @pl.loop(0, TOKEN_CHUNKS)
                    def _(chunk):
                        token_line.copy(way, step, (chunk,)).wait_send()

    @pl.loop(0, 2 * groups + steps)
    def _(g):
        @pl.when(g < groups)
        def _():
            @pl.when((g >= 2) | ((g == 1) & jnp.logical_not(at_end)))
            def _():
                await_beside(g)

            @pl.loop(0, chan_count)
            def _(owner):
                @pl.when(jnp.logical_not(projects_early(g, owner)))
                def _():
                    project(g, owner)

            featurize(g)

            @pl.when(x == 0)
            def _():
                before_copy(g).start()

            for at in range(2):

                @pl.when((x == 0) & (g == at))
                def _():
                    send_weights(groups - 1, [2 * at, 2 * at + 1])

            @pl.when(g == 0)
            def _():
                forward(groups - 2, 2)
                forward(groups - 2, 3)

            convolve(g)
            begin(g)

            @pl.when(g < 2)
            def _():
                forward(groups - 1, 2 * g)
                forward(groups - 1, 2 * g + 1)

            @pl.when(g == 0)
            def _():
                out_load.wait()

            accumulate(z, g)

        @pl.when(g == groups + 1)
        def _():
            settle()

        @pl.loop(0, 2)
        def _(k):
            way = jnp.where(z < chan_count // 2, 1 - k, k)
            lag = jnp.where(at_end, groups, 1 + k)
            for step in range(steps):
                at = g - lag - step * jnp.where(at_end, 1, 2 - k)

                @pl.when((at >= 0) & (at < groups))
                def _():
                    relay(way, step, at)

    @blocks(rows)
    def _(i):
        result[at_rows(i), :] = total[at_rows(i), :].astype(jnp.bfloat16)

    @pl.loop(0, groups)
    def _(g):
        swap_copy(g).wait_send()

        for way in range(2):
            for step in range(steps):

                @pl.when(line.sends(way, step))
                def _():
                    for of in range(2):
                        line.copy(way, step, (g, of)).wait_send()


def chip_body(tokens, norm_gain, proj_weight, short_filter, long_filter, skip_gain, out_weight):
    chan_count = lax.axis_size("chan")
    rows, width = tokens.shape
    depth, branches, local_chan = proj_weight.shape
    length, share = 2 * rows, local_chan // 2
    groups = share // LANES
    steps = chan_count - 1
    dma = pltpu.SemaphoreType.DMA
    f32, bf16 = jnp.float32, jnp.bfloat16
    vmem = pl.BlockSpec(memory_space=pltpu.VMEM)
    return pl.pallas_call(
        functools.partial(block_kernel, chan_count),
        out_shape=jax.ShapeDtypeStruct((rows, width), bf16),
        in_specs=[ANY, vmem, ANY, vmem, ANY, vmem, ANY],
        out_specs=vmem,
        scratch_shapes=[
            pltpu.VMEM((chan_count, length, width), bf16),
            pltpu.VMEM((groups, 4, depth, branches * LANES), bf16),
            pltpu.VMEM((2, chan_count, 8, LANES), f32),
            pltpu.VMEM((length, LANES), f32),
            pltpu.VMEM((groups, length, branches * LANES), f32),
            pltpu.VMEM((rows, width), bf16),
            pltpu.VMEM(out_weight.shape, bf16),
            pltpu.VMEM((2 * length, length), bf16),
            pltpu.VMEM((groups, 2 * length, LANES), bf16),
            pltpu.VMEM((2, length, LANES), f32),
            pltpu.VMEM((groups, 4, length, LANES), bf16),
            pltpu.VMEM((2, 2 * length, LANES), f32),
            pltpu.VMEM((2 * length, LANES), bf16),
            pltpu.VMEM((groups, branches, 16, LANES), bf16),
            pltpu.VMEM((groups, branches, 16, LANES), bf16),
            pltpu.VMEM((branches, length + 16, LANES), f32),
            pltpu.VMEM((length, LANES), bf16),
            pltpu.VMEM((groups, length, LANES), bf16),
            pltpu.VMEM((groups, length, LANES), bf16),
            pltpu.VMEM((groups, rows, LANES), bf16),
            pltpu.VMEM((chan_count, groups, 2, rows, LANES), bf16),
            pltpu.VMEM((rows, width), f32),
            dma((8,)),
            dma((3 + 2 * steps,)),
            dma((3 + 2 * steps,)),
            dma((2, steps, TOKEN_CHUNKS)),
            dma((2, steps, TOKEN_CHUNKS)),
            dma((2 * chan_count - 1,)),
            dma((2, chan_count)),
            dma((2, groups, WEIGHT_CHUNKS)),
            dma((2, groups, WEIGHT_CHUNKS)),
            dma((2, groups, WEIGHT_CHUNKS)),
            dma((2, groups, WEIGHT_CHUNKS)),
            dma((4,)),
            dma((4,)),
            dma((groups,)),
            dma((groups,)),
            dma((groups,)),
            dma((groups,)),
            dma((groups,)),
            dma((groups,)),
            dma((2, steps, groups, 2)),
            dma((2, steps, groups, 2)),
        ],
        compiler_params=pltpu.CompilerParams(
            collective_id=0, has_side_effects=True, vmem_limit_bytes=63 * 1024 * 1024
        ),
        name="block",
    )(
        tokens,
        norm_gain[None, :],
        proj_weight.transpose(1, 0, 2),
        short_filter,
        long_filter,
        skip_gain[None, :],
        out_weight,
    )


def select_body(mesh):
    if (mesh.shape["groups"], mesh.shape["seq"], mesh.shape["chan"]) == (2, 4, 4):
        return chip_body
    return body


def solution(mesh):
    placed = (
        P(("groups", "seq"), "chan"),
        P(),
        P("seq", None, "chan"),
        P(None, None, "chan"),
        P("chan", "seq"),
        P("chan"),
        P(None, "chan"),
    )
    return jax.shard_map(
        select_body(mesh), mesh=mesh, in_specs=placed, out_specs=P(("groups", "seq"), "chan"), check_vma=False
    )
```

```python
import functools
import math

import jax
import jax.numpy as jnp
import numpy as np
from jax import lax
from jax.experimental import pallas as pl
from jax.experimental.pallas import tpu as pltpu
from jax.sharding import PartitionSpec as P

SHORT = 3


EPSILON = 1e-06
HIGHEST = lax.Precision.HIGHEST


def from_behind(value, axis, steps):
    count = lax.axis_size(axis)
    initial, last = (max(0, -steps), min(count, count - steps))
    return lax.ppermute(value, axis, [(source, source + steps) for source in range(initial, last)])


def angle_table(row_count, col_count, period, sign):
    row_index = lax.iota(jnp.int32, row_count)[:, None]
    col_index = lax.iota(jnp.int32, col_count)[None, :]
    angles = (row_index * col_index % period).astype(jnp.float32) * (sign * 2.0 * math.pi / period)
    return (jnp.cos(angles), jnp.sin(angles))


def forward_spectrum(signal_rows, first, second):
    channels = signal_rows.shape[0]
    grid_rows = signal_rows.reshape(channels, first, second)
    cos_first, sin_first = angle_table(first, first, first, -1.0)
    part_re = jnp.einsum("cab,ak->ckb", grid_rows, cos_first, precision=HIGHEST)
    part_im = jnp.einsum("cab,ak->ckb", grid_rows, sin_first, precision=HIGHEST)
    twist_cos, twist_sin = angle_table(first, second, first * second, -1.0)
    part_re, part_im = (
        part_re * twist_cos - part_im * twist_sin,
        part_re * twist_sin + part_im * twist_cos,
    )
    cos_second, sin_second = angle_table(second, second, second, -1.0)
    spectrum_real = jnp.einsum("ckb,bm->ckm", part_re, cos_second, precision=HIGHEST) - jnp.einsum(
        "ckb,bm->ckm", part_im, sin_second, precision=HIGHEST
    )
    spec_im = jnp.einsum("ckb,bm->ckm", part_re, sin_second, precision=HIGHEST) + jnp.einsum(
        "ckb,bm->ckm", part_im, cos_second, precision=HIGHEST
    )
    return (spectrum_real, spec_im)


def inverse_spectrum(spectrum_real, spec_im, first, second):
    channels = spectrum_real.shape[0]
    cos_second, sin_second = angle_table(second, second, second, 1.0)
    part_re = jnp.einsum("ckm,bm->ckb", spectrum_real, cos_second, precision=HIGHEST) - jnp.einsum(
        "ckm,bm->ckb", spec_im, sin_second, precision=HIGHEST
    )
    part_im = jnp.einsum("ckm,bm->ckb", spectrum_real, sin_second, precision=HIGHEST) + jnp.einsum(
        "ckm,bm->ckb", spec_im, cos_second, precision=HIGHEST
    )
    twist_cos, twist_sin = angle_table(first, second, first * second, 1.0)
    part_re, part_im = (
        part_re * twist_cos - part_im * twist_sin,
        part_re * twist_sin + part_im * twist_cos,
    )
    cos_first, sin_first = angle_table(first, first, first, 1.0)
    result = jnp.einsum("ckb,ak->cab", part_re, cos_first, precision=HIGHEST) - jnp.einsum(
        "ckb,ak->cab", part_im, sin_first, precision=HIGHEST
    )
    return result.reshape(channels, first * second) / (first * second)


def spectral_conv(signal_rows, filter_rows):
    channels, length = signal_rows.shape
    padded_len = 2 * length
    log_len = padded_len.bit_length() - 1
    first = 1 << log_len // 2
    second = padded_len // first
    zeros_tail = jnp.zeros((channels, length), jnp.float32)
    sig_re, sig_im = forward_spectrum(
        jnp.concatenate([signal_rows, zeros_tail], axis=1), first, second
    )
    tap_re, tap_im = forward_spectrum(
        jnp.concatenate([filter_rows, zeros_tail], axis=1), first, second
    )
    prod_re = sig_re * tap_re - sig_im * tap_im
    prod_im = sig_re * tap_im + sig_im * tap_re
    return inverse_spectrum(prod_re, prod_im, first, second)[:, :length]


def short_filter_output(projected, rim_cells, kernel_coefficients):
    count = kernel_coefficients.shape[0]
    steps_len = projected.shape[2]
    extended = jnp.concatenate([rim_cells, projected], axis=2).astype(jnp.float32)
    total = jnp.zeros(projected.shape, jnp.float32)
    for tap in range(count):
        total = (
            total
            + kernel_coefficients[tap][:, :, None]
            * extended[:, :, count - 1 - tap : count - 1 - tap + steps_len]
        )
    return total.astype(jnp.bfloat16)


def hyena_mixer(keys_rows, values_rows, long_taps, skip_part):
    middle = keys_rows.astype(jnp.float32) * values_rows.astype(jnp.float32)
    return (spectral_conv(middle, long_taps) + skip_part[:, None] * middle).astype(jnp.bfloat16)


def body(tokens, norm_gain, proj_weight, short_filter, long_filter, skip_gain, out_weight):
    seq_count = lax.axis_size("seq")
    local_rows = tokens.shape[0]
    local_chan = proj_weight.shape[2]
    subset = local_chan // seq_count
    length = local_rows * seq_count
    offset = lax.axis_index("seq") * subset
    whole = lax.all_gather(tokens, "chan", axis=1, tiled=True)
    wide = whole.astype(jnp.float32)
    rescaled_signal = (
        wide * lax.rsqrt(jnp.mean(wide * wide, axis=1, keepdims=True) + EPSILON) * norm_gain
    ).astype(jnp.bfloat16)
    projected = lax.dot_general(
        lax.all_gather(proj_weight, "seq", axis=0, tiled=True),
        rescaled_signal,
        (((0,), (1,)), ((), ())),
        preferred_element_type=jnp.float32,
    ).astype(jnp.bfloat16)
    taps_grid = long_filter.reshape(1, seq_count, subset, local_rows)
    long_taps = lax.all_to_all(taps_grid, "seq", split_axis=1, concat_axis=3, tiled=True).reshape(
        subset, length
    )
    skip_part = lax.dynamic_slice_in_dim(skip_gain, offset, subset, 0)
    rim_cells = from_behind(projected[:, :, local_rows - (SHORT - 1) :], "seq", 1)
    featured = short_filter_output(projected, rim_cells, short_filter)
    pair_grid = featured[1:].reshape(2, seq_count, subset, local_rows)
    moved = lax.all_to_all(pair_grid, "seq", split_axis=1, concat_axis=3, tiled=True).reshape(
        2, subset, length
    )
    result = hyena_mixer(moved[0], moved[1], long_taps, skip_part)
    returned = lax.all_to_all(
        result.reshape(1, subset, length), "seq", split_axis=2, concat_axis=0, tiled=True
    )
    returned = returned.reshape(local_chan, local_rows)
    gated = (featured[0].astype(jnp.float32) * returned.astype(jnp.float32)).astype(jnp.bfloat16)
    full_mix = lax.all_gather(gated, "chan", axis=0, tiled=True)
    update = lax.dot_general(
        full_mix, out_weight, (((0,), (0,)), ((), ())), preferred_element_type=jnp.float32
    )
    return (tokens.astype(jnp.float32) + update).astype(jnp.bfloat16)

LANES = 128
BLOCK = 128
SPAN = 512
TOKEN_CHUNKS = 8
WEIGHT_CHUNKS = 4
ANY = pl.BlockSpec(memory_space=pl.ANY)


def remote(src, dst, send_sem, recv_sem, where):
    return pltpu.make_async_remote_copy(
        src_ref=src,
        dst_ref=dst,
        send_sem=send_sem,
        recv_sem=recv_sem,
        device_id=where,
        device_id_type=pl.DeviceIdType.MESH,
    )


class Line:
    def __init__(self, view, count, send_sem, recv_sem, place):
        self.view, self.count, self.place = view, count, place
        self.send_sem, self.recv_sem = send_sem, recv_sem
        self.me = lax.axis_index("chan")

    def move(self, way, step, piece, block, target):
        index = (way, step) + piece
        return remote(
            block, block, self.send_sem.at[index], self.recv_sem.at[index], self.place(target)
        )

    def source(self, way, step):
        return jnp.clip(self.me - (step + 1) * (1 - 2 * way), 0, self.count - 1)

    def copy(self, way, step, piece):
        owner = self.source(way, step - 1)
        target = self.source(way, -2)
        return self.move(way, step, piece, self.view(owner, *piece), target)

    def inside(self, way, by):
        place = self.me + by * (1 - 2 * way)
        return (place >= 0) & (place < self.count)

    def sends(self, way, step):
        return self.inside(way, -step) & self.inside(way, 1)

    def receives(self, way, step):
        return self.inside(way, -1 - step)

    def arrived(self, way, step, piece):
        owner = self.source(way, step)
        self.move(way, step, piece, self.view(owner, *piece), self.me).wait_recv()
        return owner


def block_kernel(
    chan_count,
    tokens,
    gain,
    weights,
    short,
    long_taps,
    skip,
    out_weight,
    result,
    stream,
    weight,
    sums,
    scale,
    partial,
    room,
    out_room,
    table,
    taps,
    turn,
    spectra,
    freq,
    mixed,
    edge_out,
    edge,
    extended,
    query,
    signal,
    before,
    ready,
    full,
    total,
    local_sem,
    mate_send,
    mate_recv,
    token_send,
    token_recv,
    sums_send,
    sums_recv,
    x_send,
    x_recv,
    y_send,
    y_recv,
    tap_send,
    tap_recv,
    edge_send,
    edge_recv,
    before_send,
    before_recv,
    swap_send,
    swap_recv,
    line_send,
    line_recv,
):
    y, s, z = (lax.axis_index(name) for name in ("groups", "seq", "chan"))
    x, core = s // 2, s % 2
    mate_s = s + 1 - 2 * core
    mate = (y, mate_s, z)
    across = (y, (1 - x) * 2 + core, z)
    aslant = (y, (1 - x) * 2 + 1 - core, z)
    beside = (1 - y, s, z)
    rows, width = tokens.shape
    length = 2 * rows
    branches, depth = weights.shape[0], weights.shape[1]
    half = depth // 2
    share = weights.shape[2] // 2
    groups = share // LANES
    rim = edge.shape[2]
    steps = chan_count - 1
    token_rows = rows // TOKEN_CHUNKS
    weight_rows = half // WEIGHT_CHUNKS

    column_peers = [mate] + [
        (y, 2 * x + of, lax.rem(z + by, chan_count))
        for by in range(1, chan_count)
        for of in (core, 1 - core)
    ]
    peers = column_peers + [across, aslant, beside]

    def rows_at(i, count, base=0):
        return pl.ds(pl.multiple_of(base + i * count, count), count)

    def at_rows(i):
        return rows_at(i, BLOCK)

    def blocks(count):
        return pl.loop(0, count // BLOCK)

    def lanes_of(base, g):
        return pl.ds(pl.multiple_of(base + g * LANES, LANES), LANES)

    tap_stage = [(0, 0), (0, length), (1, 0), (1, length)]
    tap_loads = [
        pltpu.make_async_copy(
            long_taps.at[:, pl.ds(j * LANES, LANES)],
            freq.at[which, pl.ds(start, length)],
            local_sem.at[4 + j],
        )
        for j, (which, start) in enumerate(tap_stage)
    ]
    token_load = pltpu.make_async_copy(tokens, room, local_sem.at[0])
    out_load = pltpu.make_async_copy(out_weight, out_room, local_sem.at[1])
    token_load.start()
    for copy in tap_loads:
        copy.start()
    for g in range(groups):
        for b in range(branches):
            pltpu.make_async_copy(
                weights.at[b, :, lanes_of(core * share, g)],
                weight.at[g, s, :, pl.ds(b * LANES, LANES)],
                local_sem.at[2],
            ).start()
    out_load.start()

    barrier = pltpu.get_barrier_semaphore()
    for peer in peers:
        pl.semaphore_signal(barrier, inc=1, device_id=peer, device_id_type=pl.DeviceIdType.MESH)

    sums[core, z] = jnp.zeros(sums.shape[2:], jnp.float32)
    own_gain = gain[:, pl.ds(pl.multiple_of(z * width, width), width)]
    token_load.wait()

    @blocks(rows)
    def _(i):
        raw = room[at_rows(i), :].astype(jnp.float32)
        total[at_rows(i), :] = raw
        stream[z, pl.ds(pl.multiple_of(core * rows + i * BLOCK, BLOCK), BLOCK), :] = (
            raw * own_gain
        ).astype(jnp.bfloat16)
        square = raw * raw
        found = square[:, :LANES]
        for part in range(1, width // LANES):
            found = found + square[:, part * LANES : (part + 1) * LANES]
        sums[core, z, pl.ds(i, 1), :] = jnp.sum(found.T, axis=0, keepdims=True)

    pl.semaphore_wait(barrier, len(peers))

    def token_view(owner, chunk):
        return stream.at[owner, rows_at(chunk, token_rows, core * rows), :]

    token_line = Line(
        token_view, chan_count, token_send, token_recv, lambda to: (y, s, to)
    )
    for chunk in range(TOKEN_CHUNKS):
        for way in range(2):

            @pl.when(token_line.sends(way, 0))
            def _():
                token_line.copy(way, 0, (chunk,)).start()

    def own_half(owner, of):
        return stream.at[owner, pl.ds(pl.multiple_of(of * rows, rows), rows), :]

    def mate_tokens():
        return remote(
            own_half(z, core), own_half(z, core), mate_send.at[0], mate_recv.at[0], mate
        )

    mate_tokens().start()
    sum_copies = [
        remote(
            sums.at[core, z], sums.at[core, z], sums_send.at[at], sums_recv.at[core, z], peer
        )
        for at, peer in enumerate(column_peers)
    ]
    for copy in sum_copies:
        copy.start()
    for g in range(groups):
        for b in range(branches):
            remote(
                weights.at[b, :, lanes_of((1 - core) * share, g)],
                weight.at[g, s, :, pl.ds(b * LANES, LANES)],
                mate_send.at[1],
                mate_recv.at[1],
                mate,
            ).start()

    for j, (which, start) in enumerate(tap_stage):
        tap_loads[j].wait()

        @pl.loop(0, groups)
        def _(g):
            mine = freq[which, rows_at(core * groups + g, BLOCK, start), :]
            taps[g, pl.ds(pl.multiple_of(s * rows + j * LANES, LANES), LANES), :] = mine.T.astype(
                jnp.bfloat16
            )
            other = freq[which, rows_at((1 - core) * groups + g, BLOCK, start), :]
            ready[g, j * LANES : (j + 1) * LANES, :] = other.T.astype(jnp.bfloat16)

    def tap_part(owner, part):
        return taps.at[
            :, pl.ds(pl.multiple_of(owner * rows + part * (rows // 2), rows // 2), rows // 2), :
        ]

    def taps_across(to):
        src = tap_part(s, y) if to == 0 else ready.at[
            :, pl.ds(pl.multiple_of(y * (rows // 2), rows // 2), rows // 2), :
        ]
        return remote(
            src,
            tap_part(s, y),
            tap_send.at[to],
            tap_recv.at[core],
            across if to == 0 else aslant,
        )

    def taps_beside(origin, part):
        view = tap_part(origin, part)
        return remote(view, view, tap_send.at[2 + origin], tap_recv.at[2 + origin], beside)

    def taps_mate():
        return remote(
            ready,
            taps.at[:, pl.ds(pl.multiple_of(s * rows, rows), rows), :],
            mate_send.at[2],
            mate_recv.at[2],
            mate,
        )

    @pl.when(x == 0)
    def _():
        taps_across(0).start()
        taps_across(1).start()

        @pl.loop(0, groups)
        def _(g):
            taps[g, length:, :] = jnp.zeros((length, LANES), jnp.bfloat16)

    taps_mate().start()

    def weight_view(owner, part, g, c):
        return weight.at[g, owner, rows_at(c, weight_rows, part * half), :]

    def weight_sent(to, g, c):
        view = weight_view(s, y, g, c)
        return remote(
            view, view, x_send.at[to, g, c], x_recv.at[core, g, c], across if to == 0 else aslant
        )

    def send_weights(g, chunks=range(WEIGHT_CHUNKS)):
        for c in chunks:
            for to in range(2):
                side = core if to == 0 else 1 - core
                view = weight_view(s, y, g, c)
                for b in range(branches):
                    remote(
                        weights.at[
                            b,
                            rows_at(c, weight_rows, y * half),
                            pl.ds(pl.multiple_of(side * share + g * LANES, LANES), LANES),
                        ],
                        view.at[:, pl.ds(b * LANES, LANES)],
                        x_send.at[to, g, c],
                        x_recv.at[core, g, c],
                        across if to == 0 else aslant,
                    ).start()

    for g in range(groups - 2):
        send_weights(g)
    send_weights(groups - 2, range(3))

    @pl.when(x == 1)
    def _():
        send_weights(groups - 2, [3])
        send_weights(groups - 1)

    def beside_copy(origin, part, g, c):
        view = weight_view((1 - x) * 2 + origin, part, g, c)
        return remote(view, view, y_send.at[origin, g, c], y_recv.at[origin, g, c], beside)

    def forward(g, c):
        for origin in range(2):
            view = weight_view((1 - x) * 2 + origin, y, g, c)
            remote(
                view, view, x_send.at[origin, g, c], x_recv.at[origin, g, c], beside
            ).wait_recv()
            beside_copy(origin, y, g, c).start()

    def await_beside(g):
        for c in range(WEIGHT_CHUNKS):
            for origin in range(2):
                beside_copy(origin, 1 - y, g, c).wait_recv()

    @blocks(length)
    def _(i):
        row = lax.broadcasted_iota(jnp.int32, (BLOCK, LANES), 0) + i * BLOCK
        lane = lax.broadcasted_iota(jnp.int32, (BLOCK, LANES), 1)
        unit = math.pi / (4 * length)
        odd = 2 * row + 1
        small = odd.astype(jnp.float32) * unit
        turn[0, at_rows(i), :] = jnp.cos(small)
        turn[1, at_rows(i), :] = jnp.sin(small)
        period = 8 * length
        angle = (odd * (2 * lane + 1) % period).astype(jnp.float32) * unit
        cos, sin = jnp.cos(angle), jnp.sin(angle)
        stride = (odd * (2 * LANES) % period).astype(jnp.float32) * unit
        step_cos, step_sin = jnp.cos(stride), jnp.sin(stride)
        for a in range(length // LANES):
            table[at_rows(i), a * LANES : (a + 1) * LANES] = cos.astype(jnp.bfloat16)
            table[rows_at(i, BLOCK, length), a * LANES : (a + 1) * LANES] = sin.astype(
                jnp.bfloat16
            )
            cos, sin = cos * step_cos - sin * step_sin, sin * step_cos + cos * step_sin

    for g in range(groups):

        @blocks(length)
        def _(i):
            partial[g, at_rows(i), :] = jnp.zeros((BLOCK, branches * LANES), jnp.float32)

    def spectrum(which, column):
        @pl.loop(0, 2 * length // SPAN)
        def _(i):
            at = rows_at(i, SPAN)
            freq[which, at, :] = jnp.dot(
                table[at, :], column(), preferred_element_type=jnp.float32
            )

    def spectrum_pair(columns):
        @pl.loop(0, 2 * length // SPAN)
        def _(i):
            at = rows_at(i, SPAN)
            found = jnp.dot(
                table[at, :],
                jnp.concatenate(columns(), axis=1),
                preferred_element_type=jnp.float32,
            )
            freq[0, at, :] = found[:, :LANES]
            freq[1, at, :] = found[:, LANES:]

    def tap_spectra(g):
        spectrum_pair(lambda: [taps[g, :length, :], taps[g, length:, :]])

        @blocks(length)
        def _(i):
            low, high = at_rows(i), rows_at(i, BLOCK, length)
            cos, sin = turn[0, low, :], turn[1, low, :]

            def turned(which):
                real, imag = freq[which, low, :], -freq[which, high, :]
                return (cos * real - sin * imag) / length, (cos * imag + sin * real) / length

            real, imag = turned(0)
            late_real, late_imag = turned(1)
            place = lax.broadcasted_iota(jnp.int32, (BLOCK, LANES), 0)
            sign = (1 - 2 * (place % 2)).astype(jnp.float32)
            spectra[g, 0, low, :] = real.astype(jnp.bfloat16)
            spectra[g, 1, low, :] = imag.astype(jnp.bfloat16)
            spectra[g, 2, low, :] = (late_real - sign * imag).astype(jnp.bfloat16)
            spectra[g, 3, low, :] = (late_imag + sign * real).astype(jnp.bfloat16)

    def project(g, owner):
        @pl.loop(0, length // SPAN)
        def _(i):
            at = rows_at(i, SPAN)
            partial[g, at, :] += jnp.dot(
                stream[owner, at, :], weight[g, owner], preferred_element_type=jnp.float32
            )

    at_end = (z == 0) | (z == chan_count - 1)

    def projects_early(g, owner):
        far = jnp.abs(z - owner)
        own = owner // 2 == x
        return (
            (own & ((far <= 1) | ((far == 2) & (at_end | (g == 0)))))
            | (jnp.logical_not(own) & (far <= 2) & ((g == 0) | ((g == 1) & at_end)))
        )

    def to_mate(way, step, chunk):
        block = token_view(token_line.source(way, step), chunk)
        index = 3 + way * steps + step
        return remote(block, block, mate_send.at[index], mate_recv.at[index], mate)

    def mate_half(way, step, of):
        block = own_half(token_line.source(way, step), of)
        index = 3 + way * steps + step
        return remote(block, block, mate_send.at[index], mate_recv.at[index], mate)

    def await_mate(step):
        for way in range(2):

            @pl.when(token_line.receives(way, step))
            def _():
                mate_half(way, step, 1 - core).wait_recv()

    @pl.loop(0, steps * TOKEN_CHUNKS)
    def _(tick):
        step, chunk = tick // TOKEN_CHUNKS, tick % TOKEN_CHUNKS
        for way in range(2):

            @pl.when(token_line.receives(way, step))
            def _():
                token_line.arrived(way, step, (chunk,))
                to_mate(way, step, chunk).start()

            @pl.when(
                (step + 1 < steps)
                & token_line.receives(way, step)
                & token_line.sends(way, step + 1)
            )
            def _():
                token_line.copy(way, step + 1, (chunk,)).start()

        @pl.when((tick == TOKEN_CHUNKS // 2) & (x == 1))
        def _():
            for origin in range(2):
                view = tap_part(origin, y)
                remote(
                    view, view, tap_send.at[origin], tap_recv.at[origin], beside
                ).wait_recv()
                taps_beside(origin, y).start()

        @pl.when((tick % 2 == 1) & (tick >= 3) & (tick < 7 + 4 * WEIGHT_CHUNKS))
        def _():
            at = (tick - 3) // 2
            forward(at // WEIGHT_CHUNKS, at % WEIGHT_CHUNKS)

        @pl.when(tick == TOKEN_CHUNKS)
        def _():
            mate_half_own = own_half(z, 1 - core)
            remote(
                mate_half_own, mate_half_own, mate_send.at[0], mate_recv.at[0], mate
            ).wait_recv()
            await_mate(0)
            pltpu.make_async_copy(
                weight.at[:, s], weight.at[:, s], local_sem.at[2]
            ).wait()
            other = weight.at[:, mate_s]
            remote(other, other, mate_send.at[1], mate_recv.at[1], mate).wait_recv()
            other = taps.at[:, pl.ds(pl.multiple_of(mate_s * rows, rows), rows), :]
            remote(other, other, mate_send.at[2], mate_recv.at[2], mate).wait_recv()

            @pl.when(x == 1)
            def _():
                for origin in range(2):
                    taps_beside(origin, 1 - y).wait_recv()

        @pl.when((step == 1) & (chunk % 2 == 0))
        def _():
            tap_spectra(chunk // 2)

        @pl.when(tick == 2 * TOKEN_CHUNKS)
        def _():
            await_mate(1)

        owner = 2 * x + chunk // groups
        far = jnp.abs(z - owner)

        @pl.when(
            projects_early(chunk % groups, owner)
            & (((step == 1) & (far <= 1)) | ((step == 2) & (far == 2)))
        )
        def _():
            project(chunk % groups, owner)

        @pl.when(tick == 2 * TOKEN_CHUNKS)
        def _():
            await_beside(0)

        @pl.when((tick == 2 * TOKEN_CHUNKS + TOKEN_CHUNKS // 2) & at_end)
        def _():
            await_beside(1)

        guest = 2 * (1 - x) + (chunk // 2) % 2

        @pl.when((step == 2) & (chunk % 2 == 0) & projects_early(chunk // 4, guest))
        def _():
            project(chunk // 4, guest)

    await_mate(2)
    for by in range(1, chan_count):
        for of in range(2):
            view = sums.at[of, lax.rem(z + by, chan_count)]
            remote(
                view, view, sums_send.at[0], sums_recv.at[of, lax.rem(z + by, chan_count)], mate
            ).wait_recv()
    view = sums.at[1 - core, z]
    remote(view, view, sums_send.at[0], sums_recv.at[1 - core, z], mate).wait_recv()

    @blocks(length)
    def _(i):
        of, at = i // (rows // BLOCK), i % (rows // BLOCK)
        found = sums[of, 0, pl.ds(at, 1), :]
        for owner in range(1, chan_count):
            found = found + sums[of, owner, pl.ds(at, 1), :]
        found = lax.rsqrt(found / (chan_count * width) + EPSILON)
        scale[at_rows(i), :] = jnp.broadcast_to(found, (BLOCK, LANES)).T

    taps_mate().wait_send()

    @pl.when(x == 0)
    def _():
        taps_across(0).wait_send()
        taps_across(1).wait_send()

    def edge_copy(g):
        return remote(
            edge_out.at[g], edge.at[g], edge_send.at[g], edge_recv.at[g], across
        )

    def before_copy(g):
        return remote(
            signal.at[g], before.at[g], before_send.at[g], before_recv.at[g], across
        )

    def swap_copy(g):
        return remote(
            ready.at[g], full.at[z, g, core], swap_send.at[g], swap_recv.at[g], mate
        )

    line = Line(
        lambda owner, g, of: full.at[owner, g, of],
        chan_count,
        line_send,
        line_recv,
        lambda to: (y, s, to),
    )

    def projected(g, b, at):
        return (partial[g, at, b * LANES : (b + 1) * LANES] * scale[at, :]).astype(jnp.bfloat16)

    def featurize(g):
        @pl.when(x == 0)
        def _():
            for b in range(branches):
                edge_out[g, b] = projected(g, b, pl.ds(length - rim, rim))
                extended[b, 0:rim, :] = jnp.zeros((rim, LANES), jnp.float32)
            edge_copy(g).start()

        @blocks(length)
        def _(i):
            for b in range(branches):
                extended[b, pl.ds(pl.multiple_of(rim + i * BLOCK, rim), BLOCK), :] = projected(
                    g, b, at_rows(i)
                ).astype(jnp.float32)

        @pl.when(x == 1)
        def _():
            edge_copy(g).wait_recv()
            for b in range(branches):
                extended[b, 0:rim, :] = edge[g, b].astype(jnp.float32)

        chosen = lanes_of(core * share, g)
        coefficient = [
            [short[tap, b : b + 1, chosen] for b in range(branches)] for tap in range(SHORT)
        ]

        @blocks(length)
        def _(i):
            found = []
            for b in range(branches):
                value = jnp.zeros((BLOCK, LANES), jnp.float32)
                for tap in range(SHORT):
                    value = value + coefficient[tap][b] * extended[
                        b, pl.ds(rim - tap + i * BLOCK, BLOCK), :
                    ]
                found.append(value.astype(jnp.bfloat16))
            query[at_rows(i), :] = found[0]
            signal[g, at_rows(i), :] = (
                found[1].astype(jnp.float32) * found[2].astype(jnp.float32)
            ).astype(jnp.bfloat16)

    def convolve(g):
        joint = (x == 1) & (g > 0)

        @pl.when(jnp.logical_not(joint))
        def _():
            spectrum(0, lambda: signal[g])

        def product(i, which, first):
            low, high = at_rows(i), rows_at(i, BLOCK, length)
            cos, sin = freq[which, low, :], freq[which, high, :]
            real = spectra[g, first, low, :].astype(jnp.float32)
            imag = spectra[g, first + 1, low, :].astype(jnp.float32)
            return cos * real + sin * imag, sin * real - cos * imag

        @pl.when(x == 0)
        def _():
            @blocks(length)
            def _(i):
                real, imag = product(i, 0, 0)
                mixed[at_rows(i), :] = real.astype(jnp.bfloat16)
                mixed[rows_at(i, BLOCK, length), :] = imag.astype(jnp.bfloat16)

        @pl.when(x == 1)
        def _():
            before_copy(g).wait_recv()

            @pl.when(g == 0)
            def _():
                spectrum(1, lambda: before[g])

            @pl.when(g > 0)
            def _():
                spectrum_pair(lambda: [signal[g], before[g]])

            @blocks(length)
            def _(i):
                real, imag = product(i, 0, 0)
                more_real, more_imag = product(i, 1, 2)
                mixed[at_rows(i), :] = (real + more_real).astype(jnp.bfloat16)
                mixed[rows_at(i, BLOCK, length), :] = (imag + more_imag).astype(jnp.bfloat16)

        @pl.loop(0, length // SPAN)
        def _(i):
            low, high = rows_at(i, SPAN), rows_at(i, SPAN, length)
            freq[0, low, :] = jnp.dot(
                table[low, :], mixed[:length, :], preferred_element_type=jnp.float32
            ) + jnp.dot(table[high, :], mixed[length:, :], preferred_element_type=jnp.float32)

        direct = skip[:, lanes_of(core * share, g)]

        def gated(at):
            longer = freq[0, at, :] + direct * signal[g, at, :].astype(jnp.float32)
            longer = longer.astype(jnp.bfloat16).astype(jnp.float32)
            return (query[at, :].astype(jnp.float32) * longer).astype(jnp.bfloat16)

        @blocks(rows)
        def _(i):
            full[z, g, core, at_rows(i), :] = gated(
                pl.ds(pl.multiple_of(core * rows + i * BLOCK, BLOCK), BLOCK)
            )
            ready[g, at_rows(i), :] = gated(
                pl.ds(pl.multiple_of((1 - core) * rows + i * BLOCK, BLOCK), BLOCK)
            )

    def accumulate(owner, g):
        left = pl.ds(pl.multiple_of(owner * 2 * share + g * LANES, LANES), LANES)
        right = pl.ds(pl.multiple_of((owner * 2 + 1) * share + g * LANES, LANES), LANES)

        @pl.loop(0, total.shape[1] // (2 * LANES))
        def _(i):
            cols = rows_at(i, 2 * LANES)
            block = jnp.concatenate([full[owner, g, 0], full[owner, g, 1]], axis=1)
            kernel = jnp.concatenate([out_room[left, cols], out_room[right, cols]], axis=0)
            total[:, cols] += jnp.dot(block, kernel, preferred_element_type=jnp.float32)

    def begin(g):
        swap_copy(g).start()
        for way in range(2):

            @pl.when(line.sends(way, 0))
            def _():
                line.copy(way, 0, (g, core)).start()

    def begin_other(g):
        other = full.at[z, g, 1 - core]
        remote(other, other, swap_send.at[g], swap_recv.at[g], mate).wait_recv()
        for way in range(2):

            @pl.when(line.sends(way, 0))
            def _():
                line.copy(way, 0, (g, 1 - core)).start()

    def settle():
        mate_tokens().wait_send()
        other = weight.at[:, s]
        remote(other, other, mate_send.at[1], mate_recv.at[1], mate).wait_send()
        for copy in sum_copies:
            copy.wait_send()

        @pl.when(x == 1)
        def _():
            for origin in range(2):
                taps_beside(origin, y).wait_send()

        @pl.loop(0, groups)
        def _(g):
            for c in range(WEIGHT_CHUNKS):
                for to in range(2):
                    weight_sent(to, g, c).wait_send()
                    beside_copy(to, y, g, c).wait_send()

            @pl.when(x == 0)
            def _():
                edge_copy(g).wait_send()
                before_copy(g).wait_send()

        for way in range(2):
            for step in range(steps):

                @pl.when(token_line.receives(way, step))
                def _():
                    mate_half(way, step, core).wait_send()

                @pl.when(token_line.sends(way, step))
                def _():
                    @pl.loop(0, TOKEN_CHUNKS)
                    def _(chunk):
                        token_line.copy(way, step, (chunk,)).wait_send()

    def way_of(k):
        return jnp.where(z < chan_count // 2, 1 - k, k)

    @pl.loop(0, 2 * groups + steps)
    def _(g):
        @pl.when(g < groups)
        def _():
            @pl.when((g >= 2) | ((g == 1) & jnp.logical_not(at_end)))
            def _():
                await_beside(g)

            @pl.loop(0, chan_count)
            def _(owner):
                @pl.when(jnp.logical_not(projects_early(g, owner)))
                def _():
                    project(g, owner)

            @pl.when(g == 1)
            def _():
                forward(groups - 2, 3)
                forward(groups - 1, 0)

            @pl.when(g == 2)
            def _():
                forward(groups - 1, 1)
                forward(groups - 1, 2)

        @pl.loop(0, 2)
        def _(k):
            way = way_of(k)
            for step in range(steps - 1):
                at = g - 1 - k - 2 * step

                @pl.when(
                    (at >= 0)
                    & (at < groups)
                    & line.receives(way, step)
                    & line.sends(way, step + 1)
                )
                def _():
                    for of in range(2):
                        line.arrived(way, step, (at, of))
                        line.copy(way, step + 1, (at, of)).start()

        @pl.when(g < groups)
        def _():
            featurize(g)

            @pl.when(x == 0)
            def _():
                before_copy(g).start()

                @pl.when(g == 0)
                def _():
                    send_weights(groups - 2, [3])
                    send_weights(groups - 1, [0])

                @pl.when(g == 1)
                def _():
                    send_weights(groups - 1, [1, 2, 3])

            @pl.when(g == 0)
            def _():
                forward(groups - 2, 2)

            convolve(g)
            begin(g)

            @pl.when(g == 2)
            def _():
                forward(groups - 1, 3)

            begin_other(g)

        @pl.when(g == groups)
        def _():
            out_load.wait()

        own = g - groups

        @pl.when((own >= 0) & (own < groups))
        def _():
            accumulate(z, own)

        @pl.loop(0, 2)
        def _(k):
            way = way_of(k)
            for step in range(steps):
                at = g - groups - step

                @pl.when((at >= 0) & (at < groups) & line.receives(way, step))
                def _():
                    @pl.when(jnp.logical_not(line.sends(way, step + 1)))
                    def _():
                        for of in range(2):
                            line.arrived(way, step, (at, of))

                    accumulate(line.source(way, step), at)

        @pl.when(g == groups + 1)
        def _():
            settle()

    @blocks(rows)
    def _(i):
        result[at_rows(i), :] = total[at_rows(i), :].astype(jnp.bfloat16)

    @pl.loop(0, groups)
    def _(g):
        swap_copy(g).wait_send()

        for way in range(2):
            for step in range(steps):

                @pl.when(line.sends(way, step))
                def _():
                    for of in range(2):
                        line.copy(way, step, (g, of)).wait_send()


def chip_body(tokens, norm_gain, proj_weight, short_filter, long_filter, skip_gain, out_weight):
    chan_count = lax.axis_size("chan")
    rows, width = tokens.shape
    depth, branches, local_chan = proj_weight.shape
    length, share = 2 * rows, local_chan // 2
    groups = share // LANES
    steps = chan_count - 1
    dma = pltpu.SemaphoreType.DMA
    f32, bf16 = jnp.float32, jnp.bfloat16
    vmem = pl.BlockSpec(memory_space=pltpu.VMEM)
    return pl.pallas_call(
        functools.partial(block_kernel, chan_count),
        out_shape=jax.ShapeDtypeStruct((rows, width), bf16),
        in_specs=[ANY, vmem, ANY, vmem, ANY, vmem, ANY],
        out_specs=vmem,
        scratch_shapes=[
            pltpu.VMEM((chan_count, length, width), bf16),
            pltpu.VMEM((groups, 4, depth, branches * LANES), bf16),
            pltpu.VMEM((2, chan_count, 8, LANES), f32),
            pltpu.VMEM((length, LANES), f32),
            pltpu.VMEM((groups, length, branches * LANES), f32),
            pltpu.VMEM((rows, width), bf16),
            pltpu.VMEM(out_weight.shape, bf16),
            pltpu.VMEM((2 * length, length), bf16),
            pltpu.VMEM((groups, 2 * length, LANES), bf16),
            pltpu.VMEM((2, length, LANES), f32),
            pltpu.VMEM((groups, 4, length, LANES), bf16),
            pltpu.VMEM((2, 2 * length, LANES), f32),
            pltpu.VMEM((2 * length, LANES), bf16),
            pltpu.VMEM((groups, branches, 16, LANES), bf16),
            pltpu.VMEM((groups, branches, 16, LANES), bf16),
            pltpu.VMEM((branches, length + 16, LANES), f32),
            pltpu.VMEM((length, LANES), bf16),
            pltpu.VMEM((groups, length, LANES), bf16),
            pltpu.VMEM((groups, length, LANES), bf16),
            pltpu.VMEM((groups, rows, LANES), bf16),
            pltpu.VMEM((chan_count, groups, 2, rows, LANES), bf16),
            pltpu.VMEM((rows, width), f32),
            dma((8,)),
            dma((3 + 2 * steps,)),
            dma((3 + 2 * steps,)),
            dma((2, steps, TOKEN_CHUNKS)),
            dma((2, steps, TOKEN_CHUNKS)),
            dma((2 * chan_count - 1,)),
            dma((2, chan_count)),
            dma((2, groups, WEIGHT_CHUNKS)),
            dma((2, groups, WEIGHT_CHUNKS)),
            dma((2, groups, WEIGHT_CHUNKS)),
            dma((2, groups, WEIGHT_CHUNKS)),
            dma((4,)),
            dma((4,)),
            dma((groups,)),
            dma((groups,)),
            dma((groups,)),
            dma((groups,)),
            dma((groups,)),
            dma((groups,)),
            dma((2, steps, groups, 2)),
            dma((2, steps, groups, 2)),
        ],
        compiler_params=pltpu.CompilerParams(
            collective_id=0, has_side_effects=True, vmem_limit_bytes=63 * 1024 * 1024
        ),
        name="block",
    )(
        tokens,
        norm_gain[None, :],
        proj_weight.transpose(1, 0, 2),
        short_filter,
        long_filter,
        skip_gain[None, :],
        out_weight,
    )


def select_body(mesh):
    if (mesh.shape["groups"], mesh.shape["seq"], mesh.shape["chan"]) == (2, 4, 4):
        return chip_body
    return body


def solution(mesh):
    placed = (
        P(("groups", "seq"), "chan"),
        P(),
        P("seq", None, "chan"),
        P(None, None, "chan"),
        P("chan", "seq"),
        P("chan"),
        P(None, "chan"),
    )
    return jax.shard_map(
        select_body(mesh), mesh=mesh, in_specs=placed, out_specs=P(("groups", "seq"), "chan"), check_vma=False
    )
```

```python
import functools
import math

import jax
import jax.numpy as jnp
import numpy as np
from jax import lax
from jax.experimental import pallas as pl
from jax.experimental.pallas import tpu as pltpu
from jax.sharding import PartitionSpec as P

SHORT = 3


EPSILON = 1e-06
HIGHEST = lax.Precision.HIGHEST


def from_behind(value, axis, steps):
    count = lax.axis_size(axis)
    initial, last = (max(0, -steps), min(count, count - steps))
    return lax.ppermute(value, axis, [(source, source + steps) for source in range(initial, last)])


def angle_table(row_count, col_count, period, sign):
    row_index = lax.iota(jnp.int32, row_count)[:, None]
    col_index = lax.iota(jnp.int32, col_count)[None, :]
    angles = (row_index * col_index % period).astype(jnp.float32) * (sign * 2.0 * math.pi / period)
    return (jnp.cos(angles), jnp.sin(angles))


def forward_spectrum(signal_rows, first, second):
    channels = signal_rows.shape[0]
    grid_rows = signal_rows.reshape(channels, first, second)
    cos_first, sin_first = angle_table(first, first, first, -1.0)
    part_re = jnp.einsum("cab,ak->ckb", grid_rows, cos_first, precision=HIGHEST)
    part_im = jnp.einsum("cab,ak->ckb", grid_rows, sin_first, precision=HIGHEST)
    twist_cos, twist_sin = angle_table(first, second, first * second, -1.0)
    part_re, part_im = (
        part_re * twist_cos - part_im * twist_sin,
        part_re * twist_sin + part_im * twist_cos,
    )
    cos_second, sin_second = angle_table(second, second, second, -1.0)
    spectrum_real = jnp.einsum("ckb,bm->ckm", part_re, cos_second, precision=HIGHEST) - jnp.einsum(
        "ckb,bm->ckm", part_im, sin_second, precision=HIGHEST
    )
    spec_im = jnp.einsum("ckb,bm->ckm", part_re, sin_second, precision=HIGHEST) + jnp.einsum(
        "ckb,bm->ckm", part_im, cos_second, precision=HIGHEST
    )
    return (spectrum_real, spec_im)


def inverse_spectrum(spectrum_real, spec_im, first, second):
    channels = spectrum_real.shape[0]
    cos_second, sin_second = angle_table(second, second, second, 1.0)
    part_re = jnp.einsum("ckm,bm->ckb", spectrum_real, cos_second, precision=HIGHEST) - jnp.einsum(
        "ckm,bm->ckb", spec_im, sin_second, precision=HIGHEST
    )
    part_im = jnp.einsum("ckm,bm->ckb", spectrum_real, sin_second, precision=HIGHEST) + jnp.einsum(
        "ckm,bm->ckb", spec_im, cos_second, precision=HIGHEST
    )
    twist_cos, twist_sin = angle_table(first, second, first * second, 1.0)
    part_re, part_im = (
        part_re * twist_cos - part_im * twist_sin,
        part_re * twist_sin + part_im * twist_cos,
    )
    cos_first, sin_first = angle_table(first, first, first, 1.0)
    result = jnp.einsum("ckb,ak->cab", part_re, cos_first, precision=HIGHEST) - jnp.einsum(
        "ckb,ak->cab", part_im, sin_first, precision=HIGHEST
    )
    return result.reshape(channels, first * second) / (first * second)


def spectral_conv(signal_rows, filter_rows):
    channels, length = signal_rows.shape
    padded_len = 2 * length
    log_len = padded_len.bit_length() - 1
    first = 1 << log_len // 2
    second = padded_len // first
    zeros_tail = jnp.zeros((channels, length), jnp.float32)
    sig_re, sig_im = forward_spectrum(
        jnp.concatenate([signal_rows, zeros_tail], axis=1), first, second
    )
    tap_re, tap_im = forward_spectrum(
        jnp.concatenate([filter_rows, zeros_tail], axis=1), first, second
    )
    prod_re = sig_re * tap_re - sig_im * tap_im
    prod_im = sig_re * tap_im + sig_im * tap_re
    return inverse_spectrum(prod_re, prod_im, first, second)[:, :length]


def short_filter_output(projected, rim_cells, kernel_coefficients):
    count = kernel_coefficients.shape[0]
    steps_len = projected.shape[2]
    extended = jnp.concatenate([rim_cells, projected], axis=2).astype(jnp.float32)
    total = jnp.zeros(projected.shape, jnp.float32)
    for tap in range(count):
        total = (
            total
            + kernel_coefficients[tap][:, :, None]
            * extended[:, :, count - 1 - tap : count - 1 - tap + steps_len]
        )
    return total.astype(jnp.bfloat16)


def hyena_mixer(keys_rows, values_rows, long_taps, skip_part):
    middle = keys_rows.astype(jnp.float32) * values_rows.astype(jnp.float32)
    return (spectral_conv(middle, long_taps) + skip_part[:, None] * middle).astype(jnp.bfloat16)


def body(tokens, norm_gain, proj_weight, short_filter, long_filter, skip_gain, out_weight):
    seq_count = lax.axis_size("seq")
    local_rows = tokens.shape[0]
    local_chan = proj_weight.shape[2]
    subset = local_chan // seq_count
    length = local_rows * seq_count
    offset = lax.axis_index("seq") * subset
    whole = lax.all_gather(tokens, "chan", axis=1, tiled=True)
    wide = whole.astype(jnp.float32)
    rescaled_signal = (
        wide * lax.rsqrt(jnp.mean(wide * wide, axis=1, keepdims=True) + EPSILON) * norm_gain
    ).astype(jnp.bfloat16)
    projected = lax.dot_general(
        lax.all_gather(proj_weight, "seq", axis=0, tiled=True),
        rescaled_signal,
        (((0,), (1,)), ((), ())),
        preferred_element_type=jnp.float32,
    ).astype(jnp.bfloat16)
    taps_grid = long_filter.reshape(1, seq_count, subset, local_rows)
    long_taps = lax.all_to_all(taps_grid, "seq", split_axis=1, concat_axis=3, tiled=True).reshape(
        subset, length
    )
    skip_part = lax.dynamic_slice_in_dim(skip_gain, offset, subset, 0)
    rim_cells = from_behind(projected[:, :, local_rows - (SHORT - 1) :], "seq", 1)
    featured = short_filter_output(projected, rim_cells, short_filter)
    pair_grid = featured[1:].reshape(2, seq_count, subset, local_rows)
    moved = lax.all_to_all(pair_grid, "seq", split_axis=1, concat_axis=3, tiled=True).reshape(
        2, subset, length
    )
    result = hyena_mixer(moved[0], moved[1], long_taps, skip_part)
    returned = lax.all_to_all(
        result.reshape(1, subset, length), "seq", split_axis=2, concat_axis=0, tiled=True
    )
    returned = returned.reshape(local_chan, local_rows)
    gated = (featured[0].astype(jnp.float32) * returned.astype(jnp.float32)).astype(jnp.bfloat16)
    full_mix = lax.all_gather(gated, "chan", axis=0, tiled=True)
    update = lax.dot_general(
        full_mix, out_weight, (((0,), (0,)), ((), ())), preferred_element_type=jnp.float32
    )
    return (tokens.astype(jnp.float32) + update).astype(jnp.bfloat16)

LANES = 128
BLOCK = 128
SPAN = 512
TOKEN_CHUNKS = 8
WEIGHT_CHUNKS = 4
ANY = pl.BlockSpec(memory_space=pl.ANY)


def remote(src, dst, send_sem, recv_sem, where):
    return pltpu.make_async_remote_copy(
        src_ref=src,
        dst_ref=dst,
        send_sem=send_sem,
        recv_sem=recv_sem,
        device_id=where,
        device_id_type=pl.DeviceIdType.MESH,
    )


class Line:
    def __init__(self, view, count, send_sem, recv_sem, place):
        self.view, self.count, self.place = view, count, place
        self.send_sem, self.recv_sem = send_sem, recv_sem
        self.me = lax.axis_index("chan")

    def move(self, way, step, piece, block, target):
        recv = self.recv_sem.at[(way, step) + piece]
        return remote(block, block, self.send_sem.at[way, step], recv, self.place(target))

    def drain(self, way, step, first, block):
        self.move(way, step, first, block(self.source(way, step - 1)), self.me).wait_send()

    def source(self, way, step):
        return jnp.clip(self.me - (step + 1) * (1 - 2 * way), 0, self.count - 1)

    def copy(self, way, step, piece):
        owner = self.source(way, step - 1)
        target = self.source(way, -2)
        return self.move(way, step, piece, self.view(owner, *piece), target)

    def inside(self, way, by):
        place = self.me + by * (1 - 2 * way)
        return (place >= 0) & (place < self.count)

    def sends(self, way, step):
        return self.inside(way, -step) & self.inside(way, 1)

    def receives(self, way, step):
        return self.inside(way, -1 - step)

    def arrived(self, way, step, piece):
        owner = self.source(way, step)
        self.move(way, step, piece, self.view(owner, *piece), self.me).wait_recv()
        return owner


def block_kernel(
    chan_count,
    tokens,
    gain,
    weights,
    short,
    long_taps,
    skip,
    out_weight,
    result,
    stream,
    weight,
    sums,
    scale,
    partial,
    out_room,
    table,
    taps,
    spectra,
    freq,
    mixed,
    edge_out,
    edge,
    extended,
    query,
    signal,
    before,
    ready,
    full,
    total,
    local_sem,
    mate_send,
    mate_recv,
    token_send,
    token_recv,
    sums_send,
    sums_recv,
    x_send,
    x_recv,
    y_send,
    y_recv,
    tap_send,
    tap_recv,
    edge_send,
    edge_recv,
    before_send,
    before_recv,
    swap_send,
    swap_recv,
    line_send,
    line_recv,
):
    y, s, z = (lax.axis_index(name) for name in ("groups", "seq", "chan"))
    x, core = s // 2, s % 2
    mate_s = s + 1 - 2 * core
    mate = (y, mate_s, z)
    across = (y, (1 - x) * 2 + core, z)
    aslant = (y, (1 - x) * 2 + 1 - core, z)
    beside = (1 - y, s, z)
    rows, width = tokens.shape
    length = 2 * rows
    branches, depth = weights.shape[0], weights.shape[1]
    half = depth // 2
    share = weights.shape[2] // 2
    groups = share // LANES
    rim = edge.shape[2]
    steps = chan_count - 1
    token_rows = rows // TOKEN_CHUNKS
    weight_rows = half // WEIGHT_CHUNKS

    column_peers = [mate] + [
        (y, 2 * x + of, lax.rem(z + by, chan_count))
        for by in range(1, chan_count)
        for of in (core, 1 - core)
    ]
    peers = column_peers + [across, aslant, beside]

    def rows_at(i, count, base=0):
        return pl.ds(pl.multiple_of(base + i * count, count), count)

    def at_rows(i):
        return rows_at(i, BLOCK)

    def blocks(count):
        return pl.loop(0, count // BLOCK)

    def lanes_of(base, g):
        return pl.ds(pl.multiple_of(base + g * LANES, LANES), LANES)

    tap_stage = [(0, 0), (0, length), (1, 0), (1, length)]
    tap_loads = [
        pltpu.make_async_copy(
            long_taps.at[:, pl.ds(j * LANES, LANES)],
            freq.at[which, pl.ds(start, length)],
            local_sem.at[4 + j],
        )
        for j, (which, start) in enumerate(tap_stage)
    ]
    token_load = pltpu.make_async_copy(tokens, result, local_sem.at[0])
    out_load = pltpu.make_async_copy(out_weight, out_room, local_sem.at[1])
    token_load.start()
    barrier = pltpu.get_barrier_semaphore()
    for peer in peers:
        pl.semaphore_signal(barrier, inc=1, device_id=peer, device_id_type=pl.DeviceIdType.MESH)
    for copy in tap_loads:
        copy.start()
    for g in range(groups):
        for b in range(branches):
            pltpu.make_async_copy(
                weights.at[b, :, lanes_of(core * share, g)],
                weight.at[g, s, :, pl.ds(b * LANES, LANES)],
                local_sem.at[2],
            ).start()
    out_load.start()

    sums[core, z] = jnp.zeros(sums.shape[2:], jnp.float32)
    own_gain = gain[:, pl.ds(pl.multiple_of(z * width, width), width)]
    token_load.wait()

    @blocks(rows)
    def _(i):
        raw = result[at_rows(i), :].astype(jnp.float32)
        total[at_rows(i), :] = raw
        stream[z, pl.ds(pl.multiple_of(core * rows + i * BLOCK, BLOCK), BLOCK), :] = (
            raw * own_gain
        ).astype(jnp.bfloat16)
        square = raw * raw
        found = square[:, :LANES]
        for part in range(1, width // LANES):
            found = found + square[:, part * LANES : (part + 1) * LANES]
        sums[core, z, pl.ds(i, 1), :] = jnp.sum(found.T, axis=0, keepdims=True)

    pl.semaphore_wait(barrier, len(peers))

    def token_view(owner, chunk):
        return stream.at[owner, rows_at(chunk, token_rows, core * rows), :]

    token_line = Line(
        token_view, chan_count, token_send, token_recv, lambda to: (y, s, to)
    )
    for chunk in range(TOKEN_CHUNKS):
        for way in range(2):

            @pl.when(token_line.sends(way, 0))
            def _():
                token_line.copy(way, 0, (chunk,)).start()

    def own_half(owner, of):
        return stream.at[owner, pl.ds(pl.multiple_of(of * rows, rows), rows), :]

    def mate_tokens():
        return remote(
            own_half(z, core), own_half(z, core), mate_send.at[0], mate_recv.at[0], mate
        )

    mate_tokens().start()
    sum_copies = [
        remote(
            sums.at[core, z], sums.at[core, z], sums_send.at[at], sums_recv.at[core, z], peer
        )
        for at, peer in enumerate(column_peers)
    ]
    for copy in sum_copies:
        copy.start()
    for g in range(groups):
        for b in range(branches):
            remote(
                weights.at[b, :, lanes_of((1 - core) * share, g)],
                weight.at[g, s, :, pl.ds(b * LANES, LANES)],
                mate_send.at[1],
                mate_recv.at[1],
                mate,
            ).start()

    for j, (which, start) in enumerate(tap_stage):
        tap_loads[j].wait()

        @pl.loop(0, groups)
        def _(g):
            mine = freq[which, rows_at(core * groups + g, BLOCK, start), :]
            taps[g, pl.ds(pl.multiple_of(s * rows + j * LANES, LANES), LANES), :] = mine.T.astype(
                jnp.bfloat16
            )
            other = freq[which, rows_at((1 - core) * groups + g, BLOCK, start), :]
            ready[g, j * LANES : (j + 1) * LANES, :] = other.T.astype(jnp.bfloat16)

    def tap_part(owner, part):
        return taps.at[
            :, pl.ds(pl.multiple_of(owner * rows + part * (rows // 2), rows // 2), rows // 2), :
        ]

    def taps_across(to):
        src = tap_part(s, y) if to == 0 else ready.at[
            :, pl.ds(pl.multiple_of(y * (rows // 2), rows // 2), rows // 2), :
        ]
        return remote(
            src,
            tap_part(s, y),
            tap_send.at[to],
            tap_recv.at[core],
            across if to == 0 else aslant,
        )

    def taps_beside(origin, part):
        view = tap_part(origin, part)
        return remote(view, view, tap_send.at[2 + origin], tap_recv.at[2 + origin], beside)

    def taps_mate():
        return remote(
            ready,
            taps.at[:, pl.ds(pl.multiple_of(s * rows, rows), rows), :],
            mate_send.at[2],
            mate_recv.at[2],
            mate,
        )

    @pl.when(x == 0)
    def _():
        taps_across(0).start()
        taps_across(1).start()

        @pl.loop(0, groups)
        def _(g):
            taps[g, length:, :] = jnp.zeros((length, LANES), jnp.bfloat16)

    taps_mate().start()

    def weight_view(owner, part, g, c):
        return weight.at[g, owner, rows_at(c, weight_rows, part * half), :]

    def weight_half(owner, part):
        return weight.at[:, owner, pl.ds(pl.multiple_of(part * half, half), half), :]

    def send_weights(g, chunks=range(WEIGHT_CHUNKS)):
        for c in chunks:
            for to in range(2):
                side = core if to == 0 else 1 - core
                view = weight_view(s, y, g, c)
                for b in range(branches):
                    remote(
                        weights.at[
                            b,
                            rows_at(c, weight_rows, y * half),
                            pl.ds(pl.multiple_of(side * share + g * LANES, LANES), LANES),
                        ],
                        view.at[:, pl.ds(b * LANES, LANES)],
                        x_send.at[to],
                        x_recv.at[core, g, c],
                        across if to == 0 else aslant,
                    ).start()

    for g in range(groups - 2):
        send_weights(g)
    send_weights(groups - 2, range(3))

    at_end = (z == 0) | (z == chan_count - 1)

    @pl.when((x == 1) | at_end)
    def _():
        send_weights(groups - 2, [3])
        send_weights(groups - 1, [0, 1])

    @pl.when(x == 1)
    def _():
        send_weights(groups - 1, [2, 3])

    def beside_copy(origin, part, g, c):
        view = weight_view((1 - x) * 2 + origin, part, g, c)
        return remote(view, view, y_send.at[origin], y_recv.at[origin, g], beside)

    def forward(g, c):
        for origin in range(2):
            view = weight_view((1 - x) * 2 + origin, y, g, c)
            remote(
                view, view, x_send.at[origin], x_recv.at[origin, g, c], beside
            ).wait_recv()
            beside_copy(origin, y, g, c).start()

    def await_beside(g):
        for origin in range(2):
            view = weight.at[
                g, (1 - x) * 2 + origin, pl.ds(pl.multiple_of((1 - y) * half, half), half), :
            ]
            remote(view, view, y_send.at[origin], y_recv.at[origin, g], beside).wait_recv()

    @blocks(length)
    def _(i):
        row = lax.broadcasted_iota(jnp.int32, (BLOCK, LANES), 0) + i * BLOCK
        lane = lax.broadcasted_iota(jnp.int32, (BLOCK, LANES), 1)
        unit = math.pi / (4 * length)
        odd = 2 * row + 1
        small = odd.astype(jnp.float32) * unit
        extended[0, at_rows(i), :] = jnp.cos(small)
        extended[1, at_rows(i), :] = jnp.sin(small)
        period = 8 * length
        angle = (odd * (2 * lane + 1) % period).astype(jnp.float32) * unit
        cos, sin = jnp.cos(angle), jnp.sin(angle)
        stride = (odd * (2 * LANES) % period).astype(jnp.float32) * unit
        step_cos, step_sin = jnp.cos(stride), jnp.sin(stride)
        for a in range(length // LANES):
            table[at_rows(i), a * LANES : (a + 1) * LANES] = cos.astype(jnp.bfloat16)
            table[rows_at(i, BLOCK, length), a * LANES : (a + 1) * LANES] = sin.astype(
                jnp.bfloat16
            )
            cos, sin = cos * step_cos - sin * step_sin, sin * step_cos + cos * step_sin

    for g in range(groups):

        @blocks(length)
        def _(i):
            partial[g, at_rows(i), :] = jnp.zeros((BLOCK, branches * LANES), jnp.float32)

    def spectrum(which, column):
        @pl.loop(0, 2 * length // SPAN)
        def _(i):
            at = rows_at(i, SPAN)
            freq[which, at, :] = jnp.dot(
                table[at, :], column(), preferred_element_type=jnp.float32
            )

    def spectrum_pair(columns):
        @pl.loop(0, 2 * length // SPAN)
        def _(i):
            at = rows_at(i, SPAN)
            found = jnp.dot(
                table[at, :],
                jnp.concatenate(columns(), axis=1),
                preferred_element_type=jnp.float32,
            )
            freq[0, at, :] = found[:, :LANES]
            freq[1, at, :] = found[:, LANES:]

    def tap_spectra(g):
        spectrum_pair(lambda: [taps[g, :length, :], taps[g, length:, :]])

        @blocks(length)
        def _(i):
            low, high = at_rows(i), rows_at(i, BLOCK, length)
            cos, sin = extended[0, low, :], extended[1, low, :]

            def turned(which):
                real, imag = freq[which, low, :], -freq[which, high, :]
                return (cos * real - sin * imag) / length, (cos * imag + sin * real) / length

            real, imag = turned(0)
            late_real, late_imag = turned(1)
            place = lax.broadcasted_iota(jnp.int32, (BLOCK, LANES), 0)
            sign = (1 - 2 * (place % 2)).astype(jnp.float32)
            spectra[g, 0, low, :] = real.astype(jnp.bfloat16)
            spectra[g, 1, low, :] = imag.astype(jnp.bfloat16)
            spectra[g, 2, low, :] = (late_real - sign * imag).astype(jnp.bfloat16)
            spectra[g, 3, low, :] = (late_imag + sign * real).astype(jnp.bfloat16)

    def project(g, owner):
        @pl.loop(0, length // SPAN)
        def _(i):
            at = rows_at(i, SPAN)
            partial[g, at, :] += jnp.dot(
                stream[owner, at, :], weight[g, owner], preferred_element_type=jnp.float32
            )

    def projects_early(g, owner):
        far = jnp.abs(z - owner)
        own = owner // 2 == x
        return (
            (own & ((far <= 1) | ((far == 2) & (at_end | (g == 0)))))
            | (jnp.logical_not(own) & (far <= 2) & ((g == 0) | ((g == 1) & at_end)))
        )

    def to_mate(way, step, chunk):
        block = token_view(token_line.source(way, step), chunk)
        index = 3 + way * steps + step
        return remote(block, block, mate_send.at[index], mate_recv.at[index], mate)

    def mate_half(way, step, of):
        block = own_half(token_line.source(way, step), of)
        index = 3 + way * steps + step
        return remote(block, block, mate_send.at[index], mate_recv.at[index], mate)

    def await_mate(step):
        for way in range(2):

            @pl.when(token_line.receives(way, step))
            def _():
                mate_half(way, step, 1 - core).wait_recv()

    @pl.loop(0, steps * TOKEN_CHUNKS)
    def _(tick):
        step, chunk = tick // TOKEN_CHUNKS, tick % TOKEN_CHUNKS
        for way in range(2):

            @pl.when(token_line.receives(way, step))
            def _():
                token_line.arrived(way, step, (chunk,))
                to_mate(way, step, chunk).start()

            @pl.when(
                (step + 1 < steps)
                & token_line.receives(way, step)
                & token_line.sends(way, step + 1)
            )
            def _():
                token_line.copy(way, step + 1, (chunk,)).start()

        @pl.when((tick == TOKEN_CHUNKS // 2) & (x == 1))
        def _():
            for origin in range(2):
                view = tap_part(origin, y)
                remote(
                    view, view, tap_send.at[origin], tap_recv.at[origin], beside
                ).wait_recv()
                taps_beside(origin, y).start()

        @pl.when((tick % 2 == 1) & (tick >= 3) & (tick < 7 + 4 * WEIGHT_CHUNKS))
        def _():
            at = (tick - 3) // 2
            forward(at // WEIGHT_CHUNKS, at % WEIGHT_CHUNKS)

        @pl.when(tick == TOKEN_CHUNKS)
        def _():
            mate_half_own = own_half(z, 1 - core)
            remote(
                mate_half_own, mate_half_own, mate_send.at[0], mate_recv.at[0], mate
            ).wait_recv()
            await_mate(0)
            pltpu.make_async_copy(
                weight.at[:, s], weight.at[:, s], local_sem.at[2]
            ).wait()
            other = weight.at[:, mate_s]
            remote(other, other, mate_send.at[1], mate_recv.at[1], mate).wait_recv()
            other = taps.at[:, pl.ds(pl.multiple_of(mate_s * rows, rows), rows), :]
            remote(other, other, mate_send.at[2], mate_recv.at[2], mate).wait_recv()

            @pl.when(x == 1)
            def _():
                for origin in range(2):
                    taps_beside(origin, 1 - y).wait_recv()

        @pl.when((step == 1) & (chunk % 2 == 0))
        def _():
            tap_spectra(chunk // 2)

        @pl.when(tick == 2 * TOKEN_CHUNKS)
        def _():
            await_mate(1)

        owner = 2 * x + chunk // groups
        far = jnp.abs(z - owner)

        @pl.when(
            projects_early(chunk % groups, owner)
            & (((step == 1) & (far <= 1)) | ((step == 2) & (far == 2)))
        )
        def _():
            project(chunk % groups, owner)

        @pl.when(tick == 2 * TOKEN_CHUNKS)
        def _():
            await_beside(0)

        @pl.when((tick == 2 * TOKEN_CHUNKS + TOKEN_CHUNKS // 2) & at_end)
        def _():
            await_beside(1)

        guest = 2 * (1 - x) + (chunk // 2) % 2

        @pl.when((step == 2) & (chunk % 2 == 0) & projects_early(chunk // 4, guest))
        def _():
            project(chunk // 4, guest)

    await_mate(2)
    for by in range(1, chan_count):
        for of in range(2):
            view = sums.at[of, lax.rem(z + by, chan_count)]
            remote(
                view, view, sums_send.at[0], sums_recv.at[of, lax.rem(z + by, chan_count)], mate
            ).wait_recv()
    view = sums.at[1 - core, z]
    remote(view, view, sums_send.at[0], sums_recv.at[1 - core, z], mate).wait_recv()

    @blocks(length)
    def _(i):
        of, at = i // (rows // BLOCK), i % (rows // BLOCK)
        found = sums[of, 0, pl.ds(at, 1), :]
        for owner in range(1, chan_count):
            found = found + sums[of, owner, pl.ds(at, 1), :]
        found = lax.rsqrt(found / (chan_count * width) + EPSILON)
        scale[at_rows(i), :] = jnp.broadcast_to(found, (BLOCK, LANES)).T

    taps_mate().wait_send()

    @pl.when(x == 0)
    def _():
        taps_across(0).wait_send()
        taps_across(1).wait_send()

    def edge_copy(g):
        return remote(
            edge_out.at[g], edge.at[g], edge_send.at[0], edge_recv.at[g], across
        )

    def before_copy(g):
        return remote(
            signal.at[g], before.at[g], before_send.at[0], before_recv.at[g], across
        )

    def swap_copy(g):
        return remote(
            ready.at[g], full.at[z, g, core], swap_send.at[0], swap_recv.at[g], mate
        )

    line = Line(
        lambda owner, g, of: full.at[owner, g, of],
        chan_count,
        line_send,
        line_recv,
        lambda to: (y, s, to),
    )

    def projected(g, b, at):
        return (partial[g, at, b * LANES : (b + 1) * LANES] * scale[at, :]).astype(jnp.bfloat16)

    def featurize(g):
        @pl.when(x == 0)
        def _():
            for b in range(branches):
                edge_out[g, b] = projected(g, b, pl.ds(length - rim, rim))
                extended[b, 0:rim, :] = jnp.zeros((rim, LANES), jnp.float32)
            edge_copy(g).start()

        @blocks(length)
        def _(i):
            for b in range(branches):
                extended[b, pl.ds(pl.multiple_of(rim + i * BLOCK, rim), BLOCK), :] = projected(
                    g, b, at_rows(i)
                ).astype(jnp.float32)

        @pl.when(x == 1)
        def _():
            edge_copy(g).wait_recv()
            for b in range(branches):
                extended[b, 0:rim, :] = edge[g, b].astype(jnp.float32)

        chosen = lanes_of(core * share, g)
        coefficient = [
            [short[tap, b : b + 1, chosen] for b in range(branches)] for tap in range(SHORT)
        ]

        @blocks(length)
        def _(i):
            found = []
            for b in range(branches):
                value = jnp.zeros((BLOCK, LANES), jnp.float32)
                for tap in range(SHORT):
                    value = value + coefficient[tap][b] * extended[
                        b, pl.ds(rim - tap + i * BLOCK, BLOCK), :
                    ]
                found.append(value.astype(jnp.bfloat16))
            query[at_rows(i), :] = found[0]
            signal[g, at_rows(i), :] = (
                found[1].astype(jnp.float32) * found[2].astype(jnp.float32)
            ).astype(jnp.bfloat16)

    def convolve(g):
        joint = (x == 1) & (g > 0)

        @pl.when(jnp.logical_not(joint))
        def _():
            spectrum(0, lambda: signal[g])

        def product(i, which, first):
            low, high = at_rows(i), rows_at(i, BLOCK, length)
            cos, sin = freq[which, low, :], freq[which, high, :]
            real = spectra[g, first, low, :].astype(jnp.float32)
            imag = spectra[g, first + 1, low, :].astype(jnp.float32)
            return cos * real + sin * imag, sin * real - cos * imag

        @pl.when(x == 0)
        def _():
            @blocks(length)
            def _(i):
                real, imag = product(i, 0, 0)
                mixed[at_rows(i), :] = real.astype(jnp.bfloat16)
                mixed[rows_at(i, BLOCK, length), :] = imag.astype(jnp.bfloat16)

        @pl.when(x == 1)
        def _():
            before_copy(g).wait_recv()

            @pl.when(g == 0)
            def _():
                spectrum(1, lambda: before[g])

            @pl.when(g > 0)
            def _():
                spectrum_pair(lambda: [signal[g], before[g]])

            @blocks(length)
            def _(i):
                real, imag = product(i, 0, 0)
                more_real, more_imag = product(i, 1, 2)
                mixed[at_rows(i), :] = (real + more_real).astype(jnp.bfloat16)
                mixed[rows_at(i, BLOCK, length), :] = (imag + more_imag).astype(jnp.bfloat16)

        @pl.loop(0, length // SPAN)
        def _(i):
            low, high = rows_at(i, SPAN), rows_at(i, SPAN, length)
            freq[0, low, :] = jnp.dot(
                table[low, :], mixed[:length, :], preferred_element_type=jnp.float32
            ) + jnp.dot(table[high, :], mixed[length:, :], preferred_element_type=jnp.float32)

        direct = skip[:, lanes_of(core * share, g)]

        def gated(at):
            longer = freq[0, at, :] + direct * signal[g, at, :].astype(jnp.float32)
            longer = longer.astype(jnp.bfloat16).astype(jnp.float32)
            return (query[at, :].astype(jnp.float32) * longer).astype(jnp.bfloat16)

        @blocks(rows)
        def _(i):
            full[z, g, core, at_rows(i), :] = gated(
                pl.ds(pl.multiple_of(core * rows + i * BLOCK, BLOCK), BLOCK)
            )
            ready[g, at_rows(i), :] = gated(
                pl.ds(pl.multiple_of((1 - core) * rows + i * BLOCK, BLOCK), BLOCK)
            )

    def accumulate(owner, g):
        left = pl.ds(pl.multiple_of(owner * 2 * share + g * LANES, LANES), LANES)
        right = pl.ds(pl.multiple_of((owner * 2 + 1) * share + g * LANES, LANES), LANES)

        @pl.loop(0, total.shape[1] // (2 * LANES))
        def _(i):
            cols = rows_at(i, 2 * LANES)
            block = jnp.concatenate([full[owner, g, 0], full[owner, g, 1]], axis=1)
            kernel = jnp.concatenate([out_room[left, cols], out_room[right, cols]], axis=0)
            total[:, cols] += jnp.dot(block, kernel, preferred_element_type=jnp.float32)

    def begin(g):
        swap_copy(g).start()
        for way in range(2):

            @pl.when(line.sends(way, 0))
            def _():
                line.copy(way, 0, (g, core)).start()

    def begin_other(g):
        other = full.at[z, g, 1 - core]
        remote(other, other, swap_send.at[0], swap_recv.at[g], mate).wait_recv()
        for way in range(2):

            @pl.when(line.sends(way, 0))
            def _():
                line.copy(way, 0, (g, 1 - core)).start()

    def settle():
        mate_tokens().wait_send()
        other = weight.at[:, s]
        remote(other, other, mate_send.at[1], mate_recv.at[1], mate).wait_send()
        for copy in sum_copies:
            copy.wait_send()

        @pl.when(x == 1)
        def _():
            for origin in range(2):
                taps_beside(origin, y).wait_send()

        for at in range(2):
            view = weight_half(s, y)
            remote(view, view, x_send.at[at], x_recv.at[0, 0, 0], across).wait_send()
            view = weight_half((1 - x) * 2 + at, y)
            remote(view, view, y_send.at[at], y_recv.at[at, 0], beside).wait_send()

        @pl.when(x == 0)
        def _():
            remote(edge_out, edge, edge_send.at[0], edge_recv.at[0], across).wait_send()
            remote(signal, before, before_send.at[0], before_recv.at[0], across).wait_send()

        for way in range(2):
            for step in range(steps):

                @pl.when(token_line.receives(way, step))
                def _():
                    mate_half(way, step, core).wait_send()

                @pl.when(token_line.sends(way, step))
                def _():
                    token_line.drain(way, step, (0,), lambda owner: own_half(owner, core))

    def way_of(k):
        return jnp.where(z < chan_count // 2, 1 - k, k)

    def late_forwards(g, at, inner, outer):
        for here, pieces in ((jnp.logical_not(at_end), inner), (at_end, outer)):

            @pl.when((g == at) & here)
            def _():
                for group, c in pieces:
                    forward(group, c)

    def pass_on(way, step, at):
        @pl.when(
            (at >= 0) & (at < groups) & line.receives(way, step) & line.sends(way, step + 1)
        )
        def _():
            for of in range(2):
                line.arrived(way, step, (at, of))
                line.copy(way, step + 1, (at, of)).start()

    @pl.loop(0, 2 * groups + steps)
    def _(g):
        @pl.when(g < groups)
        def _():
            @pl.when((g >= 2) | ((g == 1) & jnp.logical_not(at_end)))
            def _():
                await_beside(g)

            @pl.loop(0, chan_count)
            def _(owner):
                @pl.when(jnp.logical_not(projects_early(g, owner)))
                def _():
                    project(g, owner)

            late_forwards(g, 1, [(groups - 2, 3), (groups - 1, 0)], [(groups - 1, 0), (groups - 1, 1)])
            late_forwards(g, 2, [(groups - 1, 1), (groups - 1, 2)], [(groups - 1, 3)])

        @pl.loop(0, 2)
        def _(k):
            pass_on(way_of(k), 0, g - 1 - k)

        @pl.when(g < groups)
        def _():
            featurize(g)

            @pl.when(x == 0)
            def _():
                before_copy(g).start()

                for at, inner, outer in (
                    (0, [(groups - 2, 3), (groups - 1, 0)], [(groups - 1, 2)]),
                    (1, [(groups - 1, 1), (groups - 1, 2)], [(groups - 1, 3)]),
                    (2, [(groups - 1, 3)], []),
                ):

                    @pl.when((g == at) & jnp.logical_not(at_end))
                    def _():
                        for group, c in inner:
                            send_weights(group, [c])

                    @pl.when((g == at) & at_end)
                    def _():
                        for group, c in outer:
                            send_weights(group, [c])

            late_forwards(g, 0, [(groups - 2, 2)], [(groups - 2, 2), (groups - 2, 3)])
            convolve(g)
            begin(g)
            late_forwards(g, 1, [], [(groups - 1, 2)])
            late_forwards(g, 2, [(groups - 1, 3)], [])
            begin_other(g)

        for step in range(1, steps - 1):
            pass_on(way_of(0), step, g - 1 - step)

        @pl.when(g == groups - 1)
        def _():
            out_load.wait()

        own = jnp.where(at_end, g - groups, g - groups + 1)

        @pl.when((own >= 0) & (own < groups))
        def _():
            accumulate(z, own)

        @pl.loop(0, 2)
        def _(k):
            way = way_of(k)
            for step in range(steps):
                at = own - jnp.where(at_end, step, 0)

                @pl.when((at >= 0) & (at < groups) & line.receives(way, step))
                def _():
                    @pl.when(jnp.logical_not(line.sends(way, step + 1)))
                    def _():
                        for of in range(2):
                            line.arrived(way, step, (at, of))

                    accumulate(line.source(way, step), at)

        @pl.when(g == groups + 1)
        def _():
            settle()

    @blocks(rows)
    def _(i):
        result[at_rows(i), :] = total[at_rows(i), :].astype(jnp.bfloat16)

    remote(ready, ready, swap_send.at[0], swap_recv.at[0], mate).wait_send()
    for way in range(2):
        for step in range(steps):

            @pl.when(line.sends(way, step))
            def _():
                line.drain(way, step, (0, 0), lambda owner: full.at[owner])


def chip_body(tokens, norm_gain, proj_weight, short_filter, long_filter, skip_gain, out_weight):
    chan_count = lax.axis_size("chan")
    rows, width = tokens.shape
    depth, branches, local_chan = proj_weight.shape
    length, share = 2 * rows, local_chan // 2
    groups = share // LANES
    steps = chan_count - 1
    dma = pltpu.SemaphoreType.DMA
    f32, bf16 = jnp.float32, jnp.bfloat16
    vmem = pl.BlockSpec(memory_space=pltpu.VMEM)
    return pl.pallas_call(
        functools.partial(block_kernel, chan_count),
        out_shape=jax.ShapeDtypeStruct((rows, width), bf16),
        in_specs=[ANY, vmem, ANY, vmem, ANY, vmem, ANY],
        out_specs=vmem,
        scratch_shapes=[
            pltpu.VMEM((chan_count, length, width), bf16),
            pltpu.VMEM((groups, 4, depth, branches * LANES), bf16),
            pltpu.VMEM((2, chan_count, 8, LANES), f32),
            pltpu.VMEM((length, LANES), f32),
            pltpu.VMEM((groups, length, branches * LANES), f32),
            pltpu.VMEM(out_weight.shape, bf16),
            pltpu.VMEM((2 * length, length), bf16),
            pltpu.VMEM((groups, 2 * length, LANES), bf16),
            pltpu.VMEM((groups, 4, length, LANES), bf16),
            pltpu.VMEM((2, 2 * length, LANES), f32),
            pltpu.VMEM((2 * length, LANES), bf16),
            pltpu.VMEM((groups, branches, 16, LANES), bf16),
            pltpu.VMEM((groups, branches, 16, LANES), bf16),
            pltpu.VMEM((branches, length + 16, LANES), f32),
            pltpu.VMEM((length, LANES), bf16),
            pltpu.VMEM((groups, length, LANES), bf16),
            pltpu.VMEM((groups, length, LANES), bf16),
            pltpu.VMEM((groups, rows, LANES), bf16),
            pltpu.VMEM((chan_count, groups, 2, rows, LANES), bf16),
            pltpu.VMEM((rows, width), f32),
            dma((8,)),
            dma((3 + 2 * steps,)),
            dma((3 + 2 * steps,)),
            dma((2, steps)),
            dma((2, steps, TOKEN_CHUNKS)),
            dma((2 * chan_count - 1,)),
            dma((2, chan_count)),
            dma((2,)),
            dma((2, groups, WEIGHT_CHUNKS)),
            dma((2,)),
            dma((2, groups)),
            dma((4,)),
            dma((4,)),
            dma((1,)),
            dma((groups,)),
            dma((1,)),
            dma((groups,)),
            dma((1,)),
            dma((groups,)),
            dma((2, steps)),
            dma((2, steps, groups, 2)),
        ],
        compiler_params=pltpu.CompilerParams(
            collective_id=0, has_side_effects=True, vmem_limit_bytes=61 * 1024 * 1024
        ),
        name="block",
    )(
        tokens,
        norm_gain[None, :],
        proj_weight.transpose(1, 0, 2),
        short_filter,
        long_filter,
        skip_gain[None, :],
        out_weight,
    )


def select_body(mesh):
    if (mesh.shape["groups"], mesh.shape["seq"], mesh.shape["chan"]) == (2, 4, 4):
        return chip_body
    return body


def solution(mesh):
    placed = (
        P(("groups", "seq"), "chan"),
        P(),
        P("seq", None, "chan"),
        P(None, None, "chan"),
        P("chan", "seq"),
        P("chan"),
        P(None, "chan"),
    )
    return jax.shard_map(
        select_body(mesh), mesh=mesh, in_specs=placed, out_specs=P(("groups", "seq"), "chan"), check_vma=False
    )
```

```python
import functools
import math

import jax
import jax.numpy as jnp
import numpy as np
from jax import lax
from jax.experimental import pallas as pl
from jax.experimental.pallas import tpu as pltpu
from jax.sharding import PartitionSpec as P

SHORT = 3


EPSILON = 1e-06
HIGHEST = lax.Precision.HIGHEST


def from_behind(value, axis, steps):
    count = lax.axis_size(axis)
    initial, last = (max(0, -steps), min(count, count - steps))
    return lax.ppermute(value, axis, [(source, source + steps) for source in range(initial, last)])


def angle_table(row_count, col_count, period, sign):
    row_index = lax.iota(jnp.int32, row_count)[:, None]
    col_index = lax.iota(jnp.int32, col_count)[None, :]
    angles = (row_index * col_index % period).astype(jnp.float32) * (sign * 2.0 * math.pi / period)
    return (jnp.cos(angles), jnp.sin(angles))


def forward_spectrum(signal_rows, first, second):
    channels = signal_rows.shape[0]
    grid_rows = signal_rows.reshape(channels, first, second)
    cos_first, sin_first = angle_table(first, first, first, -1.0)
    part_re = jnp.einsum("cab,ak->ckb", grid_rows, cos_first, precision=HIGHEST)
    part_im = jnp.einsum("cab,ak->ckb", grid_rows, sin_first, precision=HIGHEST)
    twist_cos, twist_sin = angle_table(first, second, first * second, -1.0)
    part_re, part_im = (
        part_re * twist_cos - part_im * twist_sin,
        part_re * twist_sin + part_im * twist_cos,
    )
    cos_second, sin_second = angle_table(second, second, second, -1.0)
    spectrum_real = jnp.einsum("ckb,bm->ckm", part_re, cos_second, precision=HIGHEST) - jnp.einsum(
        "ckb,bm->ckm", part_im, sin_second, precision=HIGHEST
    )
    spec_im = jnp.einsum("ckb,bm->ckm", part_re, sin_second, precision=HIGHEST) + jnp.einsum(
        "ckb,bm->ckm", part_im, cos_second, precision=HIGHEST
    )
    return (spectrum_real, spec_im)


def inverse_spectrum(spectrum_real, spec_im, first, second):
    channels = spectrum_real.shape[0]
    cos_second, sin_second = angle_table(second, second, second, 1.0)
    part_re = jnp.einsum("ckm,bm->ckb", spectrum_real, cos_second, precision=HIGHEST) - jnp.einsum(
        "ckm,bm->ckb", spec_im, sin_second, precision=HIGHEST
    )
    part_im = jnp.einsum("ckm,bm->ckb", spectrum_real, sin_second, precision=HIGHEST) + jnp.einsum(
        "ckm,bm->ckb", spec_im, cos_second, precision=HIGHEST
    )
    twist_cos, twist_sin = angle_table(first, second, first * second, 1.0)
    part_re, part_im = (
        part_re * twist_cos - part_im * twist_sin,
        part_re * twist_sin + part_im * twist_cos,
    )
    cos_first, sin_first = angle_table(first, first, first, 1.0)
    result = jnp.einsum("ckb,ak->cab", part_re, cos_first, precision=HIGHEST) - jnp.einsum(
        "ckb,ak->cab", part_im, sin_first, precision=HIGHEST
    )
    return result.reshape(channels, first * second) / (first * second)


def spectral_conv(signal_rows, filter_rows):
    channels, length = signal_rows.shape
    padded_len = 2 * length
    log_len = padded_len.bit_length() - 1
    first = 1 << log_len // 2
    second = padded_len // first
    zeros_tail = jnp.zeros((channels, length), jnp.float32)
    sig_re, sig_im = forward_spectrum(
        jnp.concatenate([signal_rows, zeros_tail], axis=1), first, second
    )
    tap_re, tap_im = forward_spectrum(
        jnp.concatenate([filter_rows, zeros_tail], axis=1), first, second
    )
    prod_re = sig_re * tap_re - sig_im * tap_im
    prod_im = sig_re * tap_im + sig_im * tap_re
    return inverse_spectrum(prod_re, prod_im, first, second)[:, :length]


def short_filter_output(projected, rim_cells, kernel_coefficients):
    count = kernel_coefficients.shape[0]
    steps_len = projected.shape[2]
    extended = jnp.concatenate([rim_cells, projected], axis=2).astype(jnp.float32)
    total = jnp.zeros(projected.shape, jnp.float32)
    for tap in range(count):
        total = (
            total
            + kernel_coefficients[tap][:, :, None]
            * extended[:, :, count - 1 - tap : count - 1 - tap + steps_len]
        )
    return total.astype(jnp.bfloat16)


def hyena_mixer(keys_rows, values_rows, long_taps, skip_part):
    middle = keys_rows.astype(jnp.float32) * values_rows.astype(jnp.float32)
    return (spectral_conv(middle, long_taps) + skip_part[:, None] * middle).astype(jnp.bfloat16)


def body(tokens, norm_gain, proj_weight, short_filter, long_filter, skip_gain, out_weight):
    seq_count = lax.axis_size("seq")
    local_rows = tokens.shape[0]
    local_chan = proj_weight.shape[2]
    subset = local_chan // seq_count
    length = local_rows * seq_count
    offset = lax.axis_index("seq") * subset
    whole = lax.all_gather(tokens, "chan", axis=1, tiled=True)
    wide = whole.astype(jnp.float32)
    rescaled_signal = (
        wide * lax.rsqrt(jnp.mean(wide * wide, axis=1, keepdims=True) + EPSILON) * norm_gain
    ).astype(jnp.bfloat16)
    projected = lax.dot_general(
        lax.all_gather(proj_weight, "seq", axis=0, tiled=True),
        rescaled_signal,
        (((0,), (1,)), ((), ())),
        preferred_element_type=jnp.float32,
    ).astype(jnp.bfloat16)
    taps_grid = long_filter.reshape(1, seq_count, subset, local_rows)
    long_taps = lax.all_to_all(taps_grid, "seq", split_axis=1, concat_axis=3, tiled=True).reshape(
        subset, length
    )
    skip_part = lax.dynamic_slice_in_dim(skip_gain, offset, subset, 0)
    rim_cells = from_behind(projected[:, :, local_rows - (SHORT - 1) :], "seq", 1)
    featured = short_filter_output(projected, rim_cells, short_filter)
    pair_grid = featured[1:].reshape(2, seq_count, subset, local_rows)
    moved = lax.all_to_all(pair_grid, "seq", split_axis=1, concat_axis=3, tiled=True).reshape(
        2, subset, length
    )
    result = hyena_mixer(moved[0], moved[1], long_taps, skip_part)
    returned = lax.all_to_all(
        result.reshape(1, subset, length), "seq", split_axis=2, concat_axis=0, tiled=True
    )
    returned = returned.reshape(local_chan, local_rows)
    gated = (featured[0].astype(jnp.float32) * returned.astype(jnp.float32)).astype(jnp.bfloat16)
    full_mix = lax.all_gather(gated, "chan", axis=0, tiled=True)
    update = lax.dot_general(
        full_mix, out_weight, (((0,), (0,)), ((), ())), preferred_element_type=jnp.float32
    )
    return (tokens.astype(jnp.float32) + update).astype(jnp.bfloat16)

LANES = 128
BLOCK = 128
SPAN = 512
TOKEN_CHUNKS = 8
WEIGHT_CHUNKS = 4
ANY = pl.BlockSpec(memory_space=pl.ANY)


def remote(src, dst, send_sem, recv_sem, where):
    return pltpu.make_async_remote_copy(
        src_ref=src,
        dst_ref=dst,
        send_sem=send_sem,
        recv_sem=recv_sem,
        device_id=where,
        device_id_type=pl.DeviceIdType.MESH,
    )


class Line:
    def __init__(self, view, count, send_sem, recv_sem, place):
        self.view, self.count, self.place = view, count, place
        self.send_sem, self.recv_sem = send_sem, recv_sem
        self.me = lax.axis_index("chan")

    def move(self, way, step, piece, block, target):
        recv = self.recv_sem.at[(way, step) + piece]
        return remote(block, block, self.send_sem.at[way, step], recv, self.place(target))

    def drain(self, way, step, first, block):
        self.move(way, step, first, block(self.source(way, step - 1)), self.me).wait_send()

    def source(self, way, step):
        return jnp.clip(self.me - (step + 1) * (1 - 2 * way), 0, self.count - 1)

    def copy(self, way, step, piece):
        owner = self.source(way, step - 1)
        target = self.source(way, -2)
        return self.move(way, step, piece, self.view(owner, *piece), target)

    def inside(self, way, by):
        place = self.me + by * (1 - 2 * way)
        return (place >= 0) & (place < self.count)

    def sends(self, way, step):
        return self.inside(way, -step) & self.inside(way, 1)

    def receives(self, way, step):
        return self.inside(way, -1 - step)

    def arrived(self, way, step, piece):
        owner = self.source(way, step)
        self.move(way, step, piece, self.view(owner, *piece), self.me).wait_recv()
        return owner


def block_kernel(
    chan_count,
    tokens,
    gain,
    weights,
    short,
    long_taps,
    skip,
    out_weight,
    result,
    stream,
    weight,
    sums,
    scale,
    partial,
    table,
    taps,
    spectra,
    freq,
    mixed,
    edge_out,
    edge,
    extended,
    query,
    signal,
    before,
    ready,
    full,
    total,
    local_sem,
    mate_send,
    mate_recv,
    token_send,
    token_recv,
    sums_send,
    sums_recv,
    x_send,
    x_recv,
    y_send,
    y_recv,
    tap_send,
    tap_recv,
    edge_send,
    edge_recv,
    before_send,
    before_recv,
    swap_send,
    swap_recv,
    line_send,
    line_recv,
):
    y, s, z = (lax.axis_index(name) for name in ("groups", "seq", "chan"))
    x, core = s // 2, s % 2
    mate_s = s + 1 - 2 * core
    mate = (y, mate_s, z)
    across = (y, (1 - x) * 2 + core, z)
    aslant = (y, (1 - x) * 2 + 1 - core, z)
    beside = (1 - y, s, z)
    rows, width = tokens.shape
    length = 2 * rows
    branches, depth = weights.shape[0], weights.shape[1]
    half = depth // 2
    share = weights.shape[2] // 2
    groups = share // LANES
    rim = edge.shape[2]
    steps = chan_count - 1
    token_rows = rows // TOKEN_CHUNKS
    weight_rows = half // WEIGHT_CHUNKS

    column_peers = [mate] + [
        (y, 2 * x + of, lax.rem(z + by, chan_count))
        for by in range(1, chan_count)
        for of in (core, 1 - core)
    ]
    peers = column_peers + [across, aslant, beside]

    def rows_at(i, count, base=0):
        return pl.ds(pl.multiple_of(base + i * count, count), count)

    def at_rows(i):
        return rows_at(i, BLOCK)

    def blocks(count):
        return pl.loop(0, count // BLOCK)

    def lanes_of(base, g):
        return pl.ds(pl.multiple_of(base + g * LANES, LANES), LANES)

    tap_stage = [(0, 0), (0, length), (1, 0), (1, length)]
    tap_loads = [
        pltpu.make_async_copy(
            long_taps.at[:, pl.ds(j * LANES, LANES)],
            freq.at[which, pl.ds(start, length)],
            local_sem.at[4 + j],
        )
        for j, (which, start) in enumerate(tap_stage)
    ]
    token_load = pltpu.make_async_copy(tokens, result, local_sem.at[0])
    token_load.start()
    barrier = pltpu.get_barrier_semaphore()
    for peer in peers:
        pl.semaphore_signal(barrier, inc=1, device_id=peer, device_id_type=pl.DeviceIdType.MESH)
    for copy in tap_loads:
        copy.start()
    for g in range(groups):
        for b in range(branches):
            pltpu.make_async_copy(
                weights.at[b, :, lanes_of(core * share, g)],
                weight.at[g, s, :, pl.ds(b * LANES, LANES)],
                local_sem.at[2],
            ).start()

    sums[core, z] = jnp.zeros(sums.shape[2:], jnp.float32)
    own_gain = gain[:, pl.ds(pl.multiple_of(z * width, width), width)]
    token_load.wait()

    @blocks(rows)
    def _(i):
        raw = result[at_rows(i), :].astype(jnp.float32)
        total[at_rows(i), :] = raw
        stream[z, pl.ds(pl.multiple_of(core * rows + i * BLOCK, BLOCK), BLOCK), :] = (
            raw * own_gain
        ).astype(jnp.bfloat16)
        square = raw * raw
        found = square[:, :LANES]
        for part in range(1, width // LANES):
            found = found + square[:, part * LANES : (part + 1) * LANES]
        sums[core, z, pl.ds(i, 1), :] = jnp.sum(found.T, axis=0, keepdims=True)

    pl.semaphore_wait(barrier, len(peers))

    def token_view(owner, chunk):
        return stream.at[owner, rows_at(chunk, token_rows, core * rows), :]

    token_line = Line(
        token_view, chan_count, token_send, token_recv, lambda to: (y, s, to)
    )
    for chunk in range(TOKEN_CHUNKS):
        for way in range(2):

            @pl.when(token_line.sends(way, 0))
            def _():
                token_line.copy(way, 0, (chunk,)).start()

    def own_half(owner, of):
        return stream.at[owner, pl.ds(pl.multiple_of(of * rows, rows), rows), :]

    def mate_tokens():
        return remote(
            own_half(z, core), own_half(z, core), mate_send.at[0], mate_recv.at[0], mate
        )

    mate_tokens().start()
    sum_copies = [
        remote(
            sums.at[core, z], sums.at[core, z], sums_send.at[at], sums_recv.at[core, z], peer
        )
        for at, peer in enumerate(column_peers)
    ]
    for copy in sum_copies:
        copy.start()
    for g in range(groups):
        for b in range(branches):
            remote(
                weights.at[b, :, lanes_of((1 - core) * share, g)],
                weight.at[g, s, :, pl.ds(b * LANES, LANES)],
                mate_send.at[1],
                mate_recv.at[1],
                mate,
            ).start()

    for j, (which, start) in enumerate(tap_stage):
        tap_loads[j].wait()

        @pl.loop(0, groups)
        def _(g):
            mine = freq[which, rows_at(core * groups + g, BLOCK, start), :]
            taps[g, pl.ds(pl.multiple_of(s * rows + j * LANES, LANES), LANES), :] = mine.T.astype(
                jnp.bfloat16
            )
            other = freq[which, rows_at((1 - core) * groups + g, BLOCK, start), :]
            ready[g, j * LANES : (j + 1) * LANES, :] = other.T.astype(jnp.bfloat16)

    def tap_part(owner, part):
        return taps.at[
            :, pl.ds(pl.multiple_of(owner * rows + part * (rows // 2), rows // 2), rows // 2), :
        ]

    def taps_across(to):
        src = tap_part(s, y) if to == 0 else ready.at[
            :, pl.ds(pl.multiple_of(y * (rows // 2), rows // 2), rows // 2), :
        ]
        return remote(
            src,
            tap_part(s, y),
            tap_send.at[to],
            tap_recv.at[core],
            across if to == 0 else aslant,
        )

    def taps_beside(origin, part):
        view = tap_part(origin, part)
        return remote(view, view, tap_send.at[2 + origin], tap_recv.at[2 + origin], beside)

    def taps_mate():
        return remote(
            ready,
            taps.at[:, pl.ds(pl.multiple_of(s * rows, rows), rows), :],
            mate_send.at[2],
            mate_recv.at[2],
            mate,
        )

    @pl.when(x == 0)
    def _():
        taps_across(0).start()
        taps_across(1).start()

        @pl.loop(0, groups)
        def _(g):
            taps[g, length:, :] = jnp.zeros((length, LANES), jnp.bfloat16)

    taps_mate().start()

    def weight_view(owner, part, g, c):
        return weight.at[g, owner, rows_at(c, weight_rows, part * half), :]

    def weight_half(owner, part):
        return weight.at[:, owner, pl.ds(pl.multiple_of(part * half, half), half), :]

    def send_weights(g, chunks=range(WEIGHT_CHUNKS)):
        for c in chunks:
            for to in range(2):
                side = core if to == 0 else 1 - core
                view = weight_view(s, y, g, c)
                for b in range(branches):
                    remote(
                        weights.at[
                            b,
                            rows_at(c, weight_rows, y * half),
                            pl.ds(pl.multiple_of(side * share + g * LANES, LANES), LANES),
                        ],
                        view.at[:, pl.ds(b * LANES, LANES)],
                        x_send.at[to],
                        x_recv.at[core, g, c],
                        across if to == 0 else aslant,
                    ).start()

    for g in range(groups - 2):
        send_weights(g)
    send_weights(groups - 2, range(3))

    at_end = (z == 0) | (z == chan_count - 1)

    @pl.when((x == 1) | at_end)
    def _():
        send_weights(groups - 2, [3])
        send_weights(groups - 1, [0, 1])

    @pl.when(x == 1)
    def _():
        send_weights(groups - 1, [2, 3])

    def beside_copy(origin, part, g, c):
        view = weight_view((1 - x) * 2 + origin, part, g, c)
        return remote(view, view, y_send.at[origin], y_recv.at[origin, g], beside)

    def forward(g, c):
        for origin in range(2):
            view = weight_view((1 - x) * 2 + origin, y, g, c)
            remote(
                view, view, x_send.at[origin], x_recv.at[origin, g, c], beside
            ).wait_recv()
            beside_copy(origin, y, g, c).start()

    def await_beside(g):
        for origin in range(2):
            view = weight.at[
                g, (1 - x) * 2 + origin, pl.ds(pl.multiple_of((1 - y) * half, half), half), :
            ]
            remote(view, view, y_send.at[origin], y_recv.at[origin, g], beside).wait_recv()

    @blocks(length)
    def _(i):
        row = lax.broadcasted_iota(jnp.int32, (BLOCK, LANES), 0) + i * BLOCK
        lane = lax.broadcasted_iota(jnp.int32, (BLOCK, LANES), 1)
        unit = math.pi / (4 * length)
        odd = 2 * row + 1
        small = odd.astype(jnp.float32) * unit
        extended[0, at_rows(i), :] = jnp.cos(small)
        extended[1, at_rows(i), :] = jnp.sin(small)
        period = 8 * length
        angle = (odd * (2 * lane + 1) % period).astype(jnp.float32) * unit
        cos, sin = jnp.cos(angle), jnp.sin(angle)
        stride = (odd * (2 * LANES) % period).astype(jnp.float32) * unit
        step_cos, step_sin = jnp.cos(stride), jnp.sin(stride)
        for a in range(length // LANES):
            table[at_rows(i), a * LANES : (a + 1) * LANES] = cos.astype(jnp.bfloat16)
            table[rows_at(i, BLOCK, length), a * LANES : (a + 1) * LANES] = sin.astype(
                jnp.bfloat16
            )
            cos, sin = cos * step_cos - sin * step_sin, sin * step_cos + cos * step_sin

    for g in range(groups):

        @blocks(length)
        def _(i):
            partial[g, at_rows(i), :] = jnp.zeros((BLOCK, branches * LANES), jnp.float32)

    def spectrum(which, column):
        @pl.loop(0, 2 * length // SPAN)
        def _(i):
            at = rows_at(i, SPAN)
            freq[which, at, :] = jnp.dot(
                table[at, :], column(), preferred_element_type=jnp.float32
            )

    def spectrum_pair(columns):
        @pl.loop(0, 2 * length // SPAN)
        def _(i):
            at = rows_at(i, SPAN)
            found = jnp.dot(
                table[at, :],
                jnp.concatenate(columns(), axis=1),
                preferred_element_type=jnp.float32,
            )
            freq[0, at, :] = found[:, :LANES]
            freq[1, at, :] = found[:, LANES:]

    def tap_spectra(g):
        spectrum_pair(lambda: [taps[g, :length, :], taps[g, length:, :]])

        @blocks(length)
        def _(i):
            low, high = at_rows(i), rows_at(i, BLOCK, length)
            cos, sin = extended[0, low, :], extended[1, low, :]

            def turned(which):
                real, imag = freq[which, low, :], -freq[which, high, :]
                return (cos * real - sin * imag) / length, (cos * imag + sin * real) / length

            real, imag = turned(0)
            late_real, late_imag = turned(1)
            place = lax.broadcasted_iota(jnp.int32, (BLOCK, LANES), 0)
            sign = (1 - 2 * (place % 2)).astype(jnp.float32)
            spectra[g, 0, low, :] = real.astype(jnp.bfloat16)
            spectra[g, 1, low, :] = imag.astype(jnp.bfloat16)
            spectra[g, 2, low, :] = (late_real - sign * imag).astype(jnp.bfloat16)
            spectra[g, 3, low, :] = (late_imag + sign * real).astype(jnp.bfloat16)

    def project(g, owner):
        @pl.loop(0, length // SPAN)
        def _(i):
            at = rows_at(i, SPAN)
            partial[g, at, :] += jnp.dot(
                stream[owner, at, :], weight[g, owner], preferred_element_type=jnp.float32
            )

    def projects_early(g, owner):
        far = jnp.abs(z - owner)
        own = owner // 2 == x
        return (
            (own & ((far <= 1) | ((far == 2) & (at_end | (g == 0)))))
            | (jnp.logical_not(own) & (far <= 2) & ((g == 0) | ((g == 1) & at_end)))
        )

    def to_mate(way, step, chunk):
        block = token_view(token_line.source(way, step), chunk)
        index = 3 + way * steps + step
        return remote(block, block, mate_send.at[index], mate_recv.at[index], mate)

    def mate_half(way, step, of):
        block = own_half(token_line.source(way, step), of)
        index = 3 + way * steps + step
        return remote(block, block, mate_send.at[index], mate_recv.at[index], mate)

    def await_mate(step):
        for way in range(2):

            @pl.when(token_line.receives(way, step))
            def _():
                mate_half(way, step, 1 - core).wait_recv()

    @pl.loop(0, steps * TOKEN_CHUNKS)
    def _(tick):
        step, chunk = tick // TOKEN_CHUNKS, tick % TOKEN_CHUNKS
        for way in range(2):

            @pl.when(token_line.receives(way, step))
            def _():
                token_line.arrived(way, step, (chunk,))
                to_mate(way, step, chunk).start()

            @pl.when(
                (step + 1 < steps)
                & token_line.receives(way, step)
                & token_line.sends(way, step + 1)
            )
            def _():
                token_line.copy(way, step + 1, (chunk,)).start()

        @pl.when((tick == TOKEN_CHUNKS // 2) & (x == 1))
        def _():
            for origin in range(2):
                view = tap_part(origin, y)
                remote(
                    view, view, tap_send.at[origin], tap_recv.at[origin], beside
                ).wait_recv()
                taps_beside(origin, y).start()

        @pl.when((tick % 2 == 1) & (tick >= 3) & (tick < 7 + 4 * WEIGHT_CHUNKS))
        def _():
            at = (tick - 3) // 2
            forward(at // WEIGHT_CHUNKS, at % WEIGHT_CHUNKS)

        @pl.when(tick == TOKEN_CHUNKS)
        def _():
            mate_half_own = own_half(z, 1 - core)
            remote(
                mate_half_own, mate_half_own, mate_send.at[0], mate_recv.at[0], mate
            ).wait_recv()
            await_mate(0)
            pltpu.make_async_copy(
                weight.at[:, s], weight.at[:, s], local_sem.at[2]
            ).wait()
            other = weight.at[:, mate_s]
            remote(other, other, mate_send.at[1], mate_recv.at[1], mate).wait_recv()
            other = taps.at[:, pl.ds(pl.multiple_of(mate_s * rows, rows), rows), :]
            remote(other, other, mate_send.at[2], mate_recv.at[2], mate).wait_recv()

            @pl.when(x == 1)
            def _():
                for origin in range(2):
                    taps_beside(origin, 1 - y).wait_recv()

        @pl.when((step == 1) & (chunk % 2 == 0))
        def _():
            tap_spectra(chunk // 2)

        @pl.when(tick == 2 * TOKEN_CHUNKS)
        def _():
            await_mate(1)

        owner = 2 * x + chunk // groups
        far = jnp.abs(z - owner)

        @pl.when(
            projects_early(chunk % groups, owner)
            & (((step == 1) & (far <= 1)) | ((step == 2) & (far == 2)))
        )
        def _():
            project(chunk % groups, owner)

        @pl.when(tick == 2 * TOKEN_CHUNKS)
        def _():
            await_beside(0)

        @pl.when((tick == 2 * TOKEN_CHUNKS + TOKEN_CHUNKS // 2) & at_end)
        def _():
            await_beside(1)

        guest = 2 * (1 - x) + (chunk // 2) % 2

        @pl.when((step == 2) & (chunk % 2 == 0) & projects_early(chunk // 4, guest))
        def _():
            project(chunk // 4, guest)

    await_mate(2)
    for by in range(1, chan_count):
        for of in range(2):
            view = sums.at[of, lax.rem(z + by, chan_count)]
            remote(
                view, view, sums_send.at[0], sums_recv.at[of, lax.rem(z + by, chan_count)], mate
            ).wait_recv()
    view = sums.at[1 - core, z]
    remote(view, view, sums_send.at[0], sums_recv.at[1 - core, z], mate).wait_recv()

    @blocks(length)
    def _(i):
        of, at = i // (rows // BLOCK), i % (rows // BLOCK)
        found = sums[of, 0, pl.ds(at, 1), :]
        for owner in range(1, chan_count):
            found = found + sums[of, owner, pl.ds(at, 1), :]
        found = lax.rsqrt(found / (chan_count * width) + EPSILON)
        scale[at_rows(i), :] = jnp.broadcast_to(found, (BLOCK, LANES)).T

    taps_mate().wait_send()

    @pl.when(x == 0)
    def _():
        taps_across(0).wait_send()
        taps_across(1).wait_send()

    def edge_copy(g):
        return remote(
            edge_out.at[g], edge.at[g], edge_send.at[0], edge_recv.at[g], across
        )

    def before_copy(g):
        return remote(
            signal.at[g], before.at[g], before_send.at[0], before_recv.at[g], across
        )

    def swap_copy(g):
        return remote(
            ready.at[g], full.at[z, g, core], swap_send.at[0], swap_recv.at[g], mate
        )

    line = Line(
        lambda owner, g, of: full.at[owner, g, of],
        chan_count,
        line_send,
        line_recv,
        lambda to: (y, s, to),
    )

    def projected(g, b, at):
        return (partial[g, at, b * LANES : (b + 1) * LANES] * scale[at, :]).astype(jnp.bfloat16)

    def featurize(g):
        @pl.when(x == 0)
        def _():
            for b in range(branches):
                edge_out[g, b] = projected(g, b, pl.ds(length - rim, rim))
                extended[b, 0:rim, :] = jnp.zeros((rim, LANES), jnp.float32)
            edge_copy(g).start()

        @blocks(length)
        def _(i):
            for b in range(branches):
                extended[b, pl.ds(pl.multiple_of(rim + i * BLOCK, rim), BLOCK), :] = projected(
                    g, b, at_rows(i)
                ).astype(jnp.float32)

        @pl.when(x == 1)
        def _():
            edge_copy(g).wait_recv()
            for b in range(branches):
                extended[b, 0:rim, :] = edge[g, b].astype(jnp.float32)

        chosen = lanes_of(core * share, g)
        coefficient = [
            [short[tap, b : b + 1, chosen] for b in range(branches)] for tap in range(SHORT)
        ]

        @blocks(length)
        def _(i):
            found = []
            for b in range(branches):
                value = jnp.zeros((BLOCK, LANES), jnp.float32)
                for tap in range(SHORT):
                    value = value + coefficient[tap][b] * extended[
                        b, pl.ds(rim - tap + i * BLOCK, BLOCK), :
                    ]
                found.append(value.astype(jnp.bfloat16))
            query[at_rows(i), :] = found[0]
            signal[g, at_rows(i), :] = (
                found[1].astype(jnp.float32) * found[2].astype(jnp.float32)
            ).astype(jnp.bfloat16)

    def convolve(g):
        joint = (x == 1) & (g > 0)

        @pl.when(jnp.logical_not(joint))
        def _():
            spectrum(0, lambda: signal[g])

        def product(i, which, first):
            low, high = at_rows(i), rows_at(i, BLOCK, length)
            cos, sin = freq[which, low, :], freq[which, high, :]
            real = spectra[g, first, low, :].astype(jnp.float32)
            imag = spectra[g, first + 1, low, :].astype(jnp.float32)
            return cos * real + sin * imag, sin * real - cos * imag

        @pl.when(x == 0)
        def _():
            @blocks(length)
            def _(i):
                real, imag = product(i, 0, 0)
                mixed[at_rows(i), :] = real.astype(jnp.bfloat16)
                mixed[rows_at(i, BLOCK, length), :] = imag.astype(jnp.bfloat16)

        @pl.when(x == 1)
        def _():
            before_copy(g).wait_recv()

            @pl.when(g == 0)
            def _():
                spectrum(1, lambda: before[g])

            @pl.when(g > 0)
            def _():
                spectrum_pair(lambda: [signal[g], before[g]])

            @blocks(length)
            def _(i):
                real, imag = product(i, 0, 0)
                more_real, more_imag = product(i, 1, 2)
                mixed[at_rows(i), :] = (real + more_real).astype(jnp.bfloat16)
                mixed[rows_at(i, BLOCK, length), :] = (imag + more_imag).astype(jnp.bfloat16)

        @pl.loop(0, length // SPAN)
        def _(i):
            low, high = rows_at(i, SPAN), rows_at(i, SPAN, length)
            freq[0, low, :] = jnp.dot(
                table[low, :], mixed[:length, :], preferred_element_type=jnp.float32
            ) + jnp.dot(table[high, :], mixed[length:, :], preferred_element_type=jnp.float32)

        direct = skip[:, lanes_of(core * share, g)]

        def gated(at):
            longer = freq[0, at, :] + direct * signal[g, at, :].astype(jnp.float32)
            longer = longer.astype(jnp.bfloat16).astype(jnp.float32)
            return (query[at, :].astype(jnp.float32) * longer).astype(jnp.bfloat16)

        @blocks(rows)
        def _(i):
            full[z, g, core, at_rows(i), :] = gated(
                pl.ds(pl.multiple_of(core * rows + i * BLOCK, BLOCK), BLOCK)
            )
            ready[g, at_rows(i), :] = gated(
                pl.ds(pl.multiple_of((1 - core) * rows + i * BLOCK, BLOCK), BLOCK)
            )

    def load_out():
        for owner in range(chan_count):
            pltpu.make_async_copy(
                out_weight.at[pl.ds(owner * length, length)], stream.at[owner], local_sem.at[1]
            ).start()

    def accumulate(owner, g):
        @pl.loop(0, total.shape[1] // (2 * LANES))
        def _(i):
            cols = rows_at(i, 2 * LANES)
            block = jnp.concatenate([full[owner, g, 0], full[owner, g, 1]], axis=1)
            kernel = jnp.concatenate(
                [stream[owner, lanes_of(of * share, g), cols] for of in range(2)], axis=0
            )
            total[:, cols] += jnp.dot(block, kernel, preferred_element_type=jnp.float32)

    def begin(g):
        swap_copy(g).start()
        for way in range(2):

            @pl.when(line.sends(way, 0))
            def _():
                line.copy(way, 0, (g, core)).start()

    def begin_other(g):
        other = full.at[z, g, 1 - core]
        remote(other, other, swap_send.at[0], swap_recv.at[g], mate).wait_recv()
        for way in range(2):

            @pl.when(line.sends(way, 0))
            def _():
                line.copy(way, 0, (g, 1 - core)).start()

    def settle():
        other = weight.at[:, s]
        remote(other, other, mate_send.at[1], mate_recv.at[1], mate).wait_send()
        for copy in sum_copies:
            copy.wait_send()

        @pl.when(x == 1)
        def _():
            for origin in range(2):
                taps_beside(origin, y).wait_send()

        for at in range(2):
            view = weight_half(s, y)
            remote(view, view, x_send.at[at], x_recv.at[0, 0, 0], across).wait_send()
            view = weight_half((1 - x) * 2 + at, y)
            remote(view, view, y_send.at[at], y_recv.at[at, 0], beside).wait_send()

        @pl.when(x == 0)
        def _():
            remote(edge_out, edge, edge_send.at[0], edge_recv.at[0], across).wait_send()
            remote(signal, before, before_send.at[0], before_recv.at[0], across).wait_send()

    def settle_tokens():
        mate_tokens().wait_send()
        for way in range(2):
            for step in range(steps):

                @pl.when(token_line.receives(way, step))
                def _():
                    mate_half(way, step, core).wait_send()

                @pl.when(token_line.sends(way, step))
                def _():
                    token_line.drain(way, step, (0,), lambda owner: own_half(owner, core))

    def way_of(k):
        return jnp.where(z < chan_count // 2, 1 - k, k)

    def late_forwards(g, at, inner, outer):
        for here, pieces in ((jnp.logical_not(at_end), inner), (at_end, outer)):

            @pl.when((g == at) & here)
            def _():
                for group, c in pieces:
                    forward(group, c)

    def pass_on(way, step, at):
        @pl.when(
            (at >= 0) & (at < groups) & line.receives(way, step) & line.sends(way, step + 1)
        )
        def _():
            for of in range(2):
                line.arrived(way, step, (at, of))
                line.copy(way, step + 1, (at, of)).start()

    near, away = way_of(0), way_of(1)

    @pl.loop(0, groups)
    def _(g):
        @pl.when(g == 3)
        def _():
            pass_on(away, 0, 1)

        @pl.when((g >= 2) | ((g == 1) & jnp.logical_not(at_end)))
        def _():
            await_beside(g)

        @pl.when(g == 3)
        def _():
            pass_on(near, 0, 2)

        @pl.loop(0, chan_count)
        def _(owner):
            @pl.when(jnp.logical_not(projects_early(g, owner)))
            def _():
                project(g, owner)

        @pl.when(g == groups - 1)
        def _():
            settle_tokens()
            load_out()

        late_forwards(g, 1, [(groups - 2, 3), (groups - 1, 0)], [(groups - 1, 0), (groups - 1, 1)])
        late_forwards(g, 2, [(groups - 1, 1), (groups - 1, 2)], [(groups - 1, 3)])

        @pl.when((g == 1) | (g == 2))
        def _():
            pass_on(near, 0, g - 1)

        @pl.when(g == 2)
        def _():
            pass_on(away, 0, 0)

        featurize(g)

        @pl.when(x == 0)
        def _():
            before_copy(g).start()

            for at, inner, outer in (
                (0, [(groups - 2, 3), (groups - 1, 0)], [(groups - 1, 2)]),
                (1, [(groups - 1, 1), (groups - 1, 2)], [(groups - 1, 3)]),
                (2, [(groups - 1, 3)], []),
            ):

                @pl.when((g == at) & jnp.logical_not(at_end))
                def _():
                    for group, c in inner:
                        send_weights(group, [c])

                @pl.when((g == at) & at_end)
                def _():
                    for group, c in outer:
                        send_weights(group, [c])

        late_forwards(g, 0, [(groups - 2, 2)], [(groups - 2, 2), (groups - 2, 3)])
        convolve(g)
        begin(g)
        late_forwards(g, 1, [], [(groups - 1, 2)])
        late_forwards(g, 2, [(groups - 1, 3)], [])
        begin_other(g)

        @pl.when(g == 2)
        def _():
            pass_on(near, 1, 0)

    pltpu.make_async_copy(stream, stream, local_sem.at[1]).wait()

    @pl.loop(0, groups + steps - 1)
    def _(n):
        for at, pieces in (
            (0, [(near, 1, 1), (away, 0, 2)]),
            (1, [(near, 0, 3), (near, 1, 2), (away, 0, 3)]),
            (3, [(near, 1, 3)]),
        ):

            @pl.when(n == at)
            def _():
                for way, step, group in pieces:
                    pass_on(way, step, group)

        @pl.when(n == 2)
        def _():
            settle()

        @pl.when(n < groups)
        def _():
            accumulate(z, n)

        @pl.loop(0, 2)
        def _(way):
            for step in range(steps):
                at = n - jnp.where(at_end, step, 0)

                @pl.when((at >= 0) & (at < groups) & line.receives(way, step))
                def _():
                    @pl.when(jnp.logical_not(line.sends(way, step + 1)))
                    def _():
                        for of in range(2):
                            line.arrived(way, step, (at, of))

                    accumulate(line.source(way, step), at)

    @blocks(rows)
    def _(i):
        result[at_rows(i), :] = total[at_rows(i), :].astype(jnp.bfloat16)

    remote(ready, ready, swap_send.at[0], swap_recv.at[0], mate).wait_send()
    for way in range(2):
        for step in range(steps):

            @pl.when(line.sends(way, step))
            def _():
                line.drain(way, step, (0, 0), lambda owner: full.at[owner])


def chip_body(tokens, norm_gain, proj_weight, short_filter, long_filter, skip_gain, out_weight):
    chan_count = lax.axis_size("chan")
    rows, width = tokens.shape
    depth, branches, local_chan = proj_weight.shape
    length, share = 2 * rows, local_chan // 2
    groups = share // LANES
    steps = chan_count - 1
    dma = pltpu.SemaphoreType.DMA
    f32, bf16 = jnp.float32, jnp.bfloat16
    vmem = pl.BlockSpec(memory_space=pltpu.VMEM)
    return pl.pallas_call(
        functools.partial(block_kernel, chan_count),
        out_shape=jax.ShapeDtypeStruct((rows, width), bf16),
        in_specs=[ANY, vmem, ANY, vmem, ANY, vmem, ANY],
        out_specs=vmem,
        scratch_shapes=[
            pltpu.VMEM((chan_count, length, width), bf16),
            pltpu.VMEM((groups, 4, depth, branches * LANES), bf16),
            pltpu.VMEM((2, chan_count, 8, LANES), f32),
            pltpu.VMEM((length, LANES), f32),
            pltpu.VMEM((groups, length, branches * LANES), f32),
            pltpu.VMEM((2 * length, length), bf16),
            pltpu.VMEM((groups, 2 * length, LANES), bf16),
            pltpu.VMEM((groups, 4, length, LANES), bf16),
            pltpu.VMEM((2, 2 * length, LANES), f32),
            pltpu.VMEM((2 * length, LANES), bf16),
            pltpu.VMEM((groups, branches, 16, LANES), bf16),
            pltpu.VMEM((groups, branches, 16, LANES), bf16),
            pltpu.VMEM((branches, length + 16, LANES), f32),
            pltpu.VMEM((length, LANES), bf16),
            pltpu.VMEM((groups, length, LANES), bf16),
            pltpu.VMEM((groups, length, LANES), bf16),
            pltpu.VMEM((groups, rows, LANES), bf16),
            pltpu.VMEM((chan_count, groups, 2, rows, LANES), bf16),
            pltpu.VMEM((rows, width), f32),
            dma((8,)),
            dma((3 + 2 * steps,)),
            dma((3 + 2 * steps,)),
            dma((2, steps)),
            dma((2, steps, TOKEN_CHUNKS)),
            dma((2 * chan_count - 1,)),
            dma((2, chan_count)),
            dma((2,)),
            dma((2, groups, WEIGHT_CHUNKS)),
            dma((2,)),
            dma((2, groups)),
            dma((4,)),
            dma((4,)),
            dma((1,)),
            dma((groups,)),
            dma((1,)),
            dma((groups,)),
            dma((1,)),
            dma((groups,)),
            dma((2, steps)),
            dma((2, steps, groups, 2)),
        ],
        compiler_params=pltpu.CompilerParams(
            collective_id=0, has_side_effects=True, vmem_limit_bytes=52 * 1024 * 1024
        ),
        name="block",
    )(
        tokens,
        norm_gain[None, :],
        proj_weight.transpose(1, 0, 2),
        short_filter,
        long_filter,
        skip_gain[None, :],
        out_weight,
    )


def select_body(mesh):
    if (mesh.shape["groups"], mesh.shape["seq"], mesh.shape["chan"]) == (2, 4, 4):
        return chip_body
    return body


def solution(mesh):
    placed = (
        P(("groups", "seq"), "chan"),
        P(),
        P("seq", None, "chan"),
        P(None, None, "chan"),
        P("chan", "seq"),
        P("chan"),
        P(None, "chan"),
    )
    return jax.shard_map(
        select_body(mesh), mesh=mesh, in_specs=placed, out_specs=P(("groups", "seq"), "chan"), check_vma=False
    )
```

```python
import functools
import math

import jax
import jax.numpy as jnp
import numpy as np
from jax import lax
from jax.experimental import pallas as pl
from jax.experimental.pallas import tpu as pltpu
from jax.sharding import PartitionSpec as P

SHORT = 3


EPSILON = 1e-06
HIGHEST = lax.Precision.HIGHEST


def from_behind(value, axis, steps):
    count = lax.axis_size(axis)
    initial, last = (max(0, -steps), min(count, count - steps))
    return lax.ppermute(value, axis, [(source, source + steps) for source in range(initial, last)])


def angle_table(row_count, col_count, period, sign):
    row_index = lax.iota(jnp.int32, row_count)[:, None]
    col_index = lax.iota(jnp.int32, col_count)[None, :]
    angles = (row_index * col_index % period).astype(jnp.float32) * (sign * 2.0 * math.pi / period)
    return (jnp.cos(angles), jnp.sin(angles))


def forward_spectrum(signal_rows, first, second):
    channels = signal_rows.shape[0]
    grid_rows = signal_rows.reshape(channels, first, second)
    cos_first, sin_first = angle_table(first, first, first, -1.0)
    part_re = jnp.einsum("cab,ak->ckb", grid_rows, cos_first, precision=HIGHEST)
    part_im = jnp.einsum("cab,ak->ckb", grid_rows, sin_first, precision=HIGHEST)
    twist_cos, twist_sin = angle_table(first, second, first * second, -1.0)
    part_re, part_im = (
        part_re * twist_cos - part_im * twist_sin,
        part_re * twist_sin + part_im * twist_cos,
    )
    cos_second, sin_second = angle_table(second, second, second, -1.0)
    spectrum_real = jnp.einsum("ckb,bm->ckm", part_re, cos_second, precision=HIGHEST) - jnp.einsum(
        "ckb,bm->ckm", part_im, sin_second, precision=HIGHEST
    )
    spec_im = jnp.einsum("ckb,bm->ckm", part_re, sin_second, precision=HIGHEST) + jnp.einsum(
        "ckb,bm->ckm", part_im, cos_second, precision=HIGHEST
    )
    return (spectrum_real, spec_im)


def inverse_spectrum(spectrum_real, spec_im, first, second):
    channels = spectrum_real.shape[0]
    cos_second, sin_second = angle_table(second, second, second, 1.0)
    part_re = jnp.einsum("ckm,bm->ckb", spectrum_real, cos_second, precision=HIGHEST) - jnp.einsum(
        "ckm,bm->ckb", spec_im, sin_second, precision=HIGHEST
    )
    part_im = jnp.einsum("ckm,bm->ckb", spectrum_real, sin_second, precision=HIGHEST) + jnp.einsum(
        "ckm,bm->ckb", spec_im, cos_second, precision=HIGHEST
    )
    twist_cos, twist_sin = angle_table(first, second, first * second, 1.0)
    part_re, part_im = (
        part_re * twist_cos - part_im * twist_sin,
        part_re * twist_sin + part_im * twist_cos,
    )
    cos_first, sin_first = angle_table(first, first, first, 1.0)
    result = jnp.einsum("ckb,ak->cab", part_re, cos_first, precision=HIGHEST) - jnp.einsum(
        "ckb,ak->cab", part_im, sin_first, precision=HIGHEST
    )
    return result.reshape(channels, first * second) / (first * second)


def spectral_conv(signal_rows, filter_rows):
    channels, length = signal_rows.shape
    padded_len = 2 * length
    log_len = padded_len.bit_length() - 1
    first = 1 << log_len // 2
    second = padded_len // first
    zeros_tail = jnp.zeros((channels, length), jnp.float32)
    sig_re, sig_im = forward_spectrum(
        jnp.concatenate([signal_rows, zeros_tail], axis=1), first, second
    )
    tap_re, tap_im = forward_spectrum(
        jnp.concatenate([filter_rows, zeros_tail], axis=1), first, second
    )
    prod_re = sig_re * tap_re - sig_im * tap_im
    prod_im = sig_re * tap_im + sig_im * tap_re
    return inverse_spectrum(prod_re, prod_im, first, second)[:, :length]


def short_filter_output(projected, rim_cells, kernel_coefficients):
    count = kernel_coefficients.shape[0]
    steps_len = projected.shape[2]
    extended = jnp.concatenate([rim_cells, projected], axis=2).astype(jnp.float32)
    total = jnp.zeros(projected.shape, jnp.float32)
    for tap in range(count):
        total = (
            total
            + kernel_coefficients[tap][:, :, None]
            * extended[:, :, count - 1 - tap : count - 1 - tap + steps_len]
        )
    return total.astype(jnp.bfloat16)


def hyena_mixer(keys_rows, values_rows, long_taps, skip_part):
    middle = keys_rows.astype(jnp.float32) * values_rows.astype(jnp.float32)
    return (spectral_conv(middle, long_taps) + skip_part[:, None] * middle).astype(jnp.bfloat16)


def body(tokens, norm_gain, proj_weight, short_filter, long_filter, skip_gain, out_weight):
    seq_count = lax.axis_size("seq")
    local_rows = tokens.shape[0]
    local_chan = proj_weight.shape[2]
    subset = local_chan // seq_count
    length = local_rows * seq_count
    offset = lax.axis_index("seq") * subset
    whole = lax.all_gather(tokens, "chan", axis=1, tiled=True)
    wide = whole.astype(jnp.float32)
    rescaled_signal = (
        wide * lax.rsqrt(jnp.mean(wide * wide, axis=1, keepdims=True) + EPSILON) * norm_gain
    ).astype(jnp.bfloat16)
    projected = lax.dot_general(
        lax.all_gather(proj_weight, "seq", axis=0, tiled=True),
        rescaled_signal,
        (((0,), (1,)), ((), ())),
        preferred_element_type=jnp.float32,
    ).astype(jnp.bfloat16)
    taps_grid = long_filter.reshape(1, seq_count, subset, local_rows)
    long_taps = lax.all_to_all(taps_grid, "seq", split_axis=1, concat_axis=3, tiled=True).reshape(
        subset, length
    )
    skip_part = lax.dynamic_slice_in_dim(skip_gain, offset, subset, 0)
    rim_cells = from_behind(projected[:, :, local_rows - (SHORT - 1) :], "seq", 1)
    featured = short_filter_output(projected, rim_cells, short_filter)
    pair_grid = featured[1:].reshape(2, seq_count, subset, local_rows)
    moved = lax.all_to_all(pair_grid, "seq", split_axis=1, concat_axis=3, tiled=True).reshape(
        2, subset, length
    )
    result = hyena_mixer(moved[0], moved[1], long_taps, skip_part)
    returned = lax.all_to_all(
        result.reshape(1, subset, length), "seq", split_axis=2, concat_axis=0, tiled=True
    )
    returned = returned.reshape(local_chan, local_rows)
    gated = (featured[0].astype(jnp.float32) * returned.astype(jnp.float32)).astype(jnp.bfloat16)
    full_mix = lax.all_gather(gated, "chan", axis=0, tiled=True)
    update = lax.dot_general(
        full_mix, out_weight, (((0,), (0,)), ((), ())), preferred_element_type=jnp.float32
    )
    return (tokens.astype(jnp.float32) + update).astype(jnp.bfloat16)

LANES = 128
BLOCK = 128
SPAN = 512
TOKEN_CHUNKS = 8
WEIGHT_CHUNKS = 4
HBM = pl.BlockSpec(memory_space=pltpu.HBM)


def remote(src, dst, send_sem, recv_sem, where):
    return pltpu.make_async_remote_copy(
        src_ref=src,
        dst_ref=dst,
        send_sem=send_sem,
        recv_sem=recv_sem,
        device_id=where,
        device_id_type=pl.DeviceIdType.MESH,
    )


class Line:
    def __init__(self, view, count, send_sem, recv_sem, place):
        self.view, self.count, self.place = view, count, place
        self.send_sem, self.recv_sem = send_sem, recv_sem
        self.me = lax.axis_index("chan")

    def move(self, way, step, piece, block, target):
        recv = self.recv_sem.at[(way, step) + piece]
        return remote(block, block, self.send_sem.at[way, step], recv, self.place(target))

    def drain(self, way, step, first, block):
        self.move(way, step, first, block(self.source(way, step - 1)), self.me).wait_send()

    def source(self, way, step):
        return jnp.clip(self.me - (step + 1) * (1 - 2 * way), 0, self.count - 1)

    def copy(self, way, step, piece):
        owner = self.source(way, step - 1)
        target = self.source(way, -2)
        return self.move(way, step, piece, self.view(owner, *piece), target)

    def inside(self, way, by):
        place = self.me + by * (1 - 2 * way)
        return (place >= 0) & (place < self.count)

    def sends(self, way, step):
        return self.inside(way, -step) & self.inside(way, 1)

    def receives(self, way, step):
        return self.inside(way, -1 - step)

    def arrived(self, way, step, piece):
        owner = self.source(way, step)
        self.move(way, step, piece, self.view(owner, *piece), self.me).wait_recv()
        return owner


def block_kernel(
    chan_count,
    tokens,
    gain_hbm,
    weights,
    short_hbm,
    long_taps,
    skip_hbm,
    out_weight,
    result,
    gain,
    short,
    skip,
    stream,
    weight,
    sums,
    scale,
    partial,
    table,
    taps,
    spectra,
    freq,
    mixed,
    edge_out,
    edge,
    extended,
    query,
    signal,
    before,
    ready,
    full,
    total,
    local_sem,
    mate_send,
    mate_recv,
    token_send,
    token_recv,
    sums_send,
    sums_recv,
    x_send,
    x_recv,
    y_send,
    y_recv,
    tap_send,
    tap_recv,
    edge_send,
    edge_recv,
    before_send,
    before_recv,
    swap_send,
    swap_recv,
    line_send,
    line_recv,
):
    y, s, z = (lax.axis_index(name) for name in ("groups", "seq", "chan"))
    x, core = s // 2, s % 2
    mate_s = s + 1 - 2 * core
    mate = (y, mate_s, z)
    across = (y, (1 - x) * 2 + core, z)
    aslant = (y, (1 - x) * 2 + 1 - core, z)
    beside = (1 - y, s, z)
    rows, width = tokens.shape
    length = 2 * rows
    branches, depth = weights.shape[0], weights.shape[1]
    half = depth // 2
    share = weights.shape[2] // 2
    groups = share // LANES
    rim = edge.shape[2]
    steps = chan_count - 1
    token_rows = rows // TOKEN_CHUNKS
    weight_rows = half // WEIGHT_CHUNKS

    column_peers = [mate] + [
        (y, 2 * x + of, lax.rem(z + by, chan_count))
        for by in range(1, chan_count)
        for of in (core, 1 - core)
    ]
    peers = column_peers + [across, aslant, beside]

    def rows_at(i, count, base=0):
        return pl.ds(pl.multiple_of(base + i * count, count), count)

    def at_rows(i):
        return rows_at(i, BLOCK)

    def blocks(count):
        return pl.loop(0, count // BLOCK)

    def lanes_of(base, g):
        return pl.ds(pl.multiple_of(base + g * LANES, LANES), LANES)

    tap_stage = [(0, 0), (0, length), (1, 0), (1, length)]
    tap_loads = [
        pltpu.make_async_copy(
            long_taps.at[:, pl.ds(j * LANES, LANES)],
            freq.at[which, pl.ds(start, length)],
            local_sem.at[4 + j],
        )
        for j, (which, start) in enumerate(tap_stage)
    ]
    token_load = pltpu.make_async_copy(tokens, result, local_sem.at[0])
    token_load.start()
    small_loads = [
        pltpu.make_async_copy(src, dst, local_sem.at[at])
        for src, dst, at in (
            (gain_hbm.at[:, pl.ds(pl.multiple_of(z * width, width), width)], gain, 3),
            (short_hbm, short, 8),
            (skip_hbm, skip, 9),
        )
    ]
    for copy in small_loads:
        copy.start()
    barrier = pltpu.get_barrier_semaphore()
    for peer in peers:
        pl.semaphore_signal(barrier, inc=1, device_id=peer, device_id_type=pl.DeviceIdType.MESH)
    for copy in tap_loads:
        copy.start()
    for g in range(groups):
        for b in range(branches):
            pltpu.make_async_copy(
                weights.at[b, :, lanes_of(core * share, g)],
                weight.at[g, s, :, pl.ds(b * LANES, LANES)],
                local_sem.at[2],
            ).start()

    sums[core, z] = jnp.zeros(sums.shape[2:], jnp.float32)
    small_loads[0].wait()
    own_gain = gain[...]
    token_load.wait()

    @blocks(rows)
    def _(i):
        raw = result[at_rows(i), :].astype(jnp.float32)
        total[at_rows(i), :] = raw
        stream[z, pl.ds(pl.multiple_of(core * rows + i * BLOCK, BLOCK), BLOCK), :] = (
            raw * own_gain
        ).astype(jnp.bfloat16)
        square = raw * raw
        found = square[:, :LANES]
        for part in range(1, width // LANES):
            found = found + square[:, part * LANES : (part + 1) * LANES]
        sums[core, z, pl.ds(i, 1), :] = jnp.sum(found.T, axis=0, keepdims=True)

    pl.semaphore_wait(barrier, len(peers))

    def token_view(owner, chunk):
        return stream.at[owner, rows_at(chunk, token_rows, core * rows), :]

    token_line = Line(
        token_view, chan_count, token_send, token_recv, lambda to: (y, s, to)
    )
    for chunk in range(TOKEN_CHUNKS):
        for way in range(2):

            @pl.when(token_line.sends(way, 0))
            def _():
                token_line.copy(way, 0, (chunk,)).start()

    def own_half(owner, of):
        return stream.at[owner, pl.ds(pl.multiple_of(of * rows, rows), rows), :]

    def mate_tokens():
        return remote(
            own_half(z, core), own_half(z, core), mate_send.at[0], mate_recv.at[0], mate
        )

    mate_tokens().start()
    sum_copies = [
        remote(
            sums.at[core, z], sums.at[core, z], sums_send.at[at], sums_recv.at[core, z], peer
        )
        for at, peer in enumerate(column_peers)
    ]
    for copy in sum_copies:
        copy.start()
    for g in range(groups):
        for b in range(branches):
            remote(
                weights.at[b, :, lanes_of((1 - core) * share, g)],
                weight.at[g, s, :, pl.ds(b * LANES, LANES)],
                mate_send.at[1],
                mate_recv.at[1],
                mate,
            ).start()

    for j, (which, start) in enumerate(tap_stage):
        tap_loads[j].wait()

        @pl.loop(0, groups)
        def _(g):
            mine = freq[which, rows_at(core * groups + g, BLOCK, start), :]
            taps[g, pl.ds(pl.multiple_of(s * rows + j * LANES, LANES), LANES), :] = mine.T.astype(
                jnp.bfloat16
            )
            other = freq[which, rows_at((1 - core) * groups + g, BLOCK, start), :]
            ready[g, j * LANES : (j + 1) * LANES, :] = other.T.astype(jnp.bfloat16)

    def tap_part(owner, part):
        return taps.at[
            :, pl.ds(pl.multiple_of(owner * rows + part * (rows // 2), rows // 2), rows // 2), :
        ]

    def taps_across(to):
        src = tap_part(s, y) if to == 0 else ready.at[
            :, pl.ds(pl.multiple_of(y * (rows // 2), rows // 2), rows // 2), :
        ]
        return remote(
            src,
            tap_part(s, y),
            tap_send.at[to],
            tap_recv.at[core],
            across if to == 0 else aslant,
        )

    def taps_beside(origin, part):
        view = tap_part(origin, part)
        return remote(view, view, tap_send.at[2 + origin], tap_recv.at[2 + origin], beside)

    def taps_mate():
        return remote(
            ready,
            taps.at[:, pl.ds(pl.multiple_of(s * rows, rows), rows), :],
            mate_send.at[2],
            mate_recv.at[2],
            mate,
        )

    @pl.when(x == 0)
    def _():
        taps_across(0).start()
        taps_across(1).start()

        @pl.loop(0, groups)
        def _(g):
            taps[g, length:, :] = jnp.zeros((length, LANES), jnp.bfloat16)

    taps_mate().start()

    def weight_view(owner, part, g, c):
        return weight.at[g, owner, rows_at(c, weight_rows, part * half), :]

    def weight_half(owner, part):
        return weight.at[:, owner, pl.ds(pl.multiple_of(part * half, half), half), :]

    def send_weights(g, chunks=range(WEIGHT_CHUNKS)):
        for c in chunks:
            for to in range(2):
                side = core if to == 0 else 1 - core
                view = weight_view(s, y, g, c)
                for b in range(branches):
                    remote(
                        weights.at[
                            b,
                            rows_at(c, weight_rows, y * half),
                            pl.ds(pl.multiple_of(side * share + g * LANES, LANES), LANES),
                        ],
                        view.at[:, pl.ds(b * LANES, LANES)],
                        x_send.at[to],
                        x_recv.at[core, g, c],
                        across if to == 0 else aslant,
                    ).start()

    for g in range(groups - 2):
        send_weights(g)
    send_weights(groups - 2, range(3))

    at_end = (z == 0) | (z == chan_count - 1)

    @pl.when((x == 1) | at_end)
    def _():
        send_weights(groups - 2, [3])
        send_weights(groups - 1, [0, 1])

    @pl.when(x == 1)
    def _():
        send_weights(groups - 1, [2, 3])

    def beside_copy(origin, part, g, c):
        view = weight_view((1 - x) * 2 + origin, part, g, c)
        return remote(view, view, y_send.at[origin], y_recv.at[origin, g], beside)

    def forward(g, c):
        for origin in range(2):
            view = weight_view((1 - x) * 2 + origin, y, g, c)
            remote(
                view, view, x_send.at[origin], x_recv.at[origin, g, c], beside
            ).wait_recv()
            beside_copy(origin, y, g, c).start()

    def await_beside(g):
        for origin in range(2):
            view = weight.at[
                g, (1 - x) * 2 + origin, pl.ds(pl.multiple_of((1 - y) * half, half), half), :
            ]
            remote(view, view, y_send.at[origin], y_recv.at[origin, g], beside).wait_recv()

    @blocks(length)
    def _(i):
        row = lax.broadcasted_iota(jnp.int32, (BLOCK, LANES), 0) + i * BLOCK
        lane = lax.broadcasted_iota(jnp.int32, (BLOCK, LANES), 1)
        unit = math.pi / (4 * length)
        odd = 2 * row + 1
        small = odd.astype(jnp.float32) * unit
        extended[0, at_rows(i), :] = jnp.cos(small)
        extended[1, at_rows(i), :] = jnp.sin(small)
        period = 8 * length
        angle = (odd * (2 * lane + 1) % period).astype(jnp.float32) * unit
        cos, sin = jnp.cos(angle), jnp.sin(angle)
        stride = (odd * (2 * LANES) % period).astype(jnp.float32) * unit
        step_cos, step_sin = jnp.cos(stride), jnp.sin(stride)
        for a in range(length // LANES):
            table[at_rows(i), a * LANES : (a + 1) * LANES] = cos.astype(jnp.bfloat16)
            table[rows_at(i, BLOCK, length), a * LANES : (a + 1) * LANES] = sin.astype(
                jnp.bfloat16
            )
            cos, sin = cos * step_cos - sin * step_sin, sin * step_cos + cos * step_sin

    for g in range(groups):

        @blocks(length)
        def _(i):
            partial[g, at_rows(i), :] = jnp.zeros((BLOCK, branches * LANES), jnp.float32)

    def spectrum(which, column):
        @pl.loop(0, 2 * length // SPAN)
        def _(i):
            at = rows_at(i, SPAN)
            freq[which, at, :] = jnp.dot(
                table[at, :], column(), preferred_element_type=jnp.float32
            )

    def spectrum_pair(columns):
        @pl.loop(0, 2 * length // SPAN)
        def _(i):
            at = rows_at(i, SPAN)
            found = jnp.dot(
                table[at, :],
                jnp.concatenate(columns(), axis=1),
                preferred_element_type=jnp.float32,
            )
            freq[0, at, :] = found[:, :LANES]
            freq[1, at, :] = found[:, LANES:]

    def tap_spectra(g):
        spectrum_pair(lambda: [taps[g, :length, :], taps[g, length:, :]])

        @blocks(length)
        def _(i):
            low, high = at_rows(i), rows_at(i, BLOCK, length)
            cos, sin = extended[0, low, :], extended[1, low, :]

            def turned(which):
                real, imag = freq[which, low, :], -freq[which, high, :]
                return (cos * real - sin * imag) / length, (cos * imag + sin * real) / length

            real, imag = turned(0)
            late_real, late_imag = turned(1)
            place = lax.broadcasted_iota(jnp.int32, (BLOCK, LANES), 0)
            sign = (1 - 2 * (place % 2)).astype(jnp.float32)
            spectra[g, 0, low, :] = real.astype(jnp.bfloat16)
            spectra[g, 1, low, :] = imag.astype(jnp.bfloat16)
            spectra[g, 2, low, :] = (late_real - sign * imag).astype(jnp.bfloat16)
            spectra[g, 3, low, :] = (late_imag + sign * real).astype(jnp.bfloat16)

    def project(g, owner):
        @pl.loop(0, length // SPAN)
        def _(i):
            at = rows_at(i, SPAN)
            partial[g, at, :] += jnp.dot(
                stream[owner, at, :], weight[g, owner], preferred_element_type=jnp.float32
            )

    def projects_early(g, owner):
        far = jnp.abs(z - owner)
        own = owner // 2 == x
        return (
            (own & ((far <= 1) | ((far == 2) & (at_end | (g == 0)))))
            | (jnp.logical_not(own) & (far <= 2) & ((g == 0) | ((g == 1) & at_end)))
        )

    def to_mate(way, step, chunk):
        block = token_view(token_line.source(way, step), chunk)
        index = 3 + way * steps + step
        return remote(block, block, mate_send.at[index], mate_recv.at[index], mate)

    def mate_half(way, step, of):
        block = own_half(token_line.source(way, step), of)
        index = 3 + way * steps + step
        return remote(block, block, mate_send.at[index], mate_recv.at[index], mate)

    def await_mate(step):
        for way in range(2):

            @pl.when(token_line.receives(way, step))
            def _():
                mate_half(way, step, 1 - core).wait_recv()

    @pl.loop(0, steps * TOKEN_CHUNKS)
    def _(tick):
        step, chunk = tick // TOKEN_CHUNKS, tick % TOKEN_CHUNKS
        for way in range(2):

            @pl.when(token_line.receives(way, step))
            def _():
                token_line.arrived(way, step, (chunk,))
                to_mate(way, step, chunk).start()

            @pl.when(
                (step + 1 < steps)
                & token_line.receives(way, step)
                & token_line.sends(way, step + 1)
            )
            def _():
                token_line.copy(way, step + 1, (chunk,)).start()

        @pl.when((tick == TOKEN_CHUNKS // 2) & (x == 1))
        def _():
            for origin in range(2):
                view = tap_part(origin, y)
                remote(
                    view, view, tap_send.at[origin], tap_recv.at[origin], beside
                ).wait_recv()
                taps_beside(origin, y).start()

        @pl.when((tick % 2 == 1) & (tick >= 3) & (tick < 7 + 4 * WEIGHT_CHUNKS))
        def _():
            at = (tick - 3) // 2
            forward(at // WEIGHT_CHUNKS, at % WEIGHT_CHUNKS)

        @pl.when(tick == TOKEN_CHUNKS)
        def _():
            mate_half_own = own_half(z, 1 - core)
            remote(
                mate_half_own, mate_half_own, mate_send.at[0], mate_recv.at[0], mate
            ).wait_recv()
            await_mate(0)
            pltpu.make_async_copy(
                weight.at[:, s], weight.at[:, s], local_sem.at[2]
            ).wait()
            other = weight.at[:, mate_s]
            remote(other, other, mate_send.at[1], mate_recv.at[1], mate).wait_recv()
            other = taps.at[:, pl.ds(pl.multiple_of(mate_s * rows, rows), rows), :]
            remote(other, other, mate_send.at[2], mate_recv.at[2], mate).wait_recv()

            @pl.when(x == 1)
            def _():
                for origin in range(2):
                    taps_beside(origin, 1 - y).wait_recv()

        @pl.when((step == 1) & (chunk % 2 == 0))
        def _():
            tap_spectra(chunk // 2)

        @pl.when(tick == 2 * TOKEN_CHUNKS)
        def _():
            await_mate(1)

        owner = 2 * x + chunk // groups
        far = jnp.abs(z - owner)

        @pl.when(
            projects_early(chunk % groups, owner)
            & (((step == 1) & (far <= 1)) | ((step == 2) & (far == 2)))
        )
        def _():
            project(chunk % groups, owner)

        @pl.when(tick == 2 * TOKEN_CHUNKS)
        def _():
            await_beside(0)

        @pl.when((tick == 2 * TOKEN_CHUNKS + TOKEN_CHUNKS // 2) & at_end)
        def _():
            await_beside(1)

        guest = 2 * (1 - x) + (chunk // 2) % 2

        @pl.when((step == 2) & (chunk % 2 == 0) & projects_early(chunk // 4, guest))
        def _():
            project(chunk // 4, guest)

    await_mate(2)
    for by in range(1, chan_count):
        for of in range(2):
            view = sums.at[of, lax.rem(z + by, chan_count)]
            remote(
                view, view, sums_send.at[0], sums_recv.at[of, lax.rem(z + by, chan_count)], mate
            ).wait_recv()
    view = sums.at[1 - core, z]
    remote(view, view, sums_send.at[0], sums_recv.at[1 - core, z], mate).wait_recv()

    @blocks(length)
    def _(i):
        of, at = i // (rows // BLOCK), i % (rows // BLOCK)
        found = sums[of, 0, pl.ds(at, 1), :]
        for owner in range(1, chan_count):
            found = found + sums[of, owner, pl.ds(at, 1), :]
        found = lax.rsqrt(found / (chan_count * width) + EPSILON)
        scale[at_rows(i), :] = jnp.broadcast_to(found, (BLOCK, LANES)).T

    taps_mate().wait_send()

    @pl.when(x == 0)
    def _():
        taps_across(0).wait_send()
        taps_across(1).wait_send()

    def edge_copy(g):
        return remote(
            edge_out.at[g], edge.at[g], edge_send.at[0], edge_recv.at[g], across
        )

    def before_copy(g):
        return remote(
            signal.at[g], before.at[g], before_send.at[0], before_recv.at[g], across
        )

    def swap_copy(g):
        return remote(
            ready.at[g], full.at[z, g, core], swap_send.at[0], swap_recv.at[g], mate
        )

    line = Line(
        lambda owner, g, of: full.at[owner, g, of],
        chan_count,
        line_send,
        line_recv,
        lambda to: (y, s, to),
    )

    def projected(g, b, at):
        return (partial[g, at, b * LANES : (b + 1) * LANES] * scale[at, :]).astype(jnp.bfloat16)

    def featurize(g):
        @pl.when(x == 0)
        def _():
            for b in range(branches):
                edge_out[g, b] = projected(g, b, pl.ds(length - rim, rim))
                extended[b, 0:rim, :] = jnp.zeros((rim, LANES), jnp.float32)
            edge_copy(g).start()

        @blocks(length)
        def _(i):
            for b in range(branches):
                extended[b, pl.ds(pl.multiple_of(rim + i * BLOCK, rim), BLOCK), :] = projected(
                    g, b, at_rows(i)
                ).astype(jnp.float32)

        @pl.when(x == 1)
        def _():
            edge_copy(g).wait_recv()
            for b in range(branches):
                extended[b, 0:rim, :] = edge[g, b].astype(jnp.float32)

        chosen = lanes_of(core * share, g)
        coefficient = [
            [short[tap, b : b + 1, chosen] for b in range(branches)] for tap in range(SHORT)
        ]

        @blocks(length)
        def _(i):
            found = []
            for b in range(branches):
                value = jnp.zeros((BLOCK, LANES), jnp.float32)
                for tap in range(SHORT):
                    value = value + coefficient[tap][b] * extended[
                        b, pl.ds(rim - tap + i * BLOCK, BLOCK), :
                    ]
                found.append(value.astype(jnp.bfloat16))
            query[at_rows(i), :] = found[0]
            signal[g, at_rows(i), :] = (
                found[1].astype(jnp.float32) * found[2].astype(jnp.float32)
            ).astype(jnp.bfloat16)

    def convolve(g):
        joint = (x == 1) & (g > 0)

        @pl.when(jnp.logical_not(joint))
        def _():
            spectrum(0, lambda: signal[g])

        def product(i, which, first):
            low, high = at_rows(i), rows_at(i, BLOCK, length)
            cos, sin = freq[which, low, :], freq[which, high, :]
            real = spectra[g, first, low, :].astype(jnp.float32)
            imag = spectra[g, first + 1, low, :].astype(jnp.float32)
            return cos * real + sin * imag, sin * real - cos * imag

        @pl.when(x == 0)
        def _():
            @blocks(length)
            def _(i):
                real, imag = product(i, 0, 0)
                mixed[at_rows(i), :] = real.astype(jnp.bfloat16)
                mixed[rows_at(i, BLOCK, length), :] = imag.astype(jnp.bfloat16)

        @pl.when(x == 1)
        def _():
            before_copy(g).wait_recv()

            @pl.when(g == 0)
            def _():
                spectrum(1, lambda: before[g])

            @pl.when(g > 0)
            def _():
                spectrum_pair(lambda: [signal[g], before[g]])

            @blocks(length)
            def _(i):
                real, imag = product(i, 0, 0)
                more_real, more_imag = product(i, 1, 2)
                mixed[at_rows(i), :] = (real + more_real).astype(jnp.bfloat16)
                mixed[rows_at(i, BLOCK, length), :] = (imag + more_imag).astype(jnp.bfloat16)

        @pl.loop(0, length // SPAN)
        def _(i):
            low, high = rows_at(i, SPAN), rows_at(i, SPAN, length)
            freq[0, low, :] = jnp.dot(
                table[low, :], mixed[:length, :], preferred_element_type=jnp.float32
            ) + jnp.dot(table[high, :], mixed[length:, :], preferred_element_type=jnp.float32)

        direct = skip[:, lanes_of(core * share, g)]

        def gated(at):
            longer = freq[0, at, :] + direct * signal[g, at, :].astype(jnp.float32)
            longer = longer.astype(jnp.bfloat16).astype(jnp.float32)
            return (query[at, :].astype(jnp.float32) * longer).astype(jnp.bfloat16)

        @blocks(rows)
        def _(i):
            full[z, g, core, at_rows(i), :] = gated(
                pl.ds(pl.multiple_of(core * rows + i * BLOCK, BLOCK), BLOCK)
            )
            ready[g, at_rows(i), :] = gated(
                pl.ds(pl.multiple_of((1 - core) * rows + i * BLOCK, BLOCK), BLOCK)
            )

    def load_out():
        for owner in range(chan_count):
            pltpu.make_async_copy(
                out_weight.at[pl.ds(owner * length, length)], stream.at[owner], local_sem.at[1]
            ).start()

    def accumulate(owner, g):
        @pl.loop(0, total.shape[1] // (2 * LANES))
        def _(i):
            cols = rows_at(i, 2 * LANES)
            block = jnp.concatenate([full[owner, g, 0], full[owner, g, 1]], axis=1)
            kernel = jnp.concatenate(
                [stream[owner, lanes_of(of * share, g), cols] for of in range(2)], axis=0
            )
            total[:, cols] += jnp.dot(block, kernel, preferred_element_type=jnp.float32)

    def begin(g):
        swap_copy(g).start()
        for way in range(2):

            @pl.when(line.sends(way, 0))
            def _():
                line.copy(way, 0, (g, core)).start()

    def begin_other(g):
        other = full.at[z, g, 1 - core]
        remote(other, other, swap_send.at[0], swap_recv.at[g], mate).wait_recv()
        for way in range(2):

            @pl.when(line.sends(way, 0))
            def _():
                line.copy(way, 0, (g, 1 - core)).start()

    def settle():
        other = weight.at[:, s]
        remote(other, other, mate_send.at[1], mate_recv.at[1], mate).wait_send()
        for copy in sum_copies:
            copy.wait_send()

        @pl.when(x == 1)
        def _():
            for origin in range(2):
                taps_beside(origin, y).wait_send()

        for at in range(2):
            view = weight_half(s, y)
            remote(view, view, x_send.at[at], x_recv.at[0, 0, 0], across).wait_send()
            view = weight_half((1 - x) * 2 + at, y)
            remote(view, view, y_send.at[at], y_recv.at[at, 0], beside).wait_send()

        @pl.when(x == 0)
        def _():
            remote(edge_out, edge, edge_send.at[0], edge_recv.at[0], across).wait_send()
            remote(signal, before, before_send.at[0], before_recv.at[0], across).wait_send()

    def settle_tokens():
        mate_tokens().wait_send()
        for way in range(2):
            for step in range(steps):

                @pl.when(token_line.receives(way, step))
                def _():
                    mate_half(way, step, core).wait_send()

                @pl.when(token_line.sends(way, step))
                def _():
                    token_line.drain(way, step, (0,), lambda owner: own_half(owner, core))

    def way_of(k):
        return jnp.where(z < chan_count // 2, 1 - k, k)

    def late_forwards(g, at, inner, outer):
        for here, pieces in ((jnp.logical_not(at_end), inner), (at_end, outer)):

            @pl.when((g == at) & here)
            def _():
                for group, c in pieces:
                    forward(group, c)

    def pass_on(way, step, at):
        @pl.when(
            (at >= 0) & (at < groups) & line.receives(way, step) & line.sends(way, step + 1)
        )
        def _():
            for of in (core, 1 - core):
                line.arrived(way, step, (at, of))
                line.copy(way, step + 1, (at, of)).start()

    for copy in small_loads[1:]:
        copy.wait()
    near, away = way_of(0), way_of(1)

    @pl.loop(0, groups)
    def _(g):
        @pl.when(g == 3)
        def _():
            pass_on(away, 0, 1)

        @pl.when((g >= 2) | ((g == 1) & jnp.logical_not(at_end)))
        def _():
            await_beside(g)

        @pl.when(g == 3)
        def _():
            pass_on(near, 0, 2)

        @pl.loop(0, chan_count)
        def _(owner):
            @pl.when(jnp.logical_not(projects_early(g, owner)))
            def _():
                project(g, owner)

        @pl.when(g == groups - 1)
        def _():
            settle_tokens()
            load_out()

        featurize(g)

        @pl.when(x == 0)
        def _():
            before_copy(g).start()

            for at, inner, outer in (
                (0, [(groups - 2, 3), (groups - 1, 0)], [(groups - 1, 2)]),
                (1, [(groups - 1, 1), (groups - 1, 2)], [(groups - 1, 3)]),
                (2, [(groups - 1, 3)], []),
            ):

                @pl.when((g == at) & jnp.logical_not(at_end))
                def _():
                    for group, c in inner:
                        send_weights(group, [c])

                @pl.when((g == at) & at_end)
                def _():
                    for group, c in outer:
                        send_weights(group, [c])

        late_forwards(g, 1, [(groups - 2, 3), (groups - 1, 0)], [(groups - 1, 0), (groups - 1, 1)])
        late_forwards(g, 2, [(groups - 1, 1), (groups - 1, 2)], [(groups - 1, 3)])

        @pl.when((g == 1) | (g == 2))
        def _():
            pass_on(near, 0, g - 1)

        @pl.when(g == 2)
        def _():
            pass_on(away, 0, 0)

        late_forwards(g, 0, [(groups - 2, 2)], [(groups - 2, 2), (groups - 2, 3)])
        convolve(g)
        begin(g)
        late_forwards(g, 1, [], [(groups - 1, 2)])
        late_forwards(g, 2, [(groups - 1, 3)], [])
        begin_other(g)

        @pl.when(g == 2)
        def _():
            pass_on(near, 1, 0)

    pltpu.make_async_copy(stream, stream, local_sem.at[1]).wait()

    @pl.loop(0, groups + steps - 1)
    def _(n):
        for at, pieces in (
            (0, [(near, 1, 1), (away, 0, 2)]),
            (1, [(near, 0, 3), (near, 1, 2), (away, 0, 3)]),
            (3, [(near, 1, 3)]),
        ):

            @pl.when(n == at)
            def _():
                for way, step, group in pieces:
                    pass_on(way, step, group)

        @pl.when(n == 2)
        def _():
            settle()

        @pl.when(n < groups)
        def _():
            accumulate(z, n)

        @pl.loop(0, 2)
        def _(way):
            for step in range(steps):
                at = n - jnp.where(at_end, step, 0)

                @pl.when((at >= 0) & (at < groups) & line.receives(way, step))
                def _():
                    @pl.when(jnp.logical_not(line.sends(way, step + 1)))
                    def _():
                        for of in range(2):
                            line.arrived(way, step, (at, of))

                    accumulate(line.source(way, step), at)

    @blocks(rows)
    def _(i):
        result[at_rows(i), :] = total[at_rows(i), :].astype(jnp.bfloat16)

    remote(ready, ready, swap_send.at[0], swap_recv.at[0], mate).wait_send()
    for way in range(2):
        for step in range(steps):

            @pl.when(line.sends(way, step))
            def _():
                line.drain(way, step, (0, 0), lambda owner: full.at[owner])


def chip_body(tokens, norm_gain, proj_weight, short_filter, long_filter, skip_gain, out_weight):
    chan_count = lax.axis_size("chan")
    rows, width = tokens.shape
    depth, branches, local_chan = proj_weight.shape
    length, share = 2 * rows, local_chan // 2
    groups = share // LANES
    steps = chan_count - 1
    dma = pltpu.SemaphoreType.DMA
    f32, bf16 = jnp.float32, jnp.bfloat16
    vmem = pl.BlockSpec(memory_space=pltpu.VMEM)
    return pl.pallas_call(
        functools.partial(block_kernel, chan_count),
        out_shape=jax.ShapeDtypeStruct((rows, width), bf16),
        in_specs=[HBM] * 7,
        out_specs=vmem,
        scratch_shapes=[
            pltpu.VMEM((1, width), f32),
            pltpu.VMEM(short_filter.shape, f32),
            pltpu.VMEM((1, local_chan), f32),
            pltpu.VMEM((chan_count, length, width), bf16),
            pltpu.VMEM((groups, 4, depth, branches * LANES), bf16),
            pltpu.VMEM((2, chan_count, 8, LANES), f32),
            pltpu.VMEM((length, LANES), f32),
            pltpu.VMEM((groups, length, branches * LANES), f32),
            pltpu.VMEM((2 * length, length), bf16),
            pltpu.VMEM((groups, 2 * length, LANES), bf16),
            pltpu.VMEM((groups, 4, length, LANES), bf16),
            pltpu.VMEM((2, 2 * length, LANES), f32),
            pltpu.VMEM((2 * length, LANES), bf16),
            pltpu.VMEM((groups, branches, 16, LANES), bf16),
            pltpu.VMEM((groups, branches, 16, LANES), bf16),
            pltpu.VMEM((branches, length + 16, LANES), f32),
            pltpu.VMEM((length, LANES), bf16),
            pltpu.VMEM((groups, length, LANES), bf16),
            pltpu.VMEM((groups, length, LANES), bf16),
            pltpu.VMEM((groups, rows, LANES), bf16),
            pltpu.VMEM((chan_count, groups, 2, rows, LANES), bf16),
            pltpu.VMEM((rows, width), f32),
            dma((10,)),
            dma((3 + 2 * steps,)),
            dma((3 + 2 * steps,)),
            dma((2, steps)),
            dma((2, steps, TOKEN_CHUNKS)),
            dma((2 * chan_count - 1,)),
            dma((2, chan_count)),
            dma((2,)),
            dma((2, groups, WEIGHT_CHUNKS)),
            dma((2,)),
            dma((2, groups)),
            dma((4,)),
            dma((4,)),
            dma((1,)),
            dma((groups,)),
            dma((1,)),
            dma((groups,)),
            dma((1,)),
            dma((groups,)),
            dma((2, steps)),
            dma((2, steps, groups, 2)),
        ],
        compiler_params=pltpu.CompilerParams(
            collective_id=0, has_side_effects=True, vmem_limit_bytes=52 * 1024 * 1024
        ),
        name="block",
    )(
        tokens,
        pltpu.with_memory_space_constraint(norm_gain[None, :], pltpu.HBM),
        proj_weight.transpose(1, 0, 2),
        pltpu.with_memory_space_constraint(short_filter, pltpu.HBM),
        long_filter,
        pltpu.with_memory_space_constraint(skip_gain[None, :], pltpu.HBM),
        out_weight,
    )


def select_body(mesh):
    if (mesh.shape["groups"], mesh.shape["seq"], mesh.shape["chan"]) == (2, 4, 4):
        return chip_body
    return body


def solution(mesh):
    placed = (
        P(("groups", "seq"), "chan"),
        P(),
        P("seq", None, "chan"),
        P(None, None, "chan"),
        P("chan", "seq"),
        P("chan"),
        P(None, "chan"),
    )
    return jax.shard_map(
        select_body(mesh), mesh=mesh, in_specs=placed, out_specs=P(("groups", "seq"), "chan"), check_vma=False
    )
```

```python
import functools
import math

import jax
import jax.numpy as jnp
import numpy as np
from jax import lax
from jax.experimental import pallas as pl
from jax.experimental.pallas import tpu as pltpu
from jax.sharding import PartitionSpec as P

SHORT = 3


EPSILON = 1e-06
HIGHEST = lax.Precision.HIGHEST


def from_behind(value, axis, steps):
    count = lax.axis_size(axis)
    initial, last = (max(0, -steps), min(count, count - steps))
    return lax.ppermute(value, axis, [(source, source + steps) for source in range(initial, last)])


def angle_table(row_count, col_count, period, sign):
    row_index = lax.iota(jnp.int32, row_count)[:, None]
    col_index = lax.iota(jnp.int32, col_count)[None, :]
    angles = (row_index * col_index % period).astype(jnp.float32) * (sign * 2.0 * math.pi / period)
    return (jnp.cos(angles), jnp.sin(angles))


def forward_spectrum(signal_rows, first, second):
    channels = signal_rows.shape[0]
    grid_rows = signal_rows.reshape(channels, first, second)
    cos_first, sin_first = angle_table(first, first, first, -1.0)
    part_re = jnp.einsum("cab,ak->ckb", grid_rows, cos_first, precision=HIGHEST)
    part_im = jnp.einsum("cab,ak->ckb", grid_rows, sin_first, precision=HIGHEST)
    twist_cos, twist_sin = angle_table(first, second, first * second, -1.0)
    part_re, part_im = (
        part_re * twist_cos - part_im * twist_sin,
        part_re * twist_sin + part_im * twist_cos,
    )
    cos_second, sin_second = angle_table(second, second, second, -1.0)
    spectrum_real = jnp.einsum("ckb,bm->ckm", part_re, cos_second, precision=HIGHEST) - jnp.einsum(
        "ckb,bm->ckm", part_im, sin_second, precision=HIGHEST
    )
    spec_im = jnp.einsum("ckb,bm->ckm", part_re, sin_second, precision=HIGHEST) + jnp.einsum(
        "ckb,bm->ckm", part_im, cos_second, precision=HIGHEST
    )
    return (spectrum_real, spec_im)


def inverse_spectrum(spectrum_real, spec_im, first, second):
    channels = spectrum_real.shape[0]
    cos_second, sin_second = angle_table(second, second, second, 1.0)
    part_re = jnp.einsum("ckm,bm->ckb", spectrum_real, cos_second, precision=HIGHEST) - jnp.einsum(
        "ckm,bm->ckb", spec_im, sin_second, precision=HIGHEST
    )
    part_im = jnp.einsum("ckm,bm->ckb", spectrum_real, sin_second, precision=HIGHEST) + jnp.einsum(
        "ckm,bm->ckb", spec_im, cos_second, precision=HIGHEST
    )
    twist_cos, twist_sin = angle_table(first, second, first * second, 1.0)
    part_re, part_im = (
        part_re * twist_cos - part_im * twist_sin,
        part_re * twist_sin + part_im * twist_cos,
    )
    cos_first, sin_first = angle_table(first, first, first, 1.0)
    result = jnp.einsum("ckb,ak->cab", part_re, cos_first, precision=HIGHEST) - jnp.einsum(
        "ckb,ak->cab", part_im, sin_first, precision=HIGHEST
    )
    return result.reshape(channels, first * second) / (first * second)


def spectral_conv(signal_rows, filter_rows):
    channels, length = signal_rows.shape
    padded_len = 2 * length
    log_len = padded_len.bit_length() - 1
    first = 1 << log_len // 2
    second = padded_len // first
    zeros_tail = jnp.zeros((channels, length), jnp.float32)
    sig_re, sig_im = forward_spectrum(
        jnp.concatenate([signal_rows, zeros_tail], axis=1), first, second
    )
    tap_re, tap_im = forward_spectrum(
        jnp.concatenate([filter_rows, zeros_tail], axis=1), first, second
    )
    prod_re = sig_re * tap_re - sig_im * tap_im
    prod_im = sig_re * tap_im + sig_im * tap_re
    return inverse_spectrum(prod_re, prod_im, first, second)[:, :length]


def short_filter_output(projected, rim_cells, kernel_coefficients):
    count = kernel_coefficients.shape[0]
    steps_len = projected.shape[2]
    extended = jnp.concatenate([rim_cells, projected], axis=2).astype(jnp.float32)
    total = jnp.zeros(projected.shape, jnp.float32)
    for tap in range(count):
        total = (
            total
            + kernel_coefficients[tap][:, :, None]
            * extended[:, :, count - 1 - tap : count - 1 - tap + steps_len]
        )
    return total.astype(jnp.bfloat16)


def hyena_mixer(keys_rows, values_rows, long_taps, skip_part):
    middle = keys_rows.astype(jnp.float32) * values_rows.astype(jnp.float32)
    return (spectral_conv(middle, long_taps) + skip_part[:, None] * middle).astype(jnp.bfloat16)


def body(tokens, norm_gain, proj_weight, short_filter, long_filter, skip_gain, out_weight):
    seq_count = lax.axis_size("seq")
    local_rows = tokens.shape[0]
    local_chan = proj_weight.shape[2]
    subset = local_chan // seq_count
    length = local_rows * seq_count
    offset = lax.axis_index("seq") * subset
    whole = lax.all_gather(tokens, "chan", axis=1, tiled=True)
    wide = whole.astype(jnp.float32)
    rescaled_signal = (
        wide * lax.rsqrt(jnp.mean(wide * wide, axis=1, keepdims=True) + EPSILON) * norm_gain
    ).astype(jnp.bfloat16)
    projected = lax.dot_general(
        lax.all_gather(proj_weight, "seq", axis=0, tiled=True),
        rescaled_signal,
        (((0,), (1,)), ((), ())),
        preferred_element_type=jnp.float32,
    ).astype(jnp.bfloat16)
    taps_grid = long_filter.reshape(1, seq_count, subset, local_rows)
    long_taps = lax.all_to_all(taps_grid, "seq", split_axis=1, concat_axis=3, tiled=True).reshape(
        subset, length
    )
    skip_part = lax.dynamic_slice_in_dim(skip_gain, offset, subset, 0)
    rim_cells = from_behind(projected[:, :, local_rows - (SHORT - 1) :], "seq", 1)
    featured = short_filter_output(projected, rim_cells, short_filter)
    pair_grid = featured[1:].reshape(2, seq_count, subset, local_rows)
    moved = lax.all_to_all(pair_grid, "seq", split_axis=1, concat_axis=3, tiled=True).reshape(
        2, subset, length
    )
    result = hyena_mixer(moved[0], moved[1], long_taps, skip_part)
    returned = lax.all_to_all(
        result.reshape(1, subset, length), "seq", split_axis=2, concat_axis=0, tiled=True
    )
    returned = returned.reshape(local_chan, local_rows)
    gated = (featured[0].astype(jnp.float32) * returned.astype(jnp.float32)).astype(jnp.bfloat16)
    full_mix = lax.all_gather(gated, "chan", axis=0, tiled=True)
    update = lax.dot_general(
        full_mix, out_weight, (((0,), (0,)), ((), ())), preferred_element_type=jnp.float32
    )
    return (tokens.astype(jnp.float32) + update).astype(jnp.bfloat16)

LANES = 128
BLOCK = 128
SPAN = 512
TOKEN_CHUNKS = 8
WEIGHT_CHUNKS = 4
HBM = pl.BlockSpec(memory_space=pltpu.HBM)


def remote(src, dst, send_sem, recv_sem, where):
    return pltpu.make_async_remote_copy(
        src_ref=src,
        dst_ref=dst,
        send_sem=send_sem,
        recv_sem=recv_sem,
        device_id=where,
        device_id_type=pl.DeviceIdType.MESH,
    )


class Line:
    def __init__(self, view, count, send_sem, recv_sem, place):
        self.view, self.count, self.place = view, count, place
        self.send_sem, self.recv_sem = send_sem, recv_sem
        self.me = lax.axis_index("chan")

    def move(self, way, step, piece, block, target):
        recv = self.recv_sem.at[(way, step) + piece]
        return remote(block, block, self.send_sem.at[way, step], recv, self.place(target))

    def drain(self, way, step, first, block):
        self.move(way, step, first, block(self.source(way, step - 1)), self.me).wait_send()

    def source(self, way, step):
        return jnp.clip(self.me - (step + 1) * (1 - 2 * way), 0, self.count - 1)

    def copy(self, way, step, piece):
        owner = self.source(way, step - 1)
        target = self.source(way, -2)
        return self.move(way, step, piece, self.view(owner, *piece), target)

    def inside(self, way, by):
        place = self.me + by * (1 - 2 * way)
        return (place >= 0) & (place < self.count)

    def sends(self, way, step):
        return self.inside(way, -step) & self.inside(way, 1)

    def receives(self, way, step):
        return self.inside(way, -1 - step)

    def arrived(self, way, step, piece):
        owner = self.source(way, step)
        self.move(way, step, piece, self.view(owner, *piece), self.me).wait_recv()
        return owner


def block_kernel(
    chan_count,
    tokens,
    gain_hbm,
    weights,
    short_hbm,
    long_taps,
    skip_hbm,
    out_weight,
    result,
    gain,
    short,
    skip,
    stream,
    weight,
    sums,
    scale,
    partial,
    table,
    taps,
    spectra,
    freq,
    mixed,
    edge_out,
    edge,
    extended,
    query,
    signal,
    before,
    ready,
    full,
    total,
    local_sem,
    mate_send,
    mate_recv,
    token_send,
    token_recv,
    sums_send,
    sums_recv,
    x_send,
    x_recv,
    y_send,
    y_recv,
    tap_send,
    tap_recv,
    edge_send,
    edge_recv,
    before_send,
    before_recv,
    swap_send,
    swap_recv,
    line_send,
    line_recv,
):
    y, s, z = (lax.axis_index(name) for name in ("groups", "seq", "chan"))
    x, core = s // 2, s % 2
    mate_s = s + 1 - 2 * core
    mate = (y, mate_s, z)
    across = (y, (1 - x) * 2 + core, z)
    aslant = (y, (1 - x) * 2 + 1 - core, z)
    beside = (1 - y, s, z)
    rows, width = tokens.shape
    length = 2 * rows
    branches, depth = weights.shape[0], weights.shape[1]
    half = depth // 2
    share = weights.shape[2] // 2
    groups = share // LANES
    rim = edge.shape[2]
    steps = chan_count - 1
    token_rows = rows // TOKEN_CHUNKS
    weight_rows = half // WEIGHT_CHUNKS

    column_peers = [mate] + [
        (y, 2 * x + of, lax.rem(z + by, chan_count))
        for by in range(1, chan_count)
        for of in (core, 1 - core)
    ]
    peers = column_peers + [across, aslant, beside]

    def rows_at(i, count, base=0):
        return pl.ds(pl.multiple_of(base + i * count, count), count)

    def at_rows(i):
        return rows_at(i, BLOCK)

    def blocks(count):
        return pl.loop(0, count // BLOCK)

    def lanes_of(base, g):
        return pl.ds(pl.multiple_of(base + g * LANES, LANES), LANES)

    tap_stage = [(0, 0), (0, length), (1, 0), (1, length)]
    tap_loads = [
        pltpu.make_async_copy(
            long_taps.at[:, pl.ds(j * LANES, LANES)],
            freq.at[which, pl.ds(start, length)],
            local_sem.at[4 + j],
        )
        for j, (which, start) in enumerate(tap_stage)
    ]
    token_load = pltpu.make_async_copy(tokens, result, local_sem.at[0])
    token_load.start()
    small_loads = [
        pltpu.make_async_copy(src, dst, local_sem.at[at])
        for src, dst, at in (
            (gain_hbm.at[:, pl.ds(pl.multiple_of(z * width, width), width)], gain, 3),
            (short_hbm, short, 8),
            (skip_hbm, skip, 9),
        )
    ]
    for copy in small_loads:
        copy.start()
    barrier = pltpu.get_barrier_semaphore()
    for peer in peers:
        pl.semaphore_signal(barrier, inc=1, device_id=peer, device_id_type=pl.DeviceIdType.MESH)
    for copy in tap_loads:
        copy.start()
    for g in range(groups):
        for b in range(branches):
            pltpu.make_async_copy(
                weights.at[b, :, lanes_of(core * share, g)],
                weight.at[g, s, :, pl.ds(b * LANES, LANES)],
                local_sem.at[2],
            ).start()

    sums[core, z] = jnp.zeros(sums.shape[2:], jnp.float32)
    small_loads[0].wait()
    own_gain = gain[...]
    token_load.wait()

    @blocks(rows)
    def _(i):
        raw = result[at_rows(i), :].astype(jnp.float32)
        total[at_rows(i), :] = raw
        stream[z, pl.ds(pl.multiple_of(core * rows + i * BLOCK, BLOCK), BLOCK), :] = (
            raw * own_gain
        ).astype(jnp.bfloat16)
        square = raw * raw
        found = square[:, :LANES]
        for part in range(1, width // LANES):
            found = found + square[:, part * LANES : (part + 1) * LANES]
        sums[core, z, pl.ds(i, 1), :] = jnp.sum(found.T, axis=0, keepdims=True)

    pl.semaphore_wait(barrier, len(peers))

    def token_view(owner, chunk):
        return stream.at[owner, rows_at(chunk, token_rows, core * rows), :]

    token_line = Line(
        token_view, chan_count, token_send, token_recv, lambda to: (y, s, to)
    )
    for chunk in range(TOKEN_CHUNKS):
        for way in range(2):

            @pl.when(token_line.sends(way, 0))
            def _():
                token_line.copy(way, 0, (chunk,)).start()

    def own_half(owner, of):
        return stream.at[owner, pl.ds(pl.multiple_of(of * rows, rows), rows), :]

    def mate_tokens():
        return remote(
            own_half(z, core), own_half(z, core), mate_send.at[0], mate_recv.at[0], mate
        )

    mate_tokens().start()
    sum_copies = [
        remote(
            sums.at[core, z], sums.at[core, z], sums_send.at[at], sums_recv.at[core, z], peer
        )
        for at, peer in enumerate(column_peers)
    ]
    for copy in sum_copies:
        copy.start()
    for g in range(groups):
        for b in range(branches):
            remote(
                weights.at[b, :, lanes_of((1 - core) * share, g)],
                weight.at[g, s, :, pl.ds(b * LANES, LANES)],
                mate_send.at[1],
                mate_recv.at[1],
                mate,
            ).start()

    for j, (which, start) in enumerate(tap_stage):
        tap_loads[j].wait()

        @pl.loop(0, groups)
        def _(g):
            mine = freq[which, rows_at(core * groups + g, BLOCK, start), :]
            taps[g, pl.ds(pl.multiple_of(s * rows + j * LANES, LANES), LANES), :] = mine.T.astype(
                jnp.bfloat16
            )
            other = freq[which, rows_at((1 - core) * groups + g, BLOCK, start), :]
            ready[g, j * LANES : (j + 1) * LANES, :] = other.T.astype(jnp.bfloat16)

    def tap_part(owner, part):
        return taps.at[
            :, pl.ds(pl.multiple_of(owner * rows + part * (rows // 2), rows // 2), rows // 2), :
        ]

    def taps_across(to):
        src = tap_part(s, y) if to == 0 else ready.at[
            :, pl.ds(pl.multiple_of(y * (rows // 2), rows // 2), rows // 2), :
        ]
        return remote(
            src,
            tap_part(s, y),
            tap_send.at[to],
            tap_recv.at[core],
            across if to == 0 else aslant,
        )

    def taps_beside(origin, part):
        view = tap_part(origin, part)
        return remote(view, view, tap_send.at[2 + origin], tap_recv.at[2 + origin], beside)

    def taps_mate():
        return remote(
            ready,
            taps.at[:, pl.ds(pl.multiple_of(s * rows, rows), rows), :],
            mate_send.at[2],
            mate_recv.at[2],
            mate,
        )

    @pl.when(x == 0)
    def _():
        taps_across(0).start()
        taps_across(1).start()

        @pl.loop(0, groups)
        def _(g):
            taps[g, length:, :] = jnp.zeros((length, LANES), jnp.bfloat16)

    taps_mate().start()

    def weight_view(owner, part, g, c):
        return weight.at[g, owner, rows_at(c, weight_rows, part * half), :]

    def weight_half(owner, part):
        return weight.at[:, owner, pl.ds(pl.multiple_of(part * half, half), half), :]

    def send_weights(g, chunks=range(WEIGHT_CHUNKS)):
        for c in chunks:
            for to in range(2):
                side = core if to == 0 else 1 - core
                view = weight_view(s, y, g, c)
                for b in range(branches):
                    remote(
                        weights.at[
                            b,
                            rows_at(c, weight_rows, y * half),
                            pl.ds(pl.multiple_of(side * share + g * LANES, LANES), LANES),
                        ],
                        view.at[:, pl.ds(b * LANES, LANES)],
                        x_send.at[to],
                        x_recv.at[core, g, c],
                        across if to == 0 else aslant,
                    ).start()

    for g in range(groups - 2):
        send_weights(g)
    send_weights(groups - 2, range(3))

    at_end = (z == 0) | (z == chan_count - 1)

    @pl.when((x == 1) | at_end)
    def _():
        send_weights(groups - 2, [3])
        send_weights(groups - 1, [0, 1])

    @pl.when(x == 1)
    def _():
        send_weights(groups - 1, [2, 3])

    def beside_copy(origin, part, g, c):
        view = weight_view((1 - x) * 2 + origin, part, g, c)
        return remote(view, view, y_send.at[origin], y_recv.at[origin, g], beside)

    def forward(g, c):
        for origin in range(2):
            view = weight_view((1 - x) * 2 + origin, y, g, c)
            remote(
                view, view, x_send.at[origin], x_recv.at[origin, g, c], beside
            ).wait_recv()
            beside_copy(origin, y, g, c).start()

    def await_beside(g):
        for origin in range(2):
            view = weight.at[
                g, (1 - x) * 2 + origin, pl.ds(pl.multiple_of((1 - y) * half, half), half), :
            ]
            remote(view, view, y_send.at[origin], y_recv.at[origin, g], beside).wait_recv()

    @blocks(length)
    def _(i):
        row = lax.broadcasted_iota(jnp.int32, (BLOCK, LANES), 0) + i * BLOCK
        lane = lax.broadcasted_iota(jnp.int32, (BLOCK, LANES), 1)
        unit = math.pi / (4 * length)
        odd = 2 * row + 1
        small = odd.astype(jnp.float32) * unit
        extended[0, at_rows(i), :] = jnp.cos(small)
        extended[1, at_rows(i), :] = jnp.sin(small)
        period = 8 * length
        angle = (odd * (2 * lane + 1) % period).astype(jnp.float32) * unit
        cos, sin = jnp.cos(angle), jnp.sin(angle)
        stride = (odd * (2 * LANES) % period).astype(jnp.float32) * unit
        step_cos, step_sin = jnp.cos(stride), jnp.sin(stride)
        for a in range(length // LANES):
            table[at_rows(i), a * LANES : (a + 1) * LANES] = cos.astype(jnp.bfloat16)
            table[rows_at(i, BLOCK, length), a * LANES : (a + 1) * LANES] = sin.astype(
                jnp.bfloat16
            )
            cos, sin = cos * step_cos - sin * step_sin, sin * step_cos + cos * step_sin

    for g in range(groups):

        @blocks(length)
        def _(i):
            partial[g, at_rows(i), :] = jnp.zeros((BLOCK, branches * LANES), jnp.float32)

    def spectrum(which, column):
        @pl.loop(0, 2 * length // SPAN)
        def _(i):
            at = rows_at(i, SPAN)
            freq[which, at, :] = jnp.dot(
                table[at, :], column(), preferred_element_type=jnp.float32
            )

    def spectrum_pair(columns):
        @pl.loop(0, 2 * length // SPAN)
        def _(i):
            at = rows_at(i, SPAN)
            found = jnp.dot(
                table[at, :],
                jnp.concatenate(columns(), axis=1),
                preferred_element_type=jnp.float32,
            )
            freq[0, at, :] = found[:, :LANES]
            freq[1, at, :] = found[:, LANES:]

    def tap_spectra(g):
        spectrum_pair(lambda: [taps[g, :length, :], taps[g, length:, :]])

        @blocks(length)
        def _(i):
            low, high = at_rows(i), rows_at(i, BLOCK, length)
            cos, sin = extended[0, low, :], extended[1, low, :]

            def turned(which):
                real, imag = freq[which, low, :], -freq[which, high, :]
                return (cos * real - sin * imag) / length, (cos * imag + sin * real) / length

            real, imag = turned(0)
            late_real, late_imag = turned(1)
            place = lax.broadcasted_iota(jnp.int32, (BLOCK, LANES), 0)
            sign = (1 - 2 * (place % 2)).astype(jnp.float32)
            spectra[g, 0, low, :] = real.astype(jnp.bfloat16)
            spectra[g, 1, low, :] = imag.astype(jnp.bfloat16)
            spectra[g, 2, low, :] = (late_real - sign * imag).astype(jnp.bfloat16)
            spectra[g, 3, low, :] = (late_imag + sign * real).astype(jnp.bfloat16)

    def project(g, owner):
        @pl.loop(0, length // SPAN)
        def _(i):
            at = rows_at(i, SPAN)
            partial[g, at, :] += jnp.dot(
                stream[owner, at, :], weight[g, owner], preferred_element_type=jnp.float32
            )

    def projects_early(g, owner):
        far = jnp.abs(z - owner)
        own = owner // 2 == x
        return (
            (own & ((far <= 1) | ((far == 2) & (at_end | (g == 0)))))
            | (jnp.logical_not(own) & (far <= 2) & ((g == 0) | ((g == 1) & at_end)))
        )

    def to_mate(way, step, chunk):
        block = token_view(token_line.source(way, step), chunk)
        index = 3 + way * steps + step
        return remote(block, block, mate_send.at[index], mate_recv.at[index], mate)

    def mate_half(way, step, of):
        block = own_half(token_line.source(way, step), of)
        index = 3 + way * steps + step
        return remote(block, block, mate_send.at[index], mate_recv.at[index], mate)

    def await_mate(step):
        for way in range(2):

            @pl.when(token_line.receives(way, step))
            def _():
                mate_half(way, step, 1 - core).wait_recv()

    @pl.loop(0, steps * TOKEN_CHUNKS)
    def _(tick):
        step, chunk = tick // TOKEN_CHUNKS, tick % TOKEN_CHUNKS
        for way in range(2):

            @pl.when(token_line.receives(way, step))
            def _():
                token_line.arrived(way, step, (chunk,))
                to_mate(way, step, chunk).start()

            @pl.when(
                (step + 1 < steps)
                & token_line.receives(way, step)
                & token_line.sends(way, step + 1)
            )
            def _():
                token_line.copy(way, step + 1, (chunk,)).start()

        @pl.when((tick == TOKEN_CHUNKS // 2) & (x == 1))
        def _():
            for origin in range(2):
                view = tap_part(origin, y)
                remote(
                    view, view, tap_send.at[origin], tap_recv.at[origin], beside
                ).wait_recv()
                taps_beside(origin, y).start()

        @pl.when((tick % 2 == 1) & (tick >= 3) & (tick < 7 + 4 * WEIGHT_CHUNKS))
        def _():
            at = (tick - 3) // 2
            forward(at // WEIGHT_CHUNKS, at % WEIGHT_CHUNKS)

        @pl.when(tick == TOKEN_CHUNKS)
        def _():
            mate_half_own = own_half(z, 1 - core)
            remote(
                mate_half_own, mate_half_own, mate_send.at[0], mate_recv.at[0], mate
            ).wait_recv()
            await_mate(0)
            pltpu.make_async_copy(
                weight.at[:, s], weight.at[:, s], local_sem.at[2]
            ).wait()
            other = weight.at[:, mate_s]
            remote(other, other, mate_send.at[1], mate_recv.at[1], mate).wait_recv()
            other = taps.at[:, pl.ds(pl.multiple_of(mate_s * rows, rows), rows), :]
            remote(other, other, mate_send.at[2], mate_recv.at[2], mate).wait_recv()

            @pl.when(x == 1)
            def _():
                for origin in range(2):
                    taps_beside(origin, 1 - y).wait_recv()

        @pl.when((step == 1) & (chunk % 2 == 0))
        def _():
            tap_spectra(chunk // 2)

        @pl.when(tick == 2 * TOKEN_CHUNKS)
        def _():
            await_mate(1)

        owner = 2 * x + chunk // groups
        far = jnp.abs(z - owner)

        @pl.when(
            projects_early(chunk % groups, owner)
            & (((step == 1) & (far <= 1)) | ((step == 2) & (far == 2)))
        )
        def _():
            project(chunk % groups, owner)

        @pl.when(tick == 2 * TOKEN_CHUNKS)
        def _():
            await_beside(0)

        @pl.when((tick == 2 * TOKEN_CHUNKS + TOKEN_CHUNKS // 2) & at_end)
        def _():
            await_beside(1)

        guest = 2 * (1 - x) + (chunk // 2) % 2

        @pl.when((step == 2) & (chunk % 2 == 0) & projects_early(chunk // 4, guest))
        def _():
            project(chunk // 4, guest)

    await_mate(2)
    for by in range(1, chan_count):
        for of in range(2):
            view = sums.at[of, lax.rem(z + by, chan_count)]
            remote(
                view, view, sums_send.at[0], sums_recv.at[of, lax.rem(z + by, chan_count)], mate
            ).wait_recv()
    view = sums.at[1 - core, z]
    remote(view, view, sums_send.at[0], sums_recv.at[1 - core, z], mate).wait_recv()

    @blocks(length)
    def _(i):
        of, at = i // (rows // BLOCK), i % (rows // BLOCK)
        found = sums[of, 0, pl.ds(at, 1), :]
        for owner in range(1, chan_count):
            found = found + sums[of, owner, pl.ds(at, 1), :]
        found = lax.rsqrt(found / (chan_count * width) + EPSILON)
        scale[at_rows(i), :] = jnp.broadcast_to(found, (BLOCK, LANES)).T

    taps_mate().wait_send()

    @pl.when(x == 0)
    def _():
        taps_across(0).wait_send()
        taps_across(1).wait_send()

    def edge_copy(g):
        return remote(
            edge_out.at[g], edge.at[g], edge_send.at[0], edge_recv.at[g], across
        )

    def before_copy(g):
        return remote(
            signal.at[g], before.at[g], before_send.at[0], before_recv.at[g], across
        )

    def swap_copy(g):
        return remote(
            ready.at[g], full.at[z, g, core], swap_send.at[0], swap_recv.at[g], mate
        )

    line = Line(
        lambda owner, g, of: full.at[owner, g, of],
        chan_count,
        line_send,
        line_recv,
        lambda to: (y, s, to),
    )

    def projected(g, b, at):
        return (partial[g, at, b * LANES : (b + 1) * LANES] * scale[at, :]).astype(jnp.bfloat16)

    def featurize(g):
        @pl.when(x == 0)
        def _():
            for b in range(branches):
                edge_out[g, b] = projected(g, b, pl.ds(length - rim, rim))
                extended[b, 0:rim, :] = jnp.zeros((rim, LANES), jnp.float32)
            edge_copy(g).start()

        @blocks(length)
        def _(i):
            for b in range(branches):
                extended[b, pl.ds(pl.multiple_of(rim + i * BLOCK, rim), BLOCK), :] = projected(
                    g, b, at_rows(i)
                ).astype(jnp.float32)

        @pl.when(x == 1)
        def _():
            edge_copy(g).wait_recv()
            for b in range(branches):
                extended[b, 0:rim, :] = edge[g, b].astype(jnp.float32)

        chosen = lanes_of(core * share, g)
        coefficient = [
            [short[tap, b : b + 1, chosen] for b in range(branches)] for tap in range(SHORT)
        ]

        @blocks(length)
        def _(i):
            found = []
            for b in range(branches):
                value = jnp.zeros((BLOCK, LANES), jnp.float32)
                for tap in range(SHORT):
                    value = value + coefficient[tap][b] * extended[
                        b, pl.ds(rim - tap + i * BLOCK, BLOCK), :
                    ]
                found.append(value.astype(jnp.bfloat16))
            query[at_rows(i), :] = found[0]
            signal[g, at_rows(i), :] = (
                found[1].astype(jnp.float32) * found[2].astype(jnp.float32)
            ).astype(jnp.bfloat16)

    def convolve(g):
        joint = (x == 1) & (g > 0)

        @pl.when(jnp.logical_not(joint))
        def _():
            spectrum(0, lambda: signal[g])

        def product(i, which, first):
            low, high = at_rows(i), rows_at(i, BLOCK, length)
            cos, sin = freq[which, low, :], freq[which, high, :]
            real = spectra[g, first, low, :].astype(jnp.float32)
            imag = spectra[g, first + 1, low, :].astype(jnp.float32)
            return cos * real + sin * imag, sin * real - cos * imag

        @pl.when(x == 0)
        def _():
            @blocks(length)
            def _(i):
                real, imag = product(i, 0, 0)
                mixed[at_rows(i), :] = real.astype(jnp.bfloat16)
                mixed[rows_at(i, BLOCK, length), :] = imag.astype(jnp.bfloat16)

        @pl.when(x == 1)
        def _():
            before_copy(g).wait_recv()

            @pl.when(g == 0)
            def _():
                spectrum(1, lambda: before[g])

            @pl.when(g > 0)
            def _():
                spectrum_pair(lambda: [signal[g], before[g]])

            @blocks(length)
            def _(i):
                real, imag = product(i, 0, 0)
                more_real, more_imag = product(i, 1, 2)
                mixed[at_rows(i), :] = (real + more_real).astype(jnp.bfloat16)
                mixed[rows_at(i, BLOCK, length), :] = (imag + more_imag).astype(jnp.bfloat16)

        @pl.loop(0, length // SPAN)
        def _(i):
            low, high = rows_at(i, SPAN), rows_at(i, SPAN, length)
            freq[0, low, :] = jnp.dot(
                table[low, :], mixed[:length, :], preferred_element_type=jnp.float32
            ) + jnp.dot(table[high, :], mixed[length:, :], preferred_element_type=jnp.float32)

        direct = skip[:, lanes_of(core * share, g)]

        def gated(at):
            longer = freq[0, at, :] + direct * signal[g, at, :].astype(jnp.float32)
            longer = longer.astype(jnp.bfloat16).astype(jnp.float32)
            return (query[at, :].astype(jnp.float32) * longer).astype(jnp.bfloat16)

        @blocks(rows)
        def _(i):
            full[z, g, core, at_rows(i), :] = gated(
                pl.ds(pl.multiple_of(core * rows + i * BLOCK, BLOCK), BLOCK)
            )
            ready[g, at_rows(i), :] = gated(
                pl.ds(pl.multiple_of((1 - core) * rows + i * BLOCK, BLOCK), BLOCK)
            )

    def load_out():
        for owner in range(chan_count):
            pltpu.make_async_copy(
                out_weight.at[pl.ds(owner * length, length)], stream.at[owner], local_sem.at[1]
            ).start()

    def accumulate(owner, g):
        @pl.loop(0, total.shape[1] // (2 * LANES))
        def _(i):
            cols = rows_at(i, 2 * LANES)
            block = jnp.concatenate([full[owner, g, 0], full[owner, g, 1]], axis=1)
            kernel = jnp.concatenate(
                [stream[owner, lanes_of(of * share, g), cols] for of in range(2)], axis=0
            )
            total[:, cols] += jnp.dot(block, kernel, preferred_element_type=jnp.float32)

    def begin(g):
        swap_copy(g).start()
        for way in range(2):

            @pl.when(line.sends(way, 0))
            def _():
                line.copy(way, 0, (g, core)).start()

    def begin_other(g):
        other = full.at[z, g, 1 - core]
        remote(other, other, swap_send.at[0], swap_recv.at[g], mate).wait_recv()
        for way in range(2):

            @pl.when(line.sends(way, 0))
            def _():
                line.copy(way, 0, (g, 1 - core)).start()

    def settle():
        other = weight.at[:, s]
        remote(other, other, mate_send.at[1], mate_recv.at[1], mate).wait_send()
        for copy in sum_copies:
            copy.wait_send()

        @pl.when(x == 1)
        def _():
            for origin in range(2):
                taps_beside(origin, y).wait_send()

        for at in range(2):
            view = weight_half(s, y)
            remote(view, view, x_send.at[at], x_recv.at[0, 0, 0], across).wait_send()
            view = weight_half((1 - x) * 2 + at, y)
            remote(view, view, y_send.at[at], y_recv.at[at, 0], beside).wait_send()

        @pl.when(x == 0)
        def _():
            remote(edge_out, edge, edge_send.at[0], edge_recv.at[0], across).wait_send()
            remote(signal, before, before_send.at[0], before_recv.at[0], across).wait_send()

    def settle_tokens():
        mate_tokens().wait_send()
        for way in range(2):
            for step in range(steps):

                @pl.when(token_line.receives(way, step))
                def _():
                    mate_half(way, step, core).wait_send()

                @pl.when(token_line.sends(way, step))
                def _():
                    token_line.drain(way, step, (0,), lambda owner: own_half(owner, core))

    def way_of(k):
        return jnp.where(z < chan_count // 2, 1 - k, k)

    def late_forwards(g, at, inner, outer):
        for here, pieces in ((jnp.logical_not(at_end), inner), (at_end, outer)):

            @pl.when((g == at) & here)
            def _():
                for group, c in pieces:
                    forward(group, c)

    def pass_on(way, step, at):
        @pl.when(
            (at >= 0) & (at < groups) & line.receives(way, step) & line.sends(way, step + 1)
        )
        def _():
            for of in (core, 1 - core):
                line.arrived(way, step, (at, of))
                line.copy(way, step + 1, (at, of)).start()

    for copy in small_loads[1:]:
        copy.wait()
    near, away = way_of(0), way_of(1)

    @pl.loop(0, groups)
    def _(g):
        @pl.when(g == 3)
        def _():
            pass_on(near, 0, 2)
            pass_on(near, 1, 0)

        late_forwards(g, 3, [(groups - 1, 3)], [])

        @pl.when(g == 3)
        def _():
            pass_on(away, 0, 1)

        @pl.when((g >= 2) | ((g == 1) & jnp.logical_not(at_end)))
        def _():
            await_beside(g)

        @pl.loop(0, chan_count)
        def _(owner):
            @pl.when(jnp.logical_not(projects_early(g, owner)))
            def _():
                project(g, owner)

        @pl.when(g == groups - 1)
        def _():
            settle_tokens()
            load_out()

        featurize(g)

        @pl.when(x == 0)
        def _():
            before_copy(g).start()

            for at, inner, outer in (
                (0, [], [(groups - 1, 2)]),
                (1, [(groups - 2, 3), (groups - 1, 0)], [(groups - 1, 3)]),
                (2, [(groups - 1, 1), (groups - 1, 2), (groups - 1, 3)], []),
            ):

                @pl.when((g == at) & jnp.logical_not(at_end))
                def _():
                    for group, c in inner:
                        send_weights(group, [c])

                @pl.when((g == at) & at_end)
                def _():
                    for group, c in outer:
                        send_weights(group, [c])

        late_forwards(g, 1, [(groups - 2, 3)], [(groups - 1, 0), (groups - 1, 1)])
        late_forwards(g, 2, [(groups - 1, 0)], [(groups - 1, 3)])

        @pl.when((g == 1) | (g == 2))
        def _():
            pass_on(near, 0, g - 1)

        late_forwards(g, 0, [(groups - 2, 2)], [(groups - 2, 2), (groups - 2, 3)])
        convolve(g)
        begin(g)
        late_forwards(g, 1, [], [(groups - 1, 2)])
        begin_other(g)

        @pl.when(g == 2)
        def _():
            pass_on(away, 0, 0)

        late_forwards(g, 2, [(groups - 1, 1), (groups - 1, 2)], [])

    pltpu.make_async_copy(stream, stream, local_sem.at[1]).wait()

    @pl.loop(0, groups + steps - 1)
    def _(n):
        for at, pieces in (
            (0, [(near, 1, 1), (away, 0, 2)]),
            (1, [(near, 0, 3), (near, 1, 2), (away, 0, 3)]),
            (3, [(near, 1, 3)]),
        ):

            @pl.when(n == at)
            def _():
                for way, step, group in pieces:
                    pass_on(way, step, group)

        @pl.when(n == 2)
        def _():
            settle()

        @pl.when(n < groups)
        def _():
            accumulate(z, n)

        @pl.loop(0, 2)
        def _(way):
            for step in range(steps):
                at = n - jnp.where(at_end, step, 0)

                @pl.when((at >= 0) & (at < groups) & line.receives(way, step))
                def _():
                    @pl.when(jnp.logical_not(line.sends(way, step + 1)))
                    def _():
                        for of in range(2):
                            line.arrived(way, step, (at, of))

                    accumulate(line.source(way, step), at)

    @blocks(rows)
    def _(i):
        result[at_rows(i), :] = total[at_rows(i), :].astype(jnp.bfloat16)

    remote(ready, ready, swap_send.at[0], swap_recv.at[0], mate).wait_send()
    for way in range(2):
        for step in range(steps):

            @pl.when(line.sends(way, step))
            def _():
                line.drain(way, step, (0, 0), lambda owner: full.at[owner])


def chip_body(tokens, norm_gain, proj_weight, short_filter, long_filter, skip_gain, out_weight):
    chan_count = lax.axis_size("chan")
    rows, width = tokens.shape
    depth, branches, local_chan = proj_weight.shape
    length, share = 2 * rows, local_chan // 2
    groups = share // LANES
    steps = chan_count - 1
    dma = pltpu.SemaphoreType.DMA
    f32, bf16 = jnp.float32, jnp.bfloat16
    vmem = pl.BlockSpec(memory_space=pltpu.VMEM)
    return pl.pallas_call(
        functools.partial(block_kernel, chan_count),
        out_shape=jax.ShapeDtypeStruct((rows, width), bf16),
        in_specs=[HBM] * 7,
        out_specs=vmem,
        scratch_shapes=[
            pltpu.VMEM((1, width), f32),
            pltpu.VMEM(short_filter.shape, f32),
            pltpu.VMEM((1, local_chan), f32),
            pltpu.VMEM((chan_count, length, width), bf16),
            pltpu.VMEM((groups, 4, depth, branches * LANES), bf16),
            pltpu.VMEM((2, chan_count, 8, LANES), f32),
            pltpu.VMEM((length, LANES), f32),
            pltpu.VMEM((groups, length, branches * LANES), f32),
            pltpu.VMEM((2 * length, length), bf16),
            pltpu.VMEM((groups, 2 * length, LANES), bf16),
            pltpu.VMEM((groups, 4, length, LANES), bf16),
            pltpu.VMEM((2, 2 * length, LANES), f32),
            pltpu.VMEM((2 * length, LANES), bf16),
            pltpu.VMEM((groups, branches, 16, LANES), bf16),
            pltpu.VMEM((groups, branches, 16, LANES), bf16),
            pltpu.VMEM((branches, length + 16, LANES), f32),
            pltpu.VMEM((length, LANES), bf16),
            pltpu.VMEM((groups, length, LANES), bf16),
            pltpu.VMEM((groups, length, LANES), bf16),
            pltpu.VMEM((groups, rows, LANES), bf16),
            pltpu.VMEM((chan_count, groups, 2, rows, LANES), bf16),
            pltpu.VMEM((rows, width), f32),
            dma((10,)),
            dma((3 + 2 * steps,)),
            dma((3 + 2 * steps,)),
            dma((2, steps)),
            dma((2, steps, TOKEN_CHUNKS)),
            dma((2 * chan_count - 1,)),
            dma((2, chan_count)),
            dma((2,)),
            dma((2, groups, WEIGHT_CHUNKS)),
            dma((2,)),
            dma((2, groups)),
            dma((4,)),
            dma((4,)),
            dma((1,)),
            dma((groups,)),
            dma((1,)),
            dma((groups,)),
            dma((1,)),
            dma((groups,)),
            dma((2, steps)),
            dma((2, steps, groups, 2)),
        ],
        compiler_params=pltpu.CompilerParams(
            collective_id=0, has_side_effects=True, vmem_limit_bytes=52 * 1024 * 1024
        ),
        name="block",
    )(
        tokens,
        pltpu.with_memory_space_constraint(norm_gain[None, :], pltpu.HBM),
        proj_weight.transpose(1, 0, 2),
        pltpu.with_memory_space_constraint(short_filter, pltpu.HBM),
        long_filter,
        pltpu.with_memory_space_constraint(skip_gain[None, :], pltpu.HBM),
        out_weight,
    )


def select_body(mesh):
    if (mesh.shape["groups"], mesh.shape["seq"], mesh.shape["chan"]) == (2, 4, 4):
        return chip_body
    return body


def solution(mesh):
    placed = (
        P(("groups", "seq"), "chan"),
        P(),
        P("seq", None, "chan"),
        P(None, None, "chan"),
        P("chan", "seq"),
        P("chan"),
        P(None, "chan"),
    )
    return jax.shard_map(
        select_body(mesh), mesh=mesh, in_specs=placed, out_specs=P(("groups", "seq"), "chan"), check_vma=False
    )
```

```python
import functools
import math

import jax
import jax.numpy as jnp
import numpy as np
from jax import lax
from jax.experimental import pallas as pl
from jax.experimental.pallas import tpu as pltpu
from jax.sharding import PartitionSpec as P

SHORT = 3


EPSILON = 1e-06
HIGHEST = lax.Precision.HIGHEST


def from_behind(value, axis, steps):
    count = lax.axis_size(axis)
    initial, last = (max(0, -steps), min(count, count - steps))
    return lax.ppermute(value, axis, [(source, source + steps) for source in range(initial, last)])


def angle_table(row_count, col_count, period, sign):
    row_index = lax.iota(jnp.int32, row_count)[:, None]
    col_index = lax.iota(jnp.int32, col_count)[None, :]
    angles = (row_index * col_index % period).astype(jnp.float32) * (sign * 2.0 * math.pi / period)
    return (jnp.cos(angles), jnp.sin(angles))


def forward_spectrum(signal_rows, first, second):
    channels = signal_rows.shape[0]
    grid_rows = signal_rows.reshape(channels, first, second)
    cos_first, sin_first = angle_table(first, first, first, -1.0)
    part_re = jnp.einsum("cab,ak->ckb", grid_rows, cos_first, precision=HIGHEST)
    part_im = jnp.einsum("cab,ak->ckb", grid_rows, sin_first, precision=HIGHEST)
    twist_cos, twist_sin = angle_table(first, second, first * second, -1.0)
    part_re, part_im = (
        part_re * twist_cos - part_im * twist_sin,
        part_re * twist_sin + part_im * twist_cos,
    )
    cos_second, sin_second = angle_table(second, second, second, -1.0)
    spectrum_real = jnp.einsum("ckb,bm->ckm", part_re, cos_second, precision=HIGHEST) - jnp.einsum(
        "ckb,bm->ckm", part_im, sin_second, precision=HIGHEST
    )
    spec_im = jnp.einsum("ckb,bm->ckm", part_re, sin_second, precision=HIGHEST) + jnp.einsum(
        "ckb,bm->ckm", part_im, cos_second, precision=HIGHEST
    )
    return (spectrum_real, spec_im)


def inverse_spectrum(spectrum_real, spec_im, first, second):
    channels = spectrum_real.shape[0]
    cos_second, sin_second = angle_table(second, second, second, 1.0)
    part_re = jnp.einsum("ckm,bm->ckb", spectrum_real, cos_second, precision=HIGHEST) - jnp.einsum(
        "ckm,bm->ckb", spec_im, sin_second, precision=HIGHEST
    )
    part_im = jnp.einsum("ckm,bm->ckb", spectrum_real, sin_second, precision=HIGHEST) + jnp.einsum(
        "ckm,bm->ckb", spec_im, cos_second, precision=HIGHEST
    )
    twist_cos, twist_sin = angle_table(first, second, first * second, 1.0)
    part_re, part_im = (
        part_re * twist_cos - part_im * twist_sin,
        part_re * twist_sin + part_im * twist_cos,
    )
    cos_first, sin_first = angle_table(first, first, first, 1.0)
    result = jnp.einsum("ckb,ak->cab", part_re, cos_first, precision=HIGHEST) - jnp.einsum(
        "ckb,ak->cab", part_im, sin_first, precision=HIGHEST
    )
    return result.reshape(channels, first * second) / (first * second)


def spectral_conv(signal_rows, filter_rows):
    channels, length = signal_rows.shape
    padded_len = 2 * length
    log_len = padded_len.bit_length() - 1
    first = 1 << log_len // 2
    second = padded_len // first
    zeros_tail = jnp.zeros((channels, length), jnp.float32)
    sig_re, sig_im = forward_spectrum(
        jnp.concatenate([signal_rows, zeros_tail], axis=1), first, second
    )
    tap_re, tap_im = forward_spectrum(
        jnp.concatenate([filter_rows, zeros_tail], axis=1), first, second
    )
    prod_re = sig_re * tap_re - sig_im * tap_im
    prod_im = sig_re * tap_im + sig_im * tap_re
    return inverse_spectrum(prod_re, prod_im, first, second)[:, :length]


def short_filter_output(projected, rim_cells, kernel_coefficients):
    count = kernel_coefficients.shape[0]
    steps_len = projected.shape[2]
    extended = jnp.concatenate([rim_cells, projected], axis=2).astype(jnp.float32)
    total = jnp.zeros(projected.shape, jnp.float32)
    for tap in range(count):
        total = (
            total
            + kernel_coefficients[tap][:, :, None]
            * extended[:, :, count - 1 - tap : count - 1 - tap + steps_len]
        )
    return total.astype(jnp.bfloat16)


def hyena_mixer(keys_rows, values_rows, long_taps, skip_part):
    middle = keys_rows.astype(jnp.float32) * values_rows.astype(jnp.float32)
    return (spectral_conv(middle, long_taps) + skip_part[:, None] * middle).astype(jnp.bfloat16)


def body(tokens, norm_gain, proj_weight, short_filter, long_filter, skip_gain, out_weight):
    seq_count = lax.axis_size("seq")
    local_rows = tokens.shape[0]
    local_chan = proj_weight.shape[2]
    subset = local_chan // seq_count
    length = local_rows * seq_count
    offset = lax.axis_index("seq") * subset
    whole = lax.all_gather(tokens, "chan", axis=1, tiled=True)
    wide = whole.astype(jnp.float32)
    rescaled_signal = (
        wide * lax.rsqrt(jnp.mean(wide * wide, axis=1, keepdims=True) + EPSILON) * norm_gain
    ).astype(jnp.bfloat16)
    projected = lax.dot_general(
        lax.all_gather(proj_weight, "seq", axis=0, tiled=True),
        rescaled_signal,
        (((0,), (1,)), ((), ())),
        preferred_element_type=jnp.float32,
    ).astype(jnp.bfloat16)
    taps_grid = long_filter.reshape(1, seq_count, subset, local_rows)
    long_taps = lax.all_to_all(taps_grid, "seq", split_axis=1, concat_axis=3, tiled=True).reshape(
        subset, length
    )
    skip_part = lax.dynamic_slice_in_dim(skip_gain, offset, subset, 0)
    rim_cells = from_behind(projected[:, :, local_rows - (SHORT - 1) :], "seq", 1)
    featured = short_filter_output(projected, rim_cells, short_filter)
    pair_grid = featured[1:].reshape(2, seq_count, subset, local_rows)
    moved = lax.all_to_all(pair_grid, "seq", split_axis=1, concat_axis=3, tiled=True).reshape(
        2, subset, length
    )
    result = hyena_mixer(moved[0], moved[1], long_taps, skip_part)
    returned = lax.all_to_all(
        result.reshape(1, subset, length), "seq", split_axis=2, concat_axis=0, tiled=True
    )
    returned = returned.reshape(local_chan, local_rows)
    gated = (featured[0].astype(jnp.float32) * returned.astype(jnp.float32)).astype(jnp.bfloat16)
    full_mix = lax.all_gather(gated, "chan", axis=0, tiled=True)
    update = lax.dot_general(
        full_mix, out_weight, (((0,), (0,)), ((), ())), preferred_element_type=jnp.float32
    )
    return (tokens.astype(jnp.float32) + update).astype(jnp.bfloat16)

LANES = 128
BLOCK = 128
SPAN = 512
TOKEN_CHUNKS = 8
WEIGHT_CHUNKS = 4
HBM = pl.BlockSpec(memory_space=pltpu.HBM)


def remote(src, dst, send_sem, recv_sem, where):
    return pltpu.make_async_remote_copy(
        src_ref=src,
        dst_ref=dst,
        send_sem=send_sem,
        recv_sem=recv_sem,
        device_id=where,
        device_id_type=pl.DeviceIdType.MESH,
    )


class Line:
    def __init__(self, view, count, send_sem, recv_sem, place):
        self.view, self.count, self.place = view, count, place
        self.send_sem, self.recv_sem = send_sem, recv_sem
        self.me = lax.axis_index("chan")

    def move(self, way, step, piece, block, target):
        recv = self.recv_sem.at[(way, step) + piece]
        return remote(block, block, self.send_sem.at[way, step], recv, self.place(target))

    def drain(self, way, step, first, block):
        self.move(way, step, first, block(self.source(way, step - 1)), self.me).wait_send()

    def source(self, way, step):
        return jnp.clip(self.me - (step + 1) * (1 - 2 * way), 0, self.count - 1)

    def copy(self, way, step, piece):
        owner = self.source(way, step - 1)
        target = self.source(way, -2)
        return self.move(way, step, piece, self.view(owner, *piece), target)

    def inside(self, way, by):
        place = self.me + by * (1 - 2 * way)
        return (place >= 0) & (place < self.count)

    def sends(self, way, step):
        return self.inside(way, -step) & self.inside(way, 1)

    def receives(self, way, step):
        return self.inside(way, -1 - step)

    def arrived(self, way, step, piece):
        owner = self.source(way, step)
        self.move(way, step, piece, self.view(owner, *piece), self.me).wait_recv()
        return owner


def block_kernel(
    chan_count,
    tokens,
    gain_hbm,
    weights,
    short_hbm,
    long_taps,
    skip_hbm,
    out_weight,
    result,
    gain,
    short,
    skip,
    stream,
    weight,
    sums,
    scale,
    partial,
    table,
    taps,
    spectra,
    freq,
    mixed,
    edge_out,
    edge,
    extended,
    query,
    signal,
    before,
    ready,
    full,
    total,
    local_sem,
    mate_send,
    mate_recv,
    token_send,
    token_recv,
    sums_send,
    sums_recv,
    x_send,
    x_recv,
    y_send,
    y_recv,
    tap_send,
    tap_recv,
    edge_send,
    edge_recv,
    before_send,
    before_recv,
    swap_send,
    swap_recv,
    line_send,
    line_recv,
):
    y, s, z = (lax.axis_index(name) for name in ("groups", "seq", "chan"))
    x, core = s // 2, s % 2
    mate_s = s + 1 - 2 * core
    mate = (y, mate_s, z)
    across = (y, (1 - x) * 2 + core, z)
    aslant = (y, (1 - x) * 2 + 1 - core, z)
    beside = (1 - y, s, z)
    rows, width = tokens.shape
    length = 2 * rows
    branches, depth = weights.shape[0], weights.shape[1]
    half = depth // 2
    share = weights.shape[2] // 2
    groups = share // LANES
    rim = edge.shape[2]
    steps = chan_count - 1
    token_rows = rows // TOKEN_CHUNKS
    weight_rows = half // WEIGHT_CHUNKS

    column_peers = [mate] + [
        (y, 2 * x + of, lax.rem(z + by, chan_count))
        for by in range(1, chan_count)
        for of in (core, 1 - core)
    ]
    peers = column_peers + [across, aslant, beside]

    def rows_at(i, count, base=0):
        return pl.ds(pl.multiple_of(base + i * count, count), count)

    def at_rows(i):
        return rows_at(i, BLOCK)

    def blocks(count):
        return pl.loop(0, count // BLOCK)

    def lanes_of(base, g):
        return pl.ds(pl.multiple_of(base + g * LANES, LANES), LANES)

    tap_stage = [(0, 0), (0, length), (1, 0), (1, length)]
    tap_loads = [
        pltpu.make_async_copy(
            long_taps.at[:, pl.ds(j * LANES, LANES)],
            freq.at[which, pl.ds(start, length)],
            local_sem.at[4 + j],
        )
        for j, (which, start) in enumerate(tap_stage)
    ]
    token_load = pltpu.make_async_copy(tokens, result, local_sem.at[0])
    token_load.start()
    small_loads = [
        pltpu.make_async_copy(src, dst, local_sem.at[at])
        for src, dst, at in (
            (gain_hbm.at[:, pl.ds(pl.multiple_of(z * width, width), width)], gain, 3),
            (short_hbm, short, 8),
            (skip_hbm, skip, 9),
        )
    ]
    for copy in small_loads:
        copy.start()
    barrier = pltpu.get_barrier_semaphore()
    for peer in peers:
        pl.semaphore_signal(barrier, inc=1, device_id=peer, device_id_type=pl.DeviceIdType.MESH)
    for copy in tap_loads:
        copy.start()
    for g in range(groups):
        for b in range(branches):
            pltpu.make_async_copy(
                weights.at[b, :, lanes_of(core * share, g)],
                weight.at[g, s, :, pl.ds(b * LANES, LANES)],
                local_sem.at[2],
            ).start()

    sums[core, z] = jnp.zeros(sums.shape[2:], jnp.float32)
    small_loads[0].wait()
    own_gain = gain[...]
    token_load.wait()

    @blocks(rows)
    def _(i):
        raw = result[at_rows(i), :].astype(jnp.float32)
        total[at_rows(i), :] = raw
        stream[z, pl.ds(pl.multiple_of(core * rows + i * BLOCK, BLOCK), BLOCK), :] = (
            raw * own_gain
        ).astype(jnp.bfloat16)
        square = raw * raw
        found = square[:, :LANES]
        for part in range(1, width // LANES):
            found = found + square[:, part * LANES : (part + 1) * LANES]
        sums[core, z, pl.ds(i, 1), :] = jnp.sum(found.T, axis=0, keepdims=True)

    pl.semaphore_wait(barrier, len(peers))

    def token_view(owner, chunk):
        return stream.at[owner, rows_at(chunk, token_rows, core * rows), :]

    token_line = Line(
        token_view, chan_count, token_send, token_recv, lambda to: (y, s, to)
    )
    for chunk in range(TOKEN_CHUNKS):
        for way in range(2):

            @pl.when(token_line.sends(way, 0))
            def _():
                token_line.copy(way, 0, (chunk,)).start()

    def own_half(owner, of):
        return stream.at[owner, pl.ds(pl.multiple_of(of * rows, rows), rows), :]

    def mate_tokens():
        return remote(
            own_half(z, core), own_half(z, core), mate_send.at[0], mate_recv.at[0], mate
        )

    mate_tokens().start()
    sum_copies = [
        remote(
            sums.at[core, z], sums.at[core, z], sums_send.at[at], sums_recv.at[core, z], peer
        )
        for at, peer in enumerate(column_peers)
    ]
    for copy in sum_copies:
        copy.start()
    for g in range(groups):
        for b in range(branches):
            remote(
                weights.at[b, :, lanes_of((1 - core) * share, g)],
                weight.at[g, s, :, pl.ds(b * LANES, LANES)],
                mate_send.at[1],
                mate_recv.at[1],
                mate,
            ).start()

    for j, (which, start) in enumerate(tap_stage):
        tap_loads[j].wait()

        @pl.loop(0, groups)
        def _(g):
            mine = freq[which, rows_at(core * groups + g, BLOCK, start), :]
            taps[g, pl.ds(pl.multiple_of(s * rows + j * LANES, LANES), LANES), :] = mine.T.astype(
                jnp.bfloat16
            )
            other = freq[which, rows_at((1 - core) * groups + g, BLOCK, start), :]
            ready[g, j * LANES : (j + 1) * LANES, :] = other.T.astype(jnp.bfloat16)

    def tap_part(owner, part):
        return taps.at[
            :, pl.ds(pl.multiple_of(owner * rows + part * (rows // 2), rows // 2), rows // 2), :
        ]

    def taps_across(to):
        src = tap_part(s, y) if to == 0 else ready.at[
            :, pl.ds(pl.multiple_of(y * (rows // 2), rows // 2), rows // 2), :
        ]
        return remote(
            src,
            tap_part(s, y),
            tap_send.at[to],
            tap_recv.at[core],
            across if to == 0 else aslant,
        )

    def taps_beside(origin, part):
        view = tap_part(origin, part)
        return remote(view, view, tap_send.at[2 + origin], tap_recv.at[2 + origin], beside)

    def taps_mate():
        return remote(
            ready,
            taps.at[:, pl.ds(pl.multiple_of(s * rows, rows), rows), :],
            mate_send.at[2],
            mate_recv.at[2],
            mate,
        )

    @pl.when(x == 0)
    def _():
        taps_across(0).start()
        taps_across(1).start()

        @pl.loop(0, groups)
        def _(g):
            taps[g, length:, :] = jnp.zeros((length, LANES), jnp.bfloat16)

    taps_mate().start()

    def weight_view(owner, part, g, c):
        return weight.at[g, owner, rows_at(c, weight_rows, part * half), :]

    def weight_half(owner, part):
        return weight.at[:, owner, pl.ds(pl.multiple_of(part * half, half), half), :]

    def send_weights(g, chunks=range(WEIGHT_CHUNKS)):
        for c in chunks:
            for to in range(2):
                side = core if to == 0 else 1 - core
                view = weight_view(s, y, g, c)
                for b in range(branches):
                    remote(
                        weights.at[
                            b,
                            rows_at(c, weight_rows, y * half),
                            pl.ds(pl.multiple_of(side * share + g * LANES, LANES), LANES),
                        ],
                        view.at[:, pl.ds(b * LANES, LANES)],
                        x_send.at[to],
                        x_recv.at[core, g, c],
                        across if to == 0 else aslant,
                    ).start()

    for g in range(groups - 2):
        send_weights(g)
    send_weights(groups - 2, range(3))

    at_end = (z == 0) | (z == chan_count - 1)

    @pl.when((x == 1) | at_end)
    def _():
        send_weights(groups - 2, [3])
        send_weights(groups - 1, [0, 1])

    @pl.when(x == 1)
    def _():
        send_weights(groups - 1, [2, 3])

    def beside_copy(origin, part, g, c):
        view = weight_view((1 - x) * 2 + origin, part, g, c)
        return remote(view, view, y_send.at[origin], y_recv.at[origin, g], beside)

    def forward(g, c):
        for origin in range(2):
            view = weight_view((1 - x) * 2 + origin, y, g, c)
            remote(
                view, view, x_send.at[origin], x_recv.at[origin, g, c], beside
            ).wait_recv()
            beside_copy(origin, y, g, c).start()

    def await_beside(g):
        for origin in range(2):
            view = weight.at[
                g, (1 - x) * 2 + origin, pl.ds(pl.multiple_of((1 - y) * half, half), half), :
            ]
            remote(view, view, y_send.at[origin], y_recv.at[origin, g], beside).wait_recv()

    @blocks(length)
    def _(i):
        row = lax.broadcasted_iota(jnp.int32, (BLOCK, LANES), 0) + i * BLOCK
        lane = lax.broadcasted_iota(jnp.int32, (BLOCK, LANES), 1)
        unit = math.pi / (4 * length)
        odd = 2 * row + 1
        small = odd.astype(jnp.float32) * unit
        extended[0, at_rows(i), :] = jnp.cos(small)
        extended[1, at_rows(i), :] = jnp.sin(small)
        period = 8 * length
        angle = (odd * (2 * lane + 1) % period).astype(jnp.float32) * unit
        cos, sin = jnp.cos(angle), jnp.sin(angle)
        stride = (odd * (2 * LANES) % period).astype(jnp.float32) * unit
        step_cos, step_sin = jnp.cos(stride), jnp.sin(stride)
        for a in range(length // LANES):
            table[at_rows(i), a * LANES : (a + 1) * LANES] = cos.astype(jnp.bfloat16)
            table[rows_at(i, BLOCK, length), a * LANES : (a + 1) * LANES] = sin.astype(
                jnp.bfloat16
            )
            cos, sin = cos * step_cos - sin * step_sin, sin * step_cos + cos * step_sin

    for g in range(groups):

        @blocks(length)
        def _(i):
            partial[g, at_rows(i), :] = jnp.zeros((BLOCK, branches * LANES), jnp.float32)

    def spectrum(which, column):
        @pl.loop(0, 2 * length // SPAN)
        def _(i):
            at = rows_at(i, SPAN)
            freq[which, at, :] = jnp.dot(
                table[at, :], column(), preferred_element_type=jnp.float32
            )

    def spectrum_pair(columns):
        @pl.loop(0, 2 * length // SPAN)
        def _(i):
            at = rows_at(i, SPAN)
            found = jnp.dot(
                table[at, :],
                jnp.concatenate(columns(), axis=1),
                preferred_element_type=jnp.float32,
            )
            freq[0, at, :] = found[:, :LANES]
            freq[1, at, :] = found[:, LANES:]

    def tap_spectra(g):
        spectrum_pair(lambda: [taps[g, :length, :], taps[g, length:, :]])

        @blocks(length)
        def _(i):
            low, high = at_rows(i), rows_at(i, BLOCK, length)
            cos, sin = extended[0, low, :], extended[1, low, :]

            def turned(which):
                real, imag = freq[which, low, :], -freq[which, high, :]
                return (cos * real - sin * imag) / length, (cos * imag + sin * real) / length

            real, imag = turned(0)
            late_real, late_imag = turned(1)
            place = lax.broadcasted_iota(jnp.int32, (BLOCK, LANES), 0)
            sign = (1 - 2 * (place % 2)).astype(jnp.float32)
            spectra[g, 0, low, :] = real.astype(jnp.bfloat16)
            spectra[g, 1, low, :] = imag.astype(jnp.bfloat16)
            spectra[g, 2, low, :] = (late_real - sign * imag).astype(jnp.bfloat16)
            spectra[g, 3, low, :] = (late_imag + sign * real).astype(jnp.bfloat16)

    def project(g, owner):
        @pl.loop(0, length // SPAN)
        def _(i):
            at = rows_at(i, SPAN)
            partial[g, at, :] += jnp.dot(
                stream[owner, at, :], weight[g, owner], preferred_element_type=jnp.float32
            )

    def projects_early(g, owner):
        far = jnp.abs(z - owner)
        own = owner // 2 == x
        return (
            (own & ((far <= 1) | ((far == 2) & (at_end | (g == 0)))))
            | (jnp.logical_not(own) & (far <= 2) & ((g == 0) | ((g == 1) & at_end)))
        )

    def to_mate(way, step, chunk):
        block = token_view(token_line.source(way, step), chunk)
        index = 3 + way * steps + step
        return remote(block, block, mate_send.at[index], mate_recv.at[index], mate)

    def mate_half(way, step, of):
        block = own_half(token_line.source(way, step), of)
        index = 3 + way * steps + step
        return remote(block, block, mate_send.at[index], mate_recv.at[index], mate)

    def await_mate(step):
        for way in range(2):

            @pl.when(token_line.receives(way, step))
            def _():
                mate_half(way, step, 1 - core).wait_recv()

    @pl.loop(0, steps * TOKEN_CHUNKS)
    def _(tick):
        step, chunk = tick // TOKEN_CHUNKS, tick % TOKEN_CHUNKS
        for way in range(2):

            @pl.when(token_line.receives(way, step))
            def _():
                token_line.arrived(way, step, (chunk,))
                to_mate(way, step, chunk).start()

            @pl.when(
                (step + 1 < steps)
                & token_line.receives(way, step)
                & token_line.sends(way, step + 1)
            )
            def _():
                token_line.copy(way, step + 1, (chunk,)).start()

        @pl.when((tick == TOKEN_CHUNKS // 2) & (x == 1))
        def _():
            for origin in range(2):
                view = tap_part(origin, y)
                remote(
                    view, view, tap_send.at[origin], tap_recv.at[origin], beside
                ).wait_recv()
                taps_beside(origin, y).start()

        @pl.when((tick % 2 == 1) & (tick >= 3) & (tick < 7 + 4 * WEIGHT_CHUNKS))
        def _():
            at = (tick - 3) // 2
            forward(at // WEIGHT_CHUNKS, at % WEIGHT_CHUNKS)

        @pl.when(tick == TOKEN_CHUNKS)
        def _():
            mate_half_own = own_half(z, 1 - core)
            remote(
                mate_half_own, mate_half_own, mate_send.at[0], mate_recv.at[0], mate
            ).wait_recv()
            await_mate(0)
            pltpu.make_async_copy(
                weight.at[:, s], weight.at[:, s], local_sem.at[2]
            ).wait()
            other = weight.at[:, mate_s]
            remote(other, other, mate_send.at[1], mate_recv.at[1], mate).wait_recv()
            other = taps.at[:, pl.ds(pl.multiple_of(mate_s * rows, rows), rows), :]
            remote(other, other, mate_send.at[2], mate_recv.at[2], mate).wait_recv()

            @pl.when(x == 1)
            def _():
                for origin in range(2):
                    taps_beside(origin, 1 - y).wait_recv()

        @pl.when((step == 1) & (chunk % 2 == 0))
        def _():
            tap_spectra(chunk // 2)

        @pl.when(tick == 2 * TOKEN_CHUNKS)
        def _():
            await_mate(1)

        owner = 2 * x + chunk // groups
        far = jnp.abs(z - owner)

        @pl.when(
            projects_early(chunk % groups, owner)
            & (((step == 1) & (far <= 1)) | ((step == 2) & (far == 2)))
        )
        def _():
            project(chunk % groups, owner)

        @pl.when(tick == 2 * TOKEN_CHUNKS)
        def _():
            await_beside(0)

        @pl.when((tick == 2 * TOKEN_CHUNKS + TOKEN_CHUNKS // 2) & at_end)
        def _():
            await_beside(1)

        guest = 2 * (1 - x) + (chunk // 2) % 2

        @pl.when((step == 2) & (chunk % 2 == 0) & projects_early(chunk // 4, guest))
        def _():
            project(chunk // 4, guest)

    await_mate(2)
    for by in range(1, chan_count):
        for of in range(2):
            view = sums.at[of, lax.rem(z + by, chan_count)]
            remote(
                view, view, sums_send.at[0], sums_recv.at[of, lax.rem(z + by, chan_count)], mate
            ).wait_recv()
    view = sums.at[1 - core, z]
    remote(view, view, sums_send.at[0], sums_recv.at[1 - core, z], mate).wait_recv()

    @blocks(length)
    def _(i):
        of, at = i // (rows // BLOCK), i % (rows // BLOCK)
        found = sums[of, 0, pl.ds(at, 1), :]
        for owner in range(1, chan_count):
            found = found + sums[of, owner, pl.ds(at, 1), :]
        found = lax.rsqrt(found / (chan_count * width) + EPSILON)
        scale[at_rows(i), :] = jnp.broadcast_to(found, (BLOCK, LANES)).T

    taps_mate().wait_send()

    @pl.when(x == 0)
    def _():
        taps_across(0).wait_send()
        taps_across(1).wait_send()

    def edge_copy(g):
        return remote(
            edge_out.at[g], edge.at[g], edge_send.at[0], edge_recv.at[g], across
        )

    def before_copy(g):
        return remote(
            signal.at[g], before.at[g], before_send.at[0], before_recv.at[g], across
        )

    def swap_copy(g):
        return remote(
            ready.at[g], full.at[z, g, core], swap_send.at[0], swap_recv.at[g], mate
        )

    line = Line(
        lambda owner, g, of: full.at[owner, g, of],
        chan_count,
        line_send,
        line_recv,
        lambda to: (y, s, to),
    )

    def projected(g, b, at):
        return (partial[g, at, b * LANES : (b + 1) * LANES] * scale[at, :]).astype(jnp.bfloat16)

    def featurize(g):
        @pl.when(x == 0)
        def _():
            for b in range(branches):
                edge_out[g, b] = projected(g, b, pl.ds(length - rim, rim))
                extended[b, 0:rim, :] = jnp.zeros((rim, LANES), jnp.float32)
            edge_copy(g).start()

        @blocks(length)
        def _(i):
            for b in range(branches):
                extended[b, pl.ds(pl.multiple_of(rim + i * BLOCK, rim), BLOCK), :] = projected(
                    g, b, at_rows(i)
                ).astype(jnp.float32)

        @pl.when(x == 1)
        def _():
            edge_copy(g).wait_recv()
            for b in range(branches):
                extended[b, 0:rim, :] = edge[g, b].astype(jnp.float32)

        chosen = lanes_of(core * share, g)
        coefficient = [
            [short[tap, b : b + 1, chosen] for b in range(branches)] for tap in range(SHORT)
        ]

        @blocks(length)
        def _(i):
            found = []
            for b in range(branches):
                value = jnp.zeros((BLOCK, LANES), jnp.float32)
                for tap in range(SHORT):
                    value = value + coefficient[tap][b] * extended[
                        b, pl.ds(rim - tap + i * BLOCK, BLOCK), :
                    ]
                found.append(value.astype(jnp.bfloat16))
            query[at_rows(i), :] = found[0]
            signal[g, at_rows(i), :] = (
                found[1].astype(jnp.float32) * found[2].astype(jnp.float32)
            ).astype(jnp.bfloat16)

    def convolve(g):
        joint = (x == 1) & (g > 0)

        @pl.when(jnp.logical_not(joint))
        def _():
            spectrum(0, lambda: signal[g])

        def product(i, which, first):
            low, high = at_rows(i), rows_at(i, BLOCK, length)
            cos, sin = freq[which, low, :], freq[which, high, :]
            real = spectra[g, first, low, :].astype(jnp.float32)
            imag = spectra[g, first + 1, low, :].astype(jnp.float32)
            return cos * real + sin * imag, sin * real - cos * imag

        @pl.when(x == 0)
        def _():
            @blocks(length)
            def _(i):
                real, imag = product(i, 0, 0)
                mixed[at_rows(i), :] = real.astype(jnp.bfloat16)
                mixed[rows_at(i, BLOCK, length), :] = imag.astype(jnp.bfloat16)

        @pl.when(x == 1)
        def _():
            before_copy(g).wait_recv()

            @pl.when(g == 0)
            def _():
                spectrum(1, lambda: before[g])

            @pl.when(g > 0)
            def _():
                spectrum_pair(lambda: [signal[g], before[g]])

            @blocks(length)
            def _(i):
                real, imag = product(i, 0, 0)
                more_real, more_imag = product(i, 1, 2)
                mixed[at_rows(i), :] = (real + more_real).astype(jnp.bfloat16)
                mixed[rows_at(i, BLOCK, length), :] = (imag + more_imag).astype(jnp.bfloat16)

        @pl.loop(0, length // SPAN)
        def _(i):
            low, high = rows_at(i, SPAN), rows_at(i, SPAN, length)
            freq[0, low, :] = jnp.dot(
                table[low, :], mixed[:length, :], preferred_element_type=jnp.float32
            ) + jnp.dot(table[high, :], mixed[length:, :], preferred_element_type=jnp.float32)

        direct = skip[:, lanes_of(core * share, g)]

        def gated(at):
            longer = freq[0, at, :] + direct * signal[g, at, :].astype(jnp.float32)
            longer = longer.astype(jnp.bfloat16).astype(jnp.float32)
            return (query[at, :].astype(jnp.float32) * longer).astype(jnp.bfloat16)

        @blocks(rows)
        def _(i):
            full[z, g, core, at_rows(i), :] = gated(
                pl.ds(pl.multiple_of(core * rows + i * BLOCK, BLOCK), BLOCK)
            )
            ready[g, at_rows(i), :] = gated(
                pl.ds(pl.multiple_of((1 - core) * rows + i * BLOCK, BLOCK), BLOCK)
            )

    def load_out():
        for owner in range(chan_count):
            pltpu.make_async_copy(
                out_weight.at[pl.ds(owner * length, length)], stream.at[owner], local_sem.at[1]
            ).start()

    def accumulate(owner, g):
        @pl.loop(0, total.shape[1] // (2 * LANES))
        def _(i):
            cols = rows_at(i, 2 * LANES)
            block = jnp.concatenate([full[owner, g, 0], full[owner, g, 1]], axis=1)
            kernel = jnp.concatenate(
                [stream[owner, lanes_of(of * share, g), cols] for of in range(2)], axis=0
            )
            total[:, cols] += jnp.dot(block, kernel, preferred_element_type=jnp.float32)

    def begin(g):
        swap_copy(g).start()
        for way in range(2):

            @pl.when(line.sends(way, 0))
            def _():
                line.copy(way, 0, (g, core)).start()

    def begin_other(g):
        other = full.at[z, g, 1 - core]
        remote(other, other, swap_send.at[0], swap_recv.at[g], mate).wait_recv()
        for way in range(2):

            @pl.when(line.sends(way, 0))
            def _():
                line.copy(way, 0, (g, 1 - core)).start()

    def settle():
        other = weight.at[:, s]
        remote(other, other, mate_send.at[1], mate_recv.at[1], mate).wait_send()
        for copy in sum_copies:
            copy.wait_send()

        @pl.when(x == 1)
        def _():
            for origin in range(2):
                taps_beside(origin, y).wait_send()

        for at in range(2):
            view = weight_half(s, y)
            remote(view, view, x_send.at[at], x_recv.at[0, 0, 0], across).wait_send()
            view = weight_half((1 - x) * 2 + at, y)
            remote(view, view, y_send.at[at], y_recv.at[at, 0], beside).wait_send()

        @pl.when(x == 0)
        def _():
            remote(edge_out, edge, edge_send.at[0], edge_recv.at[0], across).wait_send()
            remote(signal, before, before_send.at[0], before_recv.at[0], across).wait_send()

    def settle_tokens():
        mate_tokens().wait_send()
        for way in range(2):
            for step in range(steps):

                @pl.when(token_line.receives(way, step))
                def _():
                    mate_half(way, step, core).wait_send()

                @pl.when(token_line.sends(way, step))
                def _():
                    token_line.drain(way, step, (0,), lambda owner: own_half(owner, core))

    def way_of(k):
        return jnp.where(z < chan_count // 2, 1 - k, k)

    def late_forwards(g, at, inner, outer):
        for here, pieces in ((jnp.logical_not(at_end), inner), (at_end, outer)):

            @pl.when((g == at) & here)
            def _():
                for group, c in pieces:
                    forward(group, c)

    def pass_on(way, step, at):
        @pl.when(
            (at >= 0) & (at < groups) & line.receives(way, step) & line.sends(way, step + 1)
        )
        def _():
            for of in (core, 1 - core):
                line.arrived(way, step, (at, of))
                line.copy(way, step + 1, (at, of)).start()

    for copy in small_loads[1:]:
        copy.wait()
    near, away = way_of(0), way_of(1)

    @pl.loop(0, groups)
    def _(g):
        late_forwards(g, 3, [(groups - 1, 3)], [])

        @pl.when(g == 3)
        def _():
            pass_on(near, 0, 2)
            pass_on(away, 0, 1)

        @pl.when((g >= 2) | ((g == 1) & jnp.logical_not(at_end)))
        def _():
            await_beside(g)

        @pl.loop(0, chan_count)
        def _(owner):
            @pl.when(jnp.logical_not(projects_early(g, owner)))
            def _():
                project(g, owner)

        @pl.when(g == groups - 1)
        def _():
            settle_tokens()
            load_out()

        featurize(g)

        @pl.when(x == 0)
        def _():
            before_copy(g).start()

            for at, inner, outer in (
                (0, [], [(groups - 1, 2)]),
                (1, [(groups - 2, 3), (groups - 1, 0)], [(groups - 1, 3)]),
                (2, [(groups - 1, 1), (groups - 1, 2), (groups - 1, 3)], []),
            ):

                @pl.when((g == at) & jnp.logical_not(at_end))
                def _():
                    for group, c in inner:
                        send_weights(group, [c])

                @pl.when((g == at) & at_end)
                def _():
                    for group, c in outer:
                        send_weights(group, [c])

        late_forwards(g, 1, [(groups - 2, 3)], [(groups - 1, 0), (groups - 1, 1)])
        late_forwards(g, 2, [(groups - 1, 0)], [(groups - 1, 3)])

        @pl.when((g == 1) | (g == 2))
        def _():
            pass_on(near, 0, g - 1)

        @pl.when(g == 3)
        def _():
            pass_on(near, 1, 0)

        late_forwards(g, 0, [(groups - 2, 2)], [(groups - 2, 2), (groups - 2, 3)])
        convolve(g)
        begin(g)
        late_forwards(g, 1, [], [(groups - 1, 2)])
        begin_other(g)

        @pl.when(g == 2)
        def _():
            pass_on(away, 0, 0)

        late_forwards(g, 2, [(groups - 1, 1), (groups - 1, 2)], [])

    pltpu.make_async_copy(stream, stream, local_sem.at[1]).wait()

    @pl.loop(0, groups + steps - 1)
    def _(n):
        for at, pieces in (
            (0, [(near, 1, 1), (away, 0, 2)]),
            (1, [(near, 0, 3), (near, 1, 2), (away, 0, 3)]),
            (3, [(near, 1, 3)]),
        ):

            @pl.when(n == at)
            def _():
                for way, step, group in pieces:
                    pass_on(way, step, group)

        @pl.when(n == 2)
        def _():
            settle()

        @pl.when(n < groups)
        def _():
            accumulate(z, n)

        @pl.loop(0, 2)
        def _(way):
            for step in range(steps):
                at = n - jnp.where(at_end, step, 0)

                @pl.when((at >= 0) & (at < groups) & line.receives(way, step))
                def _():
                    @pl.when(jnp.logical_not(line.sends(way, step + 1)))
                    def _():
                        for of in range(2):
                            line.arrived(way, step, (at, of))

                    accumulate(line.source(way, step), at)

    @blocks(rows)
    def _(i):
        result[at_rows(i), :] = total[at_rows(i), :].astype(jnp.bfloat16)

    remote(ready, ready, swap_send.at[0], swap_recv.at[0], mate).wait_send()
    for way in range(2):
        for step in range(steps):

            @pl.when(line.sends(way, step))
            def _():
                line.drain(way, step, (0, 0), lambda owner: full.at[owner])


def chip_body(tokens, norm_gain, proj_weight, short_filter, long_filter, skip_gain, out_weight):
    chan_count = lax.axis_size("chan")
    rows, width = tokens.shape
    depth, branches, local_chan = proj_weight.shape
    length, share = 2 * rows, local_chan // 2
    groups = share // LANES
    steps = chan_count - 1
    dma = pltpu.SemaphoreType.DMA
    f32, bf16 = jnp.float32, jnp.bfloat16
    vmem = pl.BlockSpec(memory_space=pltpu.VMEM)
    return pl.pallas_call(
        functools.partial(block_kernel, chan_count),
        out_shape=jax.ShapeDtypeStruct((rows, width), bf16),
        in_specs=[HBM] * 7,
        out_specs=vmem,
        scratch_shapes=[
            pltpu.VMEM((1, width), f32),
            pltpu.VMEM(short_filter.shape, f32),
            pltpu.VMEM((1, local_chan), f32),
            pltpu.VMEM((chan_count, length, width), bf16),
            pltpu.VMEM((groups, 4, depth, branches * LANES), bf16),
            pltpu.VMEM((2, chan_count, 8, LANES), f32),
            pltpu.VMEM((length, LANES), f32),
            pltpu.VMEM((groups, length, branches * LANES), f32),
            pltpu.VMEM((2 * length, length), bf16),
            pltpu.VMEM((groups, 2 * length, LANES), bf16),
            pltpu.VMEM((groups, 4, length, LANES), bf16),
            pltpu.VMEM((2, 2 * length, LANES), f32),
            pltpu.VMEM((2 * length, LANES), bf16),
            pltpu.VMEM((groups, branches, 16, LANES), bf16),
            pltpu.VMEM((groups, branches, 16, LANES), bf16),
            pltpu.VMEM((branches, length + 16, LANES), f32),
            pltpu.VMEM((length, LANES), bf16),
            pltpu.VMEM((groups, length, LANES), bf16),
            pltpu.VMEM((groups, length, LANES), bf16),
            pltpu.VMEM((groups, rows, LANES), bf16),
            pltpu.VMEM((chan_count, groups, 2, rows, LANES), bf16),
            pltpu.VMEM((rows, width), f32),
            dma((10,)),
            dma((3 + 2 * steps,)),
            dma((3 + 2 * steps,)),
            dma((2, steps)),
            dma((2, steps, TOKEN_CHUNKS)),
            dma((2 * chan_count - 1,)),
            dma((2, chan_count)),
            dma((2,)),
            dma((2, groups, WEIGHT_CHUNKS)),
            dma((2,)),
            dma((2, groups)),
            dma((4,)),
            dma((4,)),
            dma((1,)),
            dma((groups,)),
            dma((1,)),
            dma((groups,)),
            dma((1,)),
            dma((groups,)),
            dma((2, steps)),
            dma((2, steps, groups, 2)),
        ],
        compiler_params=pltpu.CompilerParams(
            collective_id=0, has_side_effects=True, vmem_limit_bytes=52 * 1024 * 1024
        ),
        name="block",
    )(
        tokens,
        pltpu.with_memory_space_constraint(norm_gain[None, :], pltpu.HBM),
        proj_weight.transpose(1, 0, 2),
        pltpu.with_memory_space_constraint(short_filter, pltpu.HBM),
        long_filter,
        pltpu.with_memory_space_constraint(skip_gain[None, :], pltpu.HBM),
        out_weight,
    )


def select_body(mesh):
    if (mesh.shape["groups"], mesh.shape["seq"], mesh.shape["chan"]) == (2, 4, 4):
        return chip_body
    return body


def solution(mesh):
    placed = (
        P(("groups", "seq"), "chan"),
        P(),
        P("seq", None, "chan"),
        P(None, None, "chan"),
        P("chan", "seq"),
        P("chan"),
        P(None, "chan"),
    )
    return jax.shard_map(
        select_body(mesh), mesh=mesh, in_specs=placed, out_specs=P(("groups", "seq"), "chan"), check_vma=False
    )
```

```python
import functools
import math

import jax
import jax.numpy as jnp
import numpy as np
from jax import lax
from jax.experimental import pallas as pl
from jax.experimental.pallas import tpu as pltpu
from jax.sharding import PartitionSpec as P

SHORT = 3


EPSILON = 1e-06
HIGHEST = lax.Precision.HIGHEST


def from_behind(value, axis, steps):
    count = lax.axis_size(axis)
    initial, last = (max(0, -steps), min(count, count - steps))
    return lax.ppermute(value, axis, [(source, source + steps) for source in range(initial, last)])


def angle_table(row_count, col_count, period, sign):
    row_index = lax.iota(jnp.int32, row_count)[:, None]
    col_index = lax.iota(jnp.int32, col_count)[None, :]
    angles = (row_index * col_index % period).astype(jnp.float32) * (sign * 2.0 * math.pi / period)
    return (jnp.cos(angles), jnp.sin(angles))


def forward_spectrum(signal_rows, first, second):
    channels = signal_rows.shape[0]
    grid_rows = signal_rows.reshape(channels, first, second)
    cos_first, sin_first = angle_table(first, first, first, -1.0)
    part_re = jnp.einsum("cab,ak->ckb", grid_rows, cos_first, precision=HIGHEST)
    part_im = jnp.einsum("cab,ak->ckb", grid_rows, sin_first, precision=HIGHEST)
    twist_cos, twist_sin = angle_table(first, second, first * second, -1.0)
    part_re, part_im = (
        part_re * twist_cos - part_im * twist_sin,
        part_re * twist_sin + part_im * twist_cos,
    )
    cos_second, sin_second = angle_table(second, second, second, -1.0)
    spectrum_real = jnp.einsum("ckb,bm->ckm", part_re, cos_second, precision=HIGHEST) - jnp.einsum(
        "ckb,bm->ckm", part_im, sin_second, precision=HIGHEST
    )
    spec_im = jnp.einsum("ckb,bm->ckm", part_re, sin_second, precision=HIGHEST) + jnp.einsum(
        "ckb,bm->ckm", part_im, cos_second, precision=HIGHEST
    )
    return (spectrum_real, spec_im)


def inverse_spectrum(spectrum_real, spec_im, first, second):
    channels = spectrum_real.shape[0]
    cos_second, sin_second = angle_table(second, second, second, 1.0)
    part_re = jnp.einsum("ckm,bm->ckb", spectrum_real, cos_second, precision=HIGHEST) - jnp.einsum(
        "ckm,bm->ckb", spec_im, sin_second, precision=HIGHEST
    )
    part_im = jnp.einsum("ckm,bm->ckb", spectrum_real, sin_second, precision=HIGHEST) + jnp.einsum(
        "ckm,bm->ckb", spec_im, cos_second, precision=HIGHEST
    )
    twist_cos, twist_sin = angle_table(first, second, first * second, 1.0)
    part_re, part_im = (
        part_re * twist_cos - part_im * twist_sin,
        part_re * twist_sin + part_im * twist_cos,
    )
    cos_first, sin_first = angle_table(first, first, first, 1.0)
    result = jnp.einsum("ckb,ak->cab", part_re, cos_first, precision=HIGHEST) - jnp.einsum(
        "ckb,ak->cab", part_im, sin_first, precision=HIGHEST
    )
    return result.reshape(channels, first * second) / (first * second)


def spectral_conv(signal_rows, filter_rows):
    channels, length = signal_rows.shape
    padded_len = 2 * length
    log_len = padded_len.bit_length() - 1
    first = 1 << log_len // 2
    second = padded_len // first
    zeros_tail = jnp.zeros((channels, length), jnp.float32)
    sig_re, sig_im = forward_spectrum(
        jnp.concatenate([signal_rows, zeros_tail], axis=1), first, second
    )
    tap_re, tap_im = forward_spectrum(
        jnp.concatenate([filter_rows, zeros_tail], axis=1), first, second
    )
    prod_re = sig_re * tap_re - sig_im * tap_im
    prod_im = sig_re * tap_im + sig_im * tap_re
    return inverse_spectrum(prod_re, prod_im, first, second)[:, :length]


def short_filter_output(projected, rim_cells, kernel_coefficients):
    count = kernel_coefficients.shape[0]
    steps_len = projected.shape[2]
    extended = jnp.concatenate([rim_cells, projected], axis=2).astype(jnp.float32)
    total = jnp.zeros(projected.shape, jnp.float32)
    for tap in range(count):
        total = (
            total
            + kernel_coefficients[tap][:, :, None]
            * extended[:, :, count - 1 - tap : count - 1 - tap + steps_len]
        )
    return total.astype(jnp.bfloat16)


def hyena_mixer(keys_rows, values_rows, long_taps, skip_part):
    middle = keys_rows.astype(jnp.float32) * values_rows.astype(jnp.float32)
    return (spectral_conv(middle, long_taps) + skip_part[:, None] * middle).astype(jnp.bfloat16)


def body(tokens, norm_gain, proj_weight, short_filter, long_filter, skip_gain, out_weight):
    seq_count = lax.axis_size("seq")
    local_rows = tokens.shape[0]
    local_chan = proj_weight.shape[2]
    subset = local_chan // seq_count
    length = local_rows * seq_count
    offset = lax.axis_index("seq") * subset
    whole = lax.all_gather(tokens, "chan", axis=1, tiled=True)
    wide = whole.astype(jnp.float32)
    rescaled_signal = (
        wide * lax.rsqrt(jnp.mean(wide * wide, axis=1, keepdims=True) + EPSILON) * norm_gain
    ).astype(jnp.bfloat16)
    projected = lax.dot_general(
        lax.all_gather(proj_weight, "seq", axis=0, tiled=True),
        rescaled_signal,
        (((0,), (1,)), ((), ())),
        preferred_element_type=jnp.float32,
    ).astype(jnp.bfloat16)
    taps_grid = long_filter.reshape(1, seq_count, subset, local_rows)
    long_taps = lax.all_to_all(taps_grid, "seq", split_axis=1, concat_axis=3, tiled=True).reshape(
        subset, length
    )
    skip_part = lax.dynamic_slice_in_dim(skip_gain, offset, subset, 0)
    rim_cells = from_behind(projected[:, :, local_rows - (SHORT - 1) :], "seq", 1)
    featured = short_filter_output(projected, rim_cells, short_filter)
    pair_grid = featured[1:].reshape(2, seq_count, subset, local_rows)
    moved = lax.all_to_all(pair_grid, "seq", split_axis=1, concat_axis=3, tiled=True).reshape(
        2, subset, length
    )
    result = hyena_mixer(moved[0], moved[1], long_taps, skip_part)
    returned = lax.all_to_all(
        result.reshape(1, subset, length), "seq", split_axis=2, concat_axis=0, tiled=True
    )
    returned = returned.reshape(local_chan, local_rows)
    gated = (featured[0].astype(jnp.float32) * returned.astype(jnp.float32)).astype(jnp.bfloat16)
    full_mix = lax.all_gather(gated, "chan", axis=0, tiled=True)
    update = lax.dot_general(
        full_mix, out_weight, (((0,), (0,)), ((), ())), preferred_element_type=jnp.float32
    )
    return (tokens.astype(jnp.float32) + update).astype(jnp.bfloat16)

LANES = 128
BLOCK = 128
SPAN = 512
TOKEN_CHUNKS = 8
WEIGHT_CHUNKS = 4
HBM = pl.BlockSpec(memory_space=pltpu.HBM)


def remote(src, dst, send_sem, recv_sem, where):
    return pltpu.make_async_remote_copy(
        src_ref=src,
        dst_ref=dst,
        send_sem=send_sem,
        recv_sem=recv_sem,
        device_id=where,
        device_id_type=pl.DeviceIdType.MESH,
    )


class Line:
    def __init__(self, view, count, send_sem, recv_sem, place):
        self.view, self.count, self.place = view, count, place
        self.send_sem, self.recv_sem = send_sem, recv_sem
        self.me = lax.axis_index("chan")

    def move(self, way, step, piece, block, target):
        recv = self.recv_sem.at[(way, step) + piece]
        return remote(block, block, self.send_sem.at[way, step], recv, self.place(target))

    def drain(self, way, step, first, block):
        self.move(way, step, first, block(self.source(way, step - 1)), self.me).wait_send()

    def source(self, way, step):
        return jnp.clip(self.me - (step + 1) * (1 - 2 * way), 0, self.count - 1)

    def copy(self, way, step, piece):
        owner = self.source(way, step - 1)
        target = self.source(way, -2)
        return self.move(way, step, piece, self.view(owner, *piece), target)

    def inside(self, way, by):
        place = self.me + by * (1 - 2 * way)
        return (place >= 0) & (place < self.count)

    def sends(self, way, step):
        return self.inside(way, -step) & self.inside(way, 1)

    def receives(self, way, step):
        return self.inside(way, -1 - step)

    def arrived(self, way, step, piece):
        owner = self.source(way, step)
        self.move(way, step, piece, self.view(owner, *piece), self.me).wait_recv()
        return owner


def block_kernel(
    chan_count,
    tokens,
    gain_hbm,
    weights,
    short_hbm,
    long_taps,
    skip_hbm,
    out_weight,
    result,
    gain,
    short,
    skip,
    stream,
    weight,
    sums,
    scale,
    partial,
    table,
    taps,
    spectra,
    freq,
    mixed,
    edge_out,
    edge,
    extended,
    query,
    signal,
    before,
    ready,
    full,
    total,
    local_sem,
    mate_send,
    mate_recv,
    token_send,
    token_recv,
    sums_send,
    sums_recv,
    x_send,
    x_recv,
    y_send,
    y_recv,
    tap_send,
    tap_recv,
    edge_send,
    edge_recv,
    before_send,
    before_recv,
    swap_send,
    swap_recv,
    line_send,
    line_recv,
):
    y, s, z = (lax.axis_index(name) for name in ("groups", "seq", "chan"))
    x, core = s // 2, s % 2
    mate_s = s + 1 - 2 * core
    mate = (y, mate_s, z)
    across = (y, (1 - x) * 2 + core, z)
    aslant = (y, (1 - x) * 2 + 1 - core, z)
    beside = (1 - y, s, z)
    rows, width = tokens.shape
    length = 2 * rows
    branches, depth = weights.shape[0], weights.shape[1]
    half = depth // 2
    share = weights.shape[2] // 2
    groups = share // LANES
    rim = edge.shape[2]
    steps = chan_count - 1
    token_rows = rows // TOKEN_CHUNKS
    weight_rows = half // WEIGHT_CHUNKS

    column_peers = [mate] + [
        (y, 2 * x + of, lax.rem(z + by, chan_count))
        for by in range(1, chan_count)
        for of in (core, 1 - core)
    ]
    peers = column_peers + [across, aslant, beside]

    def rows_at(i, count, base=0):
        return pl.ds(pl.multiple_of(base + i * count, count), count)

    def at_rows(i):
        return rows_at(i, BLOCK)

    def blocks(count):
        return pl.loop(0, count // BLOCK)

    def lanes_of(base, g):
        return pl.ds(pl.multiple_of(base + g * LANES, LANES), LANES)

    tap_stage = [(0, 0), (0, length), (1, 0), (1, length)]
    tap_loads = [
        pltpu.make_async_copy(
            long_taps.at[:, pl.ds(j * LANES, LANES)],
            freq.at[which, pl.ds(start, length)],
            local_sem.at[4 + j],
        )
        for j, (which, start) in enumerate(tap_stage)
    ]
    token_load = pltpu.make_async_copy(tokens, result, local_sem.at[0])
    token_load.start()
    small_loads = [
        pltpu.make_async_copy(src, dst, local_sem.at[at])
        for src, dst, at in (
            (gain_hbm.at[:, pl.ds(pl.multiple_of(z * width, width), width)], gain, 3),
            (short_hbm, short, 8),
            (skip_hbm, skip, 9),
        )
    ]
    for copy in small_loads:
        copy.start()
    barrier = pltpu.get_barrier_semaphore()
    for peer in peers:
        pl.semaphore_signal(barrier, inc=1, device_id=peer, device_id_type=pl.DeviceIdType.MESH)
    for copy in tap_loads:
        copy.start()
    for g in range(groups):
        for b in range(branches):
            pltpu.make_async_copy(
                weights.at[b, :, lanes_of(core * share, g)],
                weight.at[g, s, :, pl.ds(b * LANES, LANES)],
                local_sem.at[2],
            ).start()

    sums[core, z] = jnp.zeros(sums.shape[2:], jnp.float32)
    small_loads[0].wait()
    own_gain = gain[...]
    token_load.wait()

    @blocks(rows)
    def _(i):
        raw = result[at_rows(i), :].astype(jnp.float32)
        total[at_rows(i), :] = raw
        stream[z, pl.ds(pl.multiple_of(core * rows + i * BLOCK, BLOCK), BLOCK), :] = (
            raw * own_gain
        ).astype(jnp.bfloat16)
        square = raw * raw
        found = square[:, :LANES]
        for part in range(1, width // LANES):
            found = found + square[:, part * LANES : (part + 1) * LANES]
        sums[core, z, pl.ds(i, 1), :] = jnp.sum(found.T, axis=0, keepdims=True)

    pl.semaphore_wait(barrier, len(peers))

    def token_view(owner, chunk):
        return stream.at[owner, rows_at(chunk, token_rows, core * rows), :]

    token_line = Line(
        token_view, chan_count, token_send, token_recv, lambda to: (y, s, to)
    )
    for chunk in range(TOKEN_CHUNKS):
        for way in range(2):

            @pl.when(token_line.sends(way, 0))
            def _():
                token_line.copy(way, 0, (chunk,)).start()

    def own_half(owner, of):
        return stream.at[owner, pl.ds(pl.multiple_of(of * rows, rows), rows), :]

    def mate_tokens():
        return remote(
            own_half(z, core), own_half(z, core), mate_send.at[0], mate_recv.at[0], mate
        )

    mate_tokens().start()
    sum_copies = [
        remote(
            sums.at[core, z], sums.at[core, z], sums_send.at[at], sums_recv.at[core, z], peer
        )
        for at, peer in enumerate(column_peers)
    ]
    for copy in sum_copies:
        copy.start()
    for g in range(groups):
        for b in range(branches):
            remote(
                weights.at[b, :, lanes_of((1 - core) * share, g)],
                weight.at[g, s, :, pl.ds(b * LANES, LANES)],
                mate_send.at[1],
                mate_recv.at[1],
                mate,
            ).start()

    for j, (which, start) in enumerate(tap_stage):
        tap_loads[j].wait()

        @pl.loop(0, groups)
        def _(g):
            mine = freq[which, rows_at(core * groups + g, BLOCK, start), :]
            taps[g, pl.ds(pl.multiple_of(s * rows + j * LANES, LANES), LANES), :] = mine.T.astype(
                jnp.bfloat16
            )
            other = freq[which, rows_at((1 - core) * groups + g, BLOCK, start), :]
            ready[g, j * LANES : (j + 1) * LANES, :] = other.T.astype(jnp.bfloat16)

    def tap_part(owner, part):
        return taps.at[
            :, pl.ds(pl.multiple_of(owner * rows + part * (rows // 2), rows // 2), rows // 2), :
        ]

    def taps_across(to):
        src = tap_part(s, y) if to == 0 else ready.at[
            :, pl.ds(pl.multiple_of(y * (rows // 2), rows // 2), rows // 2), :
        ]
        return remote(
            src,
            tap_part(s, y),
            tap_send.at[to],
            tap_recv.at[core],
            across if to == 0 else aslant,
        )

    def taps_beside(origin, part):
        view = tap_part(origin, part)
        return remote(view, view, tap_send.at[2 + origin], tap_recv.at[2 + origin], beside)

    def taps_mate():
        return remote(
            ready,
            taps.at[:, pl.ds(pl.multiple_of(s * rows, rows), rows), :],
            mate_send.at[2],
            mate_recv.at[2],
            mate,
        )

    @pl.when(x == 0)
    def _():
        taps_across(0).start()
        taps_across(1).start()

        @pl.loop(0, groups)
        def _(g):
            taps[g, length:, :] = jnp.zeros((length, LANES), jnp.bfloat16)

    taps_mate().start()

    def weight_view(owner, part, g, c):
        return weight.at[g, owner, rows_at(c, weight_rows, part * half), :]

    def weight_half(owner, part):
        return weight.at[:, owner, pl.ds(pl.multiple_of(part * half, half), half), :]

    def send_weights(g, chunks=range(WEIGHT_CHUNKS)):
        for c in chunks:
            for to in range(2):
                side = core if to == 0 else 1 - core
                view = weight_view(s, y, g, c)
                for b in range(branches):
                    remote(
                        weights.at[
                            b,
                            rows_at(c, weight_rows, y * half),
                            pl.ds(pl.multiple_of(side * share + g * LANES, LANES), LANES),
                        ],
                        view.at[:, pl.ds(b * LANES, LANES)],
                        x_send.at[to],
                        x_recv.at[core, g, c],
                        across if to == 0 else aslant,
                    ).start()

    for g in range(groups - 2):
        send_weights(g)
    send_weights(groups - 2, range(3))

    at_end = (z == 0) | (z == chan_count - 1)

    @pl.when((x == 1) | at_end)
    def _():
        send_weights(groups - 2, [3])
        send_weights(groups - 1, [0, 1])

    @pl.when(x == 1)
    def _():
        send_weights(groups - 1, [2, 3])

    def beside_copy(origin, part, g, c):
        view = weight_view((1 - x) * 2 + origin, part, g, c)
        return remote(view, view, y_send.at[origin], y_recv.at[origin, g], beside)

    def forward(g, c):
        for origin in range(2):
            view = weight_view((1 - x) * 2 + origin, y, g, c)
            remote(
                view, view, x_send.at[origin], x_recv.at[origin, g, c], beside
            ).wait_recv()
            beside_copy(origin, y, g, c).start()

    def await_beside(g):
        for origin in range(2):
            view = weight.at[
                g, (1 - x) * 2 + origin, pl.ds(pl.multiple_of((1 - y) * half, half), half), :
            ]
            remote(view, view, y_send.at[origin], y_recv.at[origin, g], beside).wait_recv()

    @blocks(length)
    def _(i):
        row = lax.broadcasted_iota(jnp.int32, (BLOCK, LANES), 0) + i * BLOCK
        lane = lax.broadcasted_iota(jnp.int32, (BLOCK, LANES), 1)
        unit = math.pi / (4 * length)
        odd = 2 * row + 1
        small = odd.astype(jnp.float32) * unit
        extended[0, at_rows(i), :] = jnp.cos(small)
        extended[1, at_rows(i), :] = jnp.sin(small)
        period = 8 * length
        angle = (odd * (2 * lane + 1) % period).astype(jnp.float32) * unit
        cos, sin = jnp.cos(angle), jnp.sin(angle)
        stride = (odd * (2 * LANES) % period).astype(jnp.float32) * unit
        step_cos, step_sin = jnp.cos(stride), jnp.sin(stride)
        for a in range(length // LANES):
            table[at_rows(i), a * LANES : (a + 1) * LANES] = cos.astype(jnp.bfloat16)
            table[rows_at(i, BLOCK, length), a * LANES : (a + 1) * LANES] = sin.astype(
                jnp.bfloat16
            )
            cos, sin = cos * step_cos - sin * step_sin, sin * step_cos + cos * step_sin

    for g in range(groups):

        @blocks(length)
        def _(i):
            partial[g, at_rows(i), :] = jnp.zeros((BLOCK, branches * LANES), jnp.float32)

    def spectrum(which, column):
        @pl.loop(0, 2 * length // SPAN)
        def _(i):
            at = rows_at(i, SPAN)
            freq[which, at, :] = jnp.dot(
                table[at, :], column(), preferred_element_type=jnp.float32
            )

    def spectrum_pair(columns):
        @pl.loop(0, 2 * length // SPAN)
        def _(i):
            at = rows_at(i, SPAN)
            found = jnp.dot(
                table[at, :],
                jnp.concatenate(columns(), axis=1),
                preferred_element_type=jnp.float32,
            )
            freq[0, at, :] = found[:, :LANES]
            freq[1, at, :] = found[:, LANES:]

    def tap_spectra(g):
        spectrum_pair(lambda: [taps[g, :length, :], taps[g, length:, :]])

        @blocks(length)
        def _(i):
            low, high = at_rows(i), rows_at(i, BLOCK, length)
            cos, sin = extended[0, low, :], extended[1, low, :]

            def turned(which):
                real, imag = freq[which, low, :], -freq[which, high, :]
                return (cos * real - sin * imag) / length, (cos * imag + sin * real) / length

            real, imag = turned(0)
            late_real, late_imag = turned(1)
            place = lax.broadcasted_iota(jnp.int32, (BLOCK, LANES), 0)
            sign = (1 - 2 * (place % 2)).astype(jnp.float32)
            spectra[g, 0, low, :] = real.astype(jnp.bfloat16)
            spectra[g, 1, low, :] = imag.astype(jnp.bfloat16)
            spectra[g, 2, low, :] = (late_real - sign * imag).astype(jnp.bfloat16)
            spectra[g, 3, low, :] = (late_imag + sign * real).astype(jnp.bfloat16)

    def project(g, owner):
        @pl.loop(0, length // SPAN)
        def _(i):
            at = rows_at(i, SPAN)
            partial[g, at, :] += jnp.dot(
                stream[owner, at, :], weight[g, owner], preferred_element_type=jnp.float32
            )

    def projects_early(g, owner):
        far = jnp.abs(z - owner)
        own = owner // 2 == x
        return (
            (own & ((far <= 1) | ((far == 2) & (at_end | (g == 0)))))
            | (jnp.logical_not(own) & (far <= 2) & ((g == 0) | ((g == 1) & at_end)))
        )

    def to_mate(way, step, chunk):
        block = token_view(token_line.source(way, step), chunk)
        index = 3 + way * steps + step
        return remote(block, block, mate_send.at[index], mate_recv.at[index], mate)

    def mate_half(way, step, of):
        block = own_half(token_line.source(way, step), of)
        index = 3 + way * steps + step
        return remote(block, block, mate_send.at[index], mate_recv.at[index], mate)

    def await_mate(step):
        for way in range(2):

            @pl.when(token_line.receives(way, step))
            def _():
                mate_half(way, step, 1 - core).wait_recv()

    @pl.loop(0, steps * TOKEN_CHUNKS)
    def _(tick):
        step, chunk = tick // TOKEN_CHUNKS, tick % TOKEN_CHUNKS
        for way in range(2):

            @pl.when(token_line.receives(way, step))
            def _():
                token_line.arrived(way, step, (chunk,))
                to_mate(way, step, chunk).start()

            @pl.when(
                (step + 1 < steps)
                & token_line.receives(way, step)
                & token_line.sends(way, step + 1)
            )
            def _():
                token_line.copy(way, step + 1, (chunk,)).start()

        @pl.when((tick == TOKEN_CHUNKS // 2) & (x == 1))
        def _():
            for origin in range(2):
                view = tap_part(origin, y)
                remote(
                    view, view, tap_send.at[origin], tap_recv.at[origin], beside
                ).wait_recv()
                taps_beside(origin, y).start()

        @pl.when((tick % 2 == 1) & (tick >= 3) & (tick < 7 + 4 * WEIGHT_CHUNKS))
        def _():
            at = (tick - 3) // 2
            forward(at // WEIGHT_CHUNKS, at % WEIGHT_CHUNKS)

        @pl.when(tick == TOKEN_CHUNKS)
        def _():
            mate_half_own = own_half(z, 1 - core)
            remote(
                mate_half_own, mate_half_own, mate_send.at[0], mate_recv.at[0], mate
            ).wait_recv()
            await_mate(0)
            pltpu.make_async_copy(
                weight.at[:, s], weight.at[:, s], local_sem.at[2]
            ).wait()
            other = weight.at[:, mate_s]
            remote(other, other, mate_send.at[1], mate_recv.at[1], mate).wait_recv()
            other = taps.at[:, pl.ds(pl.multiple_of(mate_s * rows, rows), rows), :]
            remote(other, other, mate_send.at[2], mate_recv.at[2], mate).wait_recv()

            @pl.when(x == 1)
            def _():
                for origin in range(2):
                    taps_beside(origin, 1 - y).wait_recv()

        @pl.when((step == 1) & (chunk % 2 == 0))
        def _():
            tap_spectra(chunk // 2)

        @pl.when(tick == 2 * TOKEN_CHUNKS)
        def _():
            await_mate(1)

        owner = 2 * x + chunk // groups
        far = jnp.abs(z - owner)

        @pl.when(
            projects_early(chunk % groups, owner)
            & (((step == 1) & (far <= 1)) | ((step == 2) & (far == 2)))
        )
        def _():
            project(chunk % groups, owner)

        @pl.when(tick == 2 * TOKEN_CHUNKS)
        def _():
            await_beside(0)

        @pl.when((tick == 2 * TOKEN_CHUNKS + TOKEN_CHUNKS // 2) & at_end)
        def _():
            await_beside(1)

        guest = 2 * (1 - x) + (chunk // 2) % 2

        @pl.when((step == 2) & (chunk % 2 == 0) & projects_early(chunk // 4, guest))
        def _():
            project(chunk // 4, guest)

    await_mate(2)
    for by in range(1, chan_count):
        for of in range(2):
            view = sums.at[of, lax.rem(z + by, chan_count)]
            remote(
                view, view, sums_send.at[0], sums_recv.at[of, lax.rem(z + by, chan_count)], mate
            ).wait_recv()
    view = sums.at[1 - core, z]
    remote(view, view, sums_send.at[0], sums_recv.at[1 - core, z], mate).wait_recv()

    @blocks(length)
    def _(i):
        of, at = i // (rows // BLOCK), i % (rows // BLOCK)
        found = sums[of, 0, pl.ds(at, 1), :]
        for owner in range(1, chan_count):
            found = found + sums[of, owner, pl.ds(at, 1), :]
        found = lax.rsqrt(found / (chan_count * width) + EPSILON)
        scale[at_rows(i), :] = jnp.broadcast_to(found, (BLOCK, LANES)).T

    taps_mate().wait_send()

    @pl.when(x == 0)
    def _():
        taps_across(0).wait_send()
        taps_across(1).wait_send()

    def edge_copy(g):
        return remote(
            edge_out.at[g], edge.at[g], edge_send.at[0], edge_recv.at[g], across
        )

    def before_copy(g):
        return remote(
            signal.at[g], before.at[g], before_send.at[0], before_recv.at[g], across
        )

    def swap_copy(g):
        return remote(
            ready.at[g], full.at[z, g, core], swap_send.at[0], swap_recv.at[g], mate
        )

    line = Line(
        lambda owner, g, of: full.at[owner, g, of],
        chan_count,
        line_send,
        line_recv,
        lambda to: (y, s, to),
    )

    def projected(g, b, at):
        return (partial[g, at, b * LANES : (b + 1) * LANES] * scale[at, :]).astype(jnp.bfloat16)

    def featurize(g):
        @pl.when(x == 0)
        def _():
            for b in range(branches):
                edge_out[g, b] = projected(g, b, pl.ds(length - rim, rim))
                extended[b, 0:rim, :] = jnp.zeros((rim, LANES), jnp.float32)
            edge_copy(g).start()

        @blocks(length)
        def _(i):
            for b in range(branches):
                extended[b, pl.ds(pl.multiple_of(rim + i * BLOCK, rim), BLOCK), :] = projected(
                    g, b, at_rows(i)
                ).astype(jnp.float32)

        @pl.when(x == 1)
        def _():
            edge_copy(g).wait_recv()
            for b in range(branches):
                extended[b, 0:rim, :] = edge[g, b].astype(jnp.float32)

        chosen = lanes_of(core * share, g)
        coefficient = [
            [short[tap, b : b + 1, chosen] for b in range(branches)] for tap in range(SHORT)
        ]

        @blocks(length)
        def _(i):
            found = []
            for b in range(branches):
                value = jnp.zeros((BLOCK, LANES), jnp.float32)
                for tap in range(SHORT):
                    value = value + coefficient[tap][b] * extended[
                        b, pl.ds(rim - tap + i * BLOCK, BLOCK), :
                    ]
                found.append(value.astype(jnp.bfloat16))
            query[at_rows(i), :] = found[0]
            signal[g, at_rows(i), :] = (
                found[1].astype(jnp.float32) * found[2].astype(jnp.float32)
            ).astype(jnp.bfloat16)

    def convolve(g):
        joint = (x == 1) & (g > 0)

        @pl.when(jnp.logical_not(joint))
        def _():
            spectrum(0, lambda: signal[g])

        def product(i, which, first):
            low, high = at_rows(i), rows_at(i, BLOCK, length)
            cos, sin = freq[which, low, :], freq[which, high, :]
            real = spectra[g, first, low, :].astype(jnp.float32)
            imag = spectra[g, first + 1, low, :].astype(jnp.float32)
            return cos * real + sin * imag, sin * real - cos * imag

        @pl.when(x == 0)
        def _():
            @blocks(length)
            def _(i):
                real, imag = product(i, 0, 0)
                mixed[at_rows(i), :] = real.astype(jnp.bfloat16)
                mixed[rows_at(i, BLOCK, length), :] = imag.astype(jnp.bfloat16)

        @pl.when(x == 1)
        def _():
            before_copy(g).wait_recv()

            @pl.when(g == 0)
            def _():
                spectrum(1, lambda: before[g])

            @pl.when(g > 0)
            def _():
                spectrum_pair(lambda: [signal[g], before[g]])

            @blocks(length)
            def _(i):
                real, imag = product(i, 0, 0)
                more_real, more_imag = product(i, 1, 2)
                mixed[at_rows(i), :] = (real + more_real).astype(jnp.bfloat16)
                mixed[rows_at(i, BLOCK, length), :] = (imag + more_imag).astype(jnp.bfloat16)

        @pl.loop(0, length // SPAN)
        def _(i):
            low, high = rows_at(i, SPAN), rows_at(i, SPAN, length)
            freq[0, low, :] = jnp.dot(
                table[low, :], mixed[:length, :], preferred_element_type=jnp.float32
            ) + jnp.dot(table[high, :], mixed[length:, :], preferred_element_type=jnp.float32)

        direct = skip[:, lanes_of(core * share, g)]

        def gated(at):
            longer = freq[0, at, :] + direct * signal[g, at, :].astype(jnp.float32)
            longer = longer.astype(jnp.bfloat16).astype(jnp.float32)
            return (query[at, :].astype(jnp.float32) * longer).astype(jnp.bfloat16)

        @blocks(rows)
        def _(i):
            full[z, g, core, at_rows(i), :] = gated(
                pl.ds(pl.multiple_of(core * rows + i * BLOCK, BLOCK), BLOCK)
            )
            ready[g, at_rows(i), :] = gated(
                pl.ds(pl.multiple_of((1 - core) * rows + i * BLOCK, BLOCK), BLOCK)
            )

    def load_out():
        for owner in range(chan_count):
            pltpu.make_async_copy(
                out_weight.at[pl.ds(owner * length, length)], stream.at[owner], local_sem.at[1]
            ).start()

    def accumulate(owner, g):
        @pl.loop(0, total.shape[1] // (2 * LANES))
        def _(i):
            cols = rows_at(i, 2 * LANES)
            block = jnp.concatenate([full[owner, g, 0], full[owner, g, 1]], axis=1)
            kernel = jnp.concatenate(
                [stream[owner, lanes_of(of * share, g), cols] for of in range(2)], axis=0
            )
            total[:, cols] += jnp.dot(block, kernel, preferred_element_type=jnp.float32)

    def begin(g):
        swap_copy(g).start()
        for way in range(2):

            @pl.when(line.sends(way, 0))
            def _():
                line.copy(way, 0, (g, core)).start()

    def begin_other(g):
        other = full.at[z, g, 1 - core]
        remote(other, other, swap_send.at[0], swap_recv.at[g], mate).wait_recv()
        for way in range(2):

            @pl.when(line.sends(way, 0))
            def _():
                line.copy(way, 0, (g, 1 - core)).start()

    def settle():
        other = weight.at[:, s]
        remote(other, other, mate_send.at[1], mate_recv.at[1], mate).wait_send()
        for copy in sum_copies:
            copy.wait_send()

        @pl.when(x == 1)
        def _():
            for origin in range(2):
                taps_beside(origin, y).wait_send()

        for at in range(2):
            view = weight_half(s, y)
            remote(view, view, x_send.at[at], x_recv.at[0, 0, 0], across).wait_send()
            view = weight_half((1 - x) * 2 + at, y)
            remote(view, view, y_send.at[at], y_recv.at[at, 0], beside).wait_send()

        @pl.when(x == 0)
        def _():
            remote(edge_out, edge, edge_send.at[0], edge_recv.at[0], across).wait_send()
            remote(signal, before, before_send.at[0], before_recv.at[0], across).wait_send()

    def settle_tokens():
        mate_tokens().wait_send()
        for way in range(2):
            for step in range(steps):

                @pl.when(token_line.receives(way, step))
                def _():
                    mate_half(way, step, core).wait_send()

                @pl.when(token_line.sends(way, step))
                def _():
                    token_line.drain(way, step, (0,), lambda owner: own_half(owner, core))

    def way_of(k):
        return jnp.where(z < chan_count // 2, 1 - k, k)

    def late_forwards(g, at, inner, outer):
        for here, pieces in ((jnp.logical_not(at_end), inner), (at_end, outer)):

            @pl.when((g == at) & here)
            def _():
                for group, c in pieces:
                    forward(group, c)

    def pass_on(way, step, at):
        @pl.when(
            (at >= 0) & (at < groups) & line.receives(way, step) & line.sends(way, step + 1)
        )
        def _():
            for of in (core, 1 - core):
                line.arrived(way, step, (at, of))
                line.copy(way, step + 1, (at, of)).start()

    for copy in small_loads[1:]:
        copy.wait()
    near, away = way_of(0), way_of(1)

    @pl.loop(0, groups)
    def _(g):
        @pl.when(g == 3)
        def _():
            pass_on(away, 0, 1)
            pass_on(near, 0, 2)

        @pl.when((g >= 2) | ((g == 1) & jnp.logical_not(at_end)))
        def _():
            await_beside(g)

        @pl.loop(0, chan_count)
        def _(owner):
            @pl.when(jnp.logical_not(projects_early(g, owner)))
            def _():
                project(g, owner)

        @pl.when(g == groups - 1)
        def _():
            settle_tokens()
            load_out()

        featurize(g)

        @pl.when(x == 0)
        def _():
            before_copy(g).start()

            for at, inner, outer in (
                (0, [], [(groups - 1, 2)]),
                (1, [(groups - 2, 3), (groups - 1, 0), (groups - 1, 1)], [(groups - 1, 3)]),
                (2, [(groups - 1, 2), (groups - 1, 3)], []),
            ):

                @pl.when((g == at) & jnp.logical_not(at_end))
                def _():
                    for group, c in inner:
                        send_weights(group, [c])

                @pl.when((g == at) & at_end)
                def _():
                    for group, c in outer:
                        send_weights(group, [c])

        late_forwards(g, 1, [(groups - 2, 3)], [(groups - 1, 0), (groups - 1, 1)])
        late_forwards(g, 2, [(groups - 1, 0), (groups - 1, 1)], [(groups - 1, 3)])

        @pl.when((g == 1) | (g == 2))
        def _():
            pass_on(near, 0, g - 1)

        @pl.when(g == 2)
        def _():
            pass_on(away, 0, 0)

        late_forwards(g, 0, [(groups - 2, 2)], [(groups - 2, 2), (groups - 2, 3)])
        convolve(g)
        begin(g)
        late_forwards(g, 1, [], [(groups - 1, 2)])
        begin_other(g)

        late_forwards(g, 2, [(groups - 1, 2)], [])

        @pl.when(g == 2)
        def _():
            pass_on(near, 1, 0)

        late_forwards(g, 2, [(groups - 1, 3)], [])

    pltpu.make_async_copy(stream, stream, local_sem.at[1]).wait()

    @pl.loop(0, groups + steps - 1)
    def _(n):
        for at, pieces in (
            (0, [(near, 1, 1), (away, 0, 2)]),
            (1, [(near, 0, 3), (near, 1, 2), (away, 0, 3)]),
            (3, [(near, 1, 3)]),
        ):

            @pl.when(n == at)
            def _():
                for way, step, group in pieces:
                    pass_on(way, step, group)

        @pl.when(n == 2)
        def _():
            settle()

        @pl.when(n < groups)
        def _():
            accumulate(z, n)

        @pl.loop(0, 2)
        def _(way):
            for step in range(steps):
                at = n - jnp.where(at_end, step, 0)

                @pl.when((at >= 0) & (at < groups) & line.receives(way, step))
                def _():
                    @pl.when(jnp.logical_not(line.sends(way, step + 1)))
                    def _():
                        for of in range(2):
                            line.arrived(way, step, (at, of))

                    accumulate(line.source(way, step), at)

    @blocks(rows)
    def _(i):
        result[at_rows(i), :] = total[at_rows(i), :].astype(jnp.bfloat16)

    remote(ready, ready, swap_send.at[0], swap_recv.at[0], mate).wait_send()
    for way in range(2):
        for step in range(steps):

            @pl.when(line.sends(way, step))
            def _():
                line.drain(way, step, (0, 0), lambda owner: full.at[owner])


def chip_body(tokens, norm_gain, proj_weight, short_filter, long_filter, skip_gain, out_weight):
    chan_count = lax.axis_size("chan")
    rows, width = tokens.shape
    depth, branches, local_chan = proj_weight.shape
    length, share = 2 * rows, local_chan // 2
    groups = share // LANES
    steps = chan_count - 1
    dma = pltpu.SemaphoreType.DMA
    f32, bf16 = jnp.float32, jnp.bfloat16
    vmem = pl.BlockSpec(memory_space=pltpu.VMEM)
    return pl.pallas_call(
        functools.partial(block_kernel, chan_count),
        out_shape=jax.ShapeDtypeStruct((rows, width), bf16),
        in_specs=[HBM] * 7,
        out_specs=vmem,
        scratch_shapes=[
            pltpu.VMEM((1, width), f32),
            pltpu.VMEM(short_filter.shape, f32),
            pltpu.VMEM((1, local_chan), f32),
            pltpu.VMEM((chan_count, length, width), bf16),
            pltpu.VMEM((groups, 4, depth, branches * LANES), bf16),
            pltpu.VMEM((2, chan_count, 8, LANES), f32),
            pltpu.VMEM((length, LANES), f32),
            pltpu.VMEM((groups, length, branches * LANES), f32),
            pltpu.VMEM((2 * length, length), bf16),
            pltpu.VMEM((groups, 2 * length, LANES), bf16),
            pltpu.VMEM((groups, 4, length, LANES), bf16),
            pltpu.VMEM((2, 2 * length, LANES), f32),
            pltpu.VMEM((2 * length, LANES), bf16),
            pltpu.VMEM((groups, branches, 16, LANES), bf16),
            pltpu.VMEM((groups, branches, 16, LANES), bf16),
            pltpu.VMEM((branches, length + 16, LANES), f32),
            pltpu.VMEM((length, LANES), bf16),
            pltpu.VMEM((groups, length, LANES), bf16),
            pltpu.VMEM((groups, length, LANES), bf16),
            pltpu.VMEM((groups, rows, LANES), bf16),
            pltpu.VMEM((chan_count, groups, 2, rows, LANES), bf16),
            pltpu.VMEM((rows, width), f32),
            dma((10,)),
            dma((3 + 2 * steps,)),
            dma((3 + 2 * steps,)),
            dma((2, steps)),
            dma((2, steps, TOKEN_CHUNKS)),
            dma((2 * chan_count - 1,)),
            dma((2, chan_count)),
            dma((2,)),
            dma((2, groups, WEIGHT_CHUNKS)),
            dma((2,)),
            dma((2, groups)),
            dma((4,)),
            dma((4,)),
            dma((1,)),
            dma((groups,)),
            dma((1,)),
            dma((groups,)),
            dma((1,)),
            dma((groups,)),
            dma((2, steps)),
            dma((2, steps, groups, 2)),
        ],
        compiler_params=pltpu.CompilerParams(
            collective_id=0, has_side_effects=True, vmem_limit_bytes=52 * 1024 * 1024
        ),
        name="block",
    )(
        tokens,
        pltpu.with_memory_space_constraint(norm_gain[None, :], pltpu.HBM),
        proj_weight.transpose(1, 0, 2),
        pltpu.with_memory_space_constraint(short_filter, pltpu.HBM),
        long_filter,
        pltpu.with_memory_space_constraint(skip_gain[None, :], pltpu.HBM),
        out_weight,
    )


def select_body(mesh):
    if (mesh.shape["groups"], mesh.shape["seq"], mesh.shape["chan"]) == (2, 4, 4):
        return chip_body
    return body


def solution(mesh):
    placed = (
        P(("groups", "seq"), "chan"),
        P(),
        P("seq", None, "chan"),
        P(None, None, "chan"),
        P("chan", "seq"),
        P("chan"),
        P(None, "chan"),
    )
    return jax.shard_map(
        select_body(mesh), mesh=mesh, in_specs=placed, out_specs=P(("groups", "seq"), "chan"), check_vma=False
    )
```

```python
import functools
import math

import jax
import jax.numpy as jnp
import numpy as np
from jax import lax
from jax.experimental import pallas as pl
from jax.experimental.pallas import tpu as pltpu
from jax.sharding import PartitionSpec as P

SHORT = 3


EPSILON = 1e-06
HIGHEST = lax.Precision.HIGHEST


def from_behind(value, axis, steps):
    count = lax.axis_size(axis)
    initial, last = (max(0, -steps), min(count, count - steps))
    return lax.ppermute(value, axis, [(source, source + steps) for source in range(initial, last)])


def angle_table(row_count, col_count, period, sign):
    row_index = lax.iota(jnp.int32, row_count)[:, None]
    col_index = lax.iota(jnp.int32, col_count)[None, :]
    angles = (row_index * col_index % period).astype(jnp.float32) * (sign * 2.0 * math.pi / period)
    return (jnp.cos(angles), jnp.sin(angles))


def forward_spectrum(signal_rows, first, second):
    channels = signal_rows.shape[0]
    grid_rows = signal_rows.reshape(channels, first, second)
    cos_first, sin_first = angle_table(first, first, first, -1.0)
    part_re = jnp.einsum("cab,ak->ckb", grid_rows, cos_first, precision=HIGHEST)
    part_im = jnp.einsum("cab,ak->ckb", grid_rows, sin_first, precision=HIGHEST)
    twist_cos, twist_sin = angle_table(first, second, first * second, -1.0)
    part_re, part_im = (
        part_re * twist_cos - part_im * twist_sin,
        part_re * twist_sin + part_im * twist_cos,
    )
    cos_second, sin_second = angle_table(second, second, second, -1.0)
    spectrum_real = jnp.einsum("ckb,bm->ckm", part_re, cos_second, precision=HIGHEST) - jnp.einsum(
        "ckb,bm->ckm", part_im, sin_second, precision=HIGHEST
    )
    spec_im = jnp.einsum("ckb,bm->ckm", part_re, sin_second, precision=HIGHEST) + jnp.einsum(
        "ckb,bm->ckm", part_im, cos_second, precision=HIGHEST
    )
    return (spectrum_real, spec_im)


def inverse_spectrum(spectrum_real, spec_im, first, second):
    channels = spectrum_real.shape[0]
    cos_second, sin_second = angle_table(second, second, second, 1.0)
    part_re = jnp.einsum("ckm,bm->ckb", spectrum_real, cos_second, precision=HIGHEST) - jnp.einsum(
        "ckm,bm->ckb", spec_im, sin_second, precision=HIGHEST
    )
    part_im = jnp.einsum("ckm,bm->ckb", spectrum_real, sin_second, precision=HIGHEST) + jnp.einsum(
        "ckm,bm->ckb", spec_im, cos_second, precision=HIGHEST
    )
    twist_cos, twist_sin = angle_table(first, second, first * second, 1.0)
    part_re, part_im = (
        part_re * twist_cos - part_im * twist_sin,
        part_re * twist_sin + part_im * twist_cos,
    )
    cos_first, sin_first = angle_table(first, first, first, 1.0)
    result = jnp.einsum("ckb,ak->cab", part_re, cos_first, precision=HIGHEST) - jnp.einsum(
        "ckb,ak->cab", part_im, sin_first, precision=HIGHEST
    )
    return result.reshape(channels, first * second) / (first * second)


def spectral_conv(signal_rows, filter_rows):
    channels, length = signal_rows.shape
    padded_len = 2 * length
    log_len = padded_len.bit_length() - 1
    first = 1 << log_len // 2
    second = padded_len // first
    zeros_tail = jnp.zeros((channels, length), jnp.float32)
    sig_re, sig_im = forward_spectrum(
        jnp.concatenate([signal_rows, zeros_tail], axis=1), first, second
    )
    tap_re, tap_im = forward_spectrum(
        jnp.concatenate([filter_rows, zeros_tail], axis=1), first, second
    )
    prod_re = sig_re * tap_re - sig_im * tap_im
    prod_im = sig_re * tap_im + sig_im * tap_re
    return inverse_spectrum(prod_re, prod_im, first, second)[:, :length]


def short_filter_output(projected, rim_cells, kernel_coefficients):
    count = kernel_coefficients.shape[0]
    steps_len = projected.shape[2]
    extended = jnp.concatenate([rim_cells, projected], axis=2).astype(jnp.float32)
    total = jnp.zeros(projected.shape, jnp.float32)
    for tap in range(count):
        total = (
            total
            + kernel_coefficients[tap][:, :, None]
            * extended[:, :, count - 1 - tap : count - 1 - tap + steps_len]
        )
    return total.astype(jnp.bfloat16)


def hyena_mixer(keys_rows, values_rows, long_taps, skip_part):
    middle = keys_rows.astype(jnp.float32) * values_rows.astype(jnp.float32)
    return (spectral_conv(middle, long_taps) + skip_part[:, None] * middle).astype(jnp.bfloat16)


def body(tokens, norm_gain, proj_weight, short_filter, long_filter, skip_gain, out_weight):
    seq_count = lax.axis_size("seq")
    local_rows = tokens.shape[0]
    local_chan = proj_weight.shape[2]
    subset = local_chan // seq_count
    length = local_rows * seq_count
    offset = lax.axis_index("seq") * subset
    whole = lax.all_gather(tokens, "chan", axis=1, tiled=True)
    wide = whole.astype(jnp.float32)
    rescaled_signal = (
        wide * lax.rsqrt(jnp.mean(wide * wide, axis=1, keepdims=True) + EPSILON) * norm_gain
    ).astype(jnp.bfloat16)
    projected = lax.dot_general(
        lax.all_gather(proj_weight, "seq", axis=0, tiled=True),
        rescaled_signal,
        (((0,), (1,)), ((), ())),
        preferred_element_type=jnp.float32,
    ).astype(jnp.bfloat16)
    taps_grid = long_filter.reshape(1, seq_count, subset, local_rows)
    long_taps = lax.all_to_all(taps_grid, "seq", split_axis=1, concat_axis=3, tiled=True).reshape(
        subset, length
    )
    skip_part = lax.dynamic_slice_in_dim(skip_gain, offset, subset, 0)
    rim_cells = from_behind(projected[:, :, local_rows - (SHORT - 1) :], "seq", 1)
    featured = short_filter_output(projected, rim_cells, short_filter)
    pair_grid = featured[1:].reshape(2, seq_count, subset, local_rows)
    moved = lax.all_to_all(pair_grid, "seq", split_axis=1, concat_axis=3, tiled=True).reshape(
        2, subset, length
    )
    result = hyena_mixer(moved[0], moved[1], long_taps, skip_part)
    returned = lax.all_to_all(
        result.reshape(1, subset, length), "seq", split_axis=2, concat_axis=0, tiled=True
    )
    returned = returned.reshape(local_chan, local_rows)
    gated = (featured[0].astype(jnp.float32) * returned.astype(jnp.float32)).astype(jnp.bfloat16)
    full_mix = lax.all_gather(gated, "chan", axis=0, tiled=True)
    update = lax.dot_general(
        full_mix, out_weight, (((0,), (0,)), ((), ())), preferred_element_type=jnp.float32
    )
    return (tokens.astype(jnp.float32) + update).astype(jnp.bfloat16)

LANES = 128
BLOCK = 128
SPAN = 512
TOKEN_CHUNKS = 8
WEIGHT_CHUNKS = 4
HBM = pl.BlockSpec(memory_space=pltpu.HBM)


def remote(src, dst, send_sem, recv_sem, where):
    return pltpu.make_async_remote_copy(
        src_ref=src,
        dst_ref=dst,
        send_sem=send_sem,
        recv_sem=recv_sem,
        device_id=where,
        device_id_type=pl.DeviceIdType.MESH,
    )


class Line:
    def __init__(self, view, count, send_sem, recv_sem, place):
        self.view, self.count, self.place = view, count, place
        self.send_sem, self.recv_sem = send_sem, recv_sem
        self.me = lax.axis_index("chan")

    def move(self, way, step, piece, block, target):
        slot = jnp.minimum(jnp.where(way == 0, step, target + step), self.count - 2)
        recv = self.recv_sem.at[(slot,) + piece]
        return remote(block, block, self.send_sem.at[way, step], recv, self.place(target))

    def drain(self, way, step, first, block):
        self.move(way, step, first, block(self.source(way, step - 1)), self.me).wait_send()

    def source(self, way, step):
        return jnp.clip(self.me - (step + 1) * (1 - 2 * way), 0, self.count - 1)

    def copy(self, way, step, piece):
        owner = self.source(way, step - 1)
        target = self.source(way, -2)
        return self.move(way, step, piece, self.view(owner, *piece), target)

    def inside(self, way, by):
        place = self.me + by * (1 - 2 * way)
        return (place >= 0) & (place < self.count)

    def sends(self, way, step):
        return self.inside(way, -step) & self.inside(way, 1)

    def receives(self, way, step):
        return self.inside(way, -1 - step)

    def arrived(self, way, step, piece):
        owner = self.source(way, step)
        self.move(way, step, piece, self.view(owner, *piece), self.me).wait_recv()
        return owner


def block_kernel(
    chan_count,
    tokens,
    gain_hbm,
    weights,
    short_hbm,
    long_taps,
    skip_hbm,
    out_weight,
    result,
    gain,
    short,
    skip,
    stream,
    weight,
    sums,
    scale,
    partial,
    table,
    taps,
    spectra,
    freq,
    mixed,
    edge_out,
    edge,
    extended,
    query,
    signal,
    before,
    ready,
    full,
    total,
    local_sem,
    mate_send,
    mate_recv,
    token_send,
    token_recv,
    sums_send,
    sums_recv,
    x_send,
    x_recv,
    y_send,
    y_recv,
    tap_send,
    tap_recv,
    edge_send,
    edge_recv,
    before_send,
    before_recv,
    swap_send,
    swap_recv,
    line_send,
    line_recv,
):
    y, s, z = (lax.axis_index(name) for name in ("groups", "seq", "chan"))
    x, core = s // 2, s % 2
    mate_s = s + 1 - 2 * core
    mate = (y, mate_s, z)
    across = (y, (1 - x) * 2 + core, z)
    aslant = (y, (1 - x) * 2 + 1 - core, z)
    beside = (1 - y, s, z)
    rows, width = tokens.shape
    length = 2 * rows
    branches, depth = weights.shape[0], weights.shape[1]
    half = depth // 2
    share = weights.shape[2] // 2
    groups = share // LANES
    rim = edge.shape[2]
    steps = chan_count - 1
    token_rows = rows // TOKEN_CHUNKS
    weight_rows = half // WEIGHT_CHUNKS

    column_peers = [mate] + [
        (y, 2 * x + of, lax.rem(z + by, chan_count))
        for by in range(1, chan_count)
        for of in (core, 1 - core)
    ]
    peers = column_peers + [across, aslant, beside]

    def rows_at(i, count, base=0):
        return pl.ds(pl.multiple_of(base + i * count, count), count)

    def at_rows(i):
        return rows_at(i, BLOCK)

    def blocks(count):
        return pl.loop(0, count // BLOCK)

    def lanes_of(base, g):
        return pl.ds(pl.multiple_of(base + g * LANES, LANES), LANES)

    tap_stage = [(0, 0), (0, length), (1, 0), (1, length)]
    tap_loads = [
        pltpu.make_async_copy(
            long_taps.at[:, pl.ds(j * LANES, LANES)],
            freq.at[which, pl.ds(start, length)],
            local_sem.at[4 + j],
        )
        for j, (which, start) in enumerate(tap_stage)
    ]
    token_load = pltpu.make_async_copy(tokens, result, local_sem.at[0])
    token_load.start()
    small_loads = [
        pltpu.make_async_copy(src, dst, local_sem.at[at])
        for src, dst, at in (
            (gain_hbm.at[:, pl.ds(pl.multiple_of(z * width, width), width)], gain, 3),
            (short_hbm, short, 8),
            (skip_hbm, skip, 9),
        )
    ]
    for copy in small_loads:
        copy.start()
    barrier = pltpu.get_barrier_semaphore()
    for peer in peers:
        pl.semaphore_signal(barrier, inc=1, device_id=peer, device_id_type=pl.DeviceIdType.MESH)
    for copy in tap_loads:
        copy.start()
    for g in range(groups):
        for b in range(branches):
            pltpu.make_async_copy(
                weights.at[b, :, lanes_of(core * share, g)],
                weight.at[g, s, :, pl.ds(b * LANES, LANES)],
                local_sem.at[2],
            ).start()

    sums[core, z] = jnp.zeros(sums.shape[2:], jnp.float32)
    small_loads[0].wait()
    own_gain = gain[...]
    token_load.wait()

    @blocks(rows)
    def _(i):
        raw = result[at_rows(i), :].astype(jnp.float32)
        total[at_rows(i), :] = raw
        stream[z, pl.ds(pl.multiple_of(core * rows + i * BLOCK, BLOCK), BLOCK), :] = (
            raw * own_gain
        ).astype(jnp.bfloat16)
        square = raw * raw
        found = square[:, :LANES]
        for part in range(1, width // LANES):
            found = found + square[:, part * LANES : (part + 1) * LANES]
        sums[core, z, pl.ds(i, 1), :] = jnp.sum(found.T, axis=0, keepdims=True)

    pl.semaphore_wait(barrier, len(peers))

    def token_view(owner, chunk):
        return stream.at[owner, rows_at(chunk, token_rows, core * rows), :]

    token_line = Line(
        token_view, chan_count, token_send, token_recv, lambda to: (y, s, to)
    )
    for chunk in range(TOKEN_CHUNKS):
        for way in range(2):

            @pl.when(token_line.sends(way, 0))
            def _():
                token_line.copy(way, 0, (chunk,)).start()

    def own_half(owner, of):
        return stream.at[owner, pl.ds(pl.multiple_of(of * rows, rows), rows), :]

    def mate_tokens():
        return remote(
            own_half(z, core), own_half(z, core), mate_send.at[0], mate_recv.at[0], mate
        )

    mate_tokens().start()
    sum_copies = [
        remote(
            sums.at[core, z], sums.at[core, z], sums_send.at[at], sums_recv.at[core, z], peer
        )
        for at, peer in enumerate(column_peers)
    ]
    for copy in sum_copies:
        copy.start()
    for g in range(groups):
        for b in range(branches):
            remote(
                weights.at[b, :, lanes_of((1 - core) * share, g)],
                weight.at[g, s, :, pl.ds(b * LANES, LANES)],
                mate_send.at[1],
                mate_recv.at[1],
                mate,
            ).start()

    for j, (which, start) in enumerate(tap_stage):
        tap_loads[j].wait()

        @pl.loop(0, groups)
        def _(g):
            mine = freq[which, rows_at(core * groups + g, BLOCK, start), :]
            taps[g, pl.ds(pl.multiple_of(s * rows + j * LANES, LANES), LANES), :] = mine.T.astype(
                jnp.bfloat16
            )
            other = freq[which, rows_at((1 - core) * groups + g, BLOCK, start), :]
            ready[g, j * LANES : (j + 1) * LANES, :] = other.T.astype(jnp.bfloat16)

    def tap_part(owner, part):
        return taps.at[
            :, pl.ds(pl.multiple_of(owner * rows + part * (rows // 2), rows // 2), rows // 2), :
        ]

    def taps_across(to):
        src = tap_part(s, y) if to == 0 else ready.at[
            :, pl.ds(pl.multiple_of(y * (rows // 2), rows // 2), rows // 2), :
        ]
        return remote(
            src,
            tap_part(s, y),
            tap_send.at[to],
            tap_recv.at[core],
            across if to == 0 else aslant,
        )

    def taps_beside(origin, part):
        view = tap_part(origin, part)
        return remote(view, view, tap_send.at[2 + origin], tap_recv.at[2 + origin], beside)

    def taps_mate():
        return remote(
            ready,
            taps.at[:, pl.ds(pl.multiple_of(s * rows, rows), rows), :],
            mate_send.at[2],
            mate_recv.at[2],
            mate,
        )

    @pl.when(x == 0)
    def _():
        taps_across(0).start()
        taps_across(1).start()

        @pl.loop(0, groups)
        def _(g):
            taps[g, length:, :] = jnp.zeros((length, LANES), jnp.bfloat16)

    taps_mate().start()

    def weight_view(owner, part, g, c):
        return weight.at[g, owner, rows_at(c, weight_rows, part * half), :]

    def weight_half(owner, part):
        return weight.at[:, owner, pl.ds(pl.multiple_of(part * half, half), half), :]

    def send_weights(g, chunks=range(WEIGHT_CHUNKS)):
        for c in chunks:
            for to in range(2):
                side = core if to == 0 else 1 - core
                view = weight_view(s, y, g, c)
                for b in range(branches):
                    remote(
                        weights.at[
                            b,
                            rows_at(c, weight_rows, y * half),
                            pl.ds(pl.multiple_of(side * share + g * LANES, LANES), LANES),
                        ],
                        view.at[:, pl.ds(b * LANES, LANES)],
                        x_send.at[to],
                        x_recv.at[core, g, c],
                        across if to == 0 else aslant,
                    ).start()

    for g in range(groups - 2):
        send_weights(g)
    send_weights(groups - 2, range(3))

    at_end = (z == 0) | (z == chan_count - 1)

    @pl.when((x == 1) | at_end)
    def _():
        send_weights(groups - 2, [3])
        send_weights(groups - 1, [0, 1])

    @pl.when(x == 1)
    def _():
        send_weights(groups - 1, [2, 3])

    def beside_copy(origin, part, g, c):
        view = weight_view((1 - x) * 2 + origin, part, g, c)
        return remote(view, view, y_send.at[origin], y_recv.at[origin, g], beside)

    def forward(g, c):
        for origin in range(2):
            view = weight_view((1 - x) * 2 + origin, y, g, c)
            remote(
                view, view, x_send.at[origin], x_recv.at[origin, g, c], beside
            ).wait_recv()
            beside_copy(origin, y, g, c).start()

    def await_beside(g):
        for origin in range(2):
            view = weight.at[
                g, (1 - x) * 2 + origin, pl.ds(pl.multiple_of((1 - y) * half, half), half), :
            ]
            remote(view, view, y_send.at[origin], y_recv.at[origin, g], beside).wait_recv()

    @blocks(length)
    def _(i):
        row = lax.broadcasted_iota(jnp.int32, (BLOCK, LANES), 0) + i * BLOCK
        lane = lax.broadcasted_iota(jnp.int32, (BLOCK, LANES), 1)
        unit = math.pi / (4 * length)
        odd = 2 * row + 1
        small = odd.astype(jnp.float32) * unit
        extended[0, at_rows(i), :] = jnp.cos(small)
        extended[1, at_rows(i), :] = jnp.sin(small)
        period = 8 * length
        angle = (odd * (2 * lane + 1) % period).astype(jnp.float32) * unit
        cos, sin = jnp.cos(angle), jnp.sin(angle)
        stride = (odd * (2 * LANES) % period).astype(jnp.float32) * unit
        step_cos, step_sin = jnp.cos(stride), jnp.sin(stride)
        for a in range(length // LANES):
            table[at_rows(i), a * LANES : (a + 1) * LANES] = cos.astype(jnp.bfloat16)
            table[rows_at(i, BLOCK, length), a * LANES : (a + 1) * LANES] = sin.astype(
                jnp.bfloat16
            )
            cos, sin = cos * step_cos - sin * step_sin, sin * step_cos + cos * step_sin

    for g in range(groups):

        @blocks(length)
        def _(i):
            partial[g, at_rows(i), :] = jnp.zeros((BLOCK, branches * LANES), jnp.float32)

    def spectrum(which, column):
        @pl.loop(0, 2 * length // SPAN)
        def _(i):
            at = rows_at(i, SPAN)
            freq[which, at, :] = jnp.dot(
                table[at, :], column(), preferred_element_type=jnp.float32
            )

    def spectrum_pair(columns):
        @pl.loop(0, 2 * length // SPAN)
        def _(i):
            at = rows_at(i, SPAN)
            found = jnp.dot(
                table[at, :],
                jnp.concatenate(columns(), axis=1),
                preferred_element_type=jnp.float32,
            )
            freq[0, at, :] = found[:, :LANES]
            freq[1, at, :] = found[:, LANES:]

    def tap_spectra(g):
        spectrum_pair(lambda: [taps[g, :length, :], taps[g, length:, :]])

        @blocks(length)
        def _(i):
            low, high = at_rows(i), rows_at(i, BLOCK, length)
            cos, sin = extended[0, low, :], extended[1, low, :]

            def turned(which):
                real, imag = freq[which, low, :], -freq[which, high, :]
                return (cos * real - sin * imag) / length, (cos * imag + sin * real) / length

            real, imag = turned(0)
            late_real, late_imag = turned(1)
            place = lax.broadcasted_iota(jnp.int32, (BLOCK, LANES), 0)
            sign = (1 - 2 * (place % 2)).astype(jnp.float32)
            spectra[g, 0, low, :] = real.astype(jnp.bfloat16)
            spectra[g, 1, low, :] = imag.astype(jnp.bfloat16)
            spectra[g, 2, low, :] = (late_real - sign * imag).astype(jnp.bfloat16)
            spectra[g, 3, low, :] = (late_imag + sign * real).astype(jnp.bfloat16)

    def project(g, owner):
        @pl.loop(0, length // SPAN)
        def _(i):
            at = rows_at(i, SPAN)
            partial[g, at, :] += jnp.dot(
                stream[owner, at, :], weight[g, owner], preferred_element_type=jnp.float32
            )

    def projects_early(g, owner):
        far = jnp.abs(z - owner)
        own = owner // 2 == x
        return (
            (own & ((far <= 1) | ((far == 2) & (at_end | (g == 0)))))
            | (jnp.logical_not(own) & (far <= 2) & ((g == 0) | ((g == 1) & at_end)))
        )

    def to_mate(way, step, chunk):
        block = token_view(token_line.source(way, step), chunk)
        index = 3 + way * steps + step
        return remote(block, block, mate_send.at[index], mate_recv.at[index], mate)

    def mate_half(way, step, of):
        block = own_half(token_line.source(way, step), of)
        index = 3 + way * steps + step
        return remote(block, block, mate_send.at[index], mate_recv.at[index], mate)

    def await_mate(step):
        for way in range(2):

            @pl.when(token_line.receives(way, step))
            def _():
                mate_half(way, step, 1 - core).wait_recv()

    @pl.loop(0, steps * TOKEN_CHUNKS)
    def _(tick):
        step, chunk = tick // TOKEN_CHUNKS, tick % TOKEN_CHUNKS
        for way in range(2):

            @pl.when(token_line.receives(way, step))
            def _():
                token_line.arrived(way, step, (chunk,))
                to_mate(way, step, chunk).start()

            @pl.when(
                (step + 1 < steps)
                & token_line.receives(way, step)
                & token_line.sends(way, step + 1)
            )
            def _():
                token_line.copy(way, step + 1, (chunk,)).start()

        @pl.when((tick == TOKEN_CHUNKS // 2) & (x == 1))
        def _():
            for origin in range(2):
                view = tap_part(origin, y)
                remote(
                    view, view, tap_send.at[origin], tap_recv.at[origin], beside
                ).wait_recv()
                taps_beside(origin, y).start()

        @pl.when((tick % 2 == 1) & (tick >= 3) & (tick < 7 + 4 * WEIGHT_CHUNKS))
        def _():
            at = (tick - 3) // 2
            forward(at // WEIGHT_CHUNKS, at % WEIGHT_CHUNKS)

        @pl.when(tick == TOKEN_CHUNKS)
        def _():
            mate_half_own = own_half(z, 1 - core)
            remote(
                mate_half_own, mate_half_own, mate_send.at[0], mate_recv.at[0], mate
            ).wait_recv()
            await_mate(0)
            pltpu.make_async_copy(
                weight.at[:, s], weight.at[:, s], local_sem.at[2]
            ).wait()
            other = weight.at[:, mate_s]
            remote(other, other, mate_send.at[1], mate_recv.at[1], mate).wait_recv()
            other = taps.at[:, pl.ds(pl.multiple_of(mate_s * rows, rows), rows), :]
            remote(other, other, mate_send.at[2], mate_recv.at[2], mate).wait_recv()

            @pl.when(x == 1)
            def _():
                for origin in range(2):
                    taps_beside(origin, 1 - y).wait_recv()

        @pl.when((step == 1) & (chunk % 2 == 0))
        def _():
            tap_spectra(chunk // 2)

        @pl.when(tick == 2 * TOKEN_CHUNKS)
        def _():
            await_mate(1)

        owner = 2 * x + chunk // groups
        far = jnp.abs(z - owner)

        @pl.when(
            projects_early(chunk % groups, owner)
            & (((step == 1) & (far <= 1)) | ((step == 2) & (far == 2)))
        )
        def _():
            project(chunk % groups, owner)

        @pl.when(tick == 2 * TOKEN_CHUNKS)
        def _():
            await_beside(0)

        @pl.when((tick == 2 * TOKEN_CHUNKS + TOKEN_CHUNKS // 2) & at_end)
        def _():
            await_beside(1)

        guest = 2 * (1 - x) + (chunk // 2) % 2

        @pl.when((step == 2) & (chunk % 2 == 0) & projects_early(chunk // 4, guest))
        def _():
            project(chunk // 4, guest)

    await_mate(2)
    for by in range(1, chan_count):
        for of in range(2):
            view = sums.at[of, lax.rem(z + by, chan_count)]
            remote(
                view, view, sums_send.at[0], sums_recv.at[of, lax.rem(z + by, chan_count)], mate
            ).wait_recv()
    view = sums.at[1 - core, z]
    remote(view, view, sums_send.at[0], sums_recv.at[1 - core, z], mate).wait_recv()

    @blocks(length)
    def _(i):
        of, at = i // (rows // BLOCK), i % (rows // BLOCK)
        found = sums[of, 0, pl.ds(at, 1), :]
        for owner in range(1, chan_count):
            found = found + sums[of, owner, pl.ds(at, 1), :]
        found = lax.rsqrt(found / (chan_count * width) + EPSILON)
        scale[at_rows(i), :] = jnp.broadcast_to(found, (BLOCK, LANES)).T

    taps_mate().wait_send()

    @pl.when(x == 0)
    def _():
        taps_across(0).wait_send()
        taps_across(1).wait_send()

    def edge_copy(g):
        return remote(
            edge_out.at[g], edge.at[g], edge_send.at[0], edge_recv.at[g], across
        )

    def before_copy(g):
        return remote(
            signal.at[g], before.at[g], before_send.at[0], before_recv.at[g], across
        )

    def swap_copy(g):
        return remote(
            ready.at[g], full.at[z, g, core], swap_send.at[0], swap_recv.at[g], mate
        )

    line = Line(
        lambda owner, g, of: full.at[owner, g, of],
        chan_count,
        line_send,
        line_recv,
        lambda to: (y, s, to),
    )

    def projected(g, b, at):
        return (partial[g, at, b * LANES : (b + 1) * LANES] * scale[at, :]).astype(jnp.bfloat16)

    def featurize(g):
        @pl.when(x == 0)
        def _():
            for b in range(branches):
                edge_out[g, b] = projected(g, b, pl.ds(length - rim, rim))
                extended[b, 0:rim, :] = jnp.zeros((rim, LANES), jnp.float32)
            edge_copy(g).start()

        @blocks(length)
        def _(i):
            for b in range(branches):
                extended[b, pl.ds(pl.multiple_of(rim + i * BLOCK, rim), BLOCK), :] = projected(
                    g, b, at_rows(i)
                ).astype(jnp.float32)

        @pl.when(x == 1)
        def _():
            edge_copy(g).wait_recv()
            for b in range(branches):
                extended[b, 0:rim, :] = edge[g, b].astype(jnp.float32)

        chosen = lanes_of(core * share, g)
        coefficient = [
            [short[tap, b : b + 1, chosen] for b in range(branches)] for tap in range(SHORT)
        ]

        @blocks(length)
        def _(i):
            found = []
            for b in range(branches):
                value = jnp.zeros((BLOCK, LANES), jnp.float32)
                for tap in range(SHORT):
                    value = value + coefficient[tap][b] * extended[
                        b, pl.ds(rim - tap + i * BLOCK, BLOCK), :
                    ]
                found.append(value.astype(jnp.bfloat16))
            query[at_rows(i), :] = found[0]
            signal[g, at_rows(i), :] = (
                found[1].astype(jnp.float32) * found[2].astype(jnp.float32)
            ).astype(jnp.bfloat16)

    def convolve(g):
        joint = (x == 1) & (g > 0)

        @pl.when(jnp.logical_not(joint))
        def _():
            spectrum(0, lambda: signal[g])

        def product(i, which, first):
            low, high = at_rows(i), rows_at(i, BLOCK, length)
            cos, sin = freq[which, low, :], freq[which, high, :]
            real = spectra[g, first, low, :].astype(jnp.float32)
            imag = spectra[g, first + 1, low, :].astype(jnp.float32)
            return cos * real + sin * imag, sin * real - cos * imag

        @pl.when(x == 0)
        def _():
            @blocks(length)
            def _(i):
                real, imag = product(i, 0, 0)
                mixed[at_rows(i), :] = real.astype(jnp.bfloat16)
                mixed[rows_at(i, BLOCK, length), :] = imag.astype(jnp.bfloat16)

        @pl.when(x == 1)
        def _():
            before_copy(g).wait_recv()

            @pl.when(g == 0)
            def _():
                spectrum(1, lambda: before[g])

            @pl.when(g > 0)
            def _():
                spectrum_pair(lambda: [signal[g], before[g]])

            @blocks(length)
            def _(i):
                real, imag = product(i, 0, 0)
                more_real, more_imag = product(i, 1, 2)
                mixed[at_rows(i), :] = (real + more_real).astype(jnp.bfloat16)
                mixed[rows_at(i, BLOCK, length), :] = (imag + more_imag).astype(jnp.bfloat16)

        @pl.loop(0, length // SPAN)
        def _(i):
            low, high = rows_at(i, SPAN), rows_at(i, SPAN, length)
            freq[0, low, :] = jnp.dot(
                table[low, :], mixed[:length, :], preferred_element_type=jnp.float32
            ) + jnp.dot(table[high, :], mixed[length:, :], preferred_element_type=jnp.float32)

        direct = skip[:, lanes_of(core * share, g)]

        def gated(at):
            longer = freq[0, at, :] + direct * signal[g, at, :].astype(jnp.float32)
            longer = longer.astype(jnp.bfloat16).astype(jnp.float32)
            return (query[at, :].astype(jnp.float32) * longer).astype(jnp.bfloat16)

        @blocks(rows)
        def _(i):
            full[z, g, core, at_rows(i), :] = gated(
                pl.ds(pl.multiple_of(core * rows + i * BLOCK, BLOCK), BLOCK)
            )
            ready[g, at_rows(i), :] = gated(
                pl.ds(pl.multiple_of((1 - core) * rows + i * BLOCK, BLOCK), BLOCK)
            )

    def load_out():
        for owner in range(chan_count):
            pltpu.make_async_copy(
                out_weight.at[pl.ds(owner * length, length)], stream.at[owner], local_sem.at[1]
            ).start()

    def accumulate(owner, g):
        @pl.loop(0, total.shape[1] // (2 * LANES))
        def _(i):
            cols = rows_at(i, 2 * LANES)
            block = jnp.concatenate([full[owner, g, 0], full[owner, g, 1]], axis=1)
            kernel = jnp.concatenate(
                [stream[owner, lanes_of(of * share, g), cols] for of in range(2)], axis=0
            )
            total[:, cols] += jnp.dot(block, kernel, preferred_element_type=jnp.float32)

    def begin(g):
        swap_copy(g).start()
        for way in range(2):

            @pl.when(line.sends(way, 0))
            def _():
                line.copy(way, 0, (g, core)).start()

    def begin_other(g):
        other = full.at[z, g, 1 - core]
        remote(other, other, swap_send.at[0], swap_recv.at[g], mate).wait_recv()
        for way in range(2):

            @pl.when(line.sends(way, 0))
            def _():
                line.copy(way, 0, (g, 1 - core)).start()

    def settle():
        other = weight.at[:, s]
        remote(other, other, mate_send.at[1], mate_recv.at[1], mate).wait_send()
        for copy in sum_copies:
            copy.wait_send()

        @pl.when(x == 1)
        def _():
            for origin in range(2):
                taps_beside(origin, y).wait_send()

        for at in range(2):
            view = weight_half(s, y)
            remote(view, view, x_send.at[at], x_recv.at[0, 0, 0], across).wait_send()
            view = weight_half((1 - x) * 2 + at, y)
            remote(view, view, y_send.at[at], y_recv.at[at, 0], beside).wait_send()

        @pl.when(x == 0)
        def _():
            remote(edge_out, edge, edge_send.at[0], edge_recv.at[0], across).wait_send()
            remote(signal, before, before_send.at[0], before_recv.at[0], across).wait_send()

    def settle_tokens():
        mate_tokens().wait_send()
        for way in range(2):
            for step in range(steps):

                @pl.when(token_line.receives(way, step))
                def _():
                    mate_half(way, step, core).wait_send()

                @pl.when(token_line.sends(way, step))
                def _():
                    token_line.drain(way, step, (0,), lambda owner: own_half(owner, core))

    def way_of(k):
        return jnp.where(z < chan_count // 2, 1 - k, k)

    def late_forwards(g, at, inner, outer):
        for here, pieces in ((jnp.logical_not(at_end), inner), (at_end, outer)):

            @pl.when((g == at) & here)
            def _():
                for group, c in pieces:
                    forward(group, c)

    def pass_on(way, step, at):
        @pl.when(
            (at >= 0) & (at < groups) & line.receives(way, step) & line.sends(way, step + 1)
        )
        def _():
            for of in (core, 1 - core):
                line.arrived(way, step, (at, of))
                line.copy(way, step + 1, (at, of)).start()

    for copy in small_loads[1:]:
        copy.wait()
    near, away = way_of(0), way_of(1)

    @pl.loop(0, groups)
    def _(g):
        @pl.when(g == 3)
        def _():
            pass_on(away, 0, 1)
            pass_on(near, 0, 2)

        @pl.when((g >= 2) | ((g == 1) & jnp.logical_not(at_end)))
        def _():
            await_beside(g)

        @pl.loop(0, chan_count)
        def _(owner):
            @pl.when(jnp.logical_not(projects_early(g, owner)))
            def _():
                project(g, owner)

        @pl.when(g == groups - 1)
        def _():
            settle_tokens()
            load_out()

        featurize(g)

        @pl.when(x == 0)
        def _():
            before_copy(g).start()

            for at, inner, outer in (
                (0, [], [(groups - 1, 2)]),
                (1, [(groups - 2, 3), (groups - 1, 0), (groups - 1, 1)], [(groups - 1, 3)]),
                (2, [(groups - 1, 2), (groups - 1, 3)], []),
            ):

                @pl.when((g == at) & jnp.logical_not(at_end))
                def _():
                    for group, c in inner:
                        send_weights(group, [c])

                @pl.when((g == at) & at_end)
                def _():
                    for group, c in outer:
                        send_weights(group, [c])

        late_forwards(g, 1, [(groups - 2, 3)], [(groups - 1, 0), (groups - 1, 1)])
        late_forwards(g, 2, [(groups - 1, 0), (groups - 1, 1)], [(groups - 1, 3)])

        @pl.when((g == 1) | (g == 2))
        def _():
            pass_on(near, 0, g - 1)

        @pl.when(g == 2)
        def _():
            pass_on(away, 0, 0)

        @pl.when(g == 3)
        def _():
            pass_on(near, 1, 1)
            pass_on(away, 0, 2)

        late_forwards(g, 0, [(groups - 2, 2)], [(groups - 2, 2), (groups - 2, 3)])
        convolve(g)
        begin(g)
        late_forwards(g, 1, [], [(groups - 1, 2)])
        begin_other(g)

        late_forwards(g, 2, [(groups - 1, 2), (groups - 1, 3)], [])

        @pl.when(g == 2)
        def _():
            pass_on(near, 1, 0)

    pltpu.make_async_copy(stream, stream, local_sem.at[1]).wait()

    @pl.loop(0, groups + steps - 1)
    def _(n):
        for at, pieces in (
            (0, [(near, 1, 2)]),
            (1, [(near, 0, 3), (away, 0, 3)]),
            (3, [(near, 1, 3)]),
        ):

            @pl.when(n == at)
            def _():
                for way, step, group in pieces:
                    pass_on(way, step, group)

        @pl.when(n == 2)
        def _():
            settle()

        @pl.when(n < groups)
        def _():
            accumulate(z, n)

        @pl.loop(0, 2)
        def _(way):
            for step in range(steps):
                at = n - jnp.where(at_end, step, 0)

                @pl.when((at >= 0) & (at < groups) & line.receives(way, step))
                def _():
                    @pl.when(jnp.logical_not(line.sends(way, step + 1)))
                    def _():
                        for of in range(2):
                            line.arrived(way, step, (at, of))

                    accumulate(line.source(way, step), at)

    @blocks(rows)
    def _(i):
        result[at_rows(i), :] = total[at_rows(i), :].astype(jnp.bfloat16)

    remote(ready, ready, swap_send.at[0], swap_recv.at[0], mate).wait_send()
    for way in range(2):
        for step in range(steps):

            @pl.when(line.sends(way, step))
            def _():
                line.drain(way, step, (0, 0), lambda owner: full.at[owner])


def chip_body(tokens, norm_gain, proj_weight, short_filter, long_filter, skip_gain, out_weight):
    chan_count = lax.axis_size("chan")
    rows, width = tokens.shape
    depth, branches, local_chan = proj_weight.shape
    length, share = 2 * rows, local_chan // 2
    groups = share // LANES
    steps = chan_count - 1
    dma = pltpu.SemaphoreType.DMA
    f32, bf16 = jnp.float32, jnp.bfloat16
    vmem = pl.BlockSpec(memory_space=pltpu.VMEM)
    return pl.pallas_call(
        functools.partial(block_kernel, chan_count),
        out_shape=jax.ShapeDtypeStruct((rows, width), bf16),
        in_specs=[HBM] * 7,
        out_specs=vmem,
        scratch_shapes=[
            pltpu.VMEM((1, width), f32),
            pltpu.VMEM(short_filter.shape, f32),
            pltpu.VMEM((1, local_chan), f32),
            pltpu.VMEM((chan_count, length, width), bf16),
            pltpu.VMEM((groups, 4, depth, branches * LANES), bf16),
            pltpu.VMEM((2, chan_count, 8, LANES), f32),
            pltpu.VMEM((length, LANES), f32),
            pltpu.VMEM((groups, length, branches * LANES), f32),
            pltpu.VMEM((2 * length, length), bf16),
            pltpu.VMEM((groups, 2 * length, LANES), bf16),
            pltpu.VMEM((groups, 4, length, LANES), bf16),
            pltpu.VMEM((2, 2 * length, LANES), f32),
            pltpu.VMEM((2 * length, LANES), bf16),
            pltpu.VMEM((groups, branches, 16, LANES), bf16),
            pltpu.VMEM((groups, branches, 16, LANES), bf16),
            pltpu.VMEM((branches, length + 16, LANES), f32),
            pltpu.VMEM((length, LANES), bf16),
            pltpu.VMEM((groups, length, LANES), bf16),
            pltpu.VMEM((groups, length, LANES), bf16),
            pltpu.VMEM((groups, rows, LANES), bf16),
            pltpu.VMEM((chan_count, groups, 2, rows, LANES), bf16),
            pltpu.VMEM((rows, width), f32),
            dma((10,)),
            dma((3 + 2 * steps,)),
            dma((3 + 2 * steps,)),
            dma((2, steps)),
            dma((steps, TOKEN_CHUNKS)),
            dma((2 * chan_count - 1,)),
            dma((2, chan_count)),
            dma((2,)),
            dma((2, groups, WEIGHT_CHUNKS)),
            dma((2,)),
            dma((2, groups)),
            dma((4,)),
            dma((4,)),
            dma((1,)),
            dma((groups,)),
            dma((1,)),
            dma((groups,)),
            dma((1,)),
            dma((groups,)),
            dma((2, steps)),
            dma((steps, groups, 2)),
        ],
        compiler_params=pltpu.CompilerParams(
            collective_id=0, has_side_effects=True, vmem_limit_bytes=52 * 1024 * 1024
        ),
        name="block",
    )(
        tokens,
        pltpu.with_memory_space_constraint(norm_gain[None, :], pltpu.HBM),
        proj_weight.transpose(1, 0, 2),
        pltpu.with_memory_space_constraint(short_filter, pltpu.HBM),
        long_filter,
        pltpu.with_memory_space_constraint(skip_gain[None, :], pltpu.HBM),
        out_weight,
    )


def select_body(mesh):
    if (mesh.shape["groups"], mesh.shape["seq"], mesh.shape["chan"]) == (2, 4, 4):
        return chip_body
    return body


def solution(mesh):
    placed = (
        P(("groups", "seq"), "chan"),
        P(),
        P("seq", None, "chan"),
        P(None, None, "chan"),
        P("chan", "seq"),
        P("chan"),
        P(None, "chan"),
    )
    return jax.shard_map(
        select_body(mesh), mesh=mesh, in_specs=placed, out_specs=P(("groups", "seq"), "chan"), check_vma=False
    )
```

```python
import functools
import math

import jax
import jax.numpy as jnp
import numpy as np
from jax import lax
from jax.experimental import pallas as pl
from jax.experimental.pallas import tpu as pltpu
from jax.sharding import PartitionSpec as P

SHORT = 3


EPSILON = 1e-06
HIGHEST = lax.Precision.HIGHEST


def from_behind(value, axis, steps):
    count = lax.axis_size(axis)
    initial, last = (max(0, -steps), min(count, count - steps))
    return lax.ppermute(value, axis, [(source, source + steps) for source in range(initial, last)])


def angle_table(row_count, col_count, period, sign):
    row_index = lax.iota(jnp.int32, row_count)[:, None]
    col_index = lax.iota(jnp.int32, col_count)[None, :]
    angles = (row_index * col_index % period).astype(jnp.float32) * (sign * 2.0 * math.pi / period)
    return (jnp.cos(angles), jnp.sin(angles))


def forward_spectrum(signal_rows, first, second):
    channels = signal_rows.shape[0]
    grid_rows = signal_rows.reshape(channels, first, second)
    cos_first, sin_first = angle_table(first, first, first, -1.0)
    part_re = jnp.einsum("cab,ak->ckb", grid_rows, cos_first, precision=HIGHEST)
    part_im = jnp.einsum("cab,ak->ckb", grid_rows, sin_first, precision=HIGHEST)
    twist_cos, twist_sin = angle_table(first, second, first * second, -1.0)
    part_re, part_im = (
        part_re * twist_cos - part_im * twist_sin,
        part_re * twist_sin + part_im * twist_cos,
    )
    cos_second, sin_second = angle_table(second, second, second, -1.0)
    spectrum_real = jnp.einsum("ckb,bm->ckm", part_re, cos_second, precision=HIGHEST) - jnp.einsum(
        "ckb,bm->ckm", part_im, sin_second, precision=HIGHEST
    )
    spec_im = jnp.einsum("ckb,bm->ckm", part_re, sin_second, precision=HIGHEST) + jnp.einsum(
        "ckb,bm->ckm", part_im, cos_second, precision=HIGHEST
    )
    return (spectrum_real, spec_im)


def inverse_spectrum(spectrum_real, spec_im, first, second):
    channels = spectrum_real.shape[0]
    cos_second, sin_second = angle_table(second, second, second, 1.0)
    part_re = jnp.einsum("ckm,bm->ckb", spectrum_real, cos_second, precision=HIGHEST) - jnp.einsum(
        "ckm,bm->ckb", spec_im, sin_second, precision=HIGHEST
    )
    part_im = jnp.einsum("ckm,bm->ckb", spectrum_real, sin_second, precision=HIGHEST) + jnp.einsum(
        "ckm,bm->ckb", spec_im, cos_second, precision=HIGHEST
    )
    twist_cos, twist_sin = angle_table(first, second, first * second, 1.0)
    part_re, part_im = (
        part_re * twist_cos - part_im * twist_sin,
        part_re * twist_sin + part_im * twist_cos,
    )
    cos_first, sin_first = angle_table(first, first, first, 1.0)
    result = jnp.einsum("ckb,ak->cab", part_re, cos_first, precision=HIGHEST) - jnp.einsum(
        "ckb,ak->cab", part_im, sin_first, precision=HIGHEST
    )
    return result.reshape(channels, first * second) / (first * second)


def spectral_conv(signal_rows, filter_rows):
    channels, length = signal_rows.shape
    padded_len = 2 * length
    log_len = padded_len.bit_length() - 1
    first = 1 << log_len // 2
    second = padded_len // first
    zeros_tail = jnp.zeros((channels, length), jnp.float32)
    sig_re, sig_im = forward_spectrum(
        jnp.concatenate([signal_rows, zeros_tail], axis=1), first, second
    )
    tap_re, tap_im = forward_spectrum(
        jnp.concatenate([filter_rows, zeros_tail], axis=1), first, second
    )
    prod_re = sig_re * tap_re - sig_im * tap_im
    prod_im = sig_re * tap_im + sig_im * tap_re
    return inverse_spectrum(prod_re, prod_im, first, second)[:, :length]


def short_filter_output(projected, rim_cells, kernel_coefficients):
    count = kernel_coefficients.shape[0]
    steps_len = projected.shape[2]
    extended = jnp.concatenate([rim_cells, projected], axis=2).astype(jnp.float32)
    total = jnp.zeros(projected.shape, jnp.float32)
    for tap in range(count):
        total = (
            total
            + kernel_coefficients[tap][:, :, None]
            * extended[:, :, count - 1 - tap : count - 1 - tap + steps_len]
        )
    return total.astype(jnp.bfloat16)


def hyena_mixer(keys_rows, values_rows, long_taps, skip_part):
    middle = keys_rows.astype(jnp.float32) * values_rows.astype(jnp.float32)
    return (spectral_conv(middle, long_taps) + skip_part[:, None] * middle).astype(jnp.bfloat16)


def body(tokens, norm_gain, proj_weight, short_filter, long_filter, skip_gain, out_weight):
    seq_count = lax.axis_size("seq")
    local_rows = tokens.shape[0]
    local_chan = proj_weight.shape[2]
    subset = local_chan // seq_count
    length = local_rows * seq_count
    offset = lax.axis_index("seq") * subset
    whole = lax.all_gather(tokens, "chan", axis=1, tiled=True)
    wide = whole.astype(jnp.float32)
    rescaled_signal = (
        wide * lax.rsqrt(jnp.mean(wide * wide, axis=1, keepdims=True) + EPSILON) * norm_gain
    ).astype(jnp.bfloat16)
    projected = lax.dot_general(
        lax.all_gather(proj_weight, "seq", axis=0, tiled=True),
        rescaled_signal,
        (((0,), (1,)), ((), ())),
        preferred_element_type=jnp.float32,
    ).astype(jnp.bfloat16)
    taps_grid = long_filter.reshape(1, seq_count, subset, local_rows)
    long_taps = lax.all_to_all(taps_grid, "seq", split_axis=1, concat_axis=3, tiled=True).reshape(
        subset, length
    )
    skip_part = lax.dynamic_slice_in_dim(skip_gain, offset, subset, 0)
    rim_cells = from_behind(projected[:, :, local_rows - (SHORT - 1) :], "seq", 1)
    featured = short_filter_output(projected, rim_cells, short_filter)
    pair_grid = featured[1:].reshape(2, seq_count, subset, local_rows)
    moved = lax.all_to_all(pair_grid, "seq", split_axis=1, concat_axis=3, tiled=True).reshape(
        2, subset, length
    )
    result = hyena_mixer(moved[0], moved[1], long_taps, skip_part)
    returned = lax.all_to_all(
        result.reshape(1, subset, length), "seq", split_axis=2, concat_axis=0, tiled=True
    )
    returned = returned.reshape(local_chan, local_rows)
    gated = (featured[0].astype(jnp.float32) * returned.astype(jnp.float32)).astype(jnp.bfloat16)
    full_mix = lax.all_gather(gated, "chan", axis=0, tiled=True)
    update = lax.dot_general(
        full_mix, out_weight, (((0,), (0,)), ((), ())), preferred_element_type=jnp.float32
    )
    return (tokens.astype(jnp.float32) + update).astype(jnp.bfloat16)

LANES = 128
BLOCK = 128
SPAN = 512
TOKEN_CHUNKS = 8
WEIGHT_CHUNKS = 4
HBM = pl.BlockSpec(memory_space=pltpu.HBM)


def remote(src, dst, send_sem, recv_sem, where):
    return pltpu.make_async_remote_copy(
        src_ref=src,
        dst_ref=dst,
        send_sem=send_sem,
        recv_sem=recv_sem,
        device_id=where,
        device_id_type=pl.DeviceIdType.MESH,
    )


class Line:
    def __init__(self, view, count, send_sem, recv_sem, place):
        self.view, self.count, self.place = view, count, place
        self.send_sem, self.recv_sem = send_sem, recv_sem
        self.me = lax.axis_index("chan")

    def move(self, way, step, piece, block, target):
        slot = jnp.minimum(jnp.where(way == 0, step, target + step), self.count - 2)
        recv = self.recv_sem.at[(slot,) + piece]
        return remote(block, block, self.send_sem.at[way, step], recv, self.place(target))

    def drain(self, way, step, first, block):
        self.move(way, step, first, block(self.source(way, step - 1)), self.me).wait_send()

    def source(self, way, step):
        return jnp.clip(self.me - (step + 1) * (1 - 2 * way), 0, self.count - 1)

    def copy(self, way, step, piece):
        owner = self.source(way, step - 1)
        target = self.source(way, -2)
        return self.move(way, step, piece, self.view(owner, *piece), target)

    def inside(self, way, by):
        place = self.me + by * (1 - 2 * way)
        return (place >= 0) & (place < self.count)

    def sends(self, way, step):
        return self.inside(way, -step) & self.inside(way, 1)

    def receives(self, way, step):
        return self.inside(way, -1 - step)

    def arrived(self, way, step, piece):
        owner = self.source(way, step)
        self.move(way, step, piece, self.view(owner, *piece), self.me).wait_recv()
        return owner


def block_kernel(
    chan_count,
    tokens,
    gain_hbm,
    weights,
    short_hbm,
    long_taps,
    skip_hbm,
    out_weight,
    result,
    gain,
    short,
    skip,
    stream,
    weight,
    sums,
    scale,
    partial,
    table,
    taps,
    spectra,
    freq,
    mixed,
    edge_out,
    edge,
    extended,
    query,
    signal,
    before,
    ready,
    full,
    total,
    local_sem,
    mate_send,
    mate_recv,
    token_send,
    token_recv,
    sums_send,
    sums_recv,
    x_send,
    x_recv,
    y_send,
    y_recv,
    tap_send,
    tap_recv,
    edge_send,
    edge_recv,
    before_send,
    before_recv,
    swap_send,
    swap_recv,
    line_send,
    line_recv,
):
    y, s, z = (lax.axis_index(name) for name in ("groups", "seq", "chan"))
    x, core = s // 2, s % 2
    mate_s = s + 1 - 2 * core
    mate = (y, mate_s, z)
    across = (y, (1 - x) * 2 + core, z)
    aslant = (y, (1 - x) * 2 + 1 - core, z)
    beside = (1 - y, s, z)
    rows, width = tokens.shape
    length = 2 * rows
    branches, depth = weights.shape[0], weights.shape[1]
    half = depth // 2
    share = weights.shape[2] // 2
    groups = share // LANES
    rim = edge.shape[2]
    steps = chan_count - 1
    token_rows = rows // TOKEN_CHUNKS
    weight_rows = half // WEIGHT_CHUNKS

    column_peers = [mate] + [
        (y, 2 * x + of, lax.rem(z + by, chan_count))
        for by in range(1, chan_count)
        for of in (core, 1 - core)
    ]
    peers = column_peers + [across, aslant, beside]

    def rows_at(i, count, base=0):
        return pl.ds(pl.multiple_of(base + i * count, count), count)

    def at_rows(i):
        return rows_at(i, BLOCK)

    def blocks(count):
        return pl.loop(0, count // BLOCK)

    def lanes_of(base, g):
        return pl.ds(pl.multiple_of(base + g * LANES, LANES), LANES)

    tap_stage = [(0, 0), (0, length), (1, 0), (1, length)]
    tap_loads = [
        pltpu.make_async_copy(
            long_taps.at[:, pl.ds(j * LANES, LANES)],
            freq.at[which, pl.ds(start, length)],
            local_sem.at[4 + j],
        )
        for j, (which, start) in enumerate(tap_stage)
    ]
    token_load = pltpu.make_async_copy(tokens, result, local_sem.at[0])
    token_load.start()
    small_loads = [
        pltpu.make_async_copy(src, dst, local_sem.at[at])
        for src, dst, at in (
            (gain_hbm.at[:, pl.ds(pl.multiple_of(z * width, width), width)], gain, 3),
            (short_hbm, short, 8),
            (skip_hbm, skip, 9),
        )
    ]
    for copy in small_loads:
        copy.start()
    barrier = pltpu.get_barrier_semaphore()
    for peer in peers:
        pl.semaphore_signal(barrier, inc=1, device_id=peer, device_id_type=pl.DeviceIdType.MESH)
    for copy in tap_loads:
        copy.start()
    for g in range(groups):
        for b in range(branches):
            pltpu.make_async_copy(
                weights.at[b, :, lanes_of(core * share, g)],
                weight.at[g, s, :, pl.ds(b * LANES, LANES)],
                local_sem.at[2],
            ).start()

    sums[core, z] = jnp.zeros(sums.shape[2:], jnp.float32)
    small_loads[0].wait()
    own_gain = gain[...]
    token_load.wait()

    @blocks(rows)
    def _(i):
        raw = result[at_rows(i), :].astype(jnp.float32)
        total[at_rows(i), :] = raw
        stream[z, pl.ds(pl.multiple_of(core * rows + i * BLOCK, BLOCK), BLOCK), :] = (
            raw * own_gain
        ).astype(jnp.bfloat16)
        square = raw * raw
        found = square[:, :LANES]
        for part in range(1, width // LANES):
            found = found + square[:, part * LANES : (part + 1) * LANES]
        sums[core, z, pl.ds(i, 1), :] = jnp.sum(found.T, axis=0, keepdims=True)

    pl.semaphore_wait(barrier, len(peers))

    def token_view(owner, chunk):
        return stream.at[owner, rows_at(chunk, token_rows, core * rows), :]

    token_line = Line(
        token_view, chan_count, token_send, token_recv, lambda to: (y, s, to)
    )
    for chunk in range(TOKEN_CHUNKS):
        for way in range(2):

            @pl.when(token_line.sends(way, 0))
            def _():
                token_line.copy(way, 0, (chunk,)).start()

    def own_half(owner, of):
        return stream.at[owner, pl.ds(pl.multiple_of(of * rows, rows), rows), :]

    def mate_tokens():
        return remote(
            own_half(z, core), own_half(z, core), mate_send.at[0], mate_recv.at[0], mate
        )

    mate_tokens().start()
    sum_copies = [
        remote(
            sums.at[core, z], sums.at[core, z], sums_send.at[at], sums_recv.at[core, z], peer
        )
        for at, peer in enumerate(column_peers)
    ]
    for copy in sum_copies:
        copy.start()
    for g in range(groups):
        for b in range(branches):
            remote(
                weights.at[b, :, lanes_of((1 - core) * share, g)],
                weight.at[g, s, :, pl.ds(b * LANES, LANES)],
                mate_send.at[1],
                mate_recv.at[1],
                mate,
            ).start()

    for j, (which, start) in enumerate(tap_stage):
        tap_loads[j].wait()

        @pl.loop(0, groups)
        def _(g):
            mine = freq[which, rows_at(core * groups + g, BLOCK, start), :]
            taps[g, pl.ds(pl.multiple_of(s * rows + j * LANES, LANES), LANES), :] = mine.T.astype(
                jnp.bfloat16
            )
            other = freq[which, rows_at((1 - core) * groups + g, BLOCK, start), :]
            ready[g, j * LANES : (j + 1) * LANES, :] = other.T.astype(jnp.bfloat16)

    def tap_part(owner, part):
        return taps.at[
            :, pl.ds(pl.multiple_of(owner * rows + part * (rows // 2), rows // 2), rows // 2), :
        ]

    def taps_across(to):
        src = tap_part(s, y) if to == 0 else ready.at[
            :, pl.ds(pl.multiple_of(y * (rows // 2), rows // 2), rows // 2), :
        ]
        return remote(
            src,
            tap_part(s, y),
            tap_send.at[to],
            tap_recv.at[core],
            across if to == 0 else aslant,
        )

    def taps_beside(origin, part):
        view = tap_part(origin, part)
        return remote(view, view, tap_send.at[2 + origin], tap_recv.at[2 + origin], beside)

    def taps_mate():
        return remote(
            ready,
            taps.at[:, pl.ds(pl.multiple_of(s * rows, rows), rows), :],
            mate_send.at[2],
            mate_recv.at[2],
            mate,
        )

    @pl.when(x == 0)
    def _():
        taps_across(0).start()
        taps_across(1).start()

        @pl.loop(0, groups)
        def _(g):
            taps[g, length:, :] = jnp.zeros((length, LANES), jnp.bfloat16)

    taps_mate().start()

    def weight_view(owner, part, g, c):
        return weight.at[g, owner, rows_at(c, weight_rows, part * half), :]

    def weight_half(owner, part):
        return weight.at[:, owner, pl.ds(pl.multiple_of(part * half, half), half), :]

    def send_weights(g, chunks=range(WEIGHT_CHUNKS)):
        for c in chunks:
            for to in range(2):
                side = core if to == 0 else 1 - core
                view = weight_view(s, y, g, c)
                for b in range(branches):
                    remote(
                        weights.at[
                            b,
                            rows_at(c, weight_rows, y * half),
                            pl.ds(pl.multiple_of(side * share + g * LANES, LANES), LANES),
                        ],
                        view.at[:, pl.ds(b * LANES, LANES)],
                        x_send.at[to],
                        x_recv.at[core, g, c],
                        across if to == 0 else aslant,
                    ).start()

    for g in range(groups - 2):
        send_weights(g)
    send_weights(groups - 2, range(2))

    at_end = (z == 0) | (z == chan_count - 1)

    @pl.when((x == 1) | at_end)
    def _():
        send_weights(groups - 2, [2, 3])
        send_weights(groups - 1, [0, 1])

    @pl.when(x == 1)
    def _():
        send_weights(groups - 1, [2, 3])

    def beside_copy(origin, part, g, c):
        view = weight_view((1 - x) * 2 + origin, part, g, c)
        return remote(view, view, y_send.at[origin], y_recv.at[origin, g], beside)

    def forward(g, c):
        for origin in range(2):
            view = weight_view((1 - x) * 2 + origin, y, g, c)
            remote(
                view, view, x_send.at[origin], x_recv.at[origin, g, c], beside
            ).wait_recv()
            beside_copy(origin, y, g, c).start()

    def await_beside(g):
        for origin in range(2):
            view = weight.at[
                g, (1 - x) * 2 + origin, pl.ds(pl.multiple_of((1 - y) * half, half), half), :
            ]
            remote(view, view, y_send.at[origin], y_recv.at[origin, g], beside).wait_recv()

    @blocks(length)
    def _(i):
        row = lax.broadcasted_iota(jnp.int32, (BLOCK, LANES), 0) + i * BLOCK
        lane = lax.broadcasted_iota(jnp.int32, (BLOCK, LANES), 1)
        unit = math.pi / (4 * length)
        odd = 2 * row + 1
        small = odd.astype(jnp.float32) * unit
        extended[0, at_rows(i), :] = jnp.cos(small)
        extended[1, at_rows(i), :] = jnp.sin(small)
        period = 8 * length
        angle = (odd * (2 * lane + 1) % period).astype(jnp.float32) * unit
        cos, sin = jnp.cos(angle), jnp.sin(angle)
        stride = (odd * (2 * LANES) % period).astype(jnp.float32) * unit
        step_cos, step_sin = jnp.cos(stride), jnp.sin(stride)
        for a in range(length // LANES):
            table[at_rows(i), a * LANES : (a + 1) * LANES] = cos.astype(jnp.bfloat16)
            table[rows_at(i, BLOCK, length), a * LANES : (a + 1) * LANES] = sin.astype(
                jnp.bfloat16
            )
            cos, sin = cos * step_cos - sin * step_sin, sin * step_cos + cos * step_sin

    for g in range(groups):

        @blocks(length)
        def _(i):
            partial[g, at_rows(i), :] = jnp.zeros((BLOCK, branches * LANES), jnp.float32)

    def spectrum(which, column):
        @pl.loop(0, 2 * length // SPAN)
        def _(i):
            at = rows_at(i, SPAN)
            freq[which, at, :] = jnp.dot(
                table[at, :], column(), preferred_element_type=jnp.float32
            )

    def spectrum_pair(columns):
        @pl.loop(0, 2 * length // SPAN)
        def _(i):
            at = rows_at(i, SPAN)
            found = jnp.dot(
                table[at, :],
                jnp.concatenate(columns(), axis=1),
                preferred_element_type=jnp.float32,
            )
            freq[0, at, :] = found[:, :LANES]
            freq[1, at, :] = found[:, LANES:]

    def tap_spectra(g):
        spectrum_pair(lambda: [taps[g, :length, :], taps[g, length:, :]])

        @blocks(length)
        def _(i):
            low, high = at_rows(i), rows_at(i, BLOCK, length)
            cos, sin = extended[0, low, :], extended[1, low, :]

            def turned(which):
                real, imag = freq[which, low, :], -freq[which, high, :]
                return (cos * real - sin * imag) / length, (cos * imag + sin * real) / length

            real, imag = turned(0)
            late_real, late_imag = turned(1)
            place = lax.broadcasted_iota(jnp.int32, (BLOCK, LANES), 0)
            sign = (1 - 2 * (place % 2)).astype(jnp.float32)
            spectra[g, 0, low, :] = real.astype(jnp.bfloat16)
            spectra[g, 1, low, :] = imag.astype(jnp.bfloat16)
            spectra[g, 2, low, :] = (late_real - sign * imag).astype(jnp.bfloat16)
            spectra[g, 3, low, :] = (late_imag + sign * real).astype(jnp.bfloat16)

    def project(g, owner):
        @pl.loop(0, length // SPAN)
        def _(i):
            at = rows_at(i, SPAN)
            partial[g, at, :] += jnp.dot(
                stream[owner, at, :], weight[g, owner], preferred_element_type=jnp.float32
            )

    def projects_early(g, owner):
        far = jnp.abs(z - owner)
        own = owner // 2 == x
        return (
            (own & ((far <= 1) | ((far == 2) & (at_end | (g == 0)))))
            | (jnp.logical_not(own) & (far <= 2) & ((g == 0) | ((g == 1) & at_end)))
        )

    def to_mate(way, step, chunk):
        block = token_view(token_line.source(way, step), chunk)
        index = 3 + way * steps + step
        return remote(block, block, mate_send.at[index], mate_recv.at[index], mate)

    def mate_half(way, step, of):
        block = own_half(token_line.source(way, step), of)
        index = 3 + way * steps + step
        return remote(block, block, mate_send.at[index], mate_recv.at[index], mate)

    def await_mate(step):
        for way in range(2):

            @pl.when(token_line.receives(way, step))
            def _():
                mate_half(way, step, 1 - core).wait_recv()

    @pl.loop(0, steps * TOKEN_CHUNKS)
    def _(tick):
        step, chunk = tick // TOKEN_CHUNKS, tick % TOKEN_CHUNKS
        for way in range(2):

            @pl.when(token_line.receives(way, step))
            def _():
                token_line.arrived(way, step, (chunk,))
                to_mate(way, step, chunk).start()

            @pl.when(
                (step + 1 < steps)
                & token_line.receives(way, step)
                & token_line.sends(way, step + 1)
            )
            def _():
                token_line.copy(way, step + 1, (chunk,)).start()

        @pl.when((tick == TOKEN_CHUNKS // 2) & (x == 1))
        def _():
            for origin in range(2):
                view = tap_part(origin, y)
                remote(
                    view, view, tap_send.at[origin], tap_recv.at[origin], beside
                ).wait_recv()
                taps_beside(origin, y).start()

        @pl.when((tick % 2 == 1) & (tick >= 3) & (tick < 7 + 4 * WEIGHT_CHUNKS))
        def _():
            at = (tick - 3) // 2
            forward(at // WEIGHT_CHUNKS, at % WEIGHT_CHUNKS)

        @pl.when(tick == TOKEN_CHUNKS)
        def _():
            mate_half_own = own_half(z, 1 - core)
            remote(
                mate_half_own, mate_half_own, mate_send.at[0], mate_recv.at[0], mate
            ).wait_recv()
            await_mate(0)
            pltpu.make_async_copy(
                weight.at[:, s], weight.at[:, s], local_sem.at[2]
            ).wait()
            other = weight.at[:, mate_s]
            remote(other, other, mate_send.at[1], mate_recv.at[1], mate).wait_recv()
            other = taps.at[:, pl.ds(pl.multiple_of(mate_s * rows, rows), rows), :]
            remote(other, other, mate_send.at[2], mate_recv.at[2], mate).wait_recv()

            @pl.when(x == 1)
            def _():
                for origin in range(2):
                    taps_beside(origin, 1 - y).wait_recv()

        @pl.when((step == 1) & (chunk % 2 == 0))
        def _():
            tap_spectra(chunk // 2)

        @pl.when(tick == 2 * TOKEN_CHUNKS)
        def _():
            await_mate(1)

        owner = 2 * x + chunk // groups
        far = jnp.abs(z - owner)

        @pl.when(
            projects_early(chunk % groups, owner)
            & (((step == 1) & (far <= 1)) | ((step == 2) & (far == 2)))
        )
        def _():
            project(chunk % groups, owner)

        @pl.when(tick == 2 * TOKEN_CHUNKS)
        def _():
            await_beside(0)

        @pl.when((tick == 2 * TOKEN_CHUNKS + TOKEN_CHUNKS // 2) & at_end)
        def _():
            await_beside(1)

        guest = 2 * (1 - x) + (chunk // 2) % 2

        @pl.when((step == 2) & (chunk % 2 == 0) & projects_early(chunk // 4, guest))
        def _():
            project(chunk // 4, guest)

    await_mate(2)
    for by in range(1, chan_count):
        for of in range(2):
            view = sums.at[of, lax.rem(z + by, chan_count)]
            remote(
                view, view, sums_send.at[0], sums_recv.at[of, lax.rem(z + by, chan_count)], mate
            ).wait_recv()
    view = sums.at[1 - core, z]
    remote(view, view, sums_send.at[0], sums_recv.at[1 - core, z], mate).wait_recv()

    @blocks(length)
    def _(i):
        of, at = i // (rows // BLOCK), i % (rows // BLOCK)
        found = sums[of, 0, pl.ds(at, 1), :]
        for owner in range(1, chan_count):
            found = found + sums[of, owner, pl.ds(at, 1), :]
        found = lax.rsqrt(found / (chan_count * width) + EPSILON)
        scale[at_rows(i), :] = jnp.broadcast_to(found, (BLOCK, LANES)).T

    taps_mate().wait_send()

    @pl.when(x == 0)
    def _():
        taps_across(0).wait_send()
        taps_across(1).wait_send()

    def edge_copy(g):
        return remote(
            edge_out.at[g], edge.at[g], edge_send.at[0], edge_recv.at[g], across
        )

    def before_copy(g):
        return remote(
            signal.at[g], before.at[g], before_send.at[0], before_recv.at[g], across
        )

    def swap_copy(g):
        return remote(
            ready.at[g], full.at[z, g, core], swap_send.at[0], swap_recv.at[g], mate
        )

    line = Line(
        lambda owner, g, of: full.at[owner, g, of],
        chan_count,
        line_send,
        line_recv,
        lambda to: (y, s, to),
    )

    def projected(g, b, at):
        return (partial[g, at, b * LANES : (b + 1) * LANES] * scale[at, :]).astype(jnp.bfloat16)

    def featurize(g):
        @pl.when(x == 0)
        def _():
            for b in range(branches):
                edge_out[g, b] = projected(g, b, pl.ds(length - rim, rim))
                extended[b, 0:rim, :] = jnp.zeros((rim, LANES), jnp.float32)
            edge_copy(g).start()

        @blocks(length)
        def _(i):
            for b in range(branches):
                extended[b, pl.ds(pl.multiple_of(rim + i * BLOCK, rim), BLOCK), :] = projected(
                    g, b, at_rows(i)
                ).astype(jnp.float32)

        @pl.when(x == 1)
        def _():
            edge_copy(g).wait_recv()
            for b in range(branches):
                extended[b, 0:rim, :] = edge[g, b].astype(jnp.float32)

        chosen = lanes_of(core * share, g)
        coefficient = [
            [short[tap, b : b + 1, chosen] for b in range(branches)] for tap in range(SHORT)
        ]

        @blocks(length)
        def _(i):
            found = []
            for b in range(branches):
                value = jnp.zeros((BLOCK, LANES), jnp.float32)
                for tap in range(SHORT):
                    value = value + coefficient[tap][b] * extended[
                        b, pl.ds(rim - tap + i * BLOCK, BLOCK), :
                    ]
                found.append(value.astype(jnp.bfloat16))
            query[at_rows(i), :] = found[0]
            signal[g, at_rows(i), :] = (
                found[1].astype(jnp.float32) * found[2].astype(jnp.float32)
            ).astype(jnp.bfloat16)

    def convolve(g):
        joint = (x == 1) & (g > 0)

        @pl.when(jnp.logical_not(joint))
        def _():
            spectrum(0, lambda: signal[g])

        def product(i, which, first):
            low, high = at_rows(i), rows_at(i, BLOCK, length)
            cos, sin = freq[which, low, :], freq[which, high, :]
            real = spectra[g, first, low, :].astype(jnp.float32)
            imag = spectra[g, first + 1, low, :].astype(jnp.float32)
            return cos * real + sin * imag, sin * real - cos * imag

        @pl.when(x == 0)
        def _():
            @blocks(length)
            def _(i):
                real, imag = product(i, 0, 0)
                mixed[at_rows(i), :] = real.astype(jnp.bfloat16)
                mixed[rows_at(i, BLOCK, length), :] = imag.astype(jnp.bfloat16)

        @pl.when(x == 1)
        def _():
            before_copy(g).wait_recv()

            @pl.when(g == 0)
            def _():
                spectrum(1, lambda: before[g])

            @pl.when(g > 0)
            def _():
                spectrum_pair(lambda: [signal[g], before[g]])

            @blocks(length)
            def _(i):
                real, imag = product(i, 0, 0)
                more_real, more_imag = product(i, 1, 2)
                mixed[at_rows(i), :] = (real + more_real).astype(jnp.bfloat16)
                mixed[rows_at(i, BLOCK, length), :] = (imag + more_imag).astype(jnp.bfloat16)

        @pl.loop(0, length // SPAN)
        def _(i):
            low, high = rows_at(i, SPAN), rows_at(i, SPAN, length)
            freq[0, low, :] = jnp.dot(
                table[low, :], mixed[:length, :], preferred_element_type=jnp.float32
            ) + jnp.dot(table[high, :], mixed[length:, :], preferred_element_type=jnp.float32)

        direct = skip[:, lanes_of(core * share, g)]

        def gated(at):
            longer = freq[0, at, :] + direct * signal[g, at, :].astype(jnp.float32)
            longer = longer.astype(jnp.bfloat16).astype(jnp.float32)
            return (query[at, :].astype(jnp.float32) * longer).astype(jnp.bfloat16)

        @blocks(rows)
        def _(i):
            full[z, g, core, at_rows(i), :] = gated(
                pl.ds(pl.multiple_of(core * rows + i * BLOCK, BLOCK), BLOCK)
            )
            ready[g, at_rows(i), :] = gated(
                pl.ds(pl.multiple_of((1 - core) * rows + i * BLOCK, BLOCK), BLOCK)
            )

    def load_out():
        for owner in range(chan_count):
            pltpu.make_async_copy(
                out_weight.at[pl.ds(owner * length, length)], stream.at[owner], local_sem.at[1]
            ).start()

    def accumulate(owner, g):
        @pl.loop(0, total.shape[1] // (2 * LANES))
        def _(i):
            cols = rows_at(i, 2 * LANES)
            block = jnp.concatenate([full[owner, g, 0], full[owner, g, 1]], axis=1)
            kernel = jnp.concatenate(
                [stream[owner, lanes_of(of * share, g), cols] for of in range(2)], axis=0
            )
            total[:, cols] += jnp.dot(block, kernel, preferred_element_type=jnp.float32)

    def begin(g):
        swap_copy(g).start()
        for way in range(2):

            @pl.when(line.sends(way, 0))
            def _():
                line.copy(way, 0, (g, core)).start()

    def begin_other(g):
        other = full.at[z, g, 1 - core]
        remote(other, other, swap_send.at[0], swap_recv.at[g], mate).wait_recv()
        for way in range(2):

            @pl.when(line.sends(way, 0))
            def _():
                line.copy(way, 0, (g, 1 - core)).start()

    def settle():
        other = weight.at[:, s]
        remote(other, other, mate_send.at[1], mate_recv.at[1], mate).wait_send()
        for copy in sum_copies:
            copy.wait_send()

        @pl.when(x == 1)
        def _():
            for origin in range(2):
                taps_beside(origin, y).wait_send()

        for at in range(2):
            view = weight_half(s, y)
            remote(view, view, x_send.at[at], x_recv.at[0, 0, 0], across).wait_send()
            view = weight_half((1 - x) * 2 + at, y)
            remote(view, view, y_send.at[at], y_recv.at[at, 0], beside).wait_send()

        @pl.when(x == 0)
        def _():
            remote(edge_out, edge, edge_send.at[0], edge_recv.at[0], across).wait_send()
            remote(signal, before, before_send.at[0], before_recv.at[0], across).wait_send()

    def settle_tokens():
        mate_tokens().wait_send()
        for way in range(2):
            for step in range(steps):

                @pl.when(token_line.receives(way, step))
                def _():
                    mate_half(way, step, core).wait_send()

                @pl.when(token_line.sends(way, step))
                def _():
                    token_line.drain(way, step, (0,), lambda owner: own_half(owner, core))

    def way_of(k):
        return jnp.where(z < chan_count // 2, 1 - k, k)

    def late_forwards(g, at, inner, outer):
        for here, pieces in ((jnp.logical_not(at_end), inner), (at_end, outer)):

            @pl.when((g == at) & here)
            def _():
                for group, c in pieces:
                    forward(group, c)

    def pass_on(way, step, at):
        @pl.when(
            (at >= 0) & (at < groups) & line.receives(way, step) & line.sends(way, step + 1)
        )
        def _():
            for of in (core, 1 - core):
                line.arrived(way, step, (at, of))
                line.copy(way, step + 1, (at, of)).start()

    for copy in small_loads[1:]:
        copy.wait()
    near, away = way_of(0), way_of(1)

    @pl.loop(0, groups)
    def _(g):
        @pl.when(g == 3)
        def _():
            pass_on(away, 0, 1)
            pass_on(near, 0, 2)

        @pl.when((g >= 2) | ((g == 1) & jnp.logical_not(at_end)))
        def _():
            await_beside(g)

        @pl.loop(0, chan_count)
        def _(owner):
            @pl.when(jnp.logical_not(projects_early(g, owner)))
            def _():
                project(g, owner)

        @pl.when(g == groups - 1)
        def _():
            settle_tokens()
            load_out()

        featurize(g)

        @pl.when(x == 0)
        def _():
            before_copy(g).start()

            for at, inner, outer in (
                (0, [(groups - 2, 2)], [(groups - 1, 2)]),
                (1, [(groups - 2, 3), (groups - 1, 0), (groups - 1, 1)], [(groups - 1, 3)]),
                (2, [(groups - 1, 2), (groups - 1, 3)], []),
            ):

                @pl.when((g == at) & jnp.logical_not(at_end))
                def _():
                    for group, c in inner:
                        send_weights(group, [c])

                @pl.when((g == at) & at_end)
                def _():
                    for group, c in outer:
                        send_weights(group, [c])

        @pl.when(g == 1)
        def _():
            pass_on(near, 0, 0)

        late_forwards(g, 1, [(groups - 2, 3)], [(groups - 1, 0), (groups - 1, 1)])
        late_forwards(g, 2, [(groups - 1, 0), (groups - 1, 1)], [(groups - 1, 3)])

        @pl.when(g == 2)
        def _():
            pass_on(near, 0, 1)
            pass_on(away, 0, 0)

        @pl.when(g == 3)
        def _():
            pass_on(near, 1, 1)
            pass_on(away, 0, 2)

        late_forwards(g, 0, [], [(groups - 2, 2), (groups - 2, 3)])
        convolve(g)
        begin(g)
        late_forwards(g, 0, [(groups - 2, 2)], [])
        late_forwards(g, 1, [], [(groups - 1, 2)])
        begin_other(g)

        late_forwards(g, 2, [(groups - 1, 2), (groups - 1, 3)], [])

        @pl.when(g == 2)
        def _():
            pass_on(near, 1, 0)

    pltpu.make_async_copy(stream, stream, local_sem.at[1]).wait()

    @pl.loop(0, groups + steps - 1)
    def _(n):
        for at, pieces in (
            (0, [(near, 1, 2)]),
            (1, [(near, 0, 3), (away, 0, 3)]),
            (3, [(near, 1, 3)]),
        ):

            @pl.when(n == at)
            def _():
                for way, step, group in pieces:
                    pass_on(way, step, group)

        @pl.when(n == 2)
        def _():
            settle()

        @pl.when(n < groups)
        def _():
            accumulate(z, n)

        @pl.loop(0, 2)
        def _(way):
            for step in range(steps):
                at = n - jnp.where(at_end, step, 0)

                @pl.when((at >= 0) & (at < groups) & line.receives(way, step))
                def _():
                    @pl.when(jnp.logical_not(line.sends(way, step + 1)))
                    def _():
                        for of in range(2):
                            line.arrived(way, step, (at, of))

                    accumulate(line.source(way, step), at)

    @blocks(rows)
    def _(i):
        result[at_rows(i), :] = total[at_rows(i), :].astype(jnp.bfloat16)

    remote(ready, ready, swap_send.at[0], swap_recv.at[0], mate).wait_send()
    for way in range(2):
        for step in range(steps):

            @pl.when(line.sends(way, step))
            def _():
                line.drain(way, step, (0, 0), lambda owner: full.at[owner])


def chip_body(tokens, norm_gain, proj_weight, short_filter, long_filter, skip_gain, out_weight):
    chan_count = lax.axis_size("chan")
    rows, width = tokens.shape
    depth, branches, local_chan = proj_weight.shape
    length, share = 2 * rows, local_chan // 2
    groups = share // LANES
    steps = chan_count - 1
    dma = pltpu.SemaphoreType.DMA
    f32, bf16 = jnp.float32, jnp.bfloat16
    vmem = pl.BlockSpec(memory_space=pltpu.VMEM)
    return pl.pallas_call(
        functools.partial(block_kernel, chan_count),
        out_shape=jax.ShapeDtypeStruct((rows, width), bf16),
        in_specs=[HBM] * 7,
        out_specs=vmem,
        scratch_shapes=[
            pltpu.VMEM((1, width), f32),
            pltpu.VMEM(short_filter.shape, f32),
            pltpu.VMEM((1, local_chan), f32),
            pltpu.VMEM((chan_count, length, width), bf16),
            pltpu.VMEM((groups, 4, depth, branches * LANES), bf16),
            pltpu.VMEM((2, chan_count, 8, LANES), f32),
            pltpu.VMEM((length, LANES), f32),
            pltpu.VMEM((groups, length, branches * LANES), f32),
            pltpu.VMEM((2 * length, length), bf16),
            pltpu.VMEM((groups, 2 * length, LANES), bf16),
            pltpu.VMEM((groups, 4, length, LANES), bf16),
            pltpu.VMEM((2, 2 * length, LANES), f32),
            pltpu.VMEM((2 * length, LANES), bf16),
            pltpu.VMEM((groups, branches, 16, LANES), bf16),
            pltpu.VMEM((groups, branches, 16, LANES), bf16),
            pltpu.VMEM((branches, length + 16, LANES), f32),
            pltpu.VMEM((length, LANES), bf16),
            pltpu.VMEM((groups, length, LANES), bf16),
            pltpu.VMEM((groups, length, LANES), bf16),
            pltpu.VMEM((groups, rows, LANES), bf16),
            pltpu.VMEM((chan_count, groups, 2, rows, LANES), bf16),
            pltpu.VMEM((rows, width), f32),
            dma((10,)),
            dma((3 + 2 * steps,)),
            dma((3 + 2 * steps,)),
            dma((2, steps)),
            dma((steps, TOKEN_CHUNKS)),
            dma((2 * chan_count - 1,)),
            dma((2, chan_count)),
            dma((2,)),
            dma((2, groups, WEIGHT_CHUNKS)),
            dma((2,)),
            dma((2, groups)),
            dma((4,)),
            dma((4,)),
            dma((1,)),
            dma((groups,)),
            dma((1,)),
            dma((groups,)),
            dma((1,)),
            dma((groups,)),
            dma((2, steps)),
            dma((steps, groups, 2)),
        ],
        compiler_params=pltpu.CompilerParams(
            collective_id=0, has_side_effects=True, vmem_limit_bytes=52 * 1024 * 1024
        ),
        name="block",
    )(
        tokens,
        pltpu.with_memory_space_constraint(norm_gain[None, :], pltpu.HBM),
        proj_weight.transpose(1, 0, 2),
        pltpu.with_memory_space_constraint(short_filter, pltpu.HBM),
        long_filter,
        pltpu.with_memory_space_constraint(skip_gain[None, :], pltpu.HBM),
        out_weight,
    )


def select_body(mesh):
    if (mesh.shape["groups"], mesh.shape["seq"], mesh.shape["chan"]) == (2, 4, 4):
        return chip_body
    return body


def solution(mesh):
    placed = (
        P(("groups", "seq"), "chan"),
        P(),
        P("seq", None, "chan"),
        P(None, None, "chan"),
        P("chan", "seq"),
        P("chan"),
        P(None, "chan"),
    )
    return jax.shard_map(
        select_body(mesh), mesh=mesh, in_specs=placed, out_specs=P(("groups", "seq"), "chan"), check_vma=False
    )
```

```python
import functools
import math

import jax
import jax.numpy as jnp
import numpy as np
from jax import lax
from jax.experimental import pallas as pl
from jax.experimental.pallas import tpu as pltpu
from jax.sharding import PartitionSpec as P

SHORT = 3


EPSILON = 1e-06
HIGHEST = lax.Precision.HIGHEST


def from_behind(value, axis, steps):
    count = lax.axis_size(axis)
    initial, last = (max(0, -steps), min(count, count - steps))
    return lax.ppermute(value, axis, [(source, source + steps) for source in range(initial, last)])


def angle_table(row_count, col_count, period, sign):
    row_index = lax.iota(jnp.int32, row_count)[:, None]
    col_index = lax.iota(jnp.int32, col_count)[None, :]
    angles = (row_index * col_index % period).astype(jnp.float32) * (sign * 2.0 * math.pi / period)
    return (jnp.cos(angles), jnp.sin(angles))


def forward_spectrum(signal_rows, first, second):
    channels = signal_rows.shape[0]
    grid_rows = signal_rows.reshape(channels, first, second)
    cos_first, sin_first = angle_table(first, first, first, -1.0)
    part_re = jnp.einsum("cab,ak->ckb", grid_rows, cos_first, precision=HIGHEST)
    part_im = jnp.einsum("cab,ak->ckb", grid_rows, sin_first, precision=HIGHEST)
    twist_cos, twist_sin = angle_table(first, second, first * second, -1.0)
    part_re, part_im = (
        part_re * twist_cos - part_im * twist_sin,
        part_re * twist_sin + part_im * twist_cos,
    )
    cos_second, sin_second = angle_table(second, second, second, -1.0)
    spectrum_real = jnp.einsum("ckb,bm->ckm", part_re, cos_second, precision=HIGHEST) - jnp.einsum(
        "ckb,bm->ckm", part_im, sin_second, precision=HIGHEST
    )
    spec_im = jnp.einsum("ckb,bm->ckm", part_re, sin_second, precision=HIGHEST) + jnp.einsum(
        "ckb,bm->ckm", part_im, cos_second, precision=HIGHEST
    )
    return (spectrum_real, spec_im)


def inverse_spectrum(spectrum_real, spec_im, first, second):
    channels = spectrum_real.shape[0]
    cos_second, sin_second = angle_table(second, second, second, 1.0)
    part_re = jnp.einsum("ckm,bm->ckb", spectrum_real, cos_second, precision=HIGHEST) - jnp.einsum(
        "ckm,bm->ckb", spec_im, sin_second, precision=HIGHEST
    )
    part_im = jnp.einsum("ckm,bm->ckb", spectrum_real, sin_second, precision=HIGHEST) + jnp.einsum(
        "ckm,bm->ckb", spec_im, cos_second, precision=HIGHEST
    )
    twist_cos, twist_sin = angle_table(first, second, first * second, 1.0)
    part_re, part_im = (
        part_re * twist_cos - part_im * twist_sin,
        part_re * twist_sin + part_im * twist_cos,
    )
    cos_first, sin_first = angle_table(first, first, first, 1.0)
    result = jnp.einsum("ckb,ak->cab", part_re, cos_first, precision=HIGHEST) - jnp.einsum(
        "ckb,ak->cab", part_im, sin_first, precision=HIGHEST
    )
    return result.reshape(channels, first * second) / (first * second)


def spectral_conv(signal_rows, filter_rows):
    channels, length = signal_rows.shape
    padded_len = 2 * length
    log_len = padded_len.bit_length() - 1
    first = 1 << log_len // 2
    second = padded_len // first
    zeros_tail = jnp.zeros((channels, length), jnp.float32)
    sig_re, sig_im = forward_spectrum(
        jnp.concatenate([signal_rows, zeros_tail], axis=1), first, second
    )
    tap_re, tap_im = forward_spectrum(
        jnp.concatenate([filter_rows, zeros_tail], axis=1), first, second
    )
    prod_re = sig_re * tap_re - sig_im * tap_im
    prod_im = sig_re * tap_im + sig_im * tap_re
    return inverse_spectrum(prod_re, prod_im, first, second)[:, :length]


def short_filter_output(projected, rim_cells, kernel_coefficients):
    count = kernel_coefficients.shape[0]
    steps_len = projected.shape[2]
    extended = jnp.concatenate([rim_cells, projected], axis=2).astype(jnp.float32)
    total = jnp.zeros(projected.shape, jnp.float32)
    for tap in range(count):
        total = (
            total
            + kernel_coefficients[tap][:, :, None]
            * extended[:, :, count - 1 - tap : count - 1 - tap + steps_len]
        )
    return total.astype(jnp.bfloat16)


def hyena_mixer(keys_rows, values_rows, long_taps, skip_part):
    middle = keys_rows.astype(jnp.float32) * values_rows.astype(jnp.float32)
    return (spectral_conv(middle, long_taps) + skip_part[:, None] * middle).astype(jnp.bfloat16)


def body(tokens, norm_gain, proj_weight, short_filter, long_filter, skip_gain, out_weight):
    seq_count = lax.axis_size("seq")
    local_rows = tokens.shape[0]
    local_chan = proj_weight.shape[2]
    subset = local_chan // seq_count
    length = local_rows * seq_count
    offset = lax.axis_index("seq") * subset
    whole = lax.all_gather(tokens, "chan", axis=1, tiled=True)
    wide = whole.astype(jnp.float32)
    rescaled_signal = (
        wide * lax.rsqrt(jnp.mean(wide * wide, axis=1, keepdims=True) + EPSILON) * norm_gain
    ).astype(jnp.bfloat16)
    projected = lax.dot_general(
        lax.all_gather(proj_weight, "seq", axis=0, tiled=True),
        rescaled_signal,
        (((0,), (1,)), ((), ())),
        preferred_element_type=jnp.float32,
    ).astype(jnp.bfloat16)
    taps_grid = long_filter.reshape(1, seq_count, subset, local_rows)
    long_taps = lax.all_to_all(taps_grid, "seq", split_axis=1, concat_axis=3, tiled=True).reshape(
        subset, length
    )
    skip_part = lax.dynamic_slice_in_dim(skip_gain, offset, subset, 0)
    rim_cells = from_behind(projected[:, :, local_rows - (SHORT - 1) :], "seq", 1)
    featured = short_filter_output(projected, rim_cells, short_filter)
    pair_grid = featured[1:].reshape(2, seq_count, subset, local_rows)
    moved = lax.all_to_all(pair_grid, "seq", split_axis=1, concat_axis=3, tiled=True).reshape(
        2, subset, length
    )
    result = hyena_mixer(moved[0], moved[1], long_taps, skip_part)
    returned = lax.all_to_all(
        result.reshape(1, subset, length), "seq", split_axis=2, concat_axis=0, tiled=True
    )
    returned = returned.reshape(local_chan, local_rows)
    gated = (featured[0].astype(jnp.float32) * returned.astype(jnp.float32)).astype(jnp.bfloat16)
    full_mix = lax.all_gather(gated, "chan", axis=0, tiled=True)
    update = lax.dot_general(
        full_mix, out_weight, (((0,), (0,)), ((), ())), preferred_element_type=jnp.float32
    )
    return (tokens.astype(jnp.float32) + update).astype(jnp.bfloat16)

LANES = 128
BLOCK = 128
SPAN = 1024
TOKEN_CHUNKS = 8
WEIGHT_CHUNKS = 4
HBM = pl.BlockSpec(memory_space=pltpu.HBM)


def remote(src, dst, send_sem, recv_sem, where):
    return pltpu.make_async_remote_copy(
        src_ref=src,
        dst_ref=dst,
        send_sem=send_sem,
        recv_sem=recv_sem,
        device_id=where,
        device_id_type=pl.DeviceIdType.MESH,
    )


class Line:
    def __init__(self, view, count, send_sem, recv_sem, place):
        self.view, self.count, self.place = view, count, place
        self.send_sem, self.recv_sem = send_sem, recv_sem
        self.me = lax.axis_index("chan")

    def move(self, way, step, piece, block, target):
        slot = jnp.minimum(jnp.where(way == 0, step, target + step), self.count - 2)
        recv = self.recv_sem.at[(slot,) + piece]
        return remote(block, block, self.send_sem.at[way, step], recv, self.place(target))

    def drain(self, way, step, first, block):
        self.move(way, step, first, block(self.source(way, step - 1)), self.me).wait_send()

    def source(self, way, step):
        return jnp.clip(self.me - (step + 1) * (1 - 2 * way), 0, self.count - 1)

    def copy(self, way, step, piece):
        owner = self.source(way, step - 1)
        target = self.source(way, -2)
        return self.move(way, step, piece, self.view(owner, *piece), target)

    def inside(self, way, by):
        place = self.me + by * (1 - 2 * way)
        return (place >= 0) & (place < self.count)

    def sends(self, way, step):
        return self.inside(way, -step) & self.inside(way, 1)

    def receives(self, way, step):
        return self.inside(way, -1 - step)

    def arrived(self, way, step, piece):
        owner = self.source(way, step)
        self.move(way, step, piece, self.view(owner, *piece), self.me).wait_recv()
        return owner


def block_kernel(
    chan_count,
    tokens,
    gain_hbm,
    weights,
    short_hbm,
    long_taps,
    skip_hbm,
    out_weight,
    result,
    gain,
    short,
    skip,
    stream,
    weight,
    sums,
    scale,
    partial,
    table,
    taps,
    spectra,
    freq,
    mixed,
    edge_out,
    edge,
    extended,
    query,
    signal,
    before,
    ready,
    full,
    total,
    local_sem,
    mate_send,
    mate_recv,
    token_send,
    token_recv,
    sums_send,
    sums_recv,
    x_send,
    x_recv,
    y_send,
    y_recv,
    tap_send,
    tap_recv,
    edge_send,
    edge_recv,
    before_send,
    before_recv,
    swap_send,
    swap_recv,
    line_send,
    line_recv,
):
    y, s, z = (lax.axis_index(name) for name in ("groups", "seq", "chan"))
    x, core = s // 2, s % 2
    mate_s = s + 1 - 2 * core
    mate = (y, mate_s, z)
    across = (y, (1 - x) * 2 + core, z)
    aslant = (y, (1 - x) * 2 + 1 - core, z)
    beside = (1 - y, s, z)
    rows, width = tokens.shape
    length = 2 * rows
    branches, depth = weights.shape[0], weights.shape[1]
    half = depth // 2
    share = weights.shape[2] // 2
    groups = share // LANES
    rim = edge.shape[2]
    steps = chan_count - 1
    token_rows = rows // TOKEN_CHUNKS
    weight_rows = half // WEIGHT_CHUNKS

    column_peers = [mate] + [
        (y, 2 * x + of, lax.rem(z + by, chan_count))
        for by in range(1, chan_count)
        for of in (core, 1 - core)
    ]
    peers = column_peers + [across, aslant, beside]

    def rows_at(i, count, base=0):
        return pl.ds(pl.multiple_of(base + i * count, count), count)

    def at_rows(i):
        return rows_at(i, BLOCK)

    def blocks(count):
        return pl.loop(0, count // BLOCK)

    def lanes_of(base, g):
        return pl.ds(pl.multiple_of(base + g * LANES, LANES), LANES)

    tap_stage = [(0, 0), (0, length), (1, 0), (1, length)]
    tap_loads = [
        pltpu.make_async_copy(
            long_taps.at[:, pl.ds(j * LANES, LANES)],
            freq.at[which, pl.ds(start, length)],
            local_sem.at[4 + j],
        )
        for j, (which, start) in enumerate(tap_stage)
    ]
    token_load = pltpu.make_async_copy(tokens, result, local_sem.at[0])
    token_load.start()
    small_loads = [
        pltpu.make_async_copy(src, dst, local_sem.at[at])
        for src, dst, at in (
            (gain_hbm.at[:, pl.ds(pl.multiple_of(z * width, width), width)], gain, 3),
            (short_hbm, short, 8),
            (skip_hbm, skip, 9),
        )
    ]
    for copy in small_loads:
        copy.start()
    barrier = pltpu.get_barrier_semaphore()
    for peer in peers:
        pl.semaphore_signal(barrier, inc=1, device_id=peer, device_id_type=pl.DeviceIdType.MESH)
    for copy in tap_loads:
        copy.start()
    for g in range(groups):
        for b in range(branches):
            pltpu.make_async_copy(
                weights.at[b, :, lanes_of(core * share, g)],
                weight.at[g, s, :, pl.ds(b * LANES, LANES)],
                local_sem.at[2],
            ).start()

    sums[core, z] = jnp.zeros(sums.shape[2:], jnp.float32)
    small_loads[0].wait()
    own_gain = gain[...]
    token_load.wait()

    @blocks(rows)
    def _(i):
        raw = result[at_rows(i), :].astype(jnp.float32)
        total[at_rows(i), :] = raw
        stream[z, pl.ds(pl.multiple_of(core * rows + i * BLOCK, BLOCK), BLOCK), :] = (
            raw * own_gain
        ).astype(jnp.bfloat16)
        square = raw * raw
        found = square[:, :LANES]
        for part in range(1, width // LANES):
            found = found + square[:, part * LANES : (part + 1) * LANES]
        sums[core, z, pl.ds(i, 1), :] = jnp.sum(found.T, axis=0, keepdims=True)

    pl.semaphore_wait(barrier, len(peers))

    def token_view(owner, chunk):
        return stream.at[owner, rows_at(chunk, token_rows, core * rows), :]

    token_line = Line(
        token_view, chan_count, token_send, token_recv, lambda to: (y, s, to)
    )
    for chunk in range(TOKEN_CHUNKS):
        for way in range(2):

            @pl.when(token_line.sends(way, 0))
            def _():
                token_line.copy(way, 0, (chunk,)).start()

    def own_half(owner, of):
        return stream.at[owner, pl.ds(pl.multiple_of(of * rows, rows), rows), :]

    def mate_tokens():
        return remote(
            own_half(z, core), own_half(z, core), mate_send.at[0], mate_recv.at[0], mate
        )

    mate_tokens().start()
    sum_copies = [
        remote(
            sums.at[core, z], sums.at[core, z], sums_send.at[at], sums_recv.at[core, z], peer
        )
        for at, peer in enumerate(column_peers)
    ]
    for copy in sum_copies:
        copy.start()
    for g in range(groups):
        for b in range(branches):
            remote(
                weights.at[b, :, lanes_of((1 - core) * share, g)],
                weight.at[g, s, :, pl.ds(b * LANES, LANES)],
                mate_send.at[1],
                mate_recv.at[1],
                mate,
            ).start()

    for j, (which, start) in enumerate(tap_stage):
        tap_loads[j].wait()

        @pl.loop(0, groups)
        def _(g):
            mine = freq[which, rows_at(core * groups + g, BLOCK, start), :]
            taps[g, pl.ds(pl.multiple_of(s * rows + j * LANES, LANES), LANES), :] = mine.T.astype(
                jnp.bfloat16
            )
            other = freq[which, rows_at((1 - core) * groups + g, BLOCK, start), :]
            ready[g, j * LANES : (j + 1) * LANES, :] = other.T.astype(jnp.bfloat16)

    def tap_part(owner, part):
        return taps.at[
            :, pl.ds(pl.multiple_of(owner * rows + part * (rows // 2), rows // 2), rows // 2), :
        ]

    def taps_across(to):
        src = tap_part(s, y) if to == 0 else ready.at[
            :, pl.ds(pl.multiple_of(y * (rows // 2), rows // 2), rows // 2), :
        ]
        return remote(
            src,
            tap_part(s, y),
            tap_send.at[to],
            tap_recv.at[core],
            across if to == 0 else aslant,
        )

    def taps_beside(origin, part):
        view = tap_part(origin, part)
        return remote(view, view, tap_send.at[2 + origin], tap_recv.at[2 + origin], beside)

    def taps_mate():
        return remote(
            ready,
            taps.at[:, pl.ds(pl.multiple_of(s * rows, rows), rows), :],
            mate_send.at[2],
            mate_recv.at[2],
            mate,
        )

    @pl.when(x == 0)
    def _():
        taps_across(0).start()
        taps_across(1).start()

        @pl.loop(0, groups)
        def _(g):
            taps[g, length:, :] = jnp.zeros((length, LANES), jnp.bfloat16)

    taps_mate().start()

    def weight_view(owner, part, g, c):
        return weight.at[g, owner, rows_at(c, weight_rows, part * half), :]

    def weight_half(owner, part):
        return weight.at[:, owner, pl.ds(pl.multiple_of(part * half, half), half), :]

    def send_weights(g, chunks=range(WEIGHT_CHUNKS)):
        for c in chunks:
            for to in range(2):
                side = core if to == 0 else 1 - core
                view = weight_view(s, y, g, c)
                for b in range(branches):
                    remote(
                        weights.at[
                            b,
                            rows_at(c, weight_rows, y * half),
                            pl.ds(pl.multiple_of(side * share + g * LANES, LANES), LANES),
                        ],
                        view.at[:, pl.ds(b * LANES, LANES)],
                        x_send.at[to],
                        x_recv.at[core, g, c],
                        across if to == 0 else aslant,
                    ).start()

    for g in range(groups - 2):
        send_weights(g)
    send_weights(groups - 2, range(2))

    at_end = (z == 0) | (z == chan_count - 1)

    @pl.when((x == 1) | at_end)
    def _():
        send_weights(groups - 2, [2, 3])
        send_weights(groups - 1, [0, 1])

    @pl.when(x == 1)
    def _():
        send_weights(groups - 1, [2, 3])

    def beside_copy(origin, part, g, c):
        view = weight_view((1 - x) * 2 + origin, part, g, c)
        return remote(view, view, y_send.at[origin], y_recv.at[origin, g], beside)

    def forward(g, c):
        for origin in range(2):
            view = weight_view((1 - x) * 2 + origin, y, g, c)
            remote(
                view, view, x_send.at[origin], x_recv.at[origin, g, c], beside
            ).wait_recv()
            beside_copy(origin, y, g, c).start()

    def await_beside(g):
        for origin in range(2):
            view = weight.at[
                g, (1 - x) * 2 + origin, pl.ds(pl.multiple_of((1 - y) * half, half), half), :
            ]
            remote(view, view, y_send.at[origin], y_recv.at[origin, g], beside).wait_recv()

    @blocks(length)
    def _(i):
        row = lax.broadcasted_iota(jnp.int32, (BLOCK, LANES), 0) + i * BLOCK
        lane = lax.broadcasted_iota(jnp.int32, (BLOCK, LANES), 1)
        unit = math.pi / (4 * length)
        odd = 2 * row + 1
        small = odd.astype(jnp.float32) * unit
        extended[0, at_rows(i), :] = jnp.cos(small)
        extended[1, at_rows(i), :] = jnp.sin(small)
        period = 8 * length
        angle = (odd * (2 * lane + 1) % period).astype(jnp.float32) * unit
        cos, sin = jnp.cos(angle), jnp.sin(angle)
        stride = (odd * (2 * LANES) % period).astype(jnp.float32) * unit
        step_cos, step_sin = jnp.cos(stride), jnp.sin(stride)
        for a in range(length // LANES):
            table[at_rows(i), a * LANES : (a + 1) * LANES] = cos.astype(jnp.bfloat16)
            table[rows_at(i, BLOCK, length), a * LANES : (a + 1) * LANES] = sin.astype(
                jnp.bfloat16
            )
            cos, sin = cos * step_cos - sin * step_sin, sin * step_cos + cos * step_sin

    for g in range(groups):

        @blocks(length)
        def _(i):
            partial[g, at_rows(i), :] = jnp.zeros((BLOCK, branches * LANES), jnp.float32)

    def spectrum(which, column):
        @pl.loop(0, 2 * length // SPAN)
        def _(i):
            at = rows_at(i, SPAN)
            freq[which, at, :] = jnp.dot(
                table[at, :], column(), preferred_element_type=jnp.float32
            )

    def spectrum_pair(columns):
        @pl.loop(0, 2 * length // SPAN)
        def _(i):
            at = rows_at(i, SPAN)
            found = jnp.dot(
                table[at, :],
                jnp.concatenate(columns(), axis=1),
                preferred_element_type=jnp.float32,
            )
            freq[0, at, :] = found[:, :LANES]
            freq[1, at, :] = found[:, LANES:]

    def tap_spectra(g):
        spectrum_pair(lambda: [taps[g, :length, :], taps[g, length:, :]])

        @blocks(length)
        def _(i):
            low, high = at_rows(i), rows_at(i, BLOCK, length)
            cos, sin = extended[0, low, :], extended[1, low, :]

            def turned(which):
                real, imag = freq[which, low, :], -freq[which, high, :]
                return (cos * real - sin * imag) / length, (cos * imag + sin * real) / length

            real, imag = turned(0)
            late_real, late_imag = turned(1)
            place = lax.broadcasted_iota(jnp.int32, (BLOCK, LANES), 0)
            sign = (1 - 2 * (place % 2)).astype(jnp.float32)
            spectra[g, 0, low, :] = real.astype(jnp.bfloat16)
            spectra[g, 1, low, :] = imag.astype(jnp.bfloat16)
            spectra[g, 2, low, :] = (late_real - sign * imag).astype(jnp.bfloat16)
            spectra[g, 3, low, :] = (late_imag + sign * real).astype(jnp.bfloat16)

    def project(g, owner):
        @pl.loop(0, length // SPAN)
        def _(i):
            at = rows_at(i, SPAN)
            partial[g, at, :] += jnp.dot(
                stream[owner, at, :], weight[g, owner], preferred_element_type=jnp.float32
            )

    def projects_early(g, owner):
        far = jnp.abs(z - owner)
        own = owner // 2 == x
        return (
            (own & ((far <= 1) | ((far == 2) & (at_end | (g == 0)))))
            | (jnp.logical_not(own) & (far <= 2) & ((g == 0) | ((g == 1) & at_end)))
        )

    def to_mate(way, step, chunk):
        block = token_view(token_line.source(way, step), chunk)
        index = 3 + way * steps + step
        return remote(block, block, mate_send.at[index], mate_recv.at[index], mate)

    def mate_half(way, step, of):
        block = own_half(token_line.source(way, step), of)
        index = 3 + way * steps + step
        return remote(block, block, mate_send.at[index], mate_recv.at[index], mate)

    def await_mate(step):
        for way in range(2):

            @pl.when(token_line.receives(way, step))
            def _():
                mate_half(way, step, 1 - core).wait_recv()

    @pl.loop(0, steps * TOKEN_CHUNKS)
    def _(tick):
        step, chunk = tick // TOKEN_CHUNKS, tick % TOKEN_CHUNKS
        for way in range(2):

            @pl.when(token_line.receives(way, step))
            def _():
                token_line.arrived(way, step, (chunk,))
                to_mate(way, step, chunk).start()

            @pl.when(
                (step + 1 < steps)
                & token_line.receives(way, step)
                & token_line.sends(way, step + 1)
            )
            def _():
                token_line.copy(way, step + 1, (chunk,)).start()

        @pl.when((tick == TOKEN_CHUNKS // 2) & (x == 1))
        def _():
            for origin in range(2):
                view = tap_part(origin, y)
                remote(
                    view, view, tap_send.at[origin], tap_recv.at[origin], beside
                ).wait_recv()
                taps_beside(origin, y).start()

        @pl.when((tick % 2 == 1) & (tick >= 3) & (tick < 7 + 4 * WEIGHT_CHUNKS))
        def _():
            at = (tick - 3) // 2
            forward(at // WEIGHT_CHUNKS, at % WEIGHT_CHUNKS)

        @pl.when(tick == TOKEN_CHUNKS)
        def _():
            mate_half_own = own_half(z, 1 - core)
            remote(
                mate_half_own, mate_half_own, mate_send.at[0], mate_recv.at[0], mate
            ).wait_recv()
            await_mate(0)
            pltpu.make_async_copy(
                weight.at[:, s], weight.at[:, s], local_sem.at[2]
            ).wait()
            other = weight.at[:, mate_s]
            remote(other, other, mate_send.at[1], mate_recv.at[1], mate).wait_recv()
            other = taps.at[:, pl.ds(pl.multiple_of(mate_s * rows, rows), rows), :]
            remote(other, other, mate_send.at[2], mate_recv.at[2], mate).wait_recv()

            @pl.when(x == 1)
            def _():
                for origin in range(2):
                    taps_beside(origin, 1 - y).wait_recv()

        @pl.when((step == 1) & (chunk % 2 == 0))
        def _():
            tap_spectra(chunk // 2)

        @pl.when(tick == 2 * TOKEN_CHUNKS)
        def _():
            await_mate(1)

        owner = 2 * x + chunk // groups
        far = jnp.abs(z - owner)

        @pl.when(
            projects_early(chunk % groups, owner)
            & (((step == 1) & (far <= 1)) | ((step == 2) & (far == 2)))
        )
        def _():
            project(chunk % groups, owner)

        @pl.when(tick == 2 * TOKEN_CHUNKS)
        def _():
            await_beside(0)

        @pl.when((tick == 2 * TOKEN_CHUNKS + TOKEN_CHUNKS // 2) & at_end)
        def _():
            await_beside(1)

        guest = 2 * (1 - x) + (chunk // 2) % 2

        @pl.when((step == 2) & (chunk % 2 == 0) & projects_early(chunk // 4, guest))
        def _():
            project(chunk // 4, guest)

    await_mate(2)
    for by in range(1, chan_count):
        for of in range(2):
            view = sums.at[of, lax.rem(z + by, chan_count)]
            remote(
                view, view, sums_send.at[0], sums_recv.at[of, lax.rem(z + by, chan_count)], mate
            ).wait_recv()
    view = sums.at[1 - core, z]
    remote(view, view, sums_send.at[0], sums_recv.at[1 - core, z], mate).wait_recv()

    @blocks(length)
    def _(i):
        of, at = i // (rows // BLOCK), i % (rows // BLOCK)
        found = sums[of, 0, pl.ds(at, 1), :]
        for owner in range(1, chan_count):
            found = found + sums[of, owner, pl.ds(at, 1), :]
        found = lax.rsqrt(found / (chan_count * width) + EPSILON)
        scale[at_rows(i), :] = jnp.broadcast_to(found, (BLOCK, LANES)).T

    taps_mate().wait_send()

    @pl.when(x == 0)
    def _():
        taps_across(0).wait_send()
        taps_across(1).wait_send()

    def edge_copy(g):
        return remote(
            edge_out.at[g], edge.at[g], edge_send.at[0], edge_recv.at[g], across
        )

    def before_copy(g):
        return remote(
            signal.at[g], before.at[g], before_send.at[0], before_recv.at[g], across
        )

    def swap_copy(g):
        return remote(
            ready.at[g], full.at[z, g, core], swap_send.at[0], swap_recv.at[g], mate
        )

    line = Line(
        lambda owner, g, of: full.at[owner, g, of],
        chan_count,
        line_send,
        line_recv,
        lambda to: (y, s, to),
    )

    def projected(g, b, at):
        return (partial[g, at, b * LANES : (b + 1) * LANES] * scale[at, :]).astype(jnp.bfloat16)

    def featurize(g):
        @pl.when(x == 0)
        def _():
            for b in range(branches):
                edge_out[g, b] = projected(g, b, pl.ds(length - rim, rim))
                extended[b, 0:rim, :] = jnp.zeros((rim, LANES), jnp.float32)
            edge_copy(g).start()

        @blocks(length)
        def _(i):
            for b in range(branches):
                extended[b, pl.ds(pl.multiple_of(rim + i * BLOCK, rim), BLOCK), :] = projected(
                    g, b, at_rows(i)
                ).astype(jnp.float32)

        @pl.when(x == 1)
        def _():
            edge_copy(g).wait_recv()
            for b in range(branches):
                extended[b, 0:rim, :] = edge[g, b].astype(jnp.float32)

        chosen = lanes_of(core * share, g)
        coefficient = [
            [short[tap, b : b + 1, chosen] for b in range(branches)] for tap in range(SHORT)
        ]

        @blocks(length)
        def _(i):
            found = []
            for b in range(branches):
                value = jnp.zeros((BLOCK, LANES), jnp.float32)
                for tap in range(SHORT):
                    value = value + coefficient[tap][b] * extended[
                        b, pl.ds(rim - tap + i * BLOCK, BLOCK), :
                    ]
                found.append(value.astype(jnp.bfloat16))
            query[at_rows(i), :] = found[0]
            signal[g, at_rows(i), :] = (
                found[1].astype(jnp.float32) * found[2].astype(jnp.float32)
            ).astype(jnp.bfloat16)

    def convolve(g):
        joint = (x == 1) & (g > 0)

        @pl.when(jnp.logical_not(joint))
        def _():
            spectrum(0, lambda: signal[g])

        def product(i, which, first):
            low, high = at_rows(i), rows_at(i, BLOCK, length)
            cos, sin = freq[which, low, :], freq[which, high, :]
            real = spectra[g, first, low, :].astype(jnp.float32)
            imag = spectra[g, first + 1, low, :].astype(jnp.float32)
            return cos * real + sin * imag, sin * real - cos * imag

        @pl.when(x == 0)
        def _():
            @blocks(length)
            def _(i):
                real, imag = product(i, 0, 0)
                mixed[at_rows(i), :] = real.astype(jnp.bfloat16)
                mixed[rows_at(i, BLOCK, length), :] = imag.astype(jnp.bfloat16)

        @pl.when(x == 1)
        def _():
            before_copy(g).wait_recv()

            @pl.when(g == 0)
            def _():
                spectrum(1, lambda: before[g])

            @pl.when(g > 0)
            def _():
                spectrum_pair(lambda: [signal[g], before[g]])

            @blocks(length)
            def _(i):
                real, imag = product(i, 0, 0)
                more_real, more_imag = product(i, 1, 2)
                mixed[at_rows(i), :] = (real + more_real).astype(jnp.bfloat16)
                mixed[rows_at(i, BLOCK, length), :] = (imag + more_imag).astype(jnp.bfloat16)

        @pl.loop(0, length // SPAN)
        def _(i):
            low, high = rows_at(i, SPAN), rows_at(i, SPAN, length)
            freq[0, low, :] = jnp.dot(
                table[low, :], mixed[:length, :], preferred_element_type=jnp.float32
            ) + jnp.dot(table[high, :], mixed[length:, :], preferred_element_type=jnp.float32)

        direct = skip[:, lanes_of(core * share, g)]

        def gated(at):
            longer = freq[0, at, :] + direct * signal[g, at, :].astype(jnp.float32)
            longer = longer.astype(jnp.bfloat16).astype(jnp.float32)
            return (query[at, :].astype(jnp.float32) * longer).astype(jnp.bfloat16)

        @blocks(rows)
        def _(i):
            full[z, g, core, at_rows(i), :] = gated(
                pl.ds(pl.multiple_of(core * rows + i * BLOCK, BLOCK), BLOCK)
            )
            ready[g, at_rows(i), :] = gated(
                pl.ds(pl.multiple_of((1 - core) * rows + i * BLOCK, BLOCK), BLOCK)
            )

    def load_out():
        for owner in range(chan_count):
            pltpu.make_async_copy(
                out_weight.at[pl.ds(owner * length, length)], stream.at[owner], local_sem.at[1]
            ).start()

    def accumulate(owner, g):
        @pl.loop(0, total.shape[1] // (2 * LANES))
        def _(i):
            cols = rows_at(i, 2 * LANES)
            block = jnp.concatenate([full[owner, g, 0], full[owner, g, 1]], axis=1)
            kernel = jnp.concatenate(
                [stream[owner, lanes_of(of * share, g), cols] for of in range(2)], axis=0
            )
            total[:, cols] += jnp.dot(block, kernel, preferred_element_type=jnp.float32)

    def begin(g):
        swap_copy(g).start()
        for way in range(2):

            @pl.when(line.sends(way, 0))
            def _():
                line.copy(way, 0, (g, core)).start()

    def begin_other(g):
        other = full.at[z, g, 1 - core]
        remote(other, other, swap_send.at[0], swap_recv.at[g], mate).wait_recv()
        for way in range(2):

            @pl.when(line.sends(way, 0))
            def _():
                line.copy(way, 0, (g, 1 - core)).start()

    def settle():
        other = weight.at[:, s]
        remote(other, other, mate_send.at[1], mate_recv.at[1], mate).wait_send()
        for copy in sum_copies:
            copy.wait_send()

        @pl.when(x == 1)
        def _():
            for origin in range(2):
                taps_beside(origin, y).wait_send()

        for at in range(2):
            view = weight_half(s, y)
            remote(view, view, x_send.at[at], x_recv.at[0, 0, 0], across).wait_send()
            view = weight_half((1 - x) * 2 + at, y)
            remote(view, view, y_send.at[at], y_recv.at[at, 0], beside).wait_send()

        @pl.when(x == 0)
        def _():
            remote(edge_out, edge, edge_send.at[0], edge_recv.at[0], across).wait_send()
            remote(signal, before, before_send.at[0], before_recv.at[0], across).wait_send()

    def settle_tokens():
        mate_tokens().wait_send()
        for way in range(2):
            for step in range(steps):

                @pl.when(token_line.receives(way, step))
                def _():
                    mate_half(way, step, core).wait_send()

                @pl.when(token_line.sends(way, step))
                def _():
                    token_line.drain(way, step, (0,), lambda owner: own_half(owner, core))

    def way_of(k):
        return jnp.where(z < chan_count // 2, 1 - k, k)

    def late_forwards(g, at, inner, outer):
        for here, pieces in ((jnp.logical_not(at_end), inner), (at_end, outer)):

            @pl.when((g == at) & here)
            def _():
                for group, c in pieces:
                    forward(group, c)

    def pass_on(way, step, at):
        @pl.when(
            (at >= 0) & (at < groups) & line.receives(way, step) & line.sends(way, step + 1)
        )
        def _():
            for of in (core, 1 - core):
                line.arrived(way, step, (at, of))
                line.copy(way, step + 1, (at, of)).start()

    for copy in small_loads[1:]:
        copy.wait()
    near, away = way_of(0), way_of(1)

    @pl.loop(0, groups)
    def _(g):
        @pl.when(g == 3)
        def _():
            pass_on(away, 0, 1)
            pass_on(near, 0, 2)

        @pl.when((g >= 2) | ((g == 1) & jnp.logical_not(at_end)))
        def _():
            await_beside(g)

        @pl.loop(0, chan_count)
        def _(owner):
            @pl.when(jnp.logical_not(projects_early(g, owner)))
            def _():
                project(g, owner)

        @pl.when(g == groups - 1)
        def _():
            settle_tokens()
            load_out()

        featurize(g)

        @pl.when(x == 0)
        def _():
            before_copy(g).start()

            for at, inner, outer in (
                (0, [(groups - 2, 2)], [(groups - 1, 2)]),
                (1, [(groups - 2, 3), (groups - 1, 0), (groups - 1, 1)], [(groups - 1, 3)]),
                (2, [(groups - 1, 2), (groups - 1, 3)], []),
            ):

                @pl.when((g == at) & jnp.logical_not(at_end))
                def _():
                    for group, c in inner:
                        send_weights(group, [c])

                @pl.when((g == at) & at_end)
                def _():
                    for group, c in outer:
                        send_weights(group, [c])

        @pl.when(g == 1)
        def _():
            pass_on(near, 0, 0)

        late_forwards(g, 1, [(groups - 2, 3)], [(groups - 1, 0), (groups - 1, 1)])
        late_forwards(g, 2, [(groups - 1, 0), (groups - 1, 1)], [(groups - 1, 3)])

        @pl.when(g == 2)
        def _():
            pass_on(near, 0, 1)
            pass_on(away, 0, 0)

        @pl.when(g == 3)
        def _():
            pass_on(near, 1, 1)
            pass_on(away, 0, 2)

        late_forwards(g, 0, [], [(groups - 2, 2), (groups - 2, 3)])
        convolve(g)
        begin(g)
        late_forwards(g, 0, [(groups - 2, 2)], [])
        late_forwards(g, 1, [], [(groups - 1, 2)])
        begin_other(g)

        late_forwards(g, 2, [(groups - 1, 2), (groups - 1, 3)], [])

        @pl.when(g == 2)
        def _():
            pass_on(near, 1, 0)

    pltpu.make_async_copy(stream, stream, local_sem.at[1]).wait()

    @pl.loop(0, groups + steps - 1)
    def _(n):
        for at, pieces in (
            (0, [(near, 1, 2)]),
            (1, [(away, 0, 3), (near, 0, 3)]),
            (3, [(near, 1, 3)]),
        ):

            @pl.when(n == at)
            def _():
                for way, step, group in pieces:
                    pass_on(way, step, group)

        @pl.when(n == 2)
        def _():
            settle()

        @pl.when(n < groups)
        def _():
            accumulate(z, n)

        @pl.loop(0, 2)
        def _(way):
            for step in range(steps):
                at = n - jnp.where(at_end, step, 0)

                @pl.when((at >= 0) & (at < groups) & line.receives(way, step))
                def _():
                    @pl.when(jnp.logical_not(line.sends(way, step + 1)))
                    def _():
                        for of in range(2):
                            line.arrived(way, step, (at, of))

                    accumulate(line.source(way, step), at)

    @blocks(rows)
    def _(i):
        result[at_rows(i), :] = total[at_rows(i), :].astype(jnp.bfloat16)

    remote(ready, ready, swap_send.at[0], swap_recv.at[0], mate).wait_send()
    for way in range(2):
        for step in range(steps):

            @pl.when(line.sends(way, step))
            def _():
                line.drain(way, step, (0, 0), lambda owner: full.at[owner])


def chip_body(tokens, norm_gain, proj_weight, short_filter, long_filter, skip_gain, out_weight):
    chan_count = lax.axis_size("chan")
    rows, width = tokens.shape
    depth, branches, local_chan = proj_weight.shape
    length, share = 2 * rows, local_chan // 2
    groups = share // LANES
    steps = chan_count - 1
    dma = pltpu.SemaphoreType.DMA
    f32, bf16 = jnp.float32, jnp.bfloat16
    vmem = pl.BlockSpec(memory_space=pltpu.VMEM)
    return pl.pallas_call(
        functools.partial(block_kernel, chan_count),
        out_shape=jax.ShapeDtypeStruct((rows, width), bf16),
        in_specs=[HBM] * 7,
        out_specs=vmem,
        scratch_shapes=[
            pltpu.VMEM((1, width), f32),
            pltpu.VMEM(short_filter.shape, f32),
            pltpu.VMEM((1, local_chan), f32),
            pltpu.VMEM((chan_count, length, width), bf16),
            pltpu.VMEM((groups, 4, depth, branches * LANES), bf16),
            pltpu.VMEM((2, chan_count, 8, LANES), f32),
            pltpu.VMEM((length, LANES), f32),
            pltpu.VMEM((groups, length, branches * LANES), f32),
            pltpu.VMEM((2 * length, length), bf16),
            pltpu.VMEM((groups, 2 * length, LANES), bf16),
            pltpu.VMEM((groups, 4, length, LANES), bf16),
            pltpu.VMEM((2, 2 * length, LANES), f32),
            pltpu.VMEM((2 * length, LANES), bf16),
            pltpu.VMEM((groups, branches, 16, LANES), bf16),
            pltpu.VMEM((groups, branches, 16, LANES), bf16),
            pltpu.VMEM((branches, length + 16, LANES), f32),
            pltpu.VMEM((length, LANES), bf16),
            pltpu.VMEM((groups, length, LANES), bf16),
            pltpu.VMEM((groups, length, LANES), bf16),
            pltpu.VMEM((groups, rows, LANES), bf16),
            pltpu.VMEM((chan_count, groups, 2, rows, LANES), bf16),
            pltpu.VMEM((rows, width), f32),
            dma((10,)),
            dma((3 + 2 * steps,)),
            dma((3 + 2 * steps,)),
            dma((2, steps)),
            dma((steps, TOKEN_CHUNKS)),
            dma((2 * chan_count - 1,)),
            dma((2, chan_count)),
            dma((2,)),
            dma((2, groups, WEIGHT_CHUNKS)),
            dma((2,)),
            dma((2, groups)),
            dma((4,)),
            dma((4,)),
            dma((1,)),
            dma((groups,)),
            dma((1,)),
            dma((groups,)),
            dma((1,)),
            dma((groups,)),
            dma((2, steps)),
            dma((steps, groups, 2)),
        ],
        compiler_params=pltpu.CompilerParams(
            collective_id=0, has_side_effects=True, vmem_limit_bytes=52 * 1024 * 1024
        ),
        name="block",
    )(
        tokens,
        pltpu.with_memory_space_constraint(norm_gain[None, :], pltpu.HBM),
        proj_weight.transpose(1, 0, 2),
        pltpu.with_memory_space_constraint(short_filter, pltpu.HBM),
        long_filter,
        pltpu.with_memory_space_constraint(skip_gain[None, :], pltpu.HBM),
        out_weight,
    )


def select_body(mesh):
    if (mesh.shape["groups"], mesh.shape["seq"], mesh.shape["chan"]) == (2, 4, 4):
        return chip_body
    return body


def solution(mesh):
    placed = (
        P(("groups", "seq"), "chan"),
        P(),
        P("seq", None, "chan"),
        P(None, None, "chan"),
        P("chan", "seq"),
        P("chan"),
        P(None, "chan"),
    )
    return jax.shard_map(
        select_body(mesh), mesh=mesh, in_specs=placed, out_specs=P(("groups", "seq"), "chan"), check_vma=False
    )
```

```python
import functools
import math

import jax
import jax.numpy as jnp
import numpy as np
from jax import lax
from jax.experimental import pallas as pl
from jax.experimental.pallas import tpu as pltpu
from jax.sharding import PartitionSpec as P

SHORT = 3


EPSILON = 1e-06
HIGHEST = lax.Precision.HIGHEST


def from_behind(value, axis, steps):
    count = lax.axis_size(axis)
    initial, last = (max(0, -steps), min(count, count - steps))
    return lax.ppermute(value, axis, [(source, source + steps) for source in range(initial, last)])


def angle_table(row_count, col_count, period, sign):
    row_index = lax.iota(jnp.int32, row_count)[:, None]
    col_index = lax.iota(jnp.int32, col_count)[None, :]
    angles = (row_index * col_index % period).astype(jnp.float32) * (sign * 2.0 * math.pi / period)
    return (jnp.cos(angles), jnp.sin(angles))


def forward_spectrum(signal_rows, first, second):
    channels = signal_rows.shape[0]
    grid_rows = signal_rows.reshape(channels, first, second)
    cos_first, sin_first = angle_table(first, first, first, -1.0)
    part_re = jnp.einsum("cab,ak->ckb", grid_rows, cos_first, precision=HIGHEST)
    part_im = jnp.einsum("cab,ak->ckb", grid_rows, sin_first, precision=HIGHEST)
    twist_cos, twist_sin = angle_table(first, second, first * second, -1.0)
    part_re, part_im = (
        part_re * twist_cos - part_im * twist_sin,
        part_re * twist_sin + part_im * twist_cos,
    )
    cos_second, sin_second = angle_table(second, second, second, -1.0)
    spectrum_real = jnp.einsum("ckb,bm->ckm", part_re, cos_second, precision=HIGHEST) - jnp.einsum(
        "ckb,bm->ckm", part_im, sin_second, precision=HIGHEST
    )
    spec_im = jnp.einsum("ckb,bm->ckm", part_re, sin_second, precision=HIGHEST) + jnp.einsum(
        "ckb,bm->ckm", part_im, cos_second, precision=HIGHEST
    )
    return (spectrum_real, spec_im)


def inverse_spectrum(spectrum_real, spec_im, first, second):
    channels = spectrum_real.shape[0]
    cos_second, sin_second = angle_table(second, second, second, 1.0)
    part_re = jnp.einsum("ckm,bm->ckb", spectrum_real, cos_second, precision=HIGHEST) - jnp.einsum(
        "ckm,bm->ckb", spec_im, sin_second, precision=HIGHEST
    )
    part_im = jnp.einsum("ckm,bm->ckb", spectrum_real, sin_second, precision=HIGHEST) + jnp.einsum(
        "ckm,bm->ckb", spec_im, cos_second, precision=HIGHEST
    )
    twist_cos, twist_sin = angle_table(first, second, first * second, 1.0)
    part_re, part_im = (
        part_re * twist_cos - part_im * twist_sin,
        part_re * twist_sin + part_im * twist_cos,
    )
    cos_first, sin_first = angle_table(first, first, first, 1.0)
    result = jnp.einsum("ckb,ak->cab", part_re, cos_first, precision=HIGHEST) - jnp.einsum(
        "ckb,ak->cab", part_im, sin_first, precision=HIGHEST
    )
    return result.reshape(channels, first * second) / (first * second)


def spectral_conv(signal_rows, filter_rows):
    channels, length = signal_rows.shape
    padded_len = 2 * length
    log_len = padded_len.bit_length() - 1
    first = 1 << log_len // 2
    second = padded_len // first
    zeros_tail = jnp.zeros((channels, length), jnp.float32)
    sig_re, sig_im = forward_spectrum(
        jnp.concatenate([signal_rows, zeros_tail], axis=1), first, second
    )
    tap_re, tap_im = forward_spectrum(
        jnp.concatenate([filter_rows, zeros_tail], axis=1), first, second
    )
    prod_re = sig_re * tap_re - sig_im * tap_im
    prod_im = sig_re * tap_im + sig_im * tap_re
    return inverse_spectrum(prod_re, prod_im, first, second)[:, :length]


def short_filter_output(projected, rim_cells, kernel_coefficients):
    count = kernel_coefficients.shape[0]
    steps_len = projected.shape[2]
    extended = jnp.concatenate([rim_cells, projected], axis=2).astype(jnp.float32)
    total = jnp.zeros(projected.shape, jnp.float32)
    for tap in range(count):
        total = (
            total
            + kernel_coefficients[tap][:, :, None]
            * extended[:, :, count - 1 - tap : count - 1 - tap + steps_len]
        )
    return total.astype(jnp.bfloat16)


def hyena_mixer(keys_rows, values_rows, long_taps, skip_part):
    middle = keys_rows.astype(jnp.float32) * values_rows.astype(jnp.float32)
    return (spectral_conv(middle, long_taps) + skip_part[:, None] * middle).astype(jnp.bfloat16)


def body(tokens, norm_gain, proj_weight, short_filter, long_filter, skip_gain, out_weight):
    seq_count = lax.axis_size("seq")
    local_rows = tokens.shape[0]
    local_chan = proj_weight.shape[2]
    subset = local_chan // seq_count
    length = local_rows * seq_count
    offset = lax.axis_index("seq") * subset
    whole = lax.all_gather(tokens, "chan", axis=1, tiled=True)
    wide = whole.astype(jnp.float32)
    rescaled_signal = (
        wide * lax.rsqrt(jnp.mean(wide * wide, axis=1, keepdims=True) + EPSILON) * norm_gain
    ).astype(jnp.bfloat16)
    projected = lax.dot_general(
        lax.all_gather(proj_weight, "seq", axis=0, tiled=True),
        rescaled_signal,
        (((0,), (1,)), ((), ())),
        preferred_element_type=jnp.float32,
    ).astype(jnp.bfloat16)
    taps_grid = long_filter.reshape(1, seq_count, subset, local_rows)
    long_taps = lax.all_to_all(taps_grid, "seq", split_axis=1, concat_axis=3, tiled=True).reshape(
        subset, length
    )
    skip_part = lax.dynamic_slice_in_dim(skip_gain, offset, subset, 0)
    rim_cells = from_behind(projected[:, :, local_rows - (SHORT - 1) :], "seq", 1)
    featured = short_filter_output(projected, rim_cells, short_filter)
    pair_grid = featured[1:].reshape(2, seq_count, subset, local_rows)
    moved = lax.all_to_all(pair_grid, "seq", split_axis=1, concat_axis=3, tiled=True).reshape(
        2, subset, length
    )
    result = hyena_mixer(moved[0], moved[1], long_taps, skip_part)
    returned = lax.all_to_all(
        result.reshape(1, subset, length), "seq", split_axis=2, concat_axis=0, tiled=True
    )
    returned = returned.reshape(local_chan, local_rows)
    gated = (featured[0].astype(jnp.float32) * returned.astype(jnp.float32)).astype(jnp.bfloat16)
    full_mix = lax.all_gather(gated, "chan", axis=0, tiled=True)
    update = lax.dot_general(
        full_mix, out_weight, (((0,), (0,)), ((), ())), preferred_element_type=jnp.float32
    )
    return (tokens.astype(jnp.float32) + update).astype(jnp.bfloat16)

LANES = 128
BLOCK = 128
SPAN = 1024
TOKEN_CHUNKS = 8
WEIGHT_CHUNKS = 4
HBM = pl.BlockSpec(memory_space=pltpu.HBM)


def remote(src, dst, send_sem, recv_sem, where):
    return pltpu.make_async_remote_copy(
        src_ref=src,
        dst_ref=dst,
        send_sem=send_sem,
        recv_sem=recv_sem,
        device_id=where,
        device_id_type=pl.DeviceIdType.MESH,
    )


class Line:
    def __init__(self, view, count, send_sem, recv_sem, place):
        self.view, self.count, self.place = view, count, place
        self.send_sem, self.recv_sem = send_sem, recv_sem
        self.me = lax.axis_index("chan")

    def move(self, way, step, piece, block, target):
        slot = jnp.minimum(jnp.where(way == 0, step, target + step), self.count - 2)
        recv = self.recv_sem.at[(slot,) + piece]
        return remote(block, block, self.send_sem.at[way, step], recv, self.place(target))

    def drain(self, way, step, first, block):
        self.move(way, step, first, block(self.source(way, step - 1)), self.me).wait_send()

    def source(self, way, step):
        return jnp.clip(self.me - (step + 1) * (1 - 2 * way), 0, self.count - 1)

    def copy(self, way, step, piece):
        owner = self.source(way, step - 1)
        target = self.source(way, -2)
        return self.move(way, step, piece, self.view(owner, *piece), target)

    def inside(self, way, by):
        place = self.me + by * (1 - 2 * way)
        return (place >= 0) & (place < self.count)

    def sends(self, way, step):
        return self.inside(way, -step) & self.inside(way, 1)

    def receives(self, way, step):
        return self.inside(way, -1 - step)

    def arrived(self, way, step, piece):
        owner = self.source(way, step)
        self.move(way, step, piece, self.view(owner, *piece), self.me).wait_recv()
        return owner


def block_kernel(
    chan_count,
    tokens,
    gain_hbm,
    weights,
    short_hbm,
    long_taps,
    skip_hbm,
    out_weight,
    result,
    gain,
    short,
    skip,
    stream,
    weight,
    sums,
    scale,
    partial,
    table,
    taps,
    spectra,
    freq,
    mixed,
    edge_out,
    edge,
    extended,
    query,
    signal,
    before,
    ready,
    full,
    total,
    local_sem,
    mate_send,
    mate_recv,
    token_send,
    token_recv,
    sums_send,
    sums_recv,
    x_send,
    x_recv,
    y_send,
    y_recv,
    tap_send,
    tap_recv,
    edge_send,
    edge_recv,
    before_send,
    before_recv,
    swap_send,
    swap_recv,
    line_send,
    line_recv,
):
    y, s, z = (lax.axis_index(name) for name in ("groups", "seq", "chan"))
    x, core = s // 2, s % 2
    mate_s = s + 1 - 2 * core
    mate = (y, mate_s, z)
    across = (y, (1 - x) * 2 + core, z)
    aslant = (y, (1 - x) * 2 + 1 - core, z)
    beside = (1 - y, s, z)
    rows, width = tokens.shape
    length = 2 * rows
    branches, depth = weights.shape[0], weights.shape[1]
    half = depth // 2
    share = weights.shape[2] // 2
    groups = share // LANES
    rim = edge.shape[2]
    steps = chan_count - 1
    token_rows = rows // TOKEN_CHUNKS
    weight_rows = half // WEIGHT_CHUNKS

    column_peers = [mate] + [
        (y, 2 * x + of, lax.rem(z + by, chan_count))
        for by in range(1, chan_count)
        for of in (core, 1 - core)
    ]
    peers = column_peers + [across, aslant, beside]

    def rows_at(i, count, base=0):
        return pl.ds(pl.multiple_of(base + i * count, count), count)

    def at_rows(i):
        return rows_at(i, BLOCK)

    def blocks(count):
        return pl.loop(0, count // BLOCK)

    def lanes_of(base, g):
        return pl.ds(pl.multiple_of(base + g * LANES, LANES), LANES)

    tap_stage = [(0, 0), (0, length), (1, 0), (1, length)]
    tap_loads = [
        pltpu.make_async_copy(
            long_taps.at[:, pl.ds(j * LANES, LANES)],
            freq.at[which, pl.ds(start, length)],
            local_sem.at[4 + j],
        )
        for j, (which, start) in enumerate(tap_stage)
    ]
    token_load = pltpu.make_async_copy(tokens, result, local_sem.at[0])
    token_load.start()
    small_loads = [
        pltpu.make_async_copy(src, dst, local_sem.at[at])
        for src, dst, at in (
            (gain_hbm.at[:, pl.ds(pl.multiple_of(z * width, width), width)], gain, 3),
            (short_hbm, short, 8),
            (skip_hbm, skip, 9),
        )
    ]
    for copy in small_loads:
        copy.start()
    barrier = pltpu.get_barrier_semaphore()
    for peer in peers:
        pl.semaphore_signal(barrier, inc=1, device_id=peer, device_id_type=pl.DeviceIdType.MESH)
    for copy in tap_loads:
        copy.start()
    for g in range(groups):
        for b in range(branches):
            pltpu.make_async_copy(
                weights.at[b, :, lanes_of(core * share, g)],
                weight.at[g, s, :, pl.ds(b * LANES, LANES)],
                local_sem.at[2],
            ).start()

    sums[core, z] = jnp.zeros(sums.shape[2:], jnp.float32)
    small_loads[0].wait()
    own_gain = gain[...]
    token_load.wait()

    @blocks(rows)
    def _(i):
        raw = result[at_rows(i), :].astype(jnp.float32)
        total[at_rows(i), :] = raw
        stream[z, pl.ds(pl.multiple_of(core * rows + i * BLOCK, BLOCK), BLOCK), :] = (
            raw * own_gain
        ).astype(jnp.bfloat16)
        square = raw * raw
        found = square[:, :LANES]
        for part in range(1, width // LANES):
            found = found + square[:, part * LANES : (part + 1) * LANES]
        sums[core, z, pl.ds(i, 1), :] = jnp.sum(found.T, axis=0, keepdims=True)

    pl.semaphore_wait(barrier, len(peers))

    def token_view(owner, chunk):
        return stream.at[owner, rows_at(chunk, token_rows, core * rows), :]

    token_line = Line(
        token_view, chan_count, token_send, token_recv, lambda to: (y, s, to)
    )
    for chunk in range(TOKEN_CHUNKS):
        for way in range(2):

            @pl.when(token_line.sends(way, 0))
            def _():
                token_line.copy(way, 0, (chunk,)).start()

    def own_half(owner, of):
        return stream.at[owner, pl.ds(pl.multiple_of(of * rows, rows), rows), :]

    def mate_tokens():
        return remote(
            own_half(z, core), own_half(z, core), mate_send.at[0], mate_recv.at[0], mate
        )

    mate_tokens().start()
    sum_copies = [
        remote(
            sums.at[core, z], sums.at[core, z], sums_send.at[at], sums_recv.at[core, z], peer
        )
        for at, peer in enumerate(column_peers)
    ]
    for copy in sum_copies:
        copy.start()
    for g in range(groups):
        for b in range(branches):
            remote(
                weights.at[b, :, lanes_of((1 - core) * share, g)],
                weight.at[g, s, :, pl.ds(b * LANES, LANES)],
                mate_send.at[1],
                mate_recv.at[1],
                mate,
            ).start()

    for j, (which, start) in enumerate(tap_stage):
        tap_loads[j].wait()

        @pl.loop(0, groups)
        def _(g):
            mine = freq[which, rows_at(core * groups + g, BLOCK, start), :]
            taps[g, pl.ds(pl.multiple_of(s * rows + j * LANES, LANES), LANES), :] = mine.T.astype(
                jnp.bfloat16
            )
            other = freq[which, rows_at((1 - core) * groups + g, BLOCK, start), :]
            ready[g, j * LANES : (j + 1) * LANES, :] = other.T.astype(jnp.bfloat16)

    def tap_part(owner, part):
        return taps.at[
            :, pl.ds(pl.multiple_of(owner * rows + part * (rows // 2), rows // 2), rows // 2), :
        ]

    def taps_across(to):
        src = tap_part(s, y) if to == 0 else ready.at[
            :, pl.ds(pl.multiple_of(y * (rows // 2), rows // 2), rows // 2), :
        ]
        return remote(
            src,
            tap_part(s, y),
            tap_send.at[to],
            tap_recv.at[core],
            across if to == 0 else aslant,
        )

    def taps_beside(origin, part):
        view = tap_part(origin, part)
        return remote(view, view, tap_send.at[2 + origin], tap_recv.at[2 + origin], beside)

    def taps_mate():
        return remote(
            ready,
            taps.at[:, pl.ds(pl.multiple_of(s * rows, rows), rows), :],
            mate_send.at[2],
            mate_recv.at[2],
            mate,
        )

    @pl.when(x == 0)
    def _():
        taps_across(0).start()
        taps_across(1).start()

        @pl.loop(0, groups)
        def _(g):
            taps[g, length:, :] = jnp.zeros((length, LANES), jnp.bfloat16)

    taps_mate().start()

    def weight_view(owner, part, g, c):
        return weight.at[g, owner, rows_at(c, weight_rows, part * half), :]

    def weight_half(owner, part):
        return weight.at[:, owner, pl.ds(pl.multiple_of(part * half, half), half), :]

    def send_weights(g, chunks=range(WEIGHT_CHUNKS)):
        for c in chunks:
            for to in range(2):
                side = core if to == 0 else 1 - core
                view = weight_view(s, y, g, c)
                for b in range(branches):
                    remote(
                        weights.at[
                            b,
                            rows_at(c, weight_rows, y * half),
                            pl.ds(pl.multiple_of(side * share + g * LANES, LANES), LANES),
                        ],
                        view.at[:, pl.ds(b * LANES, LANES)],
                        x_send.at[to],
                        x_recv.at[core, g, c],
                        across if to == 0 else aslant,
                    ).start()

    for g in range(groups - 2):
        send_weights(g)
    send_weights(groups - 2, range(2))

    at_end = (z == 0) | (z == chan_count - 1)

    @pl.when((x == 1) | at_end)
    def _():
        send_weights(groups - 2, [2, 3])
        send_weights(groups - 1, [0, 1])

    @pl.when(x == 1)
    def _():
        send_weights(groups - 1, [2, 3])

    def beside_copy(origin, part, g, c):
        view = weight_view((1 - x) * 2 + origin, part, g, c)
        return remote(view, view, y_send.at[origin], y_recv.at[origin, g], beside)

    def forward(g, c):
        for origin in range(2):
            view = weight_view((1 - x) * 2 + origin, y, g, c)
            remote(
                view, view, x_send.at[origin], x_recv.at[origin, g, c], beside
            ).wait_recv()
            beside_copy(origin, y, g, c).start()

    def await_beside(g):
        for origin in range(2):
            view = weight.at[
                g, (1 - x) * 2 + origin, pl.ds(pl.multiple_of((1 - y) * half, half), half), :
            ]
            remote(view, view, y_send.at[origin], y_recv.at[origin, g], beside).wait_recv()

    @blocks(length)
    def _(i):
        row = lax.broadcasted_iota(jnp.int32, (BLOCK, LANES), 0) + i * BLOCK
        lane = lax.broadcasted_iota(jnp.int32, (BLOCK, LANES), 1)
        unit = math.pi / (4 * length)
        odd = 2 * row + 1
        small = odd.astype(jnp.float32) * unit
        extended[0, at_rows(i), :] = jnp.cos(small)
        extended[1, at_rows(i), :] = jnp.sin(small)
        period = 8 * length
        angle = (odd * (2 * lane + 1) % period).astype(jnp.float32) * unit
        cos, sin = jnp.cos(angle), jnp.sin(angle)
        stride = (odd * (2 * LANES) % period).astype(jnp.float32) * unit
        step_cos, step_sin = jnp.cos(stride), jnp.sin(stride)
        for a in range(length // LANES):
            table[at_rows(i), a * LANES : (a + 1) * LANES] = cos.astype(jnp.bfloat16)
            table[rows_at(i, BLOCK, length), a * LANES : (a + 1) * LANES] = sin.astype(
                jnp.bfloat16
            )
            cos, sin = cos * step_cos - sin * step_sin, sin * step_cos + cos * step_sin

    for g in range(groups):

        @blocks(length)
        def _(i):
            partial[g, at_rows(i), :] = jnp.zeros((BLOCK, branches * LANES), jnp.float32)

    def spectrum(which, column):
        @pl.loop(0, 2 * length // SPAN)
        def _(i):
            at = rows_at(i, SPAN)
            freq[which, at, :] = jnp.dot(
                table[at, :], column(), preferred_element_type=jnp.float32
            )

    def spectrum_pair(columns):
        @pl.loop(0, 2 * length // SPAN)
        def _(i):
            at = rows_at(i, SPAN)
            found = jnp.dot(
                table[at, :],
                jnp.concatenate(columns(), axis=1),
                preferred_element_type=jnp.float32,
            )
            freq[0, at, :] = found[:, :LANES]
            freq[1, at, :] = found[:, LANES:]

    def tap_spectra(g):
        spectrum_pair(lambda: [taps[g, :length, :], taps[g, length:, :]])

        @blocks(length)
        def _(i):
            low, high = at_rows(i), rows_at(i, BLOCK, length)
            cos, sin = extended[0, low, :], extended[1, low, :]

            def turned(which):
                real, imag = freq[which, low, :], -freq[which, high, :]
                return (cos * real - sin * imag) / length, (cos * imag + sin * real) / length

            real, imag = turned(0)
            late_real, late_imag = turned(1)
            place = lax.broadcasted_iota(jnp.int32, (BLOCK, LANES), 0)
            sign = (1 - 2 * (place % 2)).astype(jnp.float32)
            spectra[g, 0, low, :] = real.astype(jnp.bfloat16)
            spectra[g, 1, low, :] = imag.astype(jnp.bfloat16)
            spectra[g, 2, low, :] = (late_real - sign * imag).astype(jnp.bfloat16)
            spectra[g, 3, low, :] = (late_imag + sign * real).astype(jnp.bfloat16)

    def project(g, owner):
        @pl.loop(0, length // SPAN)
        def _(i):
            at = rows_at(i, SPAN)
            partial[g, at, :] += jnp.dot(
                stream[owner, at, :], weight[g, owner], preferred_element_type=jnp.float32
            )

    def projects_early(g, owner):
        far = jnp.abs(z - owner)
        own = owner // 2 == x
        return (
            (own & ((far <= 1) | ((far == 2) & (at_end | (g == 0)))))
            | (jnp.logical_not(own) & (far <= 2) & ((g == 0) | ((g == 1) & at_end)))
        )

    def to_mate(way, step, chunk):
        block = token_view(token_line.source(way, step), chunk)
        index = 3 + way * steps + step
        return remote(block, block, mate_send.at[index], mate_recv.at[index], mate)

    def mate_half(way, step, of):
        block = own_half(token_line.source(way, step), of)
        index = 3 + way * steps + step
        return remote(block, block, mate_send.at[index], mate_recv.at[index], mate)

    def await_mate(step):
        for way in range(2):

            @pl.when(token_line.receives(way, step))
            def _():
                mate_half(way, step, 1 - core).wait_recv()

    @pl.loop(0, steps * TOKEN_CHUNKS)
    def _(tick):
        step, chunk = tick // TOKEN_CHUNKS, tick % TOKEN_CHUNKS
        for way in range(2):

            @pl.when(token_line.receives(way, step))
            def _():
                token_line.arrived(way, step, (chunk,))
                to_mate(way, step, chunk).start()

            @pl.when(
                (step + 1 < steps)
                & token_line.receives(way, step)
                & token_line.sends(way, step + 1)
            )
            def _():
                token_line.copy(way, step + 1, (chunk,)).start()

        @pl.when((tick == TOKEN_CHUNKS // 2) & (x == 1))
        def _():
            for origin in range(2):
                view = tap_part(origin, y)
                remote(
                    view, view, tap_send.at[origin], tap_recv.at[origin], beside
                ).wait_recv()
                taps_beside(origin, y).start()

        @pl.when((tick % 2 == 1) & (tick >= 3) & (tick < 7 + 4 * WEIGHT_CHUNKS))
        def _():
            at = (tick - 3) // 2
            forward(at // WEIGHT_CHUNKS, at % WEIGHT_CHUNKS)

        @pl.when(tick == TOKEN_CHUNKS)
        def _():
            mate_half_own = own_half(z, 1 - core)
            remote(
                mate_half_own, mate_half_own, mate_send.at[0], mate_recv.at[0], mate
            ).wait_recv()
            await_mate(0)
            pltpu.make_async_copy(
                weight.at[:, s], weight.at[:, s], local_sem.at[2]
            ).wait()
            other = weight.at[:, mate_s]
            remote(other, other, mate_send.at[1], mate_recv.at[1], mate).wait_recv()
            other = taps.at[:, pl.ds(pl.multiple_of(mate_s * rows, rows), rows), :]
            remote(other, other, mate_send.at[2], mate_recv.at[2], mate).wait_recv()

            @pl.when(x == 1)
            def _():
                for origin in range(2):
                    taps_beside(origin, 1 - y).wait_recv()

        @pl.when((step == 1) & (chunk % 2 == 0))
        def _():
            tap_spectra(chunk // 2)

        @pl.when(tick == 2 * TOKEN_CHUNKS)
        def _():
            await_mate(1)

        owner = 2 * x + chunk // groups
        far = jnp.abs(z - owner)

        @pl.when(
            projects_early(chunk % groups, owner)
            & (((step == 1) & (far <= 1)) | ((step == 2) & (far == 2)))
        )
        def _():
            project(chunk % groups, owner)

        @pl.when(tick == 2 * TOKEN_CHUNKS)
        def _():
            await_beside(0)

        @pl.when((tick == 2 * TOKEN_CHUNKS + TOKEN_CHUNKS // 2) & at_end)
        def _():
            await_beside(1)

        guest = 2 * (1 - x) + (chunk // 2) % 2

        @pl.when((step == 2) & (chunk % 2 == 0) & projects_early(chunk // 4, guest))
        def _():
            project(chunk // 4, guest)

    await_mate(2)
    for by in range(1, chan_count):
        for of in range(2):
            view = sums.at[of, lax.rem(z + by, chan_count)]
            remote(
                view, view, sums_send.at[0], sums_recv.at[of, lax.rem(z + by, chan_count)], mate
            ).wait_recv()
    view = sums.at[1 - core, z]
    remote(view, view, sums_send.at[0], sums_recv.at[1 - core, z], mate).wait_recv()

    @blocks(length)
    def _(i):
        of, at = i // (rows // BLOCK), i % (rows // BLOCK)
        found = sums[of, 0, pl.ds(at, 1), :]
        for owner in range(1, chan_count):
            found = found + sums[of, owner, pl.ds(at, 1), :]
        found = lax.rsqrt(found / (chan_count * width) + EPSILON)
        scale[at_rows(i), :] = jnp.broadcast_to(found, (BLOCK, LANES)).T

    taps_mate().wait_send()

    @pl.when(x == 0)
    def _():
        taps_across(0).wait_send()
        taps_across(1).wait_send()

    def edge_copy(g):
        return remote(
            edge_out.at[g], edge.at[g], edge_send.at[0], edge_recv.at[g], across
        )

    def before_copy(g):
        return remote(
            signal.at[g], before.at[g], before_send.at[0], before_recv.at[g], across
        )

    def swap_copy(g):
        return remote(
            ready.at[g], full.at[z, g, core], swap_send.at[0], swap_recv.at[g], mate
        )

    line = Line(
        lambda owner, g, of: full.at[owner, g, of],
        chan_count,
        line_send,
        line_recv,
        lambda to: (y, s, to),
    )

    def projected(g, b, at):
        return (partial[g, at, b * LANES : (b + 1) * LANES] * scale[at, :]).astype(jnp.bfloat16)

    def featurize(g):
        @pl.when(x == 0)
        def _():
            for b in range(branches):
                edge_out[g, b] = projected(g, b, pl.ds(length - rim, rim))
                extended[b, 0:rim, :] = jnp.zeros((rim, LANES), jnp.float32)
            edge_copy(g).start()

        @blocks(length)
        def _(i):
            for b in range(branches):
                extended[b, pl.ds(pl.multiple_of(rim + i * BLOCK, rim), BLOCK), :] = projected(
                    g, b, at_rows(i)
                ).astype(jnp.float32)

        @pl.when(x == 1)
        def _():
            edge_copy(g).wait_recv()
            for b in range(branches):
                extended[b, 0:rim, :] = edge[g, b].astype(jnp.float32)

        chosen = lanes_of(core * share, g)
        coefficient = [
            [short[tap, b : b + 1, chosen] for b in range(branches)] for tap in range(SHORT)
        ]

        @blocks(length)
        def _(i):
            found = []
            for b in range(branches):
                value = jnp.zeros((BLOCK, LANES), jnp.float32)
                for tap in range(SHORT):
                    value = value + coefficient[tap][b] * extended[
                        b, pl.ds(rim - tap + i * BLOCK, BLOCK), :
                    ]
                found.append(value.astype(jnp.bfloat16))
            query[at_rows(i), :] = found[0]
            signal[g, at_rows(i), :] = (
                found[1].astype(jnp.float32) * found[2].astype(jnp.float32)
            ).astype(jnp.bfloat16)

    def convolve(g):
        joint = (x == 1) & (g > 0)

        @pl.when(jnp.logical_not(joint))
        def _():
            spectrum(0, lambda: signal[g])

        def product(i, which, first):
            low, high = at_rows(i), rows_at(i, BLOCK, length)
            cos, sin = freq[which, low, :], freq[which, high, :]
            real = spectra[g, first, low, :].astype(jnp.float32)
            imag = spectra[g, first + 1, low, :].astype(jnp.float32)
            return cos * real + sin * imag, sin * real - cos * imag

        @pl.when(x == 0)
        def _():
            @blocks(length)
            def _(i):
                real, imag = product(i, 0, 0)
                mixed[at_rows(i), :] = real.astype(jnp.bfloat16)
                mixed[rows_at(i, BLOCK, length), :] = imag.astype(jnp.bfloat16)

        @pl.when(x == 1)
        def _():
            before_copy(g).wait_recv()

            @pl.when(g == 0)
            def _():
                spectrum(1, lambda: before[g])

            @pl.when(g > 0)
            def _():
                spectrum_pair(lambda: [signal[g], before[g]])

            @blocks(length)
            def _(i):
                real, imag = product(i, 0, 0)
                more_real, more_imag = product(i, 1, 2)
                mixed[at_rows(i), :] = (real + more_real).astype(jnp.bfloat16)
                mixed[rows_at(i, BLOCK, length), :] = (imag + more_imag).astype(jnp.bfloat16)

        @pl.loop(0, length // SPAN)
        def _(i):
            low, high = rows_at(i, SPAN), rows_at(i, SPAN, length)
            freq[0, low, :] = jnp.dot(
                table[low, :], mixed[:length, :], preferred_element_type=jnp.float32
            ) + jnp.dot(table[high, :], mixed[length:, :], preferred_element_type=jnp.float32)

        direct = skip[:, lanes_of(core * share, g)]

        def gated(at):
            longer = freq[0, at, :] + direct * signal[g, at, :].astype(jnp.float32)
            longer = longer.astype(jnp.bfloat16).astype(jnp.float32)
            return (query[at, :].astype(jnp.float32) * longer).astype(jnp.bfloat16)

        @blocks(rows)
        def _(i):
            full[z, g, core, at_rows(i), :] = gated(
                pl.ds(pl.multiple_of(core * rows + i * BLOCK, BLOCK), BLOCK)
            )
            ready[g, at_rows(i), :] = gated(
                pl.ds(pl.multiple_of((1 - core) * rows + i * BLOCK, BLOCK), BLOCK)
            )

    def load_out():
        for owner in range(chan_count):
            pltpu.make_async_copy(
                out_weight.at[pl.ds(owner * length, length)], stream.at[owner], local_sem.at[1]
            ).start()

    def accumulate(owner, g):
        @pl.loop(0, total.shape[1] // (2 * LANES))
        def _(i):
            cols = rows_at(i, 2 * LANES)
            block = jnp.concatenate([full[owner, g, 0], full[owner, g, 1]], axis=1)
            kernel = jnp.concatenate(
                [stream[owner, lanes_of(of * share, g), cols] for of in range(2)], axis=0
            )
            total[:, cols] += jnp.dot(block, kernel, preferred_element_type=jnp.float32)

    def begin(g):
        swap_copy(g).start()
        for way in range(2):

            @pl.when(line.sends(way, 0))
            def _():
                line.copy(way, 0, (g, core)).start()

    def begin_other(g):
        other = full.at[z, g, 1 - core]
        remote(other, other, swap_send.at[0], swap_recv.at[g], mate).wait_recv()
        for way in range(2):

            @pl.when(line.sends(way, 0))
            def _():
                line.copy(way, 0, (g, 1 - core)).start()

    def settle():
        other = weight.at[:, s]
        remote(other, other, mate_send.at[1], mate_recv.at[1], mate).wait_send()
        for copy in sum_copies:
            copy.wait_send()

        @pl.when(x == 1)
        def _():
            for origin in range(2):
                taps_beside(origin, y).wait_send()

        for at in range(2):
            view = weight_half(s, y)
            remote(view, view, x_send.at[at], x_recv.at[0, 0, 0], across).wait_send()
            view = weight_half((1 - x) * 2 + at, y)
            remote(view, view, y_send.at[at], y_recv.at[at, 0], beside).wait_send()

        @pl.when(x == 0)
        def _():
            remote(edge_out, edge, edge_send.at[0], edge_recv.at[0], across).wait_send()
            remote(signal, before, before_send.at[0], before_recv.at[0], across).wait_send()

    def settle_tokens():
        mate_tokens().wait_send()
        for way in range(2):
            for step in range(steps):

                @pl.when(token_line.receives(way, step))
                def _():
                    mate_half(way, step, core).wait_send()

                @pl.when(token_line.sends(way, step))
                def _():
                    token_line.drain(way, step, (0,), lambda owner: own_half(owner, core))

    def way_of(k):
        return jnp.where(z < chan_count // 2, 1 - k, k)

    def late_forwards(g, at, inner, outer):
        for here, pieces in ((jnp.logical_not(at_end), inner), (at_end, outer)):

            @pl.when((g == at) & here)
            def _():
                for group, c in pieces:
                    forward(group, c)

    def pass_on(way, step, at):
        @pl.when(
            (at >= 0) & (at < groups) & line.receives(way, step) & line.sends(way, step + 1)
        )
        def _():
            for of in (core, 1 - core):
                line.arrived(way, step, (at, of))
                line.copy(way, step + 1, (at, of)).start()

    for copy in small_loads[1:]:
        copy.wait()
    near, away = way_of(0), way_of(1)

    @pl.loop(0, groups)
    def _(g):
        @pl.when(g == 2)
        def _():
            pass_on(near, 0, 1)

        @pl.when(g == 3)
        def _():
            pass_on(away, 0, 1)
            pass_on(near, 0, 2)

        @pl.when((g >= 2) | ((g == 1) & jnp.logical_not(at_end)))
        def _():
            await_beside(g)

        @pl.loop(0, chan_count)
        def _(owner):
            @pl.when(jnp.logical_not(projects_early(g, owner)))
            def _():
                project(g, owner)

        @pl.when(g == groups - 1)
        def _():
            settle_tokens()
            load_out()

        featurize(g)

        @pl.when(x == 0)
        def _():
            before_copy(g).start()

            for at, inner, outer in (
                (0, [(groups - 2, 2)], [(groups - 1, 2)]),
                (1, [(groups - 2, 3), (groups - 1, 0)], [(groups - 1, 3)]),
                (2, [(groups - 1, 1), (groups - 1, 2), (groups - 1, 3)], []),
            ):

                @pl.when((g == at) & jnp.logical_not(at_end))
                def _():
                    for group, c in inner:
                        send_weights(group, [c])

                @pl.when((g == at) & at_end)
                def _():
                    for group, c in outer:
                        send_weights(group, [c])

        @pl.when(g == 1)
        def _():
            pass_on(near, 0, 0)

        late_forwards(g, 1, [], [(groups - 1, 0), (groups - 1, 1)])
        late_forwards(g, 2, [(groups - 1, 0)], [(groups - 1, 3)])

        @pl.when(g == 3)
        def _():
            pass_on(near, 1, 1)
            pass_on(away, 0, 2)

        late_forwards(g, 0, [], [(groups - 2, 2), (groups - 2, 3)])
        convolve(g)
        begin(g)
        late_forwards(g, 0, [(groups - 2, 2)], [])
        late_forwards(g, 1, [(groups - 2, 3)], [(groups - 1, 2)])
        begin_other(g)

        @pl.when(g == 2)
        def _():
            pass_on(away, 0, 0)

        late_forwards(g, 2, [(groups - 1, 1), (groups - 1, 2)], [])

        @pl.when(g == 2)
        def _():
            pass_on(near, 1, 0)

        late_forwards(g, 2, [(groups - 1, 3)], [])

    pltpu.make_async_copy(stream, stream, local_sem.at[1]).wait()

    @pl.loop(0, groups + steps - 1)
    def _(n):
        for at, pieces in (
            (0, [(near, 1, 2)]),
            (1, [(away, 0, 3), (near, 0, 3)]),
            (3, [(near, 1, 3)]),
        ):

            @pl.when(n == at)
            def _():
                for way, step, group in pieces:
                    pass_on(way, step, group)

        @pl.when(n == 2)
        def _():
            settle()

        @pl.when(n < groups)
        def _():
            accumulate(z, n)

        @pl.loop(0, 2)
        def _(way):
            for step in range(steps):
                at = n - jnp.where(at_end, step, 0)

                @pl.when((at >= 0) & (at < groups) & line.receives(way, step))
                def _():
                    @pl.when(jnp.logical_not(line.sends(way, step + 1)))
                    def _():
                        for of in range(2):
                            line.arrived(way, step, (at, of))

                    accumulate(line.source(way, step), at)

    @blocks(rows)
    def _(i):
        result[at_rows(i), :] = total[at_rows(i), :].astype(jnp.bfloat16)

    remote(ready, ready, swap_send.at[0], swap_recv.at[0], mate).wait_send()
    for way in range(2):
        for step in range(steps):

            @pl.when(line.sends(way, step))
            def _():
                line.drain(way, step, (0, 0), lambda owner: full.at[owner])


def chip_body(tokens, norm_gain, proj_weight, short_filter, long_filter, skip_gain, out_weight):
    chan_count = lax.axis_size("chan")
    rows, width = tokens.shape
    depth, branches, local_chan = proj_weight.shape
    length, share = 2 * rows, local_chan // 2
    groups = share // LANES
    steps = chan_count - 1
    dma = pltpu.SemaphoreType.DMA
    f32, bf16 = jnp.float32, jnp.bfloat16
    vmem = pl.BlockSpec(memory_space=pltpu.VMEM)
    return pl.pallas_call(
        functools.partial(block_kernel, chan_count),
        out_shape=jax.ShapeDtypeStruct((rows, width), bf16),
        in_specs=[HBM] * 7,
        out_specs=vmem,
        scratch_shapes=[
            pltpu.VMEM((1, width), f32),
            pltpu.VMEM(short_filter.shape, f32),
            pltpu.VMEM((1, local_chan), f32),
            pltpu.VMEM((chan_count, length, width), bf16),
            pltpu.VMEM((groups, 4, depth, branches * LANES), bf16),
            pltpu.VMEM((2, chan_count, 8, LANES), f32),
            pltpu.VMEM((length, LANES), f32),
            pltpu.VMEM((groups, length, branches * LANES), f32),
            pltpu.VMEM((2 * length, length), bf16),
            pltpu.VMEM((groups, 2 * length, LANES), bf16),
            pltpu.VMEM((groups, 4, length, LANES), bf16),
            pltpu.VMEM((2, 2 * length, LANES), f32),
            pltpu.VMEM((2 * length, LANES), bf16),
            pltpu.VMEM((groups, branches, 16, LANES), bf16),
            pltpu.VMEM((groups, branches, 16, LANES), bf16),
            pltpu.VMEM((branches, length + 16, LANES), f32),
            pltpu.VMEM((length, LANES), bf16),
            pltpu.VMEM((groups, length, LANES), bf16),
            pltpu.VMEM((groups, length, LANES), bf16),
            pltpu.VMEM((groups, rows, LANES), bf16),
            pltpu.VMEM((chan_count, groups, 2, rows, LANES), bf16),
            pltpu.VMEM((rows, width), f32),
            dma((10,)),
            dma((3 + 2 * steps,)),
            dma((3 + 2 * steps,)),
            dma((2, steps)),
            dma((steps, TOKEN_CHUNKS)),
            dma((2 * chan_count - 1,)),
            dma((2, chan_count)),
            dma((2,)),
            dma((2, groups, WEIGHT_CHUNKS)),
            dma((2,)),
            dma((2, groups)),
            dma((4,)),
            dma((4,)),
            dma((1,)),
            dma((groups,)),
            dma((1,)),
            dma((groups,)),
            dma((1,)),
            dma((groups,)),
            dma((2, steps)),
            dma((steps, groups, 2)),
        ],
        compiler_params=pltpu.CompilerParams(
            collective_id=0, has_side_effects=True, vmem_limit_bytes=52 * 1024 * 1024
        ),
        name="block",
    )(
        tokens,
        pltpu.with_memory_space_constraint(norm_gain[None, :], pltpu.HBM),
        proj_weight.transpose(1, 0, 2),
        pltpu.with_memory_space_constraint(short_filter, pltpu.HBM),
        long_filter,
        pltpu.with_memory_space_constraint(skip_gain[None, :], pltpu.HBM),
        out_weight,
    )


def select_body(mesh):
    if (mesh.shape["groups"], mesh.shape["seq"], mesh.shape["chan"]) == (2, 4, 4):
        return chip_body
    return body


def solution(mesh):
    placed = (
        P(("groups", "seq"), "chan"),
        P(),
        P("seq", None, "chan"),
        P(None, None, "chan"),
        P("chan", "seq"),
        P("chan"),
        P(None, "chan"),
    )
    return jax.shard_map(
        select_body(mesh), mesh=mesh, in_specs=placed, out_specs=P(("groups", "seq"), "chan"), check_vma=False
    )
```

```python
import functools
import math

import jax
import jax.numpy as jnp
import numpy as np
from jax import lax
from jax.experimental import pallas as pl
from jax.experimental.pallas import tpu as pltpu
from jax.sharding import PartitionSpec as P

SHORT = 3


EPSILON = 1e-06
HIGHEST = lax.Precision.HIGHEST


def from_behind(value, axis, steps):
    count = lax.axis_size(axis)
    initial, last = (max(0, -steps), min(count, count - steps))
    return lax.ppermute(value, axis, [(source, source + steps) for source in range(initial, last)])


def angle_table(row_count, col_count, period, sign):
    row_index = lax.iota(jnp.int32, row_count)[:, None]
    col_index = lax.iota(jnp.int32, col_count)[None, :]
    angles = (row_index * col_index % period).astype(jnp.float32) * (sign * 2.0 * math.pi / period)
    return (jnp.cos(angles), jnp.sin(angles))


def forward_spectrum(signal_rows, first, second):
    channels = signal_rows.shape[0]
    grid_rows = signal_rows.reshape(channels, first, second)
    cos_first, sin_first = angle_table(first, first, first, -1.0)
    part_re = jnp.einsum("cab,ak->ckb", grid_rows, cos_first, precision=HIGHEST)
    part_im = jnp.einsum("cab,ak->ckb", grid_rows, sin_first, precision=HIGHEST)
    twist_cos, twist_sin = angle_table(first, second, first * second, -1.0)
    part_re, part_im = (
        part_re * twist_cos - part_im * twist_sin,
        part_re * twist_sin + part_im * twist_cos,
    )
    cos_second, sin_second = angle_table(second, second, second, -1.0)
    spectrum_real = jnp.einsum("ckb,bm->ckm", part_re, cos_second, precision=HIGHEST) - jnp.einsum(
        "ckb,bm->ckm", part_im, sin_second, precision=HIGHEST
    )
    spec_im = jnp.einsum("ckb,bm->ckm", part_re, sin_second, precision=HIGHEST) + jnp.einsum(
        "ckb,bm->ckm", part_im, cos_second, precision=HIGHEST
    )
    return (spectrum_real, spec_im)


def inverse_spectrum(spectrum_real, spec_im, first, second):
    channels = spectrum_real.shape[0]
    cos_second, sin_second = angle_table(second, second, second, 1.0)
    part_re = jnp.einsum("ckm,bm->ckb", spectrum_real, cos_second, precision=HIGHEST) - jnp.einsum(
        "ckm,bm->ckb", spec_im, sin_second, precision=HIGHEST
    )
    part_im = jnp.einsum("ckm,bm->ckb", spectrum_real, sin_second, precision=HIGHEST) + jnp.einsum(
        "ckm,bm->ckb", spec_im, cos_second, precision=HIGHEST
    )
    twist_cos, twist_sin = angle_table(first, second, first * second, 1.0)
    part_re, part_im = (
        part_re * twist_cos - part_im * twist_sin,
        part_re * twist_sin + part_im * twist_cos,
    )
    cos_first, sin_first = angle_table(first, first, first, 1.0)
    result = jnp.einsum("ckb,ak->cab", part_re, cos_first, precision=HIGHEST) - jnp.einsum(
        "ckb,ak->cab", part_im, sin_first, precision=HIGHEST
    )
    return result.reshape(channels, first * second) / (first * second)


def spectral_conv(signal_rows, filter_rows):
    channels, length = signal_rows.shape
    padded_len = 2 * length
    log_len = padded_len.bit_length() - 1
    first = 1 << log_len // 2
    second = padded_len // first
    zeros_tail = jnp.zeros((channels, length), jnp.float32)
    sig_re, sig_im = forward_spectrum(
        jnp.concatenate([signal_rows, zeros_tail], axis=1), first, second
    )
    tap_re, tap_im = forward_spectrum(
        jnp.concatenate([filter_rows, zeros_tail], axis=1), first, second
    )
    prod_re = sig_re * tap_re - sig_im * tap_im
    prod_im = sig_re * tap_im + sig_im * tap_re
    return inverse_spectrum(prod_re, prod_im, first, second)[:, :length]


def short_filter_output(projected, rim_cells, kernel_coefficients):
    count = kernel_coefficients.shape[0]
    steps_len = projected.shape[2]
    extended = jnp.concatenate([rim_cells, projected], axis=2).astype(jnp.float32)
    total = jnp.zeros(projected.shape, jnp.float32)
    for tap in range(count):
        total = (
            total
            + kernel_coefficients[tap][:, :, None]
            * extended[:, :, count - 1 - tap : count - 1 - tap + steps_len]
        )
    return total.astype(jnp.bfloat16)


def hyena_mixer(keys_rows, values_rows, long_taps, skip_part):
    middle = keys_rows.astype(jnp.float32) * values_rows.astype(jnp.float32)
    return (spectral_conv(middle, long_taps) + skip_part[:, None] * middle).astype(jnp.bfloat16)


def body(tokens, norm_gain, proj_weight, short_filter, long_filter, skip_gain, out_weight):
    seq_count = lax.axis_size("seq")
    local_rows = tokens.shape[0]
    local_chan = proj_weight.shape[2]
    subset = local_chan // seq_count
    length = local_rows * seq_count
    offset = lax.axis_index("seq") * subset
    whole = lax.all_gather(tokens, "chan", axis=1, tiled=True)
    wide = whole.astype(jnp.float32)
    rescaled_signal = (
        wide * lax.rsqrt(jnp.mean(wide * wide, axis=1, keepdims=True) + EPSILON) * norm_gain
    ).astype(jnp.bfloat16)
    projected = lax.dot_general(
        lax.all_gather(proj_weight, "seq", axis=0, tiled=True),
        rescaled_signal,
        (((0,), (1,)), ((), ())),
        preferred_element_type=jnp.float32,
    ).astype(jnp.bfloat16)
    taps_grid = long_filter.reshape(1, seq_count, subset, local_rows)
    long_taps = lax.all_to_all(taps_grid, "seq", split_axis=1, concat_axis=3, tiled=True).reshape(
        subset, length
    )
    skip_part = lax.dynamic_slice_in_dim(skip_gain, offset, subset, 0)
    rim_cells = from_behind(projected[:, :, local_rows - (SHORT - 1) :], "seq", 1)
    featured = short_filter_output(projected, rim_cells, short_filter)
    pair_grid = featured[1:].reshape(2, seq_count, subset, local_rows)
    moved = lax.all_to_all(pair_grid, "seq", split_axis=1, concat_axis=3, tiled=True).reshape(
        2, subset, length
    )
    result = hyena_mixer(moved[0], moved[1], long_taps, skip_part)
    returned = lax.all_to_all(
        result.reshape(1, subset, length), "seq", split_axis=2, concat_axis=0, tiled=True
    )
    returned = returned.reshape(local_chan, local_rows)
    gated = (featured[0].astype(jnp.float32) * returned.astype(jnp.float32)).astype(jnp.bfloat16)
    full_mix = lax.all_gather(gated, "chan", axis=0, tiled=True)
    update = lax.dot_general(
        full_mix, out_weight, (((0,), (0,)), ((), ())), preferred_element_type=jnp.float32
    )
    return (tokens.astype(jnp.float32) + update).astype(jnp.bfloat16)

LANES = 128
BLOCK = 128
SPAN = 1024
TOKEN_CHUNKS = 8
WEIGHT_CHUNKS = 4
HBM = pl.BlockSpec(memory_space=pltpu.HBM)


def remote(src, dst, send_sem, recv_sem, where):
    return pltpu.make_async_remote_copy(
        src_ref=src,
        dst_ref=dst,
        send_sem=send_sem,
        recv_sem=recv_sem,
        device_id=where,
        device_id_type=pl.DeviceIdType.MESH,
    )


class Line:
    def __init__(self, view, count, send_sem, recv_sem, place):
        self.view, self.count, self.place = view, count, place
        self.send_sem, self.recv_sem = send_sem, recv_sem
        self.me = lax.axis_index("chan")

    def move(self, way, step, piece, block, target):
        slot = jnp.minimum(jnp.where(way == 0, step, target + step), self.count - 2)
        recv = self.recv_sem.at[(slot,) + piece]
        return remote(block, block, self.send_sem.at[way, step], recv, self.place(target))

    def drain(self, way, step, first, block):
        self.move(way, step, first, block(self.source(way, step - 1)), self.me).wait_send()

    def source(self, way, step):
        return jnp.clip(self.me - (step + 1) * (1 - 2 * way), 0, self.count - 1)

    def copy(self, way, step, piece):
        owner = self.source(way, step - 1)
        target = self.source(way, -2)
        return self.move(way, step, piece, self.view(owner, *piece), target)

    def inside(self, way, by):
        place = self.me + by * (1 - 2 * way)
        return (place >= 0) & (place < self.count)

    def sends(self, way, step):
        return self.inside(way, -step) & self.inside(way, 1)

    def receives(self, way, step):
        return self.inside(way, -1 - step)

    def arrived(self, way, step, piece):
        owner = self.source(way, step)
        self.move(way, step, piece, self.view(owner, *piece), self.me).wait_recv()
        return owner


def block_kernel(
    chan_count,
    tokens,
    gain_hbm,
    weights,
    short_hbm,
    long_taps,
    skip_hbm,
    out_weight,
    result,
    gain,
    short,
    skip,
    stream,
    weight,
    sums,
    scale,
    partial,
    table,
    taps,
    spectra,
    freq,
    mixed,
    edge_out,
    edge,
    extended,
    query,
    signal,
    before,
    ready,
    full,
    total,
    local_sem,
    mate_send,
    mate_recv,
    token_send,
    token_recv,
    sums_send,
    sums_recv,
    x_send,
    x_recv,
    y_send,
    y_recv,
    tap_send,
    tap_recv,
    edge_send,
    edge_recv,
    before_send,
    before_recv,
    swap_send,
    swap_recv,
    line_send,
    line_recv,
):
    y, s, z = (lax.axis_index(name) for name in ("groups", "seq", "chan"))
    x, core = s // 2, s % 2
    mate_s = s + 1 - 2 * core
    mate = (y, mate_s, z)
    across = (y, (1 - x) * 2 + core, z)
    aslant = (y, (1 - x) * 2 + 1 - core, z)
    beside = (1 - y, s, z)
    rows, width = tokens.shape
    length = 2 * rows
    branches, depth = weights.shape[0], weights.shape[1]
    half = depth // 2
    share = weights.shape[2] // 2
    groups = share // LANES
    rim = edge.shape[2]
    steps = chan_count - 1
    token_rows = rows // TOKEN_CHUNKS
    weight_rows = half // WEIGHT_CHUNKS

    column_peers = [mate] + [
        (y, 2 * x + of, lax.rem(z + by, chan_count))
        for by in range(1, chan_count)
        for of in (core, 1 - core)
    ]
    peers = column_peers + [across, aslant, beside]

    def rows_at(i, count, base=0):
        return pl.ds(pl.multiple_of(base + i * count, count), count)

    def at_rows(i):
        return rows_at(i, BLOCK)

    def blocks(count):
        return pl.loop(0, count // BLOCK)

    def lanes_of(base, g):
        return pl.ds(pl.multiple_of(base + g * LANES, LANES), LANES)

    tap_stage = [(0, 0), (0, length), (1, 0), (1, length)]
    tap_loads = [
        pltpu.make_async_copy(
            long_taps.at[:, pl.ds(j * LANES, LANES)],
            freq.at[which, pl.ds(start, length)],
            local_sem.at[4 + j],
        )
        for j, (which, start) in enumerate(tap_stage)
    ]
    token_load = pltpu.make_async_copy(tokens, result, local_sem.at[0])
    token_load.start()
    small_loads = [
        pltpu.make_async_copy(src, dst, local_sem.at[at])
        for src, dst, at in (
            (gain_hbm.at[:, pl.ds(pl.multiple_of(z * width, width), width)], gain, 3),
            (short_hbm, short, 8),
            (skip_hbm, skip, 9),
        )
    ]
    for copy in small_loads:
        copy.start()
    barrier = pltpu.get_barrier_semaphore()
    for peer in peers:
        pl.semaphore_signal(barrier, inc=1, device_id=peer, device_id_type=pl.DeviceIdType.MESH)
    for copy in tap_loads:
        copy.start()
    for g in range(groups):
        for b in range(branches):
            pltpu.make_async_copy(
                weights.at[b, :, lanes_of(core * share, g)],
                weight.at[g, s, :, pl.ds(b * LANES, LANES)],
                local_sem.at[2],
            ).start()

    sums[core, z] = jnp.zeros(sums.shape[2:], jnp.float32)
    small_loads[0].wait()
    own_gain = gain[...]
    token_load.wait()

    @blocks(rows)
    def _(i):
        raw = result[at_rows(i), :].astype(jnp.float32)
        total[at_rows(i), :] = raw
        stream[z, pl.ds(pl.multiple_of(core * rows + i * BLOCK, BLOCK), BLOCK), :] = (
            raw * own_gain
        ).astype(jnp.bfloat16)
        square = raw * raw
        found = square[:, :LANES]
        for part in range(1, width // LANES):
            found = found + square[:, part * LANES : (part + 1) * LANES]
        sums[core, z, pl.ds(i, 1), :] = jnp.sum(found.T, axis=0, keepdims=True)

    pl.semaphore_wait(barrier, len(peers))

    def token_view(owner, chunk):
        return stream.at[owner, rows_at(chunk, token_rows, core * rows), :]

    token_line = Line(
        token_view, chan_count, token_send, token_recv, lambda to: (y, s, to)
    )
    for chunk in range(TOKEN_CHUNKS):
        for way in range(2):

            @pl.when(token_line.sends(way, 0))
            def _():
                token_line.copy(way, 0, (chunk,)).start()

    def own_half(owner, of):
        return stream.at[owner, pl.ds(pl.multiple_of(of * rows, rows), rows), :]

    def mate_tokens():
        return remote(
            own_half(z, core), own_half(z, core), mate_send.at[0], mate_recv.at[0], mate
        )

    mate_tokens().start()
    sum_copies = [
        remote(
            sums.at[core, z], sums.at[core, z], sums_send.at[at], sums_recv.at[core, z], peer
        )
        for at, peer in enumerate(column_peers)
    ]
    for copy in sum_copies:
        copy.start()
    for g in range(groups):
        for b in range(branches):
            remote(
                weights.at[b, :, lanes_of((1 - core) * share, g)],
                weight.at[g, s, :, pl.ds(b * LANES, LANES)],
                mate_send.at[1],
                mate_recv.at[1],
                mate,
            ).start()

    for j, (which, start) in enumerate(tap_stage):
        tap_loads[j].wait()

        @pl.loop(0, groups)
        def _(g):
            mine = freq[which, rows_at(core * groups + g, BLOCK, start), :]
            taps[g, pl.ds(pl.multiple_of(s * rows + j * LANES, LANES), LANES), :] = mine.T.astype(
                jnp.bfloat16
            )
            other = freq[which, rows_at((1 - core) * groups + g, BLOCK, start), :]
            ready[g, j * LANES : (j + 1) * LANES, :] = other.T.astype(jnp.bfloat16)

    def tap_part(owner, part):
        return taps.at[
            :, pl.ds(pl.multiple_of(owner * rows + part * (rows // 2), rows // 2), rows // 2), :
        ]

    def taps_across(to):
        src = tap_part(s, y) if to == 0 else ready.at[
            :, pl.ds(pl.multiple_of(y * (rows // 2), rows // 2), rows // 2), :
        ]
        return remote(
            src,
            tap_part(s, y),
            tap_send.at[to],
            tap_recv.at[core],
            across if to == 0 else aslant,
        )

    def taps_beside(origin, part):
        view = tap_part(origin, part)
        return remote(view, view, tap_send.at[2 + origin], tap_recv.at[2 + origin], beside)

    def taps_mate():
        return remote(
            ready,
            taps.at[:, pl.ds(pl.multiple_of(s * rows, rows), rows), :],
            mate_send.at[2],
            mate_recv.at[2],
            mate,
        )

    @pl.when(x == 0)
    def _():
        taps_across(0).start()
        taps_across(1).start()

        @pl.loop(0, groups)
        def _(g):
            taps[g, length:, :] = jnp.zeros((length, LANES), jnp.bfloat16)

    taps_mate().start()

    def weight_view(owner, part, g, c):
        return weight.at[g, owner, rows_at(c, weight_rows, part * half), :]

    def weight_half(owner, part):
        return weight.at[:, owner, pl.ds(pl.multiple_of(part * half, half), half), :]

    def send_weights(g, chunks=range(WEIGHT_CHUNKS)):
        for c in chunks:
            for to in range(2):
                side = core if to == 0 else 1 - core
                view = weight_view(s, y, g, c)
                for b in range(branches):
                    remote(
                        weights.at[
                            b,
                            rows_at(c, weight_rows, y * half),
                            pl.ds(pl.multiple_of(side * share + g * LANES, LANES), LANES),
                        ],
                        view.at[:, pl.ds(b * LANES, LANES)],
                        x_send.at[to],
                        x_recv.at[core, g, c],
                        across if to == 0 else aslant,
                    ).start()

    for g in range(groups - 2):
        send_weights(g)
    send_weights(groups - 2, range(2))

    at_end = (z == 0) | (z == chan_count - 1)

    @pl.when((x == 1) | at_end)
    def _():
        send_weights(groups - 2, [2, 3])
        send_weights(groups - 1, [0, 1])

    @pl.when(x == 1)
    def _():
        send_weights(groups - 1, [2, 3])

    def beside_copy(origin, part, g, c):
        view = weight_view((1 - x) * 2 + origin, part, g, c)
        return remote(view, view, y_send.at[origin], y_recv.at[origin, g], beside)

    def forward(g, c):
        for origin in range(2):
            view = weight_view((1 - x) * 2 + origin, y, g, c)
            remote(
                view, view, x_send.at[origin], x_recv.at[origin, g, c], beside
            ).wait_recv()
            beside_copy(origin, y, g, c).start()

    def await_beside(g):
        for origin in range(2):
            view = weight.at[
                g, (1 - x) * 2 + origin, pl.ds(pl.multiple_of((1 - y) * half, half), half), :
            ]
            remote(view, view, y_send.at[origin], y_recv.at[origin, g], beside).wait_recv()

    @blocks(length)
    def _(i):
        row = lax.broadcasted_iota(jnp.int32, (BLOCK, LANES), 0) + i * BLOCK
        lane = lax.broadcasted_iota(jnp.int32, (BLOCK, LANES), 1)
        unit = math.pi / (4 * length)
        odd = 2 * row + 1
        small = odd.astype(jnp.float32) * unit
        extended[0, at_rows(i), :] = jnp.cos(small)
        extended[1, at_rows(i), :] = jnp.sin(small)
        period = 8 * length
        angle = (odd * (2 * lane + 1) % period).astype(jnp.float32) * unit
        cos, sin = jnp.cos(angle), jnp.sin(angle)
        stride = (odd * (2 * LANES) % period).astype(jnp.float32) * unit
        step_cos, step_sin = jnp.cos(stride), jnp.sin(stride)
        for a in range(length // LANES):
            table[at_rows(i), a * LANES : (a + 1) * LANES] = cos.astype(jnp.bfloat16)
            table[rows_at(i, BLOCK, length), a * LANES : (a + 1) * LANES] = sin.astype(
                jnp.bfloat16
            )
            cos, sin = cos * step_cos - sin * step_sin, sin * step_cos + cos * step_sin

    for g in range(groups):

        @blocks(length)
        def _(i):
            partial[g, at_rows(i), :] = jnp.zeros((BLOCK, branches * LANES), jnp.float32)

    def spectrum(which, column):
        @pl.loop(0, 2 * length // SPAN)
        def _(i):
            at = rows_at(i, SPAN)
            freq[which, at, :] = jnp.dot(
                table[at, :], column(), preferred_element_type=jnp.float32
            )

    def spectrum_pair(columns):
        @pl.loop(0, 2 * length // SPAN)
        def _(i):
            at = rows_at(i, SPAN)
            found = jnp.dot(
                table[at, :],
                jnp.concatenate(columns(), axis=1),
                preferred_element_type=jnp.float32,
            )
            freq[0, at, :] = found[:, :LANES]
            freq[1, at, :] = found[:, LANES:]

    def tap_spectra(g):
        spectrum_pair(lambda: [taps[g, :length, :], taps[g, length:, :]])

        @blocks(length)
        def _(i):
            low, high = at_rows(i), rows_at(i, BLOCK, length)
            cos, sin = extended[0, low, :], extended[1, low, :]

            def turned(which):
                real, imag = freq[which, low, :], -freq[which, high, :]
                return (cos * real - sin * imag) / length, (cos * imag + sin * real) / length

            real, imag = turned(0)
            late_real, late_imag = turned(1)
            place = lax.broadcasted_iota(jnp.int32, (BLOCK, LANES), 0)
            sign = (1 - 2 * (place % 2)).astype(jnp.float32)
            spectra[g, 0, low, :] = real.astype(jnp.bfloat16)
            spectra[g, 1, low, :] = imag.astype(jnp.bfloat16)
            spectra[g, 2, low, :] = (late_real - sign * imag).astype(jnp.bfloat16)
            spectra[g, 3, low, :] = (late_imag + sign * real).astype(jnp.bfloat16)

    def project(g, owner):
        @pl.loop(0, length // SPAN)
        def _(i):
            at = rows_at(i, SPAN)
            partial[g, at, :] += jnp.dot(
                stream[owner, at, :], weight[g, owner], preferred_element_type=jnp.float32
            )

    def projects_early(g, owner):
        far = jnp.abs(z - owner)
        own = owner // 2 == x
        return (
            (own & ((far <= 1) | ((far == 2) & (at_end | (g == 0)))))
            | (jnp.logical_not(own) & (far <= 2) & ((g == 0) | ((g == 1) & at_end)))
        )

    def to_mate(way, step, chunk):
        block = token_view(token_line.source(way, step), chunk)
        index = 3 + way * steps + step
        return remote(block, block, mate_send.at[index], mate_recv.at[index], mate)

    def mate_half(way, step, of):
        block = own_half(token_line.source(way, step), of)
        index = 3 + way * steps + step
        return remote(block, block, mate_send.at[index], mate_recv.at[index], mate)

    def await_mate(step):
        for way in range(2):

            @pl.when(token_line.receives(way, step))
            def _():
                mate_half(way, step, 1 - core).wait_recv()

    @pl.loop(0, steps * TOKEN_CHUNKS)
    def _(tick):
        step, chunk = tick // TOKEN_CHUNKS, tick % TOKEN_CHUNKS
        for way in range(2):

            @pl.when(token_line.receives(way, step))
            def _():
                token_line.arrived(way, step, (chunk,))
                to_mate(way, step, chunk).start()

            @pl.when(
                (step + 1 < steps)
                & token_line.receives(way, step)
                & token_line.sends(way, step + 1)
            )
            def _():
                token_line.copy(way, step + 1, (chunk,)).start()

        @pl.when((tick == TOKEN_CHUNKS // 2) & (x == 1))
        def _():
            for origin in range(2):
                view = tap_part(origin, y)
                remote(
                    view, view, tap_send.at[origin], tap_recv.at[origin], beside
                ).wait_recv()
                taps_beside(origin, y).start()

        @pl.when((tick % 2 == 1) & (tick >= 3) & (tick < 7 + 4 * WEIGHT_CHUNKS))
        def _():
            at = (tick - 3) // 2
            forward(at // WEIGHT_CHUNKS, at % WEIGHT_CHUNKS)

        @pl.when(tick == TOKEN_CHUNKS)
        def _():
            mate_half_own = own_half(z, 1 - core)
            remote(
                mate_half_own, mate_half_own, mate_send.at[0], mate_recv.at[0], mate
            ).wait_recv()
            await_mate(0)
            pltpu.make_async_copy(
                weight.at[:, s], weight.at[:, s], local_sem.at[2]
            ).wait()
            other = weight.at[:, mate_s]
            remote(other, other, mate_send.at[1], mate_recv.at[1], mate).wait_recv()
            other = taps.at[:, pl.ds(pl.multiple_of(mate_s * rows, rows), rows), :]
            remote(other, other, mate_send.at[2], mate_recv.at[2], mate).wait_recv()

            @pl.when(x == 1)
            def _():
                for origin in range(2):
                    taps_beside(origin, 1 - y).wait_recv()

        @pl.when((step == 1) & (chunk % 2 == 0))
        def _():
            tap_spectra(chunk // 2)

        @pl.when(tick == 2 * TOKEN_CHUNKS)
        def _():
            await_mate(1)

        owner = 2 * x + chunk // groups
        far = jnp.abs(z - owner)

        @pl.when(
            projects_early(chunk % groups, owner)
            & (((step == 1) & (far <= 1)) | ((step == 2) & (far == 2)))
        )
        def _():
            project(chunk % groups, owner)

        @pl.when(tick == 2 * TOKEN_CHUNKS)
        def _():
            await_beside(0)

        @pl.when((tick == 2 * TOKEN_CHUNKS + TOKEN_CHUNKS // 2) & at_end)
        def _():
            await_beside(1)

        guest = 2 * (1 - x) + (chunk // 2) % 2

        @pl.when((step == 2) & (chunk % 2 == 0) & projects_early(chunk // 4, guest))
        def _():
            project(chunk // 4, guest)

    await_mate(2)
    for by in range(1, chan_count):
        for of in range(2):
            view = sums.at[of, lax.rem(z + by, chan_count)]
            remote(
                view, view, sums_send.at[0], sums_recv.at[of, lax.rem(z + by, chan_count)], mate
            ).wait_recv()
    view = sums.at[1 - core, z]
    remote(view, view, sums_send.at[0], sums_recv.at[1 - core, z], mate).wait_recv()

    @blocks(length)
    def _(i):
        of, at = i // (rows // BLOCK), i % (rows // BLOCK)
        found = sums[of, 0, pl.ds(at, 1), :]
        for owner in range(1, chan_count):
            found = found + sums[of, owner, pl.ds(at, 1), :]
        found = lax.rsqrt(found / (chan_count * width) + EPSILON)
        scale[at_rows(i), :] = jnp.broadcast_to(found, (BLOCK, LANES)).T

    taps_mate().wait_send()

    @pl.when(x == 0)
    def _():
        taps_across(0).wait_send()
        taps_across(1).wait_send()

    def edge_copy(g):
        return remote(
            edge_out.at[g], edge.at[g], edge_send.at[0], edge_recv.at[g], across
        )

    def before_copy(g):
        return remote(
            signal.at[g], before.at[g], before_send.at[0], before_recv.at[g], across
        )

    def swap_copy(g):
        return remote(
            ready.at[g], full.at[z, g, core], swap_send.at[0], swap_recv.at[g], mate
        )

    line = Line(
        lambda owner, g, of: full.at[owner, g, of],
        chan_count,
        line_send,
        line_recv,
        lambda to: (y, s, to),
    )

    def projected(g, b, at):
        return (partial[g, at, b * LANES : (b + 1) * LANES] * scale[at, :]).astype(jnp.bfloat16)

    def featurize(g):
        @pl.when(x == 0)
        def _():
            for b in range(branches):
                edge_out[g, b] = projected(g, b, pl.ds(length - rim, rim))
                extended[b, 0:rim, :] = jnp.zeros((rim, LANES), jnp.float32)
            edge_copy(g).start()

        @blocks(length)
        def _(i):
            for b in range(branches):
                extended[b, pl.ds(pl.multiple_of(rim + i * BLOCK, rim), BLOCK), :] = projected(
                    g, b, at_rows(i)
                ).astype(jnp.float32)

        @pl.when(x == 1)
        def _():
            edge_copy(g).wait_recv()
            for b in range(branches):
                extended[b, 0:rim, :] = edge[g, b].astype(jnp.float32)

        chosen = lanes_of(core * share, g)
        coefficient = [
            [short[tap, b : b + 1, chosen] for b in range(branches)] for tap in range(SHORT)
        ]

        @blocks(length)
        def _(i):
            found = []
            for b in range(branches):
                value = jnp.zeros((BLOCK, LANES), jnp.float32)
                for tap in range(SHORT):
                    value = value + coefficient[tap][b] * extended[
                        b, pl.ds(rim - tap + i * BLOCK, BLOCK), :
                    ]
                found.append(value.astype(jnp.bfloat16))
            query[at_rows(i), :] = found[0]
            signal[g, at_rows(i), :] = (
                found[1].astype(jnp.float32) * found[2].astype(jnp.float32)
            ).astype(jnp.bfloat16)

    def convolve(g):
        joint = (x == 1) & (g > 0)

        @pl.when(jnp.logical_not(joint))
        def _():
            spectrum(0, lambda: signal[g])

        def product(i, which, first):
            low, high = at_rows(i), rows_at(i, BLOCK, length)
            cos, sin = freq[which, low, :], freq[which, high, :]
            real = spectra[g, first, low, :].astype(jnp.float32)
            imag = spectra[g, first + 1, low, :].astype(jnp.float32)
            return cos * real + sin * imag, sin * real - cos * imag

        @pl.when(x == 0)
        def _():
            @blocks(length)
            def _(i):
                real, imag = product(i, 0, 0)
                mixed[at_rows(i), :] = real.astype(jnp.bfloat16)
                mixed[rows_at(i, BLOCK, length), :] = imag.astype(jnp.bfloat16)

        @pl.when(x == 1)
        def _():
            before_copy(g).wait_recv()

            @pl.when(g == 0)
            def _():
                spectrum(1, lambda: before[g])

            @pl.when(g > 0)
            def _():
                spectrum_pair(lambda: [signal[g], before[g]])

            @blocks(length)
            def _(i):
                real, imag = product(i, 0, 0)
                more_real, more_imag = product(i, 1, 2)
                mixed[at_rows(i), :] = (real + more_real).astype(jnp.bfloat16)
                mixed[rows_at(i, BLOCK, length), :] = (imag + more_imag).astype(jnp.bfloat16)

        @pl.loop(0, length // SPAN)
        def _(i):
            low, high = rows_at(i, SPAN), rows_at(i, SPAN, length)
            freq[0, low, :] = jnp.dot(
                table[low, :], mixed[:length, :], preferred_element_type=jnp.float32
            ) + jnp.dot(table[high, :], mixed[length:, :], preferred_element_type=jnp.float32)

        direct = skip[:, lanes_of(core * share, g)]

        def gated(at):
            longer = freq[0, at, :] + direct * signal[g, at, :].astype(jnp.float32)
            longer = longer.astype(jnp.bfloat16).astype(jnp.float32)
            return (query[at, :].astype(jnp.float32) * longer).astype(jnp.bfloat16)

        @blocks(rows)
        def _(i):
            full[z, g, core, at_rows(i), :] = gated(
                pl.ds(pl.multiple_of(core * rows + i * BLOCK, BLOCK), BLOCK)
            )
            ready[g, at_rows(i), :] = gated(
                pl.ds(pl.multiple_of((1 - core) * rows + i * BLOCK, BLOCK), BLOCK)
            )

    def load_out():
        for owner in range(chan_count):
            pltpu.make_async_copy(
                out_weight.at[pl.ds(owner * length, length)], stream.at[owner], local_sem.at[1]
            ).start()

    def accumulate(owner, g):
        @pl.loop(0, total.shape[1] // (8 * LANES))
        def _(i):
            cols = rows_at(i, 8 * LANES)
            block = jnp.concatenate([full[owner, g, 0], full[owner, g, 1]], axis=1)
            kernel = jnp.concatenate(
                [stream[owner, lanes_of(of * share, g), cols] for of in range(2)], axis=0
            )
            total[:, cols] += jnp.dot(block, kernel, preferred_element_type=jnp.float32)

    def begin(g):
        swap_copy(g).start()
        for way in range(2):

            @pl.when(line.sends(way, 0))
            def _():
                line.copy(way, 0, (g, core)).start()

    def begin_other(g):
        other = full.at[z, g, 1 - core]
        remote(other, other, swap_send.at[0], swap_recv.at[g], mate).wait_recv()
        for way in range(2):

            @pl.when(line.sends(way, 0))
            def _():
                line.copy(way, 0, (g, 1 - core)).start()

    def settle():
        other = weight.at[:, s]
        remote(other, other, mate_send.at[1], mate_recv.at[1], mate).wait_send()
        for copy in sum_copies:
            copy.wait_send()

        @pl.when(x == 1)
        def _():
            for origin in range(2):
                taps_beside(origin, y).wait_send()

        for at in range(2):
            view = weight_half(s, y)
            remote(view, view, x_send.at[at], x_recv.at[0, 0, 0], across).wait_send()
            view = weight_half((1 - x) * 2 + at, y)
            remote(view, view, y_send.at[at], y_recv.at[at, 0], beside).wait_send()

        @pl.when(x == 0)
        def _():
            remote(edge_out, edge, edge_send.at[0], edge_recv.at[0], across).wait_send()
            remote(signal, before, before_send.at[0], before_recv.at[0], across).wait_send()

    def settle_tokens():
        mate_tokens().wait_send()
        for way in range(2):
            for step in range(steps):

                @pl.when(token_line.receives(way, step))
                def _():
                    mate_half(way, step, core).wait_send()

                @pl.when(token_line.sends(way, step))
                def _():
                    token_line.drain(way, step, (0,), lambda owner: own_half(owner, core))

    def way_of(k):
        return jnp.where(z < chan_count // 2, 1 - k, k)

    def late_forwards(g, at, inner, outer):
        for here, pieces in ((jnp.logical_not(at_end), inner), (at_end, outer)):

            @pl.when((g == at) & here)
            def _():
                for group, c in pieces:
                    forward(group, c)

    def pass_on(way, step, at):
        @pl.when(
            (at >= 0) & (at < groups) & line.receives(way, step) & line.sends(way, step + 1)
        )
        def _():
            for of in (core, 1 - core):
                line.arrived(way, step, (at, of))
                line.copy(way, step + 1, (at, of)).start()

    for copy in small_loads[1:]:
        copy.wait()
    near, away = way_of(0), way_of(1)

    @pl.loop(0, groups)
    def _(g):
        @pl.when(g == 3)
        def _():
            pass_on(away, 0, 1)
            pass_on(near, 0, 2)

        @pl.when((g >= 2) | ((g == 1) & jnp.logical_not(at_end)))
        def _():
            await_beside(g)

        @pl.loop(0, chan_count)
        def _(owner):
            @pl.when(jnp.logical_not(projects_early(g, owner)))
            def _():
                project(g, owner)

        @pl.when(g == groups - 1)
        def _():
            settle_tokens()
            load_out()

        featurize(g)

        @pl.when(x == 0)
        def _():
            before_copy(g).start()

            for at, inner, outer in (
                (0, [(groups - 2, 2)], [(groups - 1, 2)]),
                (1, [(groups - 2, 3), (groups - 1, 0), (groups - 1, 1)], [(groups - 1, 3)]),
                (2, [(groups - 1, 2), (groups - 1, 3)], []),
            ):

                @pl.when((g == at) & jnp.logical_not(at_end))
                def _():
                    for group, c in inner:
                        send_weights(group, [c])

                @pl.when((g == at) & at_end)
                def _():
                    for group, c in outer:
                        send_weights(group, [c])

        @pl.when(g == 1)
        def _():
            pass_on(near, 0, 0)

        late_forwards(g, 1, [(groups - 2, 3)], [(groups - 1, 0), (groups - 1, 1)])
        late_forwards(g, 2, [(groups - 1, 0), (groups - 1, 1)], [(groups - 1, 3)])

        @pl.when(g == 2)
        def _():
            pass_on(near, 0, 1)
            pass_on(away, 0, 0)

        @pl.when(g == 3)
        def _():
            pass_on(near, 1, 1)
            pass_on(away, 0, 2)

        late_forwards(g, 0, [], [(groups - 2, 2), (groups - 2, 3)])
        convolve(g)
        begin(g)
        late_forwards(g, 0, [(groups - 2, 2)], [])
        late_forwards(g, 1, [], [(groups - 1, 2)])
        begin_other(g)

        late_forwards(g, 2, [(groups - 1, 2), (groups - 1, 3)], [])

        @pl.when(g == 2)
        def _():
            pass_on(near, 1, 0)

    pltpu.make_async_copy(stream, stream, local_sem.at[1]).wait()

    @pl.loop(0, groups + steps - 1)
    def _(n):
        for at, pieces in (
            (0, [(near, 1, 2)]),
            (1, [(away, 0, 3), (near, 0, 3)]),
            (3, [(near, 1, 3)]),
        ):

            @pl.when(n == at)
            def _():
                for way, step, group in pieces:
                    pass_on(way, step, group)

        @pl.when(n == 2)
        def _():
            settle()

        @pl.when(n < groups)
        def _():
            accumulate(z, n)

        @pl.loop(0, 2)
        def _(way):
            for step in range(steps):
                at = n - jnp.where(at_end, step, 0)

                @pl.when((at >= 0) & (at < groups) & line.receives(way, step))
                def _():
                    @pl.when(jnp.logical_not(line.sends(way, step + 1)))
                    def _():
                        for of in range(2):
                            line.arrived(way, step, (at, of))

                    accumulate(line.source(way, step), at)

    @blocks(rows)
    def _(i):
        result[at_rows(i), :] = total[at_rows(i), :].astype(jnp.bfloat16)

    remote(ready, ready, swap_send.at[0], swap_recv.at[0], mate).wait_send()
    for way in range(2):
        for step in range(steps):

            @pl.when(line.sends(way, step))
            def _():
                line.drain(way, step, (0, 0), lambda owner: full.at[owner])


def chip_body(tokens, norm_gain, proj_weight, short_filter, long_filter, skip_gain, out_weight):
    chan_count = lax.axis_size("chan")
    rows, width = tokens.shape
    depth, branches, local_chan = proj_weight.shape
    length, share = 2 * rows, local_chan // 2
    groups = share // LANES
    steps = chan_count - 1
    dma = pltpu.SemaphoreType.DMA
    f32, bf16 = jnp.float32, jnp.bfloat16
    vmem = pl.BlockSpec(memory_space=pltpu.VMEM)
    return pl.pallas_call(
        functools.partial(block_kernel, chan_count),
        out_shape=jax.ShapeDtypeStruct((rows, width), bf16),
        in_specs=[HBM] * 7,
        out_specs=vmem,
        scratch_shapes=[
            pltpu.VMEM((1, width), f32),
            pltpu.VMEM(short_filter.shape, f32),
            pltpu.VMEM((1, local_chan), f32),
            pltpu.VMEM((chan_count, length, width), bf16),
            pltpu.VMEM((groups, 4, depth, branches * LANES), bf16),
            pltpu.VMEM((2, chan_count, 8, LANES), f32),
            pltpu.VMEM((length, LANES), f32),
            pltpu.VMEM((groups, length, branches * LANES), f32),
            pltpu.VMEM((2 * length, length), bf16),
            pltpu.VMEM((groups, 2 * length, LANES), bf16),
            pltpu.VMEM((groups, 4, length, LANES), bf16),
            pltpu.VMEM((2, 2 * length, LANES), f32),
            pltpu.VMEM((2 * length, LANES), bf16),
            pltpu.VMEM((groups, branches, 16, LANES), bf16),
            pltpu.VMEM((groups, branches, 16, LANES), bf16),
            pltpu.VMEM((branches, length + 16, LANES), f32),
            pltpu.VMEM((length, LANES), bf16),
            pltpu.VMEM((groups, length, LANES), bf16),
            pltpu.VMEM((groups, length, LANES), bf16),
            pltpu.VMEM((groups, rows, LANES), bf16),
            pltpu.VMEM((chan_count, groups, 2, rows, LANES), bf16),
            pltpu.VMEM((rows, width), f32),
            dma((10,)),
            dma((3 + 2 * steps,)),
            dma((3 + 2 * steps,)),
            dma((2, steps)),
            dma((steps, TOKEN_CHUNKS)),
            dma((2 * chan_count - 1,)),
            dma((2, chan_count)),
            dma((2,)),
            dma((2, groups, WEIGHT_CHUNKS)),
            dma((2,)),
            dma((2, groups)),
            dma((4,)),
            dma((4,)),
            dma((1,)),
            dma((groups,)),
            dma((1,)),
            dma((groups,)),
            dma((1,)),
            dma((groups,)),
            dma((2, steps)),
            dma((steps, groups, 2)),
        ],
        compiler_params=pltpu.CompilerParams(
            collective_id=0, has_side_effects=True, vmem_limit_bytes=52 * 1024 * 1024
        ),
        name="block",
    )(
        tokens,
        pltpu.with_memory_space_constraint(norm_gain[None, :], pltpu.HBM),
        proj_weight.transpose(1, 0, 2),
        pltpu.with_memory_space_constraint(short_filter, pltpu.HBM),
        long_filter,
        pltpu.with_memory_space_constraint(skip_gain[None, :], pltpu.HBM),
        out_weight,
    )


def select_body(mesh):
    if (mesh.shape["groups"], mesh.shape["seq"], mesh.shape["chan"]) == (2, 4, 4):
        return chip_body
    return body


def solution(mesh):
    placed = (
        P(("groups", "seq"), "chan"),
        P(),
        P("seq", None, "chan"),
        P(None, None, "chan"),
        P("chan", "seq"),
        P("chan"),
        P(None, "chan"),
    )
    return jax.shard_map(
        select_body(mesh), mesh=mesh, in_specs=placed, out_specs=P(("groups", "seq"), "chan"), check_vma=False
    )
```

```python
import functools
import math

import jax
import jax.numpy as jnp
import numpy as np
from jax import lax
from jax.experimental import pallas as pl
from jax.experimental.pallas import tpu as pltpu
from jax.sharding import PartitionSpec as P

SHORT = 3


EPSILON = 1e-06
HIGHEST = lax.Precision.HIGHEST


def from_behind(value, axis, steps):
    count = lax.axis_size(axis)
    initial, last = (max(0, -steps), min(count, count - steps))
    return lax.ppermute(value, axis, [(source, source + steps) for source in range(initial, last)])


def angle_table(row_count, col_count, period, sign):
    row_index = lax.iota(jnp.int32, row_count)[:, None]
    col_index = lax.iota(jnp.int32, col_count)[None, :]
    angles = (row_index * col_index % period).astype(jnp.float32) * (sign * 2.0 * math.pi / period)
    return (jnp.cos(angles), jnp.sin(angles))


def forward_spectrum(signal_rows, first, second):
    channels = signal_rows.shape[0]
    grid_rows = signal_rows.reshape(channels, first, second)
    cos_first, sin_first = angle_table(first, first, first, -1.0)
    part_re = jnp.einsum("cab,ak->ckb", grid_rows, cos_first, precision=HIGHEST)
    part_im = jnp.einsum("cab,ak->ckb", grid_rows, sin_first, precision=HIGHEST)
    twist_cos, twist_sin = angle_table(first, second, first * second, -1.0)
    part_re, part_im = (
        part_re * twist_cos - part_im * twist_sin,
        part_re * twist_sin + part_im * twist_cos,
    )
    cos_second, sin_second = angle_table(second, second, second, -1.0)
    spectrum_real = jnp.einsum("ckb,bm->ckm", part_re, cos_second, precision=HIGHEST) - jnp.einsum(
        "ckb,bm->ckm", part_im, sin_second, precision=HIGHEST
    )
    spec_im = jnp.einsum("ckb,bm->ckm", part_re, sin_second, precision=HIGHEST) + jnp.einsum(
        "ckb,bm->ckm", part_im, cos_second, precision=HIGHEST
    )
    return (spectrum_real, spec_im)


def inverse_spectrum(spectrum_real, spec_im, first, second):
    channels = spectrum_real.shape[0]
    cos_second, sin_second = angle_table(second, second, second, 1.0)
    part_re = jnp.einsum("ckm,bm->ckb", spectrum_real, cos_second, precision=HIGHEST) - jnp.einsum(
        "ckm,bm->ckb", spec_im, sin_second, precision=HIGHEST
    )
    part_im = jnp.einsum("ckm,bm->ckb", spectrum_real, sin_second, precision=HIGHEST) + jnp.einsum(
        "ckm,bm->ckb", spec_im, cos_second, precision=HIGHEST
    )
    twist_cos, twist_sin = angle_table(first, second, first * second, 1.0)
    part_re, part_im = (
        part_re * twist_cos - part_im * twist_sin,
        part_re * twist_sin + part_im * twist_cos,
    )
    cos_first, sin_first = angle_table(first, first, first, 1.0)
    result = jnp.einsum("ckb,ak->cab", part_re, cos_first, precision=HIGHEST) - jnp.einsum(
        "ckb,ak->cab", part_im, sin_first, precision=HIGHEST
    )
    return result.reshape(channels, first * second) / (first * second)


def spectral_conv(signal_rows, filter_rows):
    channels, length = signal_rows.shape
    padded_len = 2 * length
    log_len = padded_len.bit_length() - 1
    first = 1 << log_len // 2
    second = padded_len // first
    zeros_tail = jnp.zeros((channels, length), jnp.float32)
    sig_re, sig_im = forward_spectrum(
        jnp.concatenate([signal_rows, zeros_tail], axis=1), first, second
    )
    tap_re, tap_im = forward_spectrum(
        jnp.concatenate([filter_rows, zeros_tail], axis=1), first, second
    )
    prod_re = sig_re * tap_re - sig_im * tap_im
    prod_im = sig_re * tap_im + sig_im * tap_re
    return inverse_spectrum(prod_re, prod_im, first, second)[:, :length]


def short_filter_output(projected, rim_cells, kernel_coefficients):
    count = kernel_coefficients.shape[0]
    steps_len = projected.shape[2]
    extended = jnp.concatenate([rim_cells, projected], axis=2).astype(jnp.float32)
    total = jnp.zeros(projected.shape, jnp.float32)
    for tap in range(count):
        total = (
            total
            + kernel_coefficients[tap][:, :, None]
            * extended[:, :, count - 1 - tap : count - 1 - tap + steps_len]
        )
    return total.astype(jnp.bfloat16)


def hyena_mixer(keys_rows, values_rows, long_taps, skip_part):
    middle = keys_rows.astype(jnp.float32) * values_rows.astype(jnp.float32)
    return (spectral_conv(middle, long_taps) + skip_part[:, None] * middle).astype(jnp.bfloat16)


def body(tokens, norm_gain, proj_weight, short_filter, long_filter, skip_gain, out_weight):
    seq_count = lax.axis_size("seq")
    local_rows = tokens.shape[0]
    local_chan = proj_weight.shape[2]
    subset = local_chan // seq_count
    length = local_rows * seq_count
    offset = lax.axis_index("seq") * subset
    whole = lax.all_gather(tokens, "chan", axis=1, tiled=True)
    wide = whole.astype(jnp.float32)
    rescaled_signal = (
        wide * lax.rsqrt(jnp.mean(wide * wide, axis=1, keepdims=True) + EPSILON) * norm_gain
    ).astype(jnp.bfloat16)
    projected = lax.dot_general(
        lax.all_gather(proj_weight, "seq", axis=0, tiled=True),
        rescaled_signal,
        (((0,), (1,)), ((), ())),
        preferred_element_type=jnp.float32,
    ).astype(jnp.bfloat16)
    taps_grid = long_filter.reshape(1, seq_count, subset, local_rows)
    long_taps = lax.all_to_all(taps_grid, "seq", split_axis=1, concat_axis=3, tiled=True).reshape(
        subset, length
    )
    skip_part = lax.dynamic_slice_in_dim(skip_gain, offset, subset, 0)
    rim_cells = from_behind(projected[:, :, local_rows - (SHORT - 1) :], "seq", 1)
    featured = short_filter_output(projected, rim_cells, short_filter)
    pair_grid = featured[1:].reshape(2, seq_count, subset, local_rows)
    moved = lax.all_to_all(pair_grid, "seq", split_axis=1, concat_axis=3, tiled=True).reshape(
        2, subset, length
    )
    result = hyena_mixer(moved[0], moved[1], long_taps, skip_part)
    returned = lax.all_to_all(
        result.reshape(1, subset, length), "seq", split_axis=2, concat_axis=0, tiled=True
    )
    returned = returned.reshape(local_chan, local_rows)
    gated = (featured[0].astype(jnp.float32) * returned.astype(jnp.float32)).astype(jnp.bfloat16)
    full_mix = lax.all_gather(gated, "chan", axis=0, tiled=True)
    update = lax.dot_general(
        full_mix, out_weight, (((0,), (0,)), ((), ())), preferred_element_type=jnp.float32
    )
    return (tokens.astype(jnp.float32) + update).astype(jnp.bfloat16)

LANES = 128
BLOCK = 128
SPAN = 1024
TOKEN_CHUNKS = 8
WEIGHT_CHUNKS = 4
HBM = pl.BlockSpec(memory_space=pltpu.HBM)


def remote(src, dst, send_sem, recv_sem, where):
    return pltpu.make_async_remote_copy(
        src_ref=src,
        dst_ref=dst,
        send_sem=send_sem,
        recv_sem=recv_sem,
        device_id=where,
        device_id_type=pl.DeviceIdType.MESH,
    )


class Line:
    def __init__(self, view, count, send_sem, recv_sem, place):
        self.view, self.count, self.place = view, count, place
        self.send_sem, self.recv_sem = send_sem, recv_sem
        self.me = lax.axis_index("chan")

    def move(self, way, step, piece, block, target):
        slot = jnp.minimum(jnp.where(way == 0, step, target + step), self.count - 2)
        recv = self.recv_sem.at[(slot,) + piece]
        return remote(block, block, self.send_sem.at[way, step], recv, self.place(target))

    def drain(self, way, step, first, block):
        self.move(way, step, first, block(self.source(way, step - 1)), self.me).wait_send()

    def source(self, way, step):
        return jnp.clip(self.me - (step + 1) * (1 - 2 * way), 0, self.count - 1)

    def copy(self, way, step, piece):
        owner = self.source(way, step - 1)
        target = self.source(way, -2)
        return self.move(way, step, piece, self.view(owner, *piece), target)

    def inside(self, way, by):
        place = self.me + by * (1 - 2 * way)
        return (place >= 0) & (place < self.count)

    def sends(self, way, step):
        return self.inside(way, -step) & self.inside(way, 1)

    def receives(self, way, step):
        return self.inside(way, -1 - step)

    def arrived(self, way, step, piece):
        owner = self.source(way, step)
        self.move(way, step, piece, self.view(owner, *piece), self.me).wait_recv()
        return owner


def block_kernel(
    chan_count,
    tokens,
    gain_hbm,
    weights,
    short_hbm,
    long_taps,
    skip_hbm,
    out_weight,
    result,
    gain,
    short,
    skip,
    stream,
    weight,
    sums,
    scale,
    partial,
    table,
    taps,
    spectra,
    freq,
    mixed,
    edge_out,
    edge,
    extended,
    query,
    signal,
    before,
    ready,
    full,
    total,
    local_sem,
    mate_send,
    mate_recv,
    token_send,
    token_recv,
    sums_send,
    sums_recv,
    x_send,
    x_recv,
    y_send,
    y_recv,
    tap_send,
    tap_recv,
    edge_send,
    edge_recv,
    before_send,
    before_recv,
    swap_send,
    swap_recv,
    line_send,
    line_recv,
):
    y, s, z = (lax.axis_index(name) for name in ("groups", "seq", "chan"))
    x, core = s // 2, s % 2
    mate_s = s + 1 - 2 * core
    mate = (y, mate_s, z)
    across = (y, (1 - x) * 2 + core, z)
    aslant = (y, (1 - x) * 2 + 1 - core, z)
    beside = (1 - y, s, z)
    rows, width = tokens.shape
    length = 2 * rows
    branches, depth = weights.shape[0], weights.shape[1]
    half = depth // 2
    share = weights.shape[2] // 2
    groups = share // LANES
    rim = edge.shape[2]
    steps = chan_count - 1
    token_rows = rows // TOKEN_CHUNKS
    weight_rows = half // WEIGHT_CHUNKS

    column_peers = [mate] + [
        (y, 2 * x + of, lax.rem(z + by, chan_count))
        for by in range(1, chan_count)
        for of in (core, 1 - core)
    ]
    peers = column_peers + [across, aslant, beside]

    def rows_at(i, count, base=0):
        return pl.ds(pl.multiple_of(base + i * count, count), count)

    def at_rows(i):
        return rows_at(i, BLOCK)

    def blocks(count):
        return pl.loop(0, count // BLOCK)

    def lanes_of(base, g):
        return pl.ds(pl.multiple_of(base + g * LANES, LANES), LANES)

    tap_stage = [(0, 0), (0, length), (1, 0), (1, length)]
    tap_loads = [
        pltpu.make_async_copy(
            long_taps.at[:, pl.ds(j * LANES, LANES)],
            freq.at[which, pl.ds(start, length)],
            local_sem.at[4 + j],
        )
        for j, (which, start) in enumerate(tap_stage)
    ]
    token_load = pltpu.make_async_copy(tokens, result, local_sem.at[0])
    token_load.start()
    small_loads = [
        pltpu.make_async_copy(src, dst, local_sem.at[at])
        for src, dst, at in (
            (gain_hbm.at[:, pl.ds(pl.multiple_of(z * width, width), width)], gain, 3),
            (short_hbm, short, 8),
            (skip_hbm, skip, 9),
        )
    ]
    for copy in small_loads:
        copy.start()
    barrier = pltpu.get_barrier_semaphore()
    for peer in peers:
        pl.semaphore_signal(barrier, inc=1, device_id=peer, device_id_type=pl.DeviceIdType.MESH)
    for copy in tap_loads:
        copy.start()
    for g in range(groups):
        for b in range(branches):
            pltpu.make_async_copy(
                weights.at[b, :, lanes_of(core * share, g)],
                weight.at[g, s, :, pl.ds(b * LANES, LANES)],
                local_sem.at[2],
            ).start()

    sums[core, z] = jnp.zeros(sums.shape[2:], jnp.float32)
    small_loads[0].wait()
    own_gain = gain[...]
    token_load.wait()

    @blocks(rows)
    def _(i):
        raw = result[at_rows(i), :].astype(jnp.float32)
        total[at_rows(i), :] = raw
        stream[z, pl.ds(pl.multiple_of(core * rows + i * BLOCK, BLOCK), BLOCK), :] = (
            raw * own_gain
        ).astype(jnp.bfloat16)
        square = raw * raw
        found = square[:, :LANES]
        for part in range(1, width // LANES):
            found = found + square[:, part * LANES : (part + 1) * LANES]
        sums[core, z, pl.ds(i, 1), :] = jnp.sum(found.T, axis=0, keepdims=True)

    pl.semaphore_wait(barrier, len(peers))

    def token_view(owner, chunk):
        return stream.at[owner, rows_at(chunk, token_rows, core * rows), :]

    token_line = Line(
        token_view, chan_count, token_send, token_recv, lambda to: (y, s, to)
    )
    for chunk in range(TOKEN_CHUNKS):
        for way in range(2):

            @pl.when(token_line.sends(way, 0))
            def _():
                token_line.copy(way, 0, (chunk,)).start()

    def own_half(owner, of):
        return stream.at[owner, pl.ds(pl.multiple_of(of * rows, rows), rows), :]

    def mate_tokens():
        return remote(
            own_half(z, core), own_half(z, core), mate_send.at[0], mate_recv.at[0], mate
        )

    mate_tokens().start()
    sum_copies = [
        remote(
            sums.at[core, z], sums.at[core, z], sums_send.at[at], sums_recv.at[core, z], peer
        )
        for at, peer in enumerate(column_peers)
    ]
    for copy in sum_copies:
        copy.start()
    for g in range(groups):
        for b in range(branches):
            remote(
                weights.at[b, :, lanes_of((1 - core) * share, g)],
                weight.at[g, s, :, pl.ds(b * LANES, LANES)],
                mate_send.at[1],
                mate_recv.at[1],
                mate,
            ).start()

    for j, (which, start) in enumerate(tap_stage):
        tap_loads[j].wait()

        @pl.loop(0, groups)
        def _(g):
            mine = freq[which, rows_at(core * groups + g, BLOCK, start), :]
            taps[g, pl.ds(pl.multiple_of(s * rows + j * LANES, LANES), LANES), :] = mine.T.astype(
                jnp.bfloat16
            )
            other = freq[which, rows_at((1 - core) * groups + g, BLOCK, start), :]
            ready[g, j * LANES : (j + 1) * LANES, :] = other.T.astype(jnp.bfloat16)

    def tap_part(owner, part):
        return taps.at[
            :, pl.ds(pl.multiple_of(owner * rows + part * (rows // 2), rows // 2), rows // 2), :
        ]

    def taps_across(to):
        src = tap_part(s, y) if to == 0 else ready.at[
            :, pl.ds(pl.multiple_of(y * (rows // 2), rows // 2), rows // 2), :
        ]
        return remote(
            src,
            tap_part(s, y),
            tap_send.at[to],
            tap_recv.at[core],
            across if to == 0 else aslant,
        )

    def taps_beside(origin, part):
        view = tap_part(origin, part)
        return remote(view, view, tap_send.at[2 + origin], tap_recv.at[2 + origin], beside)

    def taps_mate():
        return remote(
            ready,
            taps.at[:, pl.ds(pl.multiple_of(s * rows, rows), rows), :],
            mate_send.at[2],
            mate_recv.at[2],
            mate,
        )

    @pl.when(x == 0)
    def _():
        taps_across(0).start()
        taps_across(1).start()

        @pl.loop(0, groups)
        def _(g):
            taps[g, length:, :] = jnp.zeros((length, LANES), jnp.bfloat16)

    taps_mate().start()

    def weight_view(owner, part, g, c):
        return weight.at[g, owner, rows_at(c, weight_rows, part * half), :]

    def weight_half(owner, part):
        return weight.at[:, owner, pl.ds(pl.multiple_of(part * half, half), half), :]

    def send_weights(g, chunks=range(WEIGHT_CHUNKS)):
        for c in chunks:
            for to in range(2):
                side = core if to == 0 else 1 - core
                view = weight_view(s, y, g, c)
                for b in range(branches):
                    remote(
                        weights.at[
                            b,
                            rows_at(c, weight_rows, y * half),
                            pl.ds(pl.multiple_of(side * share + g * LANES, LANES), LANES),
                        ],
                        view.at[:, pl.ds(b * LANES, LANES)],
                        x_send.at[to],
                        x_recv.at[core, g, c],
                        across if to == 0 else aslant,
                    ).start()

    for g in range(groups - 2):
        send_weights(g)
    send_weights(groups - 2, range(2))

    at_end = (z == 0) | (z == chan_count - 1)

    @pl.when((x == 1) | at_end)
    def _():
        send_weights(groups - 2, [2, 3])
        send_weights(groups - 1, [0, 1])

    @pl.when(x == 1)
    def _():
        send_weights(groups - 1, [2, 3])

    def beside_copy(origin, part, g, c):
        view = weight_view((1 - x) * 2 + origin, part, g, c)
        return remote(view, view, y_send.at[origin], y_recv.at[origin, g], beside)

    def forward(g, c):
        for origin in range(2):
            view = weight_view((1 - x) * 2 + origin, y, g, c)
            remote(
                view, view, x_send.at[origin], x_recv.at[origin, g, c], beside
            ).wait_recv()
            beside_copy(origin, y, g, c).start()

    def await_beside(g):
        for origin in range(2):
            view = weight.at[
                g, (1 - x) * 2 + origin, pl.ds(pl.multiple_of((1 - y) * half, half), half), :
            ]
            remote(view, view, y_send.at[origin], y_recv.at[origin, g], beside).wait_recv()

    @blocks(length)
    def _(i):
        row = lax.broadcasted_iota(jnp.int32, (BLOCK, LANES), 0) + i * BLOCK
        lane = lax.broadcasted_iota(jnp.int32, (BLOCK, LANES), 1)
        unit = math.pi / (4 * length)
        odd = 2 * row + 1
        small = odd.astype(jnp.float32) * unit
        extended[0, at_rows(i), :] = jnp.cos(small)
        extended[1, at_rows(i), :] = jnp.sin(small)
        period = 8 * length
        angle = (odd * (2 * lane + 1) % period).astype(jnp.float32) * unit
        cos, sin = jnp.cos(angle), jnp.sin(angle)
        stride = (odd * (2 * LANES) % period).astype(jnp.float32) * unit
        step_cos, step_sin = jnp.cos(stride), jnp.sin(stride)
        for a in range(length // LANES):
            table[at_rows(i), a * LANES : (a + 1) * LANES] = cos.astype(jnp.bfloat16)
            table[rows_at(i, BLOCK, length), a * LANES : (a + 1) * LANES] = sin.astype(
                jnp.bfloat16
            )
            cos, sin = cos * step_cos - sin * step_sin, sin * step_cos + cos * step_sin

    for g in range(groups):

        @blocks(length)
        def _(i):
            partial[g, at_rows(i), :] = jnp.zeros((BLOCK, branches * LANES), jnp.float32)

    def spectrum(which, column):
        @pl.loop(0, 2 * length // SPAN)
        def _(i):
            at = rows_at(i, SPAN)
            freq[which, at, :] = jnp.dot(
                table[at, :], column(), preferred_element_type=jnp.float32
            )

    def spectrum_pair(columns):
        @pl.loop(0, 2 * length // SPAN)
        def _(i):
            at = rows_at(i, SPAN)
            found = jnp.dot(
                table[at, :],
                jnp.concatenate(columns(), axis=1),
                preferred_element_type=jnp.float32,
            )
            freq[0, at, :] = found[:, :LANES]
            freq[1, at, :] = found[:, LANES:]

    def tap_spectra(g):
        spectrum_pair(lambda: [taps[g, :length, :], taps[g, length:, :]])

        @blocks(length)
        def _(i):
            low, high = at_rows(i), rows_at(i, BLOCK, length)
            cos, sin = extended[0, low, :], extended[1, low, :]

            def turned(which):
                real, imag = freq[which, low, :], -freq[which, high, :]
                return (cos * real - sin * imag) / length, (cos * imag + sin * real) / length

            real, imag = turned(0)
            late_real, late_imag = turned(1)
            place = lax.broadcasted_iota(jnp.int32, (BLOCK, LANES), 0)
            sign = (1 - 2 * (place % 2)).astype(jnp.float32)
            spectra[g, 0, low, :] = real.astype(jnp.bfloat16)
            spectra[g, 1, low, :] = imag.astype(jnp.bfloat16)
            spectra[g, 2, low, :] = (late_real - sign * imag).astype(jnp.bfloat16)
            spectra[g, 3, low, :] = (late_imag + sign * real).astype(jnp.bfloat16)

    def project(g, owner):
        @pl.loop(0, length // SPAN)
        def _(i):
            at = rows_at(i, SPAN)
            partial[g, at, :] += jnp.dot(
                stream[owner, at, :], weight[g, owner], preferred_element_type=jnp.float32
            )

    def projects_early(g, owner):
        far = jnp.abs(z - owner)
        own = owner // 2 == x
        return (
            (own & ((far <= 1) | ((far == 2) & (at_end | (g == 0)))))
            | (jnp.logical_not(own) & (far <= 2) & ((g == 0) | ((g == 1) & at_end)))
        )

    def to_mate(way, step, chunk):
        block = token_view(token_line.source(way, step), chunk)
        index = 3 + way * steps + step
        return remote(block, block, mate_send.at[index], mate_recv.at[index], mate)

    def mate_half(way, step, of):
        block = own_half(token_line.source(way, step), of)
        index = 3 + way * steps + step
        return remote(block, block, mate_send.at[index], mate_recv.at[index], mate)

    def await_mate(step):
        for way in range(2):

            @pl.when(token_line.receives(way, step))
            def _():
                mate_half(way, step, 1 - core).wait_recv()

    @pl.loop(0, steps * TOKEN_CHUNKS)
    def _(tick):
        step, chunk = tick // TOKEN_CHUNKS, tick % TOKEN_CHUNKS
        for way in range(2):

            @pl.when(token_line.receives(way, step))
            def _():
                token_line.arrived(way, step, (chunk,))
                to_mate(way, step, chunk).start()

            @pl.when(
                (step + 1 < steps)
                & token_line.receives(way, step)
                & token_line.sends(way, step + 1)
            )
            def _():
                token_line.copy(way, step + 1, (chunk,)).start()

        @pl.when((tick == TOKEN_CHUNKS // 2) & (x == 1))
        def _():
            for origin in range(2):
                view = tap_part(origin, y)
                remote(
                    view, view, tap_send.at[origin], tap_recv.at[origin], beside
                ).wait_recv()
                taps_beside(origin, y).start()

        @pl.when((tick % 2 == 1) & (tick >= 3) & (tick < 7 + 4 * WEIGHT_CHUNKS))
        def _():
            at = (tick - 3) // 2
            forward(at // WEIGHT_CHUNKS, at % WEIGHT_CHUNKS)

        @pl.when(tick == TOKEN_CHUNKS)
        def _():
            mate_half_own = own_half(z, 1 - core)
            remote(
                mate_half_own, mate_half_own, mate_send.at[0], mate_recv.at[0], mate
            ).wait_recv()
            await_mate(0)
            pltpu.make_async_copy(
                weight.at[:, s], weight.at[:, s], local_sem.at[2]
            ).wait()
            other = weight.at[:, mate_s]
            remote(other, other, mate_send.at[1], mate_recv.at[1], mate).wait_recv()
            other = taps.at[:, pl.ds(pl.multiple_of(mate_s * rows, rows), rows), :]
            remote(other, other, mate_send.at[2], mate_recv.at[2], mate).wait_recv()

            @pl.when(x == 1)
            def _():
                for origin in range(2):
                    taps_beside(origin, 1 - y).wait_recv()

        @pl.when((step == 1) & (chunk % 2 == 0))
        def _():
            tap_spectra(chunk // 2)

        @pl.when(tick == 2 * TOKEN_CHUNKS)
        def _():
            await_mate(1)

        owner = 2 * x + chunk // groups
        far = jnp.abs(z - owner)

        @pl.when(
            projects_early(chunk % groups, owner)
            & (((step == 1) & (far <= 1)) | ((step == 2) & (far == 2)))
        )
        def _():
            project(chunk % groups, owner)

        @pl.when(tick == 2 * TOKEN_CHUNKS)
        def _():
            await_beside(0)

        @pl.when((tick == 2 * TOKEN_CHUNKS + TOKEN_CHUNKS // 2) & at_end)
        def _():
            await_beside(1)

        guest = 2 * (1 - x) + (chunk // 2) % 2

        @pl.when((step == 2) & (chunk % 2 == 0) & projects_early(chunk // 4, guest))
        def _():
            project(chunk // 4, guest)

    await_mate(2)
    for by in range(1, chan_count):
        for of in range(2):
            view = sums.at[of, lax.rem(z + by, chan_count)]
            remote(
                view, view, sums_send.at[0], sums_recv.at[of, lax.rem(z + by, chan_count)], mate
            ).wait_recv()
    view = sums.at[1 - core, z]
    remote(view, view, sums_send.at[0], sums_recv.at[1 - core, z], mate).wait_recv()

    @blocks(length)
    def _(i):
        of, at = i // (rows // BLOCK), i % (rows // BLOCK)
        found = sums[of, 0, pl.ds(at, 1), :]
        for owner in range(1, chan_count):
            found = found + sums[of, owner, pl.ds(at, 1), :]
        found = lax.rsqrt(found / (chan_count * width) + EPSILON)
        scale[at_rows(i), :] = jnp.broadcast_to(found, (BLOCK, LANES)).T

    taps_mate().wait_send()

    @pl.when(x == 0)
    def _():
        taps_across(0).wait_send()
        taps_across(1).wait_send()

    def edge_copy(g):
        return remote(
            edge_out.at[g], edge.at[g], edge_send.at[0], edge_recv.at[g], across
        )

    def before_copy(g):
        return remote(
            signal.at[g], before.at[g], before_send.at[0], before_recv.at[g], across
        )

    def swap_copy(g):
        return remote(
            ready.at[g], full.at[z, g, core], swap_send.at[0], swap_recv.at[g], mate
        )

    line = Line(
        lambda owner, g, of: full.at[owner, g, of],
        chan_count,
        line_send,
        line_recv,
        lambda to: (y, s, to),
    )

    def projected(g, b, at):
        return (partial[g, at, b * LANES : (b + 1) * LANES] * scale[at, :]).astype(jnp.bfloat16)

    def featurize(g):
        @pl.when(x == 0)
        def _():
            for b in range(branches):
                edge_out[g, b] = projected(g, b, pl.ds(length - rim, rim))
                extended[b, 0:rim, :] = jnp.zeros((rim, LANES), jnp.float32)
            edge_copy(g).start()

        @blocks(length)
        def _(i):
            for b in range(branches):
                extended[b, pl.ds(pl.multiple_of(rim + i * BLOCK, rim), BLOCK), :] = projected(
                    g, b, at_rows(i)
                ).astype(jnp.float32)

        @pl.when(x == 1)
        def _():
            edge_copy(g).wait_recv()
            for b in range(branches):
                extended[b, 0:rim, :] = edge[g, b].astype(jnp.float32)

        chosen = lanes_of(core * share, g)
        coefficient = [
            [short[tap, b : b + 1, chosen] for b in range(branches)] for tap in range(SHORT)
        ]

        @blocks(length)
        def _(i):
            found = []
            for b in range(branches):
                value = jnp.zeros((BLOCK, LANES), jnp.float32)
                for tap in range(SHORT):
                    value = value + coefficient[tap][b] * extended[
                        b, pl.ds(rim - tap + i * BLOCK, BLOCK), :
                    ]
                found.append(value.astype(jnp.bfloat16))
            query[at_rows(i), :] = found[0]
            signal[g, at_rows(i), :] = (
                found[1].astype(jnp.float32) * found[2].astype(jnp.float32)
            ).astype(jnp.bfloat16)

    def convolve(g):
        joint = (x == 1) & (g > 0)

        @pl.when(jnp.logical_not(joint))
        def _():
            spectrum(0, lambda: signal[g])

        def product(i, which, first):
            low, high = at_rows(i), rows_at(i, BLOCK, length)
            cos, sin = freq[which, low, :], freq[which, high, :]
            real = spectra[g, first, low, :].astype(jnp.float32)
            imag = spectra[g, first + 1, low, :].astype(jnp.float32)
            return cos * real + sin * imag, sin * real - cos * imag

        @pl.when(x == 0)
        def _():
            @blocks(length)
            def _(i):
                real, imag = product(i, 0, 0)
                mixed[at_rows(i), :] = real.astype(jnp.bfloat16)
                mixed[rows_at(i, BLOCK, length), :] = imag.astype(jnp.bfloat16)

        @pl.when(x == 1)
        def _():
            before_copy(g).wait_recv()

            @pl.when(g == 0)
            def _():
                spectrum(1, lambda: before[g])

            @pl.when(g > 0)
            def _():
                spectrum_pair(lambda: [signal[g], before[g]])

            @blocks(length)
            def _(i):
                real, imag = product(i, 0, 0)
                more_real, more_imag = product(i, 1, 2)
                mixed[at_rows(i), :] = (real + more_real).astype(jnp.bfloat16)
                mixed[rows_at(i, BLOCK, length), :] = (imag + more_imag).astype(jnp.bfloat16)

        @pl.loop(0, length // SPAN)
        def _(i):
            low, high = rows_at(i, SPAN), rows_at(i, SPAN, length)
            freq[0, low, :] = jnp.dot(
                table[low, :], mixed[:length, :], preferred_element_type=jnp.float32
            ) + jnp.dot(table[high, :], mixed[length:, :], preferred_element_type=jnp.float32)

        direct = skip[:, lanes_of(core * share, g)]

        def gated(at):
            longer = freq[0, at, :] + direct * signal[g, at, :].astype(jnp.float32)
            longer = longer.astype(jnp.bfloat16).astype(jnp.float32)
            return (query[at, :].astype(jnp.float32) * longer).astype(jnp.bfloat16)

        @blocks(rows)
        def _(i):
            full[z, g, core, at_rows(i), :] = gated(
                pl.ds(pl.multiple_of(core * rows + i * BLOCK, BLOCK), BLOCK)
            )
            ready[g, at_rows(i), :] = gated(
                pl.ds(pl.multiple_of((1 - core) * rows + i * BLOCK, BLOCK), BLOCK)
            )

    def load_out():
        for owner in range(chan_count):
            pltpu.make_async_copy(
                out_weight.at[pl.ds(owner * length, length)], stream.at[owner], local_sem.at[1]
            ).start()

    def accumulate(owner, g):
        @pl.loop(0, total.shape[1] // (8 * LANES))
        def _(i):
            cols = rows_at(i, 8 * LANES)
            block = jnp.concatenate([full[owner, g, 0], full[owner, g, 1]], axis=1)
            kernel = jnp.concatenate(
                [stream[owner, lanes_of(of * share, g), cols] for of in range(2)], axis=0
            )
            total[:, cols] += jnp.dot(block, kernel, preferred_element_type=jnp.float32)

    def begin(g):
        swap_copy(g).start()
        for way in range(2):

            @pl.when(line.sends(way, 0))
            def _():
                line.copy(way, 0, (g, core)).start()

    def begin_other(g):
        other = full.at[z, g, 1 - core]
        remote(other, other, swap_send.at[0], swap_recv.at[g], mate).wait_recv()
        for way in range(2):

            @pl.when(line.sends(way, 0))
            def _():
                line.copy(way, 0, (g, 1 - core)).start()

    def settle():
        other = weight.at[:, s]
        remote(other, other, mate_send.at[1], mate_recv.at[1], mate).wait_send()
        for copy in sum_copies:
            copy.wait_send()

        @pl.when(x == 1)
        def _():
            for origin in range(2):
                taps_beside(origin, y).wait_send()

        for at in range(2):
            view = weight_half(s, y)
            remote(view, view, x_send.at[at], x_recv.at[0, 0, 0], across).wait_send()
            view = weight_half((1 - x) * 2 + at, y)
            remote(view, view, y_send.at[at], y_recv.at[at, 0], beside).wait_send()

        @pl.when(x == 0)
        def _():
            remote(edge_out, edge, edge_send.at[0], edge_recv.at[0], across).wait_send()
            remote(signal, before, before_send.at[0], before_recv.at[0], across).wait_send()

    def settle_tokens():
        mate_tokens().wait_send()
        for way in range(2):
            for step in range(steps):

                @pl.when(token_line.receives(way, step))
                def _():
                    mate_half(way, step, core).wait_send()

                @pl.when(token_line.sends(way, step))
                def _():
                    token_line.drain(way, step, (0,), lambda owner: own_half(owner, core))

    def way_of(k):
        return jnp.where(z < chan_count // 2, 1 - k, k)

    def late_forwards(g, at, inner, outer):
        for here, pieces in ((jnp.logical_not(at_end), inner), (at_end, outer)):

            @pl.when((g == at) & here)
            def _():
                for group, c in pieces:
                    forward(group, c)

    def pass_on(way, step, at):
        @pl.when(
            (at >= 0) & (at < groups) & line.receives(way, step) & line.sends(way, step + 1)
        )
        def _():
            for of in (core, 1 - core):
                line.arrived(way, step, (at, of))
                line.copy(way, step + 1, (at, of)).start()

    for copy in small_loads[1:]:
        copy.wait()
    near, away = way_of(0), way_of(1)

    @pl.loop(0, groups)
    def _(g):
        @pl.when(g == 3)
        def _():
            pass_on(away, 0, 1)
            pass_on(near, 0, 2)

        @pl.when((g >= 2) | ((g == 1) & jnp.logical_not(at_end)))
        def _():
            await_beside(g)

        @pl.loop(0, chan_count)
        def _(owner):
            @pl.when(jnp.logical_not(projects_early(g, owner)))
            def _():
                project(g, owner)

        @pl.when(g == groups - 1)
        def _():
            settle_tokens()
            load_out()

        featurize(g)

        @pl.when(x == 0)
        def _():
            before_copy(g).start()

            for at, inner, outer in (
                (0, [(groups - 2, 2)], [(groups - 1, 2)]),
                (1, [(groups - 2, 3), (groups - 1, 0), (groups - 1, 1)], [(groups - 1, 3)]),
                (2, [(groups - 1, 2), (groups - 1, 3)], []),
            ):

                @pl.when((g == at) & jnp.logical_not(at_end))
                def _():
                    for group, c in inner:
                        send_weights(group, [c])

                @pl.when((g == at) & at_end)
                def _():
                    for group, c in outer:
                        send_weights(group, [c])

        @pl.when(g == 1)
        def _():
            pass_on(near, 0, 0)

        late_forwards(g, 1, [], [(groups - 1, 0), (groups - 1, 1)])
        late_forwards(g, 2, [(groups - 1, 0), (groups - 1, 1)], [(groups - 1, 3)])

        @pl.when(g == 2)
        def _():
            pass_on(near, 0, 1)
            pass_on(away, 0, 0)

        @pl.when(g == 3)
        def _():
            pass_on(near, 1, 1)
            pass_on(away, 0, 2)

        late_forwards(g, 0, [], [(groups - 2, 2), (groups - 2, 3)])
        convolve(g)
        begin(g)
        late_forwards(g, 0, [(groups - 2, 2)], [])
        late_forwards(g, 1, [(groups - 2, 3)], [(groups - 1, 2)])
        begin_other(g)

        late_forwards(g, 2, [(groups - 1, 2), (groups - 1, 3)], [])

        @pl.when(g == 2)
        def _():
            pass_on(near, 1, 0)

    pltpu.make_async_copy(stream, stream, local_sem.at[1]).wait()

    @pl.loop(0, groups + steps - 1)
    def _(n):
        for at, pieces in (
            (0, [(near, 1, 2)]),
            (1, [(away, 0, 3), (near, 0, 3)]),
            (3, [(near, 1, 3)]),
        ):

            @pl.when(n == at)
            def _():
                for way, step, group in pieces:
                    pass_on(way, step, group)

        @pl.when(n == 2)
        def _():
            settle()

        @pl.when(n < groups)
        def _():
            accumulate(z, n)

        @pl.loop(0, 2)
        def _(way):
            for step in range(steps):
                at = n - jnp.where(at_end, step, 0)

                @pl.when((at >= 0) & (at < groups) & line.receives(way, step))
                def _():
                    @pl.when(jnp.logical_not(line.sends(way, step + 1)))
                    def _():
                        for of in range(2):
                            line.arrived(way, step, (at, of))

                    accumulate(line.source(way, step), at)

    @blocks(rows)
    def _(i):
        result[at_rows(i), :] = total[at_rows(i), :].astype(jnp.bfloat16)

    remote(ready, ready, swap_send.at[0], swap_recv.at[0], mate).wait_send()
    for way in range(2):
        for step in range(steps):

            @pl.when(line.sends(way, step))
            def _():
                line.drain(way, step, (0, 0), lambda owner: full.at[owner])


def chip_body(tokens, norm_gain, proj_weight, short_filter, long_filter, skip_gain, out_weight):
    chan_count = lax.axis_size("chan")
    rows, width = tokens.shape
    depth, branches, local_chan = proj_weight.shape
    length, share = 2 * rows, local_chan // 2
    groups = share // LANES
    steps = chan_count - 1
    dma = pltpu.SemaphoreType.DMA
    f32, bf16 = jnp.float32, jnp.bfloat16
    vmem = pl.BlockSpec(memory_space=pltpu.VMEM)
    return pl.pallas_call(
        functools.partial(block_kernel, chan_count),
        out_shape=jax.ShapeDtypeStruct((rows, width), bf16),
        in_specs=[HBM] * 7,
        out_specs=vmem,
        scratch_shapes=[
            pltpu.VMEM((1, width), f32),
            pltpu.VMEM(short_filter.shape, f32),
            pltpu.VMEM((1, local_chan), f32),
            pltpu.VMEM((chan_count, length, width), bf16),
            pltpu.VMEM((groups, 4, depth, branches * LANES), bf16),
            pltpu.VMEM((2, chan_count, 8, LANES), f32),
            pltpu.VMEM((length, LANES), f32),
            pltpu.VMEM((groups, length, branches * LANES), f32),
            pltpu.VMEM((2 * length, length), bf16),
            pltpu.VMEM((groups, 2 * length, LANES), bf16),
            pltpu.VMEM((groups, 4, length, LANES), bf16),
            pltpu.VMEM((2, 2 * length, LANES), f32),
            pltpu.VMEM((2 * length, LANES), bf16),
            pltpu.VMEM((groups, branches, 16, LANES), bf16),
            pltpu.VMEM((groups, branches, 16, LANES), bf16),
            pltpu.VMEM((branches, length + 16, LANES), f32),
            pltpu.VMEM((length, LANES), bf16),
            pltpu.VMEM((groups, length, LANES), bf16),
            pltpu.VMEM((groups, length, LANES), bf16),
            pltpu.VMEM((groups, rows, LANES), bf16),
            pltpu.VMEM((chan_count, groups, 2, rows, LANES), bf16),
            pltpu.VMEM((rows, width), f32),
            dma((10,)),
            dma((3 + 2 * steps,)),
            dma((3 + 2 * steps,)),
            dma((2, steps)),
            dma((steps, TOKEN_CHUNKS)),
            dma((2 * chan_count - 1,)),
            dma((2, chan_count)),
            dma((2,)),
            dma((2, groups, WEIGHT_CHUNKS)),
            dma((2,)),
            dma((2, groups)),
            dma((4,)),
            dma((4,)),
            dma((1,)),
            dma((groups,)),
            dma((1,)),
            dma((groups,)),
            dma((1,)),
            dma((groups,)),
            dma((2, steps)),
            dma((steps, groups, 2)),
        ],
        compiler_params=pltpu.CompilerParams(
            collective_id=0, has_side_effects=True, vmem_limit_bytes=52 * 1024 * 1024
        ),
        name="block",
    )(
        tokens,
        pltpu.with_memory_space_constraint(norm_gain[None, :], pltpu.HBM),
        proj_weight.transpose(1, 0, 2),
        pltpu.with_memory_space_constraint(short_filter, pltpu.HBM),
        long_filter,
        pltpu.with_memory_space_constraint(skip_gain[None, :], pltpu.HBM),
        out_weight,
    )


def select_body(mesh):
    if (mesh.shape["groups"], mesh.shape["seq"], mesh.shape["chan"]) == (2, 4, 4):
        return chip_body
    return body


def solution(mesh):
    placed = (
        P(("groups", "seq"), "chan"),
        P(),
        P("seq", None, "chan"),
        P(None, None, "chan"),
        P("chan", "seq"),
        P("chan"),
        P(None, "chan"),
    )
    return jax.shard_map(
        select_body(mesh), mesh=mesh, in_specs=placed, out_specs=P(("groups", "seq"), "chan"), check_vma=False
    )
```
